32 devices in a mesh: dp: 4 (over y, x), seq: 2 (over core), tensor: 4 (over z).
Axes of the slice: x: 2, y: 2, z: 4, core: 2. Of those that a mesh axis runs over, the one named last changes fastest.
Arguments:
- tokens: bfloat16 [8, 512, 1536], P('dp', ('seq', 'tensor')), may hold values from -6 to 6
- segments: int32 [8, 512], P('dp', 'seq'), may hold values from 0 to 3, never falling along the last dimension, each value on 1 to 192 neighbouring positions
- input_gain: float32 [1536], replicated, may hold values from 0.5 to 1.5
- gate_proj: bfloat16 [1536, 3072], P(('dp', 'seq'), 'tensor'), may hold values from -0.15625 to 0.15625
- inner_proj: bfloat16 [1536, 3072], P(('dp', 'seq'), 'tensor'), may hold values from -0.15625 to 0.15625
- state_proj: bfloat16 [1536, 256], P(('dp', 'seq')), may hold values from -0.15625 to 0.15625
- step_proj: bfloat16 [1536, 48], P(('dp', 'seq'), 'tensor'), may hold values from -0.15625 to 0.15625
- conv_inner: float32 [4, 3072], replicated, may hold values from -3 to 3
- inner_bias: float32 [3072], replicated, may hold values from -0.5 to 0.5
- conv_state: float32 [4, 256], replicated, may hold values from -3 to 3
- state_bias: float32 [256], replicated, may hold values from -0.5 to 0.5
- step_bias: float32 [48], replicated, may hold values from -4.6 to -2.3
- log_rates: float32 [48], replicated, may hold values from -5.8 to 0.7
- skip_gain: float32 [48], replicated, may hold values from 0.5 to 1.5
- gated_gain: float32 [3072], replicated, may hold values from 0.5 to 1.5
- output_proj: bfloat16 [3072, 1536], P('tensor', ('dp', 'seq')), may hold values from -0.109375 to 0.109375
- cotangent: bfloat16 [8, 512, 1536], P('dp', ('seq', 'tensor')), may hold values from -6 to 6
Outputs:
- block_out: bfloat16 [8, 512, 1536], P('dp', ('seq', 'tensor'))
- grad_tokens: float32 [8, 512, 1536], P('dp', ('seq', 'tensor'))
- grad_input_gain: float32 [1536], replicated
- grad_gate_proj: float32 [1536, 3072], P(('dp', 'seq'), 'tensor')
- grad_inner_proj: float32 [1536, 3072], P(('dp', 'seq'), 'tensor')
- grad_state_proj: float32 [1536, 256], P(('dp', 'seq'))
- grad_step_proj: float32 [1536, 48], P(('dp', 'seq'), 'tensor')
- grad_conv_inner: float32 [4, 3072], replicated
- grad_inner_bias: float32 [3072], replicated
- grad_conv_state: float32 [4, 256], replicated
- grad_state_bias: float32 [256], replicated
- grad_step_bias: float32 [48], replicated
- grad_log_rates: float32 [48], replicated
- grad_skip_gain: float32 [48], replicated
- grad_gated_gain: float32 [3072], replicated
- grad_output_proj: float32 [3072, 1536], P('tensor', ('dp', 'seq'))
The draws below stay inside these ranges and needn't reach their ends.
Inputs may be any that keep to these rules, and one draw needn't show every extreme that they name: `segments`: segment ids never fall along a sequence; a document has at most 3 * 512 // (2 * max(4, 0)) tokens.
All inputs are finite; a program needn't handle non-finite values.
Results may differ from the reference program's by a relative error of at most 0.012.
The reference program's roundings to bfloat16 on the way (of `normed` and `gate_normed`) count: a program that leaves them out, or rounds other values in their place, can miss the bound.
Values may be sent and summed in bfloat16 or wider, within the bound.
A program may use at most 128 MiB of HBM per device.

```python
import math
import jax
import jax.numpy as jnp
import numpy as np
from jax import lax

D = 1536
HEADS = 48
HEAD_DIM = 64
STATE = 128
KERNEL = 4
BLOCK = 256
DI = 3072
LEN = 512
SEQS = 8


def steps_of(key, shape, cuts, least, top_value):
    def one(dim, shards_of):
        draws = jax.random.uniform(jax.random.fold_in(jax.random.fold_in(key, 6), dim), (shards_of,), jnp.float32, least / len(cuts), top_value / len(cuts))
        return jnp.repeat(jnp.exp(draws), shape[dim] // shards_of).reshape((-1,) + (1,) * (len(shape) - dim - 1))

    gain = one(*cuts[0])
    for cut in cuts[1:]:
        gain = gain * one(*cut)
    return gain


def split_up(amount, total, bound, slope):
    loads = [(1 << 20) // math.isqrt(standing ** slope) + 1 for standing in range(2, amount + 1)]
    rest, given = total - bound - (amount - 1), [1] * (amount - 1)
    while rest > 0:
        candidates = [i for i in range(amount - 1) if given[i] < bound]
        whole, remaining = sum([loads[i] for i in candidates]), rest
        for i in candidates:
            addition = min(bound - given[i], max(1, remaining * loads[i] // whole), rest)
            given[i] = given[i] + addition
            rest = rest - addition
    return np.array([bound] + given)


def ragged(rng, amount, total, most, slope):
    if amount == 2:
        one = jax.random.randint(rng, (), max(1, total - most), min(most, total - 1) + 1)
        return jnp.stack([one, total - one])
    sizes = jnp.asarray(split_up(amount, total, most, slope), jnp.int32)
    twos = (amount - 1) // 2
    donor, sink = sizes[1:1 + 2 * twos:2], sizes[2:2 + 2 * twos:2]
    margin = jnp.minimum(donor - 1, most - sink)
    passed = jax.random.randint(jax.random.fold_in(rng, 1), (twos,), 0, 1 << 20) % (margin + 1)
    sizes = sizes.at[1:1 + 2 * twos:2].set(donor - passed).at[2:2 + 2 * twos:2].set(sink + passed)
    return sizes[jax.random.permutation(jax.random.fold_in(rng, 2), amount)]


def noise(own_key, extent, spread, reach, cuts=(), held_as=jnp.bfloat16):
    values = spread * jax.random.normal(own_key, extent, jnp.float32)
    if cuts:
        values = values * steps_of(own_key, extent, cuts, -0.22, 0.18)
    return jnp.clip(values, -reach, reach).astype(held_as)


def setup_inputs(seed: int = 0) -> dict:
    key_of = jax.random.split(jax.random.key(seed), 18)
    tokens = noise(key_of[0], (SEQS, LEN, D), 1.0, 6.0, ((0, 4), (1, 8)))
    segments = jax.vmap(lambda own: jnp.searchsorted(jnp.cumsum(ragged(own, max(4, LEN // 1024), LEN, 3 * LEN // (2 * max(4, LEN // 1024)), 1)), jnp.arange(LEN), side="right"))(jax.random.split(key_of[1], SEQS)).reshape((SEQS, LEN)).astype(jnp.int32)
    input_gain = jnp.clip(1.0 + 0.1 * jax.random.normal(key_of[2], (D,), jnp.float32), 0.5, 1.5)
    gate_proj = noise(key_of[3], (D, DI), D ** -0.5, 0.15625, ((0, 8), (1, 4)))
    inner_proj = noise(key_of[4], (D, DI), D ** -0.5, 0.15625, ((0, 8), (1, 4)))
    state_proj = noise(key_of[5], (D, 2 * STATE), D ** -0.5, 0.15625, ((0, 8),))
    step_proj = noise(key_of[6], (D, HEADS), D ** -0.5, 0.15625, ((0, 8), (1, 4)))
    conv_inner = noise(key_of[7], (KERNEL, DI), KERNEL ** -0.5, 3.0, (), jnp.float32)
    inner_bias = jnp.clip(jax.random.uniform(key_of[8], (DI,), jnp.float32, -0.5, 0.5), -0.5, 0.5)
    conv_state = noise(key_of[9], (KERNEL, 2 * STATE), KERNEL ** -0.5, 3.0, (), jnp.float32)
    state_bias = jnp.clip(jax.random.uniform(key_of[10], (2 * STATE,), jnp.float32, -0.5, 0.5), -0.5, 0.5)
    step_bias = jnp.clip(jax.random.uniform(key_of[11], (HEADS,), jnp.float32, -4.6, -2.3), -4.6, -2.3)
    log_rates = jnp.clip(jax.random.uniform(key_of[12], (HEADS,), jnp.float32, -5.8, 0.7), -5.8, 0.7)
    skip_gain = jnp.clip(jax.random.uniform(key_of[13], (HEADS,), jnp.float32, 0.5, 1.5), 0.5, 1.5)
    gated_gain = jnp.clip(1.0 + 0.1 * jax.random.normal(key_of[14], (DI,), jnp.float32), 0.5, 1.5)
    output_proj = noise(key_of[15], (DI, D), DI ** -0.5, 0.109375, ((0, 4), (1, 8)))
    cotangent = noise(key_of[16], (SEQS, LEN, D), 1.0, 6.0, ((0, 4), (1, 8)))
    return {"tokens": tokens, "segments": segments, "input_gain": input_gain, "gate_proj": gate_proj, "inner_proj": inner_proj, "state_proj": state_proj, "step_proj": step_proj, "conv_inner": conv_inner, "inner_bias": inner_bias, "conv_state": conv_state, "state_bias": state_bias, "step_bias": step_bias, "log_rates": log_rates, "skip_gain": skip_gain, "gated_gain": gated_gain, "output_proj": output_proj, "cotangent": cotangent}


@jax.custom_vjp
def low(v):
    return lax.optimization_barrier(v.astype(jnp.bfloat16)).astype(jnp.float32)

@jax.custom_vjp
def low_back(v):
    return v

def low_keep(v):
    return (low(v), None)

def low_pass(kept, grad):
    return (grad,)

def back_keep(v):
    return (v, None)

def back_low(kept, grad):
    return (low(grad),)
low.defvjp(low_keep, low_pass)
low_back.defvjp(back_keep, back_low)
HIGH = lax.Precision.HIGHEST
EPS = 1e-05

def shifted_mix(values_in, seg_ids, kernel_w, kernel_b):
    length = values_in.shape[0]
    result = kernel_b[None, :] + kernel_w[0][None, :] * values_in
    for offset in range(1, KERNEL):
        moved = jnp.concatenate([jnp.zeros((offset, values_in.shape[1]), jnp.float32), values_in[:length - offset]], axis=0)
        seg_moved = jnp.concatenate([jnp.full((offset,), -1, jnp.int32), seg_ids[:length - offset]])
        same_doc = (seg_moved == seg_ids).astype(jnp.float32)
        result = result + kernel_w[offset][None, :] * moved * same_doc[:, None]
    return result

def block_step(memory, element):
    inner, deltas, log_decay, b_proj, c_proj, seg_ids, before = element
    running = jnp.cumsum(log_decay, axis=0)
    places = jnp.arange(BLOCK)
    allowed = (seg_ids[:, None] == seg_ids[None, :]) & (places[:, None] >= places[None, :])
    inside = allowed[:, :, None]
    decays = jnp.where(inside, jnp.exp(jnp.where(inside, running[:, None, :] - running[None, :, :], 0.0)), 0.0)
    scores = jnp.dot(c_proj, b_proj.T, precision=HIGH)
    mixing = decays * scores[:, :, None] * deltas[None, :, :]
    direct = jnp.einsum('ijh,jhp->ihp', mixing, inner, precision=HIGH)
    entry = jnp.exp(running) * (seg_ids == before).astype(jnp.float32)[:, None]
    from_state = jnp.einsum('in,hpn->ihp', c_proj, memory, precision=HIGH) * entry[:, :, None]
    to_end = jnp.exp(running[-1][None, :] - running) * (seg_ids == seg_ids[-1]).astype(jnp.float32)[:, None] * deltas
    inflow = jnp.einsum('jhp,jn->hpn', to_end[:, :, None] * inner, b_proj, precision=HIGH)
    passing = jnp.exp(running[-1]) * (seg_ids[-1] == before).astype(jnp.float32)
    return (passing[:, None, None] * memory + inflow, direct + from_state)

def state_space(inner, deltas, log_decay, b_proj, c_proj, seg_ids):
    length = inner.shape[0]
    pieces = length // BLOCK
    before_all = jnp.concatenate([jnp.full((1,), -1, jnp.int32), seg_ids[:-1]])
    elements = (inner.reshape(pieces, BLOCK, HEADS, HEAD_DIM), deltas.reshape(pieces, BLOCK, HEADS), log_decay.reshape(pieces, BLOCK, HEADS), b_proj.reshape(pieces, BLOCK, STATE), c_proj.reshape(pieces, BLOCK, STATE), seg_ids.reshape(pieces, BLOCK), before_all[::BLOCK])
    initial = jnp.zeros((HEADS, HEAD_DIM, STATE), jnp.float32)
    unused, outputs = lax.scan(jax.checkpoint(block_step), initial, elements)
    return outputs.reshape(length, HEADS, HEAD_DIM)

def layer_forward(values_in, seg_ids, params):
    input_gain, gate_proj, inner_proj, state_proj, step_proj, conv_inner, inner_bias, conv_state, state_bias, step_bias, log_rates, skip_gain, gated_gain, output_proj = params
    rms_in = lax.rsqrt(lax.optimization_barrier(jnp.mean(values_in * values_in, axis=-1, keepdims=True)) + EPS)
    normed = low(values_in * rms_in * input_gain[None, :])
    gate_in = low_back(jnp.dot(normed, gate_proj, precision=HIGH))
    inner_pre = low_back(low(jnp.dot(normed, inner_proj, precision=HIGH)))
    state_pre = low_back(low(jnp.dot(normed, state_proj, precision=HIGH)))
    step_raw = low_back(jnp.dot(normed, step_proj, precision=HIGH))
    inner = jax.nn.silu(shifted_mix(inner_pre, seg_ids, conv_inner, inner_bias))
    both_maps = jax.nn.silu(shifted_mix(state_pre, seg_ids, conv_state, state_bias))
    b_proj = both_maps[:, :STATE]
    c_proj = both_maps[:, STATE:]
    deltas = jax.nn.softplus(step_raw + step_bias[None, :])
    log_decay = deltas * (-jnp.exp(log_rates))[None, :]
    heads_in = inner.reshape(-1, HEADS, HEAD_DIM)
    mixed = state_space(heads_in, deltas, log_decay, b_proj, c_proj, seg_ids) + skip_gain[None, :, None] * heads_in
    mixed = mixed.reshape(-1, DI)
    gated = mixed * jax.nn.silu(gate_in)
    rms_gate = lax.rsqrt(lax.optimization_barrier(jnp.mean(gated * gated, axis=-1, keepdims=True)) + EPS)
    gate_normed = low(gated * rms_gate * gated_gain[None, :])
    return values_in + low_back(jnp.dot(gate_normed, output_proj, precision=HIGH))

def reference(tokens, segments, input_gain, gate_proj, inner_proj, state_proj, step_proj, conv_inner, inner_bias, conv_state, state_bias, step_bias, log_rates, skip_gain, gated_gain, output_proj, cotangent):
    params = tuple((weight.astype(jnp.float32) for weight in (input_gain, gate_proj, inner_proj, state_proj, step_proj, conv_inner, inner_bias, conv_state, state_bias, step_bias, log_rates, skip_gain, gated_gain, output_proj)))

    def one_sequence(summed, element):
        rows_in, seg_ids, cot_in = element
        result, backward = jax.vjp(lambda values, weights: layer_forward(values, seg_ids, weights), rows_in, params)
        grad_rows, grad_params = backward(cot_in)
        return (jax.tree.map(jnp.add, summed, grad_params), (result.astype(jnp.bfloat16), grad_rows))
    grads, (outputs, grad_tokens) = lax.scan(one_sequence, jax.tree.map(jnp.zeros_like, params), (tokens.astype(jnp.float32), segments, cotangent.astype(jnp.float32)))
    return (outputs, grad_tokens, grads[0], grads[1], grads[2], grads[3], grads[4], grads[5], grads[6], grads[7], grads[8], grads[9], grads[10], grads[11], grads[12], grads[13])
```

```python
import functools

import jax
import jax.numpy as jnp
from jax import lax
from jax.experimental import pallas as pl
from jax.experimental.pallas import tpu as pltpu
from jax.sharding import PartitionSpec as P

HEAD_DIM = 64
STATE = 128
KERNEL = 4
BLOCK = 256


EPS = 1e-05
HIGH = lax.Precision.HIGHEST


def passed_along(block, axis, distance):
    devices = range(lax.axis_size(axis))
    route = [(i - distance, i) for i in devices if i - distance in devices]
    return lax.ppermute(block, axis, route)


def entering_2(shard, axis, join, neutral):
    place = lax.axis_index(axis)
    gathered = jax.tree.map(
        lambda a, kind: lax.all_gather(a.astype(kind), axis), shard, (jnp.bfloat16, jnp.bfloat16)
    )
    state = jax.tree.map(lambda a, e: jnp.zeros_like(a) + jnp.asarray(e, a.dtype), shard, neutral)

    def one(hop, state):
        return join(
            state,
            jax.tree.map(
                lambda a, own: lax.dynamic_index_in_dim(a, hop, 0, False).astype(own.dtype),
                gathered,
                shard,
            ),
        )

    return lax.fori_loop(0, place, one, state)


def carried_in(shard, axis, combine, identity):
    length, here = (lax.axis_size(axis), lax.axis_index(axis))
    everything = jax.tree.map(
        lambda part, kind: lax.all_gather(part.astype(kind), axis),
        shard,
        jax.tree.map(lambda a: jnp.bfloat16 if a.dtype == jnp.float32 else a.dtype, shard),
    )
    start = jax.tree.map(
        lambda part, zero: jnp.broadcast_to(jnp.asarray(zero, part.dtype), part.shape),
        shard,
        identity,
    )

    def hop(k, before):
        at = length - 1 - k
        reached = at > here
        new = combine(
            before, jax.tree.map(lambda part, own: part[at].astype(own.dtype), everything, shard)
        )
        return jax.tree.map(lambda a, b: jnp.where(reached, a, b), new, before)

    return lax.fori_loop(0, length, hop, start)


def chain_link(earlier, later):
    return (earlier[0] * later[0], later[0][:, :, None, None] * earlier[1] + later[1])


def causal_mix(padded, seg_padded, kernel_w, kernel_b):
    margin = KERNEL - 1
    length = padded.shape[1] - margin
    seg_now = seg_padded[:, margin:]
    result = kernel_b + kernel_w[0] * padded[:, margin:]
    for offset in range(1, KERNEL):
        moved = padded[:, margin - offset : margin - offset + length]
        same_doc = (seg_padded[:, margin - offset : margin - offset + length] == seg_now).astype(
            jnp.float32
        )
        result = result + kernel_w[offset] * moved * same_doc[:, :, None]
    return result


def blocked(values, pieces):
    return values.reshape((values.shape[0], pieces, values.shape[1] // pieces) + values.shape[2:])


def block_sums(inner, deltas, log_decay, b_proj, seg_blocks, before):
    pieces = seg_blocks.shape[1]
    running = jnp.cumsum(blocked(log_decay, pieces), axis=2)
    same_end = (seg_blocks == seg_blocks[:, :, -1:]).astype(jnp.float32)
    to_end = (
        jnp.exp(running[:, :, -1:, :] - running) * same_end[:, :, :, None] * blocked(deltas, pieces)
    )
    inflow = jnp.einsum(
        "scjhp,scjn->schpn",
        to_end[..., None] * blocked(inner, pieces),
        blocked(b_proj, pieces),
        precision=HIGH,
    )
    passing = (
        jnp.exp(running[:, :, -1, :])
        * (seg_blocks[:, :, -1] == before).astype(jnp.float32)[:, :, None]
    )
    return (inflow, passing)


def state_reads(incoming, log_decay, c_proj, inflow, passing, seg_blocks, before):
    pieces = seg_blocks.shape[1]
    running = jnp.cumsum(blocked(log_decay, pieces), axis=2)
    memory = incoming
    entering = [memory]
    memory = passing[:, 0, :, None, None] * memory + inflow[:, 0]
    stacked = jnp.stack(entering, axis=1)
    entry = jnp.exp(running) * (seg_blocks == before[:, :, None]).astype(jnp.float32)[..., None]
    from_state = (
        jnp.einsum("scin,schpn->scihp", blocked(c_proj, pieces), stacked, precision=HIGH)
        * entry[..., None]
    )
    return (from_state, memory)


MESH = pl.DeviceIdType.MESH
BF = jnp.bfloat16
F32 = jnp.float32


def _peers():
    dp, seq, t = lax.axis_index("dp"), lax.axis_index("seq"), lax.axis_index("tensor")
    x, y = lax.rem(dp, 2), lax.div(dp, 2)
    x_dp = dp + 1 - 2 * x
    y_dp = dp + 2 - 4 * y
    d_dp = 3 - dp
    return dp, seq, t, x_dp, y_dp, d_dp


def _dev(dp, seq, t):
    return {"dp": dp, "seq": seq, "tensor": t}


def _plane_barrier(n):
    dp, seq, t, x_dp, y_dp, d_dp = _peers()
    bar = pltpu.get_barrier_semaphore()
    for who in (_dev(dp, 1 - seq, t), _dev(x_dp, seq, t), _dev(y_dp, seq, t)):
        pl.semaphore_signal(bar, inc=1, device_id=who, device_id_type=MESH)

    for step in range(1, n):
        pl.semaphore_signal(
            bar, inc=1, device_id=_dev(dp, seq, lax.rem(t + step, n)), device_id_type=MESH
        )
    pl.semaphore_wait(bar, 3 + n - 1)


class _Line:
    def __init__(self, n, ref, rows, ssem, rsem, own=None):
        self.n, self.ref, self.rows, self.ssem, self.rsem = n, ref, rows, ssem, rsem
        self.own = own

    def block(self, o):
        return self.ref.at[:, pl.ds(pl.multiple_of(o * self.rows, self.rows), self.rows), :]

    def copy(self, o, direction, own=False):
        dp, seq, t = lax.axis_index("dp"), lax.axis_index("seq"), lax.axis_index("tensor")
        return pltpu.make_async_remote_copy(
            src_ref=self.own if own else self.block(o),
            dst_ref=self.block(o),
            send_sem=self.ssem.at[0 if direction > 0 else 1, o],
            recv_sem=self.rsem.at[o],
            device_id=_dev(dp, seq, t + direction),
            device_id_type=MESH,
        )

    def step(self, d):
        n, t = self.n, lax.axis_index("tensor")
        for way in (1, -1):
            o = t - way * d
            here = jnp.logical_and(o >= 0, o < n)
            nxt = jnp.logical_and(t + way >= 0, t + way < n)

            @pl.when(here)
            def _(o=o, way=way, nxt=nxt):
                if d > 0:
                    self.copy(o, way).wait_recv()

                @pl.when(nxt)
                def _():
                    self.copy(o, way, d == 0 and self.own is not None).start()

    def finish(self):
        n, t = self.n, lax.axis_index("tensor")
        for d in range(n):
            for way in (1, -1):
                o = t - way * d
                ok = jnp.logical_and(
                    jnp.logical_and(o >= 0, o < n),
                    jnp.logical_and(t + way >= 0, t + way < n),
                )

                @pl.when(ok)
                def _(o=o, way=way):
                    self.copy(o, way).wait_send()


class _Plane:
    def __init__(self, own, full, ssem, rsem, lsem):
        self.own, self.full, self.ssem, self.rsem, self.lsem = own, full, ssem, rsem, lsem

    def copy(self, src, block, who, s):
        return pltpu.make_async_remote_copy(
            src_ref=src,
            dst_ref=self.full.at[block],
            send_sem=self.ssem.at[s],
            recv_sem=self.rsem.at[s],
            device_id=who,
            device_id_type=MESH,
        )

    def begin(self):
        dp, seq, t, x_dp, y_dp, d_dp = _peers()
        me = dp * 2 + seq
        pltpu.make_async_copy(self.own, self.full.at[me], self.lsem).start()
        self.copy(self.own, me, _dev(x_dp, seq, t), 0).start()
        self.copy(self.own, me, _dev(y_dp, seq, t), 1).start()
        self.copy(self.own, me, _dev(dp, 1 - seq, t), 3).start()

    def forward(self):
        dp, seq, t, x_dp, y_dp, d_dp = _peers()
        bx, by = x_dp * 2 + seq, y_dp * 2 + seq
        self.copy(self.own, bx, _dev(x_dp, seq, t), 0).wait_recv()
        self.copy(self.own, by, _dev(y_dp, seq, t), 1).wait_recv()

        @pl.when(seq == 0)
        def _():
            self.copy(self.full.at[by], by, _dev(x_dp, seq, t), 2).start()

        @pl.when(seq == 1)
        def _():
            self.copy(self.full.at[bx], bx, _dev(y_dp, seq, t), 2).start()

        self.copy(self.full.at[bx], bx, _dev(dp, 1 - seq, t), 4).start()
        self.copy(self.full.at[by], by, _dev(dp, 1 - seq, t), 5).start()

    def share(self):
        dp, seq, t, x_dp, y_dp, d_dp = _peers()
        bd = d_dp * 2 + seq
        self.copy(self.own, bd, _dev(x_dp, seq, t), 2).wait_recv()
        self.copy(self.full.at[bd], bd, _dev(dp, 1 - seq, t), 6).start()

    def arrive(self):
        dp, seq, t, x_dp, y_dp, d_dp = _peers()
        me = dp * 2 + seq
        pltpu.make_async_copy(self.own, self.full.at[me], self.lsem).wait()
        for s in (3, 4, 5, 6):
            self.copy(self.own, me, _dev(dp, 1 - seq, t), s).wait_recv()

    def finish(self):
        dp, seq, t, x_dp, y_dp, d_dp = _peers()
        me = dp * 2 + seq
        for s in range(7):
            self.copy(self.own, me, _dev(dp, 1 - seq, t), s).wait_send()


def gather_kernel(n, tok, gain, wg, wi, ws, wt, normed, fg, fi, fs, ft, zs, zr, ps, pr, ls):
    t = lax.axis_index("tensor")
    rows = tok.shape[1]
    _plane_barrier(n)
    planes = [
        _Plane(own, full, ps.at[i], pr.at[i], ls.at[i])
        for i, (own, full) in enumerate(((ws, fs), (wt, ft), (wi, fi), (wg, fg)))
    ]
    for p in planes[:3]:
        p.begin()
    mine = pl.ds(pl.multiple_of(t * rows, rows), rows)
    for s in range(tok.shape[0]):
        v = tok[s].astype(F32)
        rms = lax.rsqrt(jnp.mean(v * v, axis=-1, keepdims=True) + EPS)
        normed[s, mine, :] = (v * rms * gain[...]).astype(BF)
    a = _Line(n, normed, rows, zs, zr)
    a.step(0)
    planes[3].begin()
    for p in planes[:3]:
        p.forward()
    a.step(1)
    planes[3].forward()
    for p in planes[:3]:
        p.share()
    for d in range(2, n):
        a.step(d)
    planes[3].share()
    for p in planes:
        p.arrive()
    a.finish()
    for p in planes:
        p.finish()


def gather_all(n, tokens, gain, weights):
    seqs, rows, width = tokens.shape
    vm = pl.BlockSpec(memory_space=pltpu.VMEM)
    full = lambda w: jax.ShapeDtypeStruct((8,) + w.shape, w.dtype)
    act = jax.ShapeDtypeStruct((seqs, n * rows, width), BF)
    return pl.pallas_call(
        functools.partial(gather_kernel, n),
        out_shape=(act,) + tuple(full(w) for w in weights),
        in_specs=[vm] * 6,
        out_specs=(vm,) * 5,
        scratch_shapes=[
            pltpu.SemaphoreType.DMA((2, n)),
            pltpu.SemaphoreType.DMA((n,)),
            pltpu.SemaphoreType.DMA((4, 7)),
            pltpu.SemaphoreType.DMA((4, 7)),
            pltpu.SemaphoreType.DMA((4,)),
        ],
        compiler_params=pltpu.CompilerParams(
            collective_id=0, has_side_effects=True, vmem_limit_bytes=60 << 20
        ),
        name="gather_all",
    )(tokens, gain.reshape(1, width), *weights)


def _line_reduce(n, part, left, right, ssem, rsem):
    dp, seq, t = lax.axis_index("dp"), lax.axis_index("seq"), lax.axis_index("tensor")
    rows = left.shape[2]

    def copy(src, box, o, way):
        return pltpu.make_async_remote_copy(
            src_ref=src, dst_ref=box.at[o],
            send_sem=ssem.at[0 if way > 0 else 1, o], recv_sem=rsem.at[0 if way > 0 else 1, o],
            device_id=_dev(dp, seq, t + way), device_id_type=MESH,
        )

    def block(o):
        return part.at[:, pl.ds(pl.multiple_of(o * rows, rows), rows), :]

    def step(k):
        for way, box, place in ((1, left, t), (-1, right, n - 1 - t)):
            target = lambda j: n - 1 - j if way > 0 else j
            if k == 0:
                @pl.when(place == 0)
                def _():
                    for j in range(n - 1):
                        copy(block(target(j)), box, target(j), way).start()
            else:
                @pl.when(jnp.logical_and(place > 0, place <= k))
                def _():
                    o = target(k - place)
                    copy(block(o), box, o, way).wait_recv()
                    for s in range(part.shape[0]):
                        own = part[s, pl.ds(pl.multiple_of(o * rows, rows), rows), :].astype(F32)
                        box[o, s] = (box[o, s].astype(F32) + own).astype(BF)
                    copy(box.at[o], box, o, way).start()

    def final(out):
        mine = pl.ds(pl.multiple_of(t * rows, rows), rows)
        for s in range(part.shape[0]):
            out[s] = part[s, mine, :].astype(F32)

        @pl.when(t > 0)
        def _():
            copy(left.at[0], left, t, 1).wait_recv()
            for s in range(part.shape[0]):
                out[s] = out[s] + left[t, s].astype(F32)

        @pl.when(t < n - 1)
        def _():
            copy(left.at[0], right, t, -1).wait_recv()
            for s in range(part.shape[0]):
                out[s] = out[s] + right[t, s].astype(F32)

    def finish():
        for j in range(n - 1):
            for way, box, o in ((1, left, n - 1 - j), (-1, right, j)):
                sends = (t < o) if way > 0 else (t > o)

                @pl.when(sends)
                def _():
                    copy(box.at[o], box, o, way).wait_send()

    return step, final, finish


class _PlaneReduce:
    def __init__(self, part, pair, box, ssem, rsem):
        self.part, self.pair, self.box, self.ssem, self.rsem = part, pair, box, ssem, rsem

    def copy(self, src, dst, who, s):
        return pltpu.make_async_remote_copy(
            src_ref=src, dst_ref=dst, send_sem=self.ssem.at[s], recv_sem=self.rsem.at[s],
            device_id=who, device_id_type=MESH,
        )

    def begin(self):
        dp, seq, t, x_dp, y_dp, d_dp = _peers()
        for slot, chip in enumerate((d_dp, x_dp, y_dp, dp)):
            self.copy(self.part.at[chip * 2 + 1 - seq], self.pair.at[slot], _dev(dp, 1 - seq, t), slot).start()

    def _paired(self, slot, chip, also=None):
        dp, seq, t, x_dp, y_dp, d_dp = _peers()
        self.copy(self.pair.at[slot], self.pair.at[slot], _dev(dp, 1 - seq, t), slot).wait_recv()
        v = self.part[chip * 2 + seq].astype(F32) + self.pair[slot].astype(F32)
        self.pair[slot] = v.astype(BF)

    def send_far(self):
        dp, seq, t, x_dp, y_dp, d_dp = _peers()
        for slot, chip in enumerate((d_dp, x_dp, y_dp)):
            self._paired(slot, chip)
            if slot == 0:
                @pl.when(seq == 0)
                def _():
                    self.copy(self.pair.at[0], self.box.at[2], _dev(x_dp, seq, t), 4).start()

                @pl.when(seq == 1)
                def _():
                    self.copy(self.pair.at[0], self.box.at[2], _dev(y_dp, seq, t), 4).start()

        @pl.when(seq == 0)
        def _():
            self.copy(self.pair.at[1], self.box.at[0], _dev(x_dp, seq, t), 5).start()

        @pl.when(seq == 1)
        def _():
            self.copy(self.pair.at[2], self.box.at[1], _dev(y_dp, seq, t), 6).start()

    def send_near(self):
        dp, seq, t, x_dp, y_dp, d_dp = _peers()
        self.copy(self.pair.at[0], self.box.at[2], _dev(dp, seq, t), 4).wait_recv()

        @pl.when(seq == 0)
        def _():
            self.box[2] = (self.box[2].astype(F32) + self.pair[2].astype(F32)).astype(BF)
            self.copy(self.box.at[2], self.box.at[1], _dev(y_dp, seq, t), 6).start()

        @pl.when(seq == 1)
        def _():
            self.box[2] = (self.box[2].astype(F32) + self.pair[1].astype(F32)).astype(BF)
            self.copy(self.box.at[2], self.box.at[0], _dev(x_dp, seq, t), 5).start()

    def final(self, out):
        dp, seq, t, x_dp, y_dp, d_dp = _peers()
        self.copy(self.pair.at[3], self.pair.at[3], _dev(dp, seq, t), 3).wait_recv()
        self.copy(self.pair.at[0], self.box.at[0], _dev(dp, seq, t), 5).wait_recv()
        self.copy(self.pair.at[0], self.box.at[1], _dev(dp, seq, t), 6).wait_recv()
        out[...] = (
            self.part[dp * 2 + seq].astype(F32) + self.pair[3].astype(F32)
            + self.box[0].astype(F32) + self.box[1].astype(F32)
        )

    def finish(self):
        dp, seq, t, x_dp, y_dp, d_dp = _peers()
        for s in range(7):
            self.copy(self.pair.at[0], self.box.at[0], _dev(dp, 1 - seq, t), s).wait_send()


class _Smalls:
    def __init__(self, n, box, line, ssem, rsem):
        self.n, self.box, self.line, self.ssem, self.rsem = n, box, line, ssem, rsem

    def copy(self, j, who):
        return pltpu.make_async_remote_copy(
            src_ref=self.box.at[2 * j], dst_ref=self.box.at[2 * j + 1],
            send_sem=self.ssem.at[j], recv_sem=self.rsem.at[j],
            device_id=who, device_id_type=MESH,
        )

    def near(self, j):
        dp, seq, t, x_dp, y_dp, d_dp = _peers()
        return (_dev(dp, 1 - seq, t), _dev(x_dp, seq, t), _dev(y_dp, seq, t))[j]

    def begin(self, value):
        self.box[0] = value
        self.copy(0, self.near(0)).start()

    def step(self, j):
        self.copy(j, self.near(j)).wait_recv()
        total = self.box[2 * j] + self.box[2 * j + 1]
        if j < 2:
            self.box[2 * j + 2] = total
            self.copy(j + 1, self.near(j + 1)).start()
        else:
            t = lax.axis_index("tensor")
            self.line[t] = total
            for o in range(self.n):
                @pl.when(t != o)
                def _(o=o):
                    self.across(t, o).start()

    def across(self, src, who):
        dp, seq, t = lax.axis_index("dp"), lax.axis_index("seq"), lax.axis_index("tensor")
        return pltpu.make_async_remote_copy(
            src_ref=self.line.at[src], dst_ref=self.line.at[src],
            send_sem=self.ssem.at[3 + who], recv_sem=self.rsem.at[3 + src],
            device_id=_dev(dp, seq, who), device_id_type=MESH,
        )

    def final(self):
        t = lax.axis_index("tensor")
        for o in range(self.n):
            @pl.when(t != o)
            def _(o=o):
                self.across(o, o).wait_recv()

    def finish(self):
        t = lax.axis_index("tensor")
        for j in range(3):
            self.copy(j, self.near(j)).wait_send()
        for o in range(self.n):
            @pl.when(t != o)
            def _(o=o):
                self.across(t, o).wait_send()


class _LineSum:
    def __init__(self, n, part, box, out, ssem, rsem):
        self.n, self.part, self.box, self.out, self.ssem, self.rsem = n, part, box, out, ssem, rsem

    def copy(self, phase, src_block, dst_ref, who, origin):
        dp, seq = lax.axis_index("dp"), lax.axis_index("seq")
        return pltpu.make_async_remote_copy(
            src_ref=src_block, dst_ref=dst_ref,
            send_sem=self.ssem.at[phase, who], recv_sem=self.rsem.at[phase, origin],
            device_id=_dev(dp, seq, who), device_id_type=MESH,
        )

    def scatter(self):
        t = lax.axis_index("tensor")
        for o in range(self.n):
            @pl.when(t != o)
            def _(o=o):
                self.copy(0, self.part.at[o], self.box.at[t], o, t).start()

    def gather(self):
        t = lax.axis_index("tensor")
        total = self.part[t].astype(F32)
        for o in range(self.n):
            @pl.when(t != o)
            def _(o=o):
                self.copy(0, self.part.at[o], self.box.at[o], o, o).wait_recv()

            @pl.when(t == o)
            def _(o=o):
                self.box[o] = jnp.zeros(self.box.shape[1:], self.box.dtype)
        for o in range(self.n):
            total = total + self.box[o].astype(F32)
        self.out[t] = total.astype(self.out.dtype)
        for o in range(self.n):
            @pl.when(t != o)
            def _(o=o):
                self.copy(1, self.out.at[t], self.out.at[t], o, t).start()

    def arrive(self):
        t = lax.axis_index("tensor")
        for o in range(self.n):
            @pl.when(t != o)
            def _(o=o):
                self.copy(1, self.out.at[o], self.out.at[o], o, o).wait_recv()

    def finish(self):
        t = lax.axis_index("tensor")
        for o in range(self.n):
            @pl.when(t != o)
            def _(o=o):
                self.copy(0, self.part.at[o], self.box.at[o], o, o).wait_send()
                self.copy(1, self.part.at[o], self.box.at[o], o, o).wait_send()


LANES = 128


def _split(v, parts):
    out = []
    for _ in range(parts):
        b = v.astype(BF)
        out.append(b)
        v = v - b.astype(F32)
    return jnp.concatenate(out, axis=1)


def _dot(a, b, ca=1, cb=0):
    return lax.dot_general(a, b, (((ca,), (cb,)), ((), ())), preferred_element_type=F32)


def _iota(shape, axis):
    return lax.broadcasted_iota(jnp.int32, shape, axis)


def _spreader(rows, p):
    head = lax.rem(_iota((rows, LANES), 0), LANES)
    return (head == 2 * p + lax.div(_iota((rows, LANES), 1), HEAD_DIM)).astype(F32).astype(BF)


def _folder(rows, p):
    chan = lax.rem(_iota((rows, LANES), 0), LANES)
    return (_iota((rows, LANES), 1) == 2 * p + lax.div(chan, HEAD_DIM)).astype(F32).astype(BF)


def _sig(v):
    return 1.0 / (1.0 + jnp.exp(-v))


def _three(v):
    return v[:, :LANES] + v[:, LANES : 2 * LANES] + v[:, 2 * LANES :]


def _head_scalars(raw, hp, marks, length):
    v = raw + hp[0:1, :]
    delta = jnp.maximum(v, 0.0) + jnp.log1p(jnp.exp(-jnp.abs(v)))
    log_decay = -delta * jnp.exp(hp[1:2, :])
    lower = (_iota((length, length), 0) >= _iota((length, length), 1)).astype(F32).astype(BF)
    running = _three(_dot(lower, _split(log_decay, 3)))
    entry = jnp.exp(running) * marks[:, 4:5]
    to_end = jnp.exp(running[length - 1 :, :] - running) * marks[:, 5:6]
    return v, delta, log_decay, running, entry, to_end


def _marks(rows):
    full = jnp.concatenate([rows, jnp.zeros((LANES - rows.shape[0], rows.shape[1]), F32)], axis=0)
    return full.T


def _bias_matrix(rows, marks, length):
    ok = (_iota((length, length), 0) >= _iota((length, length), 1)) & (
        marks[:, 0:1] == rows[0:1, :]
    )
    return jnp.where(ok, 0.0, -1e30)


def _conv(pad, marks, taps, bias, length):
    total = bias + taps[0:1, :] * pad[8 : 8 + length, :]
    for k in range(1, KERNEL):
        total = total + taps[k : k + 1, :] * (pad[8 - k : 8 - k + length, :] * marks[:, k : k + 1])
    return total


def mix_fwd_kernel(n, pre_i, old_i, pre_s, old_s, raw, rows, hp, taps_i, bias_i, taps_s, bias_s,
                   cot, wo, normed, wg, y, u_i, u_s, entry_o, incoming, gate, cot_full, fo,
                   pad, run3, run_t, bias_m, scores, heads_hl, inflow, zs, zr, ps, pr, ls, hs):
    t = lax.axis_index("tensor")
    seqs, length, width = pre_i.shape
    pairs = width // LANES
    _plane_barrier(n)
    line = _Line(n, cot_full, cot.shape[1], zs, zr, cot)
    plane = _Plane(wo, fo, ps, pr, ls.at[0])
    own = pltpu.make_async_copy(cot, line.block(t), ls.at[1])
    own.start()
    line.step(0)
    plane.begin()

    def one(s, _):
        rw = rows[s]
        marks = _marks(rw)
        v, delta, log_decay, running, entry, to_end = _head_scalars(raw[s], hp, marks, length)
        entry_o[s] = entry
        run3[...] = _split(running, 3)
        run_t[...] = running.T
        bias_m[...] = _bias_matrix(rw, marks, length)
        heads_hl[0] = _split(delta, 2)
        heads_hl[1] = _split(to_end, 2)
        maps = []
        for half in range(2):
            ch = slice(half * STATE, (half + 1) * STATE)
            pad[0:8, :] = old_s[s, :, ch].astype(F32)
            pad[8:, :] = pre_s[s, :, ch].astype(F32)
            u = _conv(pad, marks, taps_s[:, ch], bias_s[:, ch], length)
            u_s[s, :, ch] = u
            maps.append((u * _sig(u)).astype(BF))
        b_map, c_map = maps
        scores[...] = _dot(c_map, b_map, 1, 1)

        def pair(p, _):
            @pl.when(jnp.logical_and(s == 1, p == 0))
            def _():
                line.step(1)
                plane.forward()

            @pl.when(jnp.logical_and(s == 1, p == 4))
            def _():
                plane.share()

            ch = pl.ds(pl.multiple_of(p * LANES, LANES), LANES)
            at = pl.ds(pl.multiple_of(t * width + p * LANES, LANES), LANES)
            pad[0:8, :] = old_i[s, :, ch].astype(F32)
            pad[8:, :] = pre_i[s, :, ch].astype(F32)
            u = _conv(pad, marks, taps_i[:, at], bias_i[:, at], length)
            u_i[s, :, ch] = u
            x = u * _sig(u)
            spread = _spreader(2 * LANES, p)
            xd = x * _dot(heads_hl[0], spread)
            inflow[s, :, ch] = _dot(b_map, (xd * _dot(heads_hl[1], spread)).astype(BF), 0, 0).astype(BF)
            skip = _dot(_split(hp[...], 2), spread)[2:3, :]
            total = skip * x
            xb = xd.astype(BF)
            lane = lax.div(_iota(xb.shape, 1), HEAD_DIM)
            for a in range(2):
                h = 2 * p + a
                pick = (lax.rem(_iota((3 * LANES, length), 0), LANES) == h).astype(F32).astype(BF)
                decay = jnp.exp(_dot(run3[...], pick) - run_t[pl.ds(h, 1), :] + bias_m[...])
                mixing = (decay * scores[...]).astype(BF)
                total = total + _dot(mixing, jnp.where(lane == a, xb, jnp.zeros_like(xb)))
            y[s, :, ch] = total
            return 0

        lax.fori_loop(0, pairs, pair, 0)
        return 0

    lax.fori_loop(0, seqs, one, 0)
    dp, seq = lax.axis_index("dp"), lax.axis_index("seq")
    handed = pltpu.make_async_remote_copy(
        src_ref=inflow, dst_ref=incoming, send_sem=hs.at[0], recv_sem=hs.at[1],
        device_id=_dev(dp, 1 - seq, t), device_id_type=MESH,
    )

    @pl.when(seq == 0)
    def _():
        handed.start()
        incoming[...] = jnp.zeros_like(incoming)

    line.step(2)
    flat = normed[...].reshape(seqs * length, normed.shape[2])

    def gate_part(c, _):
        ch = pl.ds(pl.multiple_of(c * 2 * LANES, 2 * LANES), 2 * LANES)
        part = _dot(flat, wg[:, :, ch].reshape(normed.shape[2], 2 * LANES))
        gate[:, :, ch] = part.reshape(seqs, length, 2 * LANES)
        return 0

    lax.fori_loop(0, width // (2 * LANES), gate_part, 0)
    for d in range(3, n):
        line.step(d)
    plane.arrive()
    own.wait()

    @pl.when(seq == 0)
    def _():
        handed.wait_send()

    @pl.when(seq == 1)
    def _():
        handed.wait_recv()

    line.finish()
    plane.finish()


def _mixer_call(kernel, ins, outs, scratch, name, cost, number):
    vm = pl.BlockSpec(memory_space=pltpu.VMEM)
    return pl.pallas_call(
        kernel,
        out_shape=outs,
        in_specs=[vm] * len(ins),
        out_specs=(vm,) * len(outs),
        scratch_shapes=scratch,
        compiler_params=pltpu.CompilerParams(
            collective_id=number, has_side_effects=True, vmem_limit_bytes=60 << 20
        ),
        cost_estimate=pl.CostEstimate(flops=cost, bytes_accessed=1 << 20, transcendentals=0),
        name=name,
    )(*ins)


def mix_fwd(n, pre_i, old_i, pre_s, old_s, raw, rows, hp, taps_i, bias_i, taps_s, bias_s, cot, wo,
            normed, wg):
    seqs, length, width = pre_i.shape
    sd = jax.ShapeDtypeStruct
    return _mixer_call(
        functools.partial(mix_fwd_kernel, n),
        (pre_i, old_i, pre_s, old_s, raw, rows, hp, taps_i, bias_i, taps_s, bias_s, cot, wo,
         normed, wg),
        (
            sd((seqs, length, width), F32),
            sd((seqs, length, width), F32),
            sd((seqs, length, 2 * STATE), F32),
            sd((seqs, length, LANES), F32),
            sd((seqs, STATE, width), BF),
            sd((seqs, length, width), F32),
            sd((seqs, length, cot.shape[2]), BF),
            sd((8,) + wo.shape, BF),
        ),
        [
            pltpu.VMEM((8 + length, LANES), F32),
            pltpu.VMEM((length, 3 * LANES), BF),
            pltpu.VMEM((LANES, length), F32),
            pltpu.VMEM((length, length), F32),
            pltpu.VMEM((length, length), F32),
            pltpu.VMEM((2, length, 2 * LANES), BF),
            pltpu.VMEM((seqs, STATE, width), BF),
            pltpu.SemaphoreType.DMA((2, n)),
            pltpu.SemaphoreType.DMA((n,)),
            pltpu.SemaphoreType.DMA((7,)),
            pltpu.SemaphoreType.DMA((7,)),
            pltpu.SemaphoreType.DMA((2,)),
            pltpu.SemaphoreType.DMA((2,)),
        ],
        "mix_fwd",
        4 * 10**9,
        3,
    )


def gate_kernel(n, y_part, u_s, entry, h0, gate, cot, wo, gain, tokens_in,
                d_mixed, d_gate, lam, po, go, gg, g_gain,
                mixed, gated, grad_gn, normed, local, acc, box, ss, rs, hs):
    dp, seq, t = lax.axis_index("dp"), lax.axis_index("seq"), lax.axis_index("tensor")
    seqs, length, width = y_part.shape
    model = cot.shape[2]
    wide = 2 * LANES
    bar = pltpu.get_barrier_semaphore()
    pl.semaphore_signal(bar, inc=1, device_id=_dev(dp, 1 - seq, t), device_id_type=MESH)
    for step in range(1, n):
        pl.semaphore_signal(
            bar, inc=1, device_id=_dev(dp, seq, lax.rem(t + step, n)), device_id_type=MESH
        )
    acc[...] = jnp.zeros_like(acc)
    g_gain[...] = jnp.zeros_like(g_gain)

    def spread_of(s, c):
        heads = _split(entry[s], 2)
        head = lax.rem(_iota((wide, wide), 0), LANES)
        one = head == 4 * c + lax.div(_iota((wide, wide), 1), HEAD_DIM)
        return _dot(heads, one.astype(F32).astype(BF))

    def maps(s):
        u = u_s[s, :, STATE:]
        return (u * _sig(u)).astype(BF)

    def first(c, _):
        ch = pl.ds(pl.multiple_of(c * wide, wide), wide)
        at = pl.ds(pl.multiple_of(t * width + c * wide, wide), wide)
        w = wo[:, :, ch].reshape(model, wide)
        for s in range(seqs):
            g = _dot(cot[s], w)
            grad_gn[s, :, ch] = g
            m = y_part[s, :, ch] + spread_of(s, c) * _dot(maps(s), h0[s, :, ch])
            z = gate[s, :, ch]
            gd = m * (z * _sig(z))
            mixed[s, :, ch] = m
            gated[s, :, ch] = gd
            sq, ds = gd * gd, g * gain[:, at] * gd
            acc[0, s] += sq[:, :LANES] + sq[:, LANES:]
            acc[1, s] += ds[:, :LANES] + ds[:, LANES:]
        return 0

    lax.fori_loop(0, width // wide, first, 0)
    ones = jnp.ones((8, wide), F32).astype(BF)
    row = _iota((8, length), 0)
    mine = jnp.zeros((8, length), F32)
    for kind in range(2):
        for s in range(seqs):
            sums = _dot(ones, _split(acc[kind, s], 2), 1, 1)
            mine = jnp.where(row == kind * seqs + s, sums, mine)
    box[t] = mine
    pl.semaphore_wait(bar, n)

    def copy(src, who):
        return pltpu.make_async_remote_copy(
            src_ref=box.at[src], dst_ref=box.at[src], send_sem=ss.at[who], recv_sem=rs.at[src],
            device_id=_dev(dp, seq, who), device_id_type=MESH,
        )

    for o in range(n):
        @pl.when(t != o)
        def _(o=o):
            copy(t, o).start()
    for o in range(n):
        @pl.when(t != o)
        def _(o=o):
            copy(o, o).wait_recv()
    full_width = n * width
    cols = _marks(jnp.sum(box[...], axis=0) / full_width)

    def second(c, _):
        ch = pl.ds(pl.multiple_of(c * wide, wide), wide)
        at = pl.ds(pl.multiple_of(t * width + c * wide, wide), wide)
        gn = gain[:, at]
        for s in range(seqs):
            rms = lax.rsqrt(cols[:, s : s + 1] + EPS)
            mean = cols[:, seqs + s : seqs + s + 1]
            g, gd, m, z = grad_gn[s, :, ch], gated[s, :, ch], mixed[s, :, ch], gate[s, :, ch]
            sg = _sig(z)
            scaled = gd * rms
            normed[s, :, ch] = (scaled * gn).astype(BF)
            g_gain[0:1, ch] += jnp.sum(g * scaled, axis=0, keepdims=True)
            d_gd = rms * (g * gn) - scaled * (rms * rms * mean)
            dm = d_gd * (z * sg)
            d_mixed[s, :, ch] = dm
            d_gate[s, :, ch] = (d_gd * m * sg * (1.0 + z * (1.0 - sg))).astype(BF)
            ed = (spread_of(s, c) * dm).astype(BF)
            local[s, :, ch] = _dot(maps(s), ed, 0, 0).astype(BF)
        return 0

    lax.fori_loop(0, width // wide, second, 0)
    handed = pltpu.make_async_remote_copy(
        src_ref=local, dst_ref=lam, send_sem=hs.at[0], recv_sem=hs.at[1],
        device_id=_dev(dp, 1 - seq, t), device_id_type=MESH,
    )

    @pl.when(seq == 1)
    def _():
        handed.start()
        lam[...] = jnp.zeros_like(lam)

    blocks = 2
    rows = blocks * wo.shape[1]

    def third(b, _):
        ch = pl.ds(pl.multiple_of(b * rows, LANES), rows)
        w = wo[pl.ds(b * blocks, blocks)].reshape(rows, width)
        total = None
        for s in range(seqs):
            po[s, :, ch] = _dot(normed[s], w, 1, 1).astype(BF)
            part = _dot(cot[s, :, ch], normed[s], 0, 0)
            total = part if total is None else total + part
        go[pl.ds(b * blocks, blocks)] = total.reshape(blocks, wo.shape[1], width).astype(BF)
        total = None
        for s in range(seqs):
            part = _dot(tokens_in[s, :, ch], d_gate[s], 0, 0)
            total = part if total is None else total + part
        gg[pl.ds(b * blocks, blocks)] = total.reshape(blocks, wo.shape[1], width).astype(BF)
        return 0

    lax.fori_loop(0, model // rows, third, 0)

    @pl.when(seq == 1)
    def _():
        handed.wait_send()

    @pl.when(seq == 0)
    def _():
        handed.wait_recv()

    for o in range(n):
        @pl.when(t != o)
        def _(o=o):
            copy(o, o).wait_send()


def gate_stage(n, y_part, u_s, entry, h0, gate, cot, wo, gain, tokens_in):
    seqs, length, width = y_part.shape
    sd = jax.ShapeDtypeStruct
    whole = pltpu.VMEM((seqs, length, width), F32)
    return _mixer_call(
        functools.partial(gate_kernel, n),
        (y_part, u_s, entry, h0, gate, cot, wo, gain, tokens_in),
        (
            sd((seqs, length, width), F32),
            sd((seqs, length, width), BF),
            sd((seqs, STATE, width), BF),
            sd((seqs, length, cot.shape[2]), BF),
            sd(wo.shape, BF),
            sd(wo.shape, BF),
            sd((8, width), F32),
        ),
        [
            whole, whole, whole,
            pltpu.VMEM((seqs, length, width), BF),
            pltpu.VMEM((seqs, STATE, width), BF),
            pltpu.VMEM((2, seqs, length, LANES), F32),
            pltpu.VMEM((n, 8, length), F32),
            pltpu.SemaphoreType.DMA((n,)),
            pltpu.SemaphoreType.DMA((n,)),
            pltpu.SemaphoreType.DMA((2,)),
        ],
        "gate_stage",
        6 * 10**9,
        2,
    )


def mix_bwd_kernel(n, dy_r, u_i, u_s, pre_i, old_i, pre_s, old_s, raw, rows, h0, lam, hp,
                   taps_i, taps_s, po, go, gg,
                   d_i, d_s, d_raw, sm_i, sm_s, sm_h, o_po, o_go, o_gg,
                   pad, moved, run3, run_t, bias_m, scores, d_scores, heads_hl,
                   acc_r, acc_c, acc_d, acc_q, d_b, d_c, lo, ro, xo, bo, xg, bg,
                   head_i, tail_i, head_s, tail_s, next_i, next_s, zs, zr, ps, pr, hs):
    t = lax.axis_index("tensor")
    seqs, length, width = pre_i.shape
    pairs = width // LANES
    _plane_barrier(n)
    step_o, final_o, finish_o = _line_reduce(n, po, lo, ro, zs, zr)
    planes = (
        _PlaneReduce(go, xo, bo, ps.at[0], pr.at[0]), _PlaneReduce(gg, xg, bg, ps.at[1], pr.at[1])
    )
    step_o(0)
    for plane in planes:
        plane.begin()
    sm_i[...] = jnp.zeros_like(sm_i)
    sm_s[...] = jnp.zeros_like(sm_s)
    sm_h[...] = jnp.zeros_like(sm_h)
    moved[0:8, :] = jnp.zeros((8, LANES), F32)
    moved[8 + length :, :] = jnp.zeros((8, LANES), F32)

    def conv_back(du, marks, taps, s, ch, d_o, head_o, tail_o, sm):
        total = None
        for k in range(KERNEL):
            m = du if k == 0 else du * marks[:, k : k + 1]
            moved[8 : 8 + length, :] = m
            sm[k : k + 1, ch] += jnp.sum(m * pad[8 - k : 8 - k + length, :], axis=0, keepdims=True)
            part = taps[k : k + 1, :] * moved[k : k + 8 + length, :]
            total = part if total is None else total + part
        sm[4:5, ch] += jnp.sum(du, axis=0, keepdims=True)
        head_o[s, :, ch] = total[0:8, :]
        d_o[s, :, ch] = total[8:, :].astype(BF)
        tail_o[s, :, ch] = total[length - 8 :, :]

    def one(s, _):
        rw = rows[s]
        marks = _marks(rw)
        v, delta, log_decay, running, entry, to_end = _head_scalars(raw[s], hp, marks, length)
        run3[...] = _split(running, 3)
        run_t[...] = running.T
        bias_m[...] = _bias_matrix(rw, marks, length)
        heads_hl[0] = _split(delta, 2)
        heads_hl[1] = _split(to_end, 2)
        heads_hl[2] = _split(entry, 2)
        ub, uc = u_s[s, :, :STATE], u_s[s, :, STATE:]
        sb, sc = _sig(ub), _sig(uc)
        b_map, c_map = (ub * sb).astype(BF), (uc * sc).astype(BF)
        scores[...] = _dot(c_map, b_map, 1, 1)
        d_scores[...] = jnp.zeros_like(d_scores)
        for acc in (acc_r, acc_c, acc_d, acc_q, d_b, d_c):
            acc[...] = jnp.zeros_like(acc)

        def pair(p, _):
            @pl.when(jnp.logical_and(s == 0, p == 2))
            def _():
                planes[0].send_far()

            @pl.when(jnp.logical_and(s == 0, p == 3))
            def _():
                planes[1].send_far()

            @pl.when(jnp.logical_and(s == 0, p == 5))
            def _():
                step_o(1)

            @pl.when(jnp.logical_and(s == 1, p == 2))
            def _():
                planes[0].send_near()

            @pl.when(jnp.logical_and(s == 1, p == 5))
            def _():
                planes[1].send_near()

            @pl.when(jnp.logical_and(s == 1, p == 4))
            def _():
                step_o(2)

            ch = pl.ds(pl.multiple_of(p * LANES, LANES), LANES)
            at = pl.ds(pl.multiple_of(t * width + p * LANES, LANES), LANES)
            u = u_i[s, :, ch]
            sg = _sig(u)
            x = u * sg
            dy = dy_r[s, :, ch]
            spread, fold = _spreader(2 * LANES, p), _folder(2 * LANES, p)
            dl = _dot(heads_hl[0], spread)
            q = _dot(heads_hl[1], spread)
            e = _dot(heads_hl[2], spread)
            xd = x * dl
            xb, db = xd.astype(BF), dy.astype(BF)
            h_in, l_in = h0[s, :, ch], lam[s, :, ch]
            c_h = _dot(c_map, h_in)
            b_l = _dot(b_map, l_in)
            qx, ed = q * xd, e * dy
            d_b[...] += _dot(qx.astype(BF), l_in, 1, 1)
            d_c[...] += _dot(ed.astype(BF), h_in, 1, 1)
            late = qx * b_l
            dxd = q * b_l
            lane = lax.div(_iota(xb.shape, 1), HEAD_DIM)
            for a in range(2):
                h = 2 * p + a
                pick = (lax.rem(_iota((3 * LANES, length), 0), LANES) == h).astype(F32).astype(BF)
                decay = jnp.exp(_dot(run3[...], pick) - run_t[pl.ds(h, 1), :] + bias_m[...])
                da = jnp.where(lane == a, db, jnp.zeros_like(db))
                ld = decay * _dot(da, xb, 1, 1)
                d_scores[...] += ld
                both = (ld * scores[...]).astype(BF)
                mixing = (decay * scores[...]).astype(BF)
                dxd = dxd + _dot(mixing, da, 0, 0)
                col = (_iota((length, LANES), 1) == h).astype(F32).astype(BF)
                row = (_iota((LANES, length), 0) == h).astype(F32).astype(BF)
                acc_r[...] += _dot(both, col)
                acc_c[...] += _dot(row, both)
            acc_r[...] += _dot(_split(ed * c_h - late, 2), fold)
            acc_d[...] += _dot(_split(dxd * x, 2), fold)
            total = jnp.broadcast_to(jnp.sum(late, axis=0, keepdims=True), (8, LANES))
            acc_q[...] += _dot(_split(total, 2), fold)
            skip = _dot(_split(hp[...], 2), spread)[2:3, :]
            sm_i[5:6, ch] += jnp.sum(dy * x, axis=0, keepdims=True)
            du = (dxd * dl + skip * dy) * (sg * (1.0 + u * (1.0 - sg)))
            pad[0:8, :] = old_i[s, :, ch].astype(F32)
            pad[8:, :] = pre_i[s, :, ch].astype(F32)
            conv_back(du, marks, taps_i[:, at], s, ch, d_i, head_i, tail_i, sm_i)
            return 0

        lax.fori_loop(0, pairs, pair, 0)
        ds = d_scores[...].astype(BF)
        grads = (d_b[...] + _dot(ds, c_map, 0, 0), d_c[...] + _dot(ds, b_map))
        for half, (g, u, sg) in enumerate(zip(grads, (ub, uc), (sb, sc))):
            ch = slice(half * STATE, (half + 1) * STATE)
            pad[0:8, :] = old_s[s, :, ch].astype(F32)
            pad[8:, :] = pre_s[s, :, ch].astype(F32)
            du = g * (sg * (1.0 + u * (1.0 - sg)))
            conv_back(du, marks, taps_s[:, ch], s, ch, d_s, head_s, tail_s, sm_s)
        d_run = acc_r[...] - acc_c[...].T
        last = _iota(d_run.shape, 0) == length - 1
        d_run = d_run + jnp.where(last, acc_q[0:1, :], 0.0)
        upper = (_iota((length, length), 0) <= _iota((length, length), 1)).astype(F32).astype(BF)
        d_log = _three(_dot(upper, _split(d_run, 3)))
        d_delta = acc_d[...] - d_log * jnp.exp(hp[1:2, :])
        d_step = d_delta * _sig(v)
        d_raw[s] = d_step.astype(BF)
        sm_h[0:1, :] += jnp.sum(d_step, axis=0, keepdims=True)
        sm_h[1:2, :] += jnp.sum(d_log * log_decay, axis=0, keepdims=True)
        return 0

    lax.fori_loop(0, seqs, one, 0)
    for k in range(3, n - 1):
        step_o(k)
    dp, seq = lax.axis_index("dp"), lax.axis_index("seq")
    handed = [
        pltpu.make_async_remote_copy(
            src_ref=a, dst_ref=b, send_sem=hs.at[2 * i], recv_sem=hs.at[2 * i + 1],
            device_id=_dev(dp, 1 - seq, t), device_id_type=MESH,
        )
        for i, (a, b) in enumerate(((head_i, next_i), (head_s, next_s)))
    ]

    @pl.when(seq == 1)
    def _():
        for c in handed:
            c.start()

    planes[0].final(o_go)

    @pl.when(seq == 0)
    def _():
        for c, box, tail, out in zip(handed, (next_i, next_s), (tail_i, tail_s), (d_i, d_s)):
            c.wait_recv()
            for s in range(seqs):
                more = jnp.concatenate([jnp.zeros_like(box[s]), box[s]], axis=0)
                out[s, length - 16 :, :] = (tail[s] + more).astype(BF)

    @pl.when(seq == 1)
    def _():
        for c in handed:
            c.wait_send()

    planes[1].final(o_gg)
    final_o(o_po)
    for plane in planes:
        plane.finish()
    finish_o()


def mix_bwd(n, dy, u_i, u_s, pre_i, old_i, pre_s, old_s, raw, rows, h0, lam, hp, taps_i, taps_s,
            po, go, gg):
    seqs, length, width = pre_i.shape
    model = po.shape[2]
    box = pltpu.VMEM((n, seqs, length // n, model), BF)
    sd = jax.ShapeDtypeStruct
    square = pltpu.VMEM((length, length), F32)
    tall = pltpu.VMEM((length, LANES), F32)
    return _mixer_call(
        functools.partial(mix_bwd_kernel, n),
        (dy, u_i, u_s, pre_i, old_i, pre_s, old_s, raw, rows, h0, lam, hp, taps_i, taps_s, po, go,
         gg),
        (
            sd((seqs, length, width), BF),
            sd((seqs, length, 2 * STATE), BF),
            sd((seqs, length, LANES), BF),
            sd((8, width), F32),
            sd((8, 2 * STATE), F32),
            sd((8, LANES), F32),
            sd((seqs, length // n, model), F32),
            sd(go.shape[1:], F32),
            sd(gg.shape[1:], F32),
        ),
        [
            pltpu.VMEM((8 + length, LANES), F32),
            pltpu.VMEM((16 + length, LANES), F32),
            pltpu.VMEM((length, 3 * LANES), BF),
            pltpu.VMEM((LANES, length), F32),
            square, square, square,
            pltpu.VMEM((3, length, 2 * LANES), BF),
            tall, pltpu.VMEM((LANES, length), F32), tall, pltpu.VMEM((8, LANES), F32), tall, tall,
            box, box,
            pltpu.VMEM((4,) + go.shape[1:], BF),
            pltpu.VMEM((3,) + go.shape[1:], BF),
            pltpu.VMEM((4,) + gg.shape[1:], BF),
            pltpu.VMEM((3,) + gg.shape[1:], BF),
            pltpu.VMEM((seqs, 8, width), F32),
            pltpu.VMEM((seqs, 16, width), F32),
            pltpu.VMEM((seqs, 8, 2 * STATE), F32),
            pltpu.VMEM((seqs, 16, 2 * STATE), F32),
            pltpu.VMEM((seqs, 8, width), F32),
            pltpu.VMEM((seqs, 8, 2 * STATE), F32),
            pltpu.SemaphoreType.DMA((2, n)),
            pltpu.SemaphoreType.DMA((2, n)),
            pltpu.SemaphoreType.DMA((2, 7)),
            pltpu.SemaphoreType.DMA((2, 7)),
            pltpu.SemaphoreType.DMA((4,)),
        ],
        "mix_bwd",
        8 * 10**9,
        4,
    )


def reduce_kernel(n, normed, dg, di, ds, dr, wg, wi, ws, wt, gain, sm_i, sm_s, sm_h, g_gain,
                  o_pg, o_gi, o_gs, o_gt, o_sm,
                  pg, gi, gs, gt, lg, rg, xi, xs, xt, bi, bs, bt, mb,
                  xp, xb, xo2, zs, zr, ps, pr, ms, mr, es, er):
    _plane_barrier(n)
    seqs, length, width = di.shape
    model = normed.shape[2]
    blocks = 2
    rows = blocks * wi.shape[1]
    small = _Smalls(n, mb, o_sm, ms, mr)
    mb[0] = jnp.zeros(mb.shape[1:], F32)
    mb[0, 0:6, :] = sm_i[0:6, :]
    mb[0, 6:7, :] = g_gain[0:1, :]
    for k in range(5):
        at = 256 * (k % 3)
        mb[0, 9 + k // 3 : 10 + k // 3, at : at + 256] = sm_s[k : k + 1, :]
    mb[0, 10:11, 512:640] = sm_h[0:1, :]
    mb[0, 10:11, 640:768] = sm_h[1:2, :]

    for b in range(model // rows):
        ch = slice(b * rows, (b + 1) * rows)
        near = slice(b * blocks, (b + 1) * blocks)
        w = [r[near].reshape(rows, r.shape[2]) for r in (wg, wi, ws, wt)]
        total = None
        for s in range(seqs):
            part = None
            for d, one in zip((dg, di, ds, dr), w):
                more = _dot(d[s], one, 1, 1)
                part = more if part is None else part + more
            pg[s, :, ch] = part.astype(BF)
            part = jnp.sum(part * normed[s, :, ch].astype(F32), axis=0, keepdims=True)
            total = part if total is None else total + part
        mb[0, 7 + b // 2 : 8 + b // 2, (b % 2) * rows : (b % 2 + 1) * rows] = total / gain[:, ch]
    step_g, final_g, finish_g = _line_reduce(n, pg, lg, rg, zs, zr)
    step_g(0)
    small.copy(0, small.near(0)).start()
    planes = [
        _PlaneReduce(part, pair, box, ps.at[i], pr.at[i])
        for i, (part, pair, box) in enumerate(((gs, xs, bs), (gt, xt, bt), (gi, xi, bi)))
    ]

    def weight(d, out):
        def one(b, _):
            ch = pl.ds(pl.multiple_of(b * rows, LANES), rows)
            total = None
            for s in range(seqs):
                part = _dot(normed[s, :, ch], d[s], 0, 0)
                total = part if total is None else total + part
            out[pl.ds(b * blocks, blocks)] = total.reshape(
                blocks, wi.shape[1], d.shape[2]
            ).astype(BF)
            return 0

        lax.fori_loop(0, model // rows, one, 0)

    weight(ds, gs)
    planes[0].begin()
    weight(dr, gt)
    planes[1].begin()
    weight(di, gi)
    planes[2].begin()
    small.step(0)
    step_g(1)
    for p in planes:
        p.send_far()
    small.step(1)
    for p in planes[:2]:
        p.send_near()
    small.step(2)
    step_g(2)
    planes[2].send_near()
    for k in range(3, n - 1):
        step_g(k)
    planes[0].final(o_gs)
    planes[1].final(o_gt)
    quarter = xp.shape[1]
    for o in range(n):
        xp[o] = o_gs[o * quarter : (o + 1) * quarter, :].astype(BF)
    state = _LineSum(n, xp, xb, xo2, es, er)
    state.scatter()
    planes[2].final(o_gi)
    state.gather()
    small.final()
    final_g(o_pg)
    state.arrive()
    for o in range(n):
        o_gs[o * quarter : (o + 1) * quarter, :] = xo2[o].astype(F32)
    for p in planes:
        p.finish()
    state.finish()
    small.finish()
    finish_g()


def reduce_all(n, normed, dg, di, ds, dr, wg, wi, ws, wt, gain, sm_i, sm_s, sm_h, g_gain):
    seqs, length, model = normed.shape
    rows = length // n
    sd = jax.ShapeDtypeStruct
    box = pltpu.VMEM((n, seqs, rows, model), BF)
    quarter = pltpu.VMEM((n, ws.shape[1] // n, ws.shape[2]), BF)
    sums = (16, wi.shape[2])
    return _mixer_call(
        functools.partial(reduce_kernel, n),
        (normed, dg, di, ds, dr, wg, wi, ws, wt, gain, sm_i, sm_s, sm_h, g_gain),
        (sd((seqs, rows, model), F32),)
        + tuple(sd(w.shape[1:], F32) for w in (wi, ws, wt))
        + (sd((n,) + sums, F32),),
        [pltpu.VMEM((seqs, length, model), BF)]
        + [pltpu.VMEM(w.shape, BF) for w in (wi, ws, wt)]
        + [box, box]
        + [pltpu.VMEM((4,) + w.shape[1:], BF) for w in (wi, ws, wt)]
        + [pltpu.VMEM((3,) + w.shape[1:], BF) for w in (wi, ws, wt)]
        + [
            pltpu.VMEM((6,) + sums, F32),
            quarter, quarter, quarter,
            pltpu.SemaphoreType.DMA((2, n)),
            pltpu.SemaphoreType.DMA((2, n)),
            pltpu.SemaphoreType.DMA((3, 7)),
            pltpu.SemaphoreType.DMA((3, 7)),
            pltpu.SemaphoreType.DMA((3 + n,)),
            pltpu.SemaphoreType.DMA((3 + n,)),
            pltpu.SemaphoreType.DMA((2, n)),
            pltpu.SemaphoreType.DMA((2, n)),
        ],
        "reduce_all",
        6 * 10**9,
        1,
    )


def emit_kernel(n, heads, tok, cot, gain, branch, rows, gg, gi, gs, gt, go, sms,
                block_out, g_tok, g_in, o_gg, o_gi, o_gs, o_gt, o_ci, o_ib, o_cs, o_sb,
                o_shift, o_rate, o_skip, o_gain, o_go):
    for s in range(tok.shape[0]):
        v = tok[s].astype(F32)
        rms = lax.rsqrt(jnp.mean(v * v, axis=-1, keepdims=True) + EPS)
        block_out[s] = (v + branch[s]).astype(BF)
        scaled = rows[s] * gain[...]
        mean = jnp.mean(scaled * v, axis=-1, keepdims=True)
        g_tok[s] = cot[s].astype(F32) + rms * scaled - v * (rms * rms * rms * mean)
    o_gg[...] = gg[...]
    o_gi[...] = gi[...]
    o_gs[...] = gs[...]
    o_gt[...] = gt[:, :heads]
    short = jnp.zeros((256 - go.shape[0], go.shape[1]), F32)
    o_go[...] = jnp.concatenate([go[...], short], axis=0).T[:, : go.shape[0]]
    width = sms.shape[2]
    shared = None
    head_rows = None
    for t in range(n):
        ch = slice(t * width, (t + 1) * width)
        o_ci[:, ch] = sms[t, 0:4, :]
        o_ib[:, ch] = sms[t, 4:5, :]
        o_gain[:, ch] = sms[t, 6:7, :]
        block = sms[t, 8:16, :]
        shared = sms[t, 7:11, :] if shared is None else shared + sms[t, 7:11, :]
        lanes = _iota((3 * width, LANES), 0)
        chan = lax.rem(lanes, width)
        to = _iota((3 * width, LANES), 1) == heads * t + lax.div(chan, HEAD_DIM)
        skips = _dot(_split(sms[t, 0:8, :], 3), to.astype(F32).astype(BF))
        lanes = lax.rem(_iota((3 * LANES, LANES), 0), LANES)
        to = (_iota((3 * LANES, LANES), 1) == heads * t + lanes) & (lanes < heads)
        to = to.astype(F32).astype(BF)
        shift = _dot(_split(block[:, 512:640], 3), to)
        rate = _dot(_split(block[:, 640:768], 3), to)
        new = (skips[5:6, :], shift[2:3, :], rate[2:3, :])
        head_rows = new if head_rows is None else tuple(a + b for a, b in zip(head_rows, new))
    every = n * heads
    o_skip[...] = head_rows[0][:, :every]
    o_shift[...] = head_rows[1][:, :every]
    o_rate[...] = head_rows[2][:, :every]
    g_in[:, :width] = shared[0:1, :]
    g_in[:, width:] = shared[1:2, :]
    for k in range(4):
        at = 256 * (k % 3)
        o_cs[k : k + 1, :] = shared[2 + k // 3 : 3 + k // 3, at : at + 256]
    o_sb[...] = shared[3:4, 256:512]


def emit_all(n, heads, tok, cot, gain, branch, rows, gg, gi, gs, gt, go, sms):
    vm = pl.BlockSpec(memory_space=pltpu.VMEM)
    sd = lambda *shape: jax.ShapeDtypeStruct(shape, F32)
    width = sms.shape[2]
    outs = (
        jax.ShapeDtypeStruct(tok.shape, BF), sd(*tok.shape), sd(1, tok.shape[2]),
        sd(*gg.shape), sd(*gi.shape), sd(*gs.shape), sd(gt.shape[0], heads),
        sd(4, n * width), sd(1, n * width), sd(4, 2 * STATE), sd(1, 2 * STATE),
        sd(1, n * heads), sd(1, n * heads), sd(1, n * heads), sd(1, n * width),
        sd(go.shape[1], go.shape[0]),
    )
    return pl.pallas_call(
        functools.partial(emit_kernel, n, heads),
        out_shape=outs,
        in_specs=[vm] * 11,
        out_specs=(vm,) * len(outs),
        compiler_params=pltpu.CompilerParams(vmem_limit_bytes=40 << 20),
        name="emit_all",
    )(tok, cot, gain, branch, rows, gg, gi, gs, gt, go, sms)


def per_device(
    tokens,
    segments,
    input_gain,
    gate_proj,
    inner_proj,
    state_proj,
    step_proj,
    conv_inner,
    inner_bias,
    conv_state,
    state_bias,
    step_bias,
    log_rates,
    skip_gain,
    gated_gain,
    output_proj,
    cotangent,
):
    tensor_count = lax.axis_size("tensor")
    tensor_rank = lax.axis_index("tensor")
    residual = tokens.astype(jnp.float32)
    rms_in = lax.rsqrt(jnp.mean(residual * residual, axis=-1, keepdims=True) + EPS)
    normed_own = (residual * rms_in * input_gain).astype(jnp.bfloat16)
    normed, cot_rows = (
        lax.all_gather(normed_own, "tensor", axis=1, tiled=True),
        lax.all_gather(cotangent, "tensor", axis=1, tiled=True),
    )
    gate_full, inner_full, state_full, step_full, output_full = (
        lax.all_gather(gate_proj, ("dp", "seq"), axis=0, tiled=True),
        lax.all_gather(inner_proj, ("dp", "seq"), axis=0, tiled=True),
        lax.all_gather(state_proj, ("dp", "seq"), axis=0, tiled=True),
        lax.all_gather(step_proj, ("dp", "seq"), axis=0, tiled=True),
        lax.all_gather(output_proj, ("dp", "seq"), axis=1, tiled=True),
    )
    gate_in = jnp.dot(normed, gate_full, preferred_element_type=jnp.float32)
    inner_low = jnp.dot(normed, inner_full, preferred_element_type=jnp.float32).astype(jnp.bfloat16)
    state_low = jnp.dot(normed, state_full, preferred_element_type=jnp.float32).astype(jnp.bfloat16)
    step_raw = jnp.dot(normed, step_full, preferred_element_type=jnp.float32)
    margin = KERNEL - 1
    seg_float = segments.astype(jnp.float32)
    prior_inner, prior_state, prior_seg = passed_along(
        (
            inner_low[:, -margin:],
            state_low[:, -margin:],
            seg_float[:, -margin:].astype(jnp.bfloat16),
        ),
        "seq",
        1,
    )
    padded_inner = jnp.concatenate([prior_inner, inner_low], axis=1).astype(jnp.float32)
    padded_state = jnp.concatenate([prior_state, state_low], axis=1).astype(jnp.float32)
    seg_padded = jnp.concatenate([prior_seg.astype(jnp.float32), seg_float], axis=1)
    pieces = segments.shape[1] // BLOCK
    seg_blocks = blocked(seg_float, pieces)
    before = jnp.concatenate(
        [prior_seg[:, -1:].astype(jnp.float32), seg_blocks[:, :-1, -1]], axis=1
    )
    width_here = inner_full.shape[1]
    heads_here = step_full.shape[1]
    chan_start = tensor_rank * width_here
    head_start = tensor_rank * heads_here
    kernel_here = lax.dynamic_slice_in_dim(conv_inner, chan_start, width_here, 1)
    bias_here = lax.dynamic_slice_in_dim(inner_bias, chan_start, width_here, 0)
    gain_here = lax.dynamic_slice_in_dim(gated_gain, chan_start, width_here, 0)
    shift_here = lax.dynamic_slice_in_dim(step_bias, head_start, heads_here, 0)
    rates_here = lax.dynamic_slice_in_dim(log_rates, head_start, heads_here, 0)
    skip_here = lax.dynamic_slice_in_dim(skip_gain, head_start, heads_here, 0)

    def mixer_front(
        pad_inner, pad_state, raw_steps, kernel_w, kernel_b, state_w, state_b, step_shift, rate_logs
    ):
        inner = jax.nn.silu(causal_mix(pad_inner, seg_padded, kernel_w, kernel_b))
        inner = inner.reshape(inner.shape[0], inner.shape[1], -1, HEAD_DIM)
        both_maps = jax.nn.silu(causal_mix(pad_state, seg_padded, state_w, state_b))
        b_proj = both_maps[:, :, :STATE]
        c_proj = both_maps[:, :, STATE:]
        deltas = jax.nn.softplus(raw_steps + step_shift)
        log_decay = deltas * -jnp.exp(rate_logs)
        inflow, passing = block_sums(inner, deltas, log_decay, b_proj, seg_blocks, before)
        return (inner, deltas, log_decay, b_proj, c_proj, inflow, passing)

    def mixer_rear(inner, deltas, log_decay, b_proj, c_proj, inflow, passing, incoming, skips):
        running = jnp.cumsum(blocked(log_decay, pieces), axis=2)
        places = jnp.arange(running.shape[2])
        allowed = (seg_blocks[:, :, :, None] == seg_blocks[:, :, None, :]) & (
            places[:, None] >= places[None, :]
        )
        inside = allowed[..., None]
        decays = jnp.where(
            inside,
            jnp.exp(jnp.where(inside, running[:, :, :, None, :] - running[:, :, None, :, :], 0.0)),
            0.0,
        )
        scores = jnp.einsum(
            "scin,scjn->scij", blocked(c_proj, pieces), blocked(b_proj, pieces), precision=HIGH
        )
        mixing = decays * scores[..., None] * blocked(deltas, pieces)[:, :, None, :, :]
        direct = jnp.einsum("scijh,scjhp->scihp", mixing, blocked(inner, pieces), precision=HIGH)
        from_state, outgoing = state_reads(
            incoming, log_decay, c_proj, inflow, passing, seg_blocks, before
        )
        heads_out = (direct + from_state).reshape(inner.shape) + skips[:, None] * inner
        return (heads_out.reshape(inner.shape[0], inner.shape[1], -1), outgoing)

    front_args = (
        padded_inner,
        padded_state,
        step_raw,
        kernel_here,
        bias_here,
        conv_state,
        state_bias,
        shift_here,
        rates_here,
    )
    front_vals = mixer_front(*front_args)
    inner, deltas, log_decay, b_proj, c_proj, inflow, passing = front_vals
    span_decay = jnp.ones(passing[:, 0].shape, jnp.float32)
    span_state = jnp.zeros(inflow[:, 0].shape, jnp.float32)
    span_state = passing[:, 0, :, None, None] * span_state + inflow[:, 0]
    span_decay = span_decay * passing[:, 0]
    identity = (jnp.ones_like(span_decay), jnp.zeros_like(span_state))
    incoming = entering_2((span_decay, span_state), "seq", chain_link, identity)[1]
    mixed, outgoing = mixer_rear(*front_vals, incoming, skip_here)
    sigmoid_z = jax.nn.sigmoid(gate_in)
    silu_z = gate_in * sigmoid_z
    gated = mixed * silu_z
    full_width = tensor_count * gated.shape[-1]
    square_sum = lax.psum(jnp.sum(gated * gated, axis=-1), "tensor")
    rms_gate = lax.rsqrt(square_sum / full_width + EPS)[..., None]
    gate_normed = (gated * rms_gate * gain_here).astype(jnp.bfloat16)
    partial_out = jnp.dot(gate_normed, output_full, preferred_element_type=jnp.float32)
    branch_rows = lax.psum_scatter(partial_out, "tensor", scatter_dimension=1, tiled=True)
    block_out = (residual + branch_rows).astype(jnp.bfloat16)
    grad_output = jnp.einsum(
        "srk,srd->kd", gate_normed, cot_rows, preferred_element_type=jnp.float32
    )
    grad_gn = jnp.einsum("srd,kd->srk", cot_rows, output_full, preferred_element_type=jnp.float32)
    scaled = grad_gn * gain_here
    dot_sum = lax.psum(jnp.sum(scaled * gated, axis=-1), "tensor")
    grad_gain_here = jnp.sum(grad_gn * gated * rms_gate, axis=(0, 1))
    grad_gated = rms_gate * scaled - gated * rms_gate**3 * (dot_sum / full_width)[..., None]
    grad_mixed = grad_gated * silu_z
    grad_gate_in = (grad_gated * mixed * sigmoid_z * (1.0 + gate_in * (1.0 - sigmoid_z))).astype(
        jnp.bfloat16
    )
    front_vals, front_back = jax.vjp(mixer_front, *front_args)
    unused_rear, rear_back = jax.vjp(mixer_rear, *front_vals, incoming, skip_here)
    inner, deltas, log_decay, b_proj, c_proj, inflow, passing = front_vals
    grad_blocks = blocked(grad_mixed.reshape(inner.shape), pieces)
    unused_reads, read_back = jax.vjp(
        lambda memory_in: state_reads(
            memory_in, log_decay, c_proj, inflow, passing, seg_blocks, before
        )[0],
        incoming,
    )
    local_grad = read_back(grad_blocks)[0]
    outgoing_grad = carried_in((span_decay, local_grad), "seq", chain_link, identity)[1]
    rear_grads = rear_back((grad_mixed, outgoing_grad))
    grad_skip_here = rear_grads[8]
    (
        pad_grad_inner,
        pad_grad_state,
        grad_step_raw,
        grad_kernel_here,
        grad_bias_here,
        grad_conv_state,
        grad_state_bias,
        grad_shift_here,
        grad_rates_here,
    ) = front_back(tuple(rear_grads[:7]))
    from_next_inner, from_next_state = passed_along(
        (pad_grad_inner[:, :margin], pad_grad_state[:, :margin]), "seq", -1
    )
    grad_inner_pre = jnp.concatenate(
        [pad_grad_inner[:, margin:-margin], pad_grad_inner[:, -margin:] + from_next_inner], axis=1
    )
    grad_state_part = jnp.concatenate(
        [pad_grad_state[:, margin:-margin], pad_grad_state[:, -margin:] + from_next_state], axis=1
    )
    grad_state_pre = lax.psum(grad_state_part, "tensor").astype(jnp.bfloat16)
    grad_inner_low = grad_inner_pre.astype(jnp.bfloat16)
    grad_step_low = grad_step_raw.astype(jnp.bfloat16)
    grad_normed = jnp.einsum(
        "srk,dk->srd", grad_gate_in, gate_full, preferred_element_type=jnp.float32
    )
    grad_normed = grad_normed + jnp.einsum(
        "srk,dk->srd", grad_inner_low, inner_full, preferred_element_type=jnp.float32
    )
    grad_normed = grad_normed + jnp.einsum(
        "srk,dk->srd", grad_step_low, step_full, preferred_element_type=jnp.float32
    )
    grad_rows = lax.psum_scatter(grad_normed, "tensor", scatter_dimension=1, tiled=True)
    own_rows = tokens.shape[1]
    state_mine = lax.dynamic_slice_in_dim(grad_state_pre, tensor_rank * own_rows, own_rows, 1)
    grad_rows = grad_rows + jnp.einsum(
        "srk,dk->srd", state_mine, state_full, preferred_element_type=jnp.float32
    )
    grad_gate_w = jnp.einsum(
        "srd,srk->dk", normed, grad_gate_in, preferred_element_type=jnp.float32
    )
    grad_inner_w = jnp.einsum(
        "srd,srk->dk", normed, grad_inner_low, preferred_element_type=jnp.float32
    )
    grad_state_w = jnp.einsum(
        "srd,srk->dk", normed, grad_state_pre, preferred_element_type=jnp.float32
    )
    grad_step_w = jnp.einsum(
        "srd,srk->dk", normed, grad_step_low, preferred_element_type=jnp.float32
    )
    shard_gate, shard_inner, shard_state, shard_step, shard_output = (
        lax.psum_scatter(grad_gate_w, ("dp", "seq"), scatter_dimension=0, tiled=True),
        lax.psum_scatter(grad_inner_w, ("dp", "seq"), scatter_dimension=0, tiled=True),
        lax.psum_scatter(grad_state_w, ("dp", "seq"), scatter_dimension=0, tiled=True),
        lax.psum_scatter(grad_step_w, ("dp", "seq"), scatter_dimension=0, tiled=True),
        lax.psum_scatter(grad_output, ("dp", "seq"), scatter_dimension=1, tiled=True),
    )
    scaled_in = grad_rows * input_gain
    grad_input_gain = jnp.sum(grad_rows * residual * rms_in, axis=(0, 1))
    grad_tokens = (
        cotangent.astype(jnp.float32)
        + rms_in * scaled_in
        - residual * rms_in**3 * jnp.mean(scaled_in * residual, axis=-1, keepdims=True)
    )

    def placed(whole, piece_grad, start, axis_number):
        return lax.dynamic_update_slice_in_dim(
            jnp.zeros_like(whole), piece_grad, start, axis_number
        )

    smalls = lax.psum(
        (
            grad_input_gain,
            placed(conv_inner, grad_kernel_here, chan_start, 1),
            placed(inner_bias, grad_bias_here, chan_start, 0),
            grad_conv_state,
            grad_state_bias,
            placed(step_bias, grad_shift_here, head_start, 0),
            placed(log_rates, grad_rates_here, head_start, 0),
            placed(skip_gain, grad_skip_here, head_start, 0),
            placed(gated_gain, grad_gain_here, chan_start, 0),
        ),
        ("dp", "seq", "tensor"),
    )
    return (
        block_out,
        grad_tokens,
        smalls[0],
        shard_gate,
        shard_inner,
        shard_state,
        shard_step,
        smalls[1],
        smalls[2],
        smalls[3],
        smalls[4],
        smalls[5],
        smalls[6],
        smalls[7],
        smalls[8],
        shard_output,
    )


def per_device_fast(
    tokens,
    segments,
    input_gain,
    gate_proj,
    inner_proj,
    state_proj,
    step_proj,
    conv_inner,
    inner_bias,
    conv_state,
    state_bias,
    step_bias,
    log_rates,
    skip_gain,
    gated_gain,
    output_proj,
    cotangent,
):
    tensor_count = lax.axis_size("tensor")
    tensor_rank = lax.axis_index("tensor")
    heads = step_proj.shape[1]
    step_wide = jnp.pad(step_proj, ((0, 0), (0, 128 - heads)))
    normed, g8, i8, s8, t8 = gather_all(
        tensor_count,
        tokens,
        input_gain,
        (gate_proj, inner_proj, state_proj, step_wide),
    )
    width = tokens.shape[2]
    inner_full = i8.reshape(width, -1)
    state_full = s8.reshape(width, -1)
    step_full = t8.reshape(width, -1)
    width_here = inner_full.shape[1]
    heads_here = heads
    head_start = tensor_rank * heads_here
    margin = 8
    inner_low = jnp.dot(normed, inner_full, preferred_element_type=jnp.float32).astype(jnp.bfloat16)
    state_low = jnp.dot(normed, state_full, preferred_element_type=jnp.float32).astype(jnp.bfloat16)
    prior_inner, prior_state = passed_along(
        (inner_low[:, -margin:], state_low[:, -margin:]), "seq", 1
    )
    step_raw = jnp.dot(normed, step_full, preferred_element_type=jnp.float32)
    prior_seg = passed_along(segments[:, 1 - KERNEL :], "seq", 1)
    seg_padded = jnp.concatenate([prior_seg, segments], axis=1)
    length = segments.shape[1]
    same = [
        seg_padded[:, KERNEL - 1 - k : KERNEL - 1 - k + length] == segments for k in range(1, KERNEL)
    ]
    same += [segments == prior_seg[:, -1:], segments == segments[:, -1:]]
    rows = jnp.stack(
        [segments.astype(jnp.float32)]
        + [m.astype(jnp.float32) for m in same]
        + [jnp.zeros(segments.shape, jnp.float32)] * 2,
        axis=1,
    )
    heads_param = jnp.pad(
        lax.dynamic_slice_in_dim(
            jnp.stack([step_bias, log_rates, skip_gain]), head_start, heads_here, 1
        ),
        ((0, 5), (0, LANES - heads_here)),
    )
    y_part, u_inner, u_state, entry, incoming, gate_in, cot_rows, o8 = mix_fwd(
        tensor_count, inner_low, prior_inner, state_low, prior_state, step_raw, rows, heads_param,
        conv_inner, inner_bias[None], conv_state, state_bias[None], cotangent, output_proj.T,
        normed, g8,
    )
    grad_mixed, grad_gate_in, outgoing_grad, partial_out, grad_output, grad_gate, grad_gain = gate_stage(
        tensor_count, y_part, u_state, entry, incoming, gate_in, cot_rows, o8, gated_gain[None], normed
    )
    (
        d_inner, d_state, d_step, sm_i, sm_s, sm_h, branch_rows, shard_output, shard_gate
    ) = mix_bwd(
        tensor_count, grad_mixed, u_inner, u_state, inner_low, prior_inner, state_low, prior_state,
        step_raw, rows, incoming, outgoing_grad, heads_param, conv_inner, conv_state,
        partial_out, grad_output, grad_gate,
    )
    gain_row = input_gain[None]
    grad_rows, shard_inner, shard_state, shard_step, sms = reduce_all(
        tensor_count, normed, grad_gate_in, d_inner, d_state, d_step, g8, i8, s8, t8, gain_row,
        sm_i, sm_s, sm_h, grad_gain,
    )
    outs = emit_all(
        tensor_count, heads, tokens, cotangent, gain_row, branch_rows, grad_rows,
        shard_gate, shard_inner, shard_state, shard_step, shard_output, sms,
    )
    flat = (2, 8, 10, 11, 12, 13, 14)
    return tuple(o[0] if i in flat else o for i, o in enumerate(outs))


def solution(mesh):
    fast = mesh.shape["dp"] == 4 and mesh.shape["seq"] == 2
    placed = (
        P("dp", ("seq", "tensor"), None),
        P("dp", "seq"),
        P(),
        P(("dp", "seq"), "tensor"),
        P(("dp", "seq"), "tensor"),
        P(("dp", "seq"), None),
        P(("dp", "seq"), "tensor"),
        P(),
        P(),
        P(),
        P(),
        P(),
        P(),
        P(),
        P(),
        P("tensor", ("dp", "seq")),
        P("dp", ("seq", "tensor"), None),
    )
    return jax.shard_map(
        per_device_fast if fast else per_device,
        mesh=mesh,
        in_specs=placed,
        out_specs=(
            P("dp", ("seq", "tensor"), None),
            P("dp", ("seq", "tensor"), None),
            P(),
            P(("dp", "seq"), "tensor"),
            P(("dp", "seq"), "tensor"),
            P(("dp", "seq"), None),
            P(("dp", "seq"), "tensor"),
            P(),
            P(),
            P(),
            P(),
            P(),
            P(),
            P(),
            P(),
            P("tensor", ("dp", "seq")),
        ),
        check_vma=False,
    )
```

```python
import functools

import jax
import jax.numpy as jnp
from jax import lax
from jax.experimental import pallas as pl
from jax.experimental.pallas import tpu as pltpu
from jax.sharding import PartitionSpec as P

HEAD_DIM = 64
STATE = 128
KERNEL = 4
BLOCK = 256


EPS = 1e-05
HIGH = lax.Precision.HIGHEST


def passed_along(block, axis, distance):
    devices = range(lax.axis_size(axis))
    route = [(i - distance, i) for i in devices if i - distance in devices]
    return lax.ppermute(block, axis, route)


def entering_2(shard, axis, join, neutral):
    place = lax.axis_index(axis)
    gathered = jax.tree.map(
        lambda a, kind: lax.all_gather(a.astype(kind), axis), shard, (jnp.bfloat16, jnp.bfloat16)
    )
    state = jax.tree.map(lambda a, e: jnp.zeros_like(a) + jnp.asarray(e, a.dtype), shard, neutral)

    def one(hop, state):
        return join(
            state,
            jax.tree.map(
                lambda a, own: lax.dynamic_index_in_dim(a, hop, 0, False).astype(own.dtype),
                gathered,
                shard,
            ),
        )

    return lax.fori_loop(0, place, one, state)


def carried_in(shard, axis, combine, identity):
    length, here = (lax.axis_size(axis), lax.axis_index(axis))
    everything = jax.tree.map(
        lambda part, kind: lax.all_gather(part.astype(kind), axis),
        shard,
        jax.tree.map(lambda a: jnp.bfloat16 if a.dtype == jnp.float32 else a.dtype, shard),
    )
    start = jax.tree.map(
        lambda part, zero: jnp.broadcast_to(jnp.asarray(zero, part.dtype), part.shape),
        shard,
        identity,
    )

    def hop(k, before):
        at = length - 1 - k
        reached = at > here
        new = combine(
            before, jax.tree.map(lambda part, own: part[at].astype(own.dtype), everything, shard)
        )
        return jax.tree.map(lambda a, b: jnp.where(reached, a, b), new, before)

    return lax.fori_loop(0, length, hop, start)


def chain_link(earlier, later):
    return (earlier[0] * later[0], later[0][:, :, None, None] * earlier[1] + later[1])


def causal_mix(padded, seg_padded, kernel_w, kernel_b):
    margin = KERNEL - 1
    length = padded.shape[1] - margin
    seg_now = seg_padded[:, margin:]
    result = kernel_b + kernel_w[0] * padded[:, margin:]
    for offset in range(1, KERNEL):
        moved = padded[:, margin - offset : margin - offset + length]
        same_doc = (seg_padded[:, margin - offset : margin - offset + length] == seg_now).astype(
            jnp.float32
        )
        result = result + kernel_w[offset] * moved * same_doc[:, :, None]
    return result


def blocked(values, pieces):
    return values.reshape((values.shape[0], pieces, values.shape[1] // pieces) + values.shape[2:])


def block_sums(inner, deltas, log_decay, b_proj, seg_blocks, before):
    pieces = seg_blocks.shape[1]
    running = jnp.cumsum(blocked(log_decay, pieces), axis=2)
    same_end = (seg_blocks == seg_blocks[:, :, -1:]).astype(jnp.float32)
    to_end = (
        jnp.exp(running[:, :, -1:, :] - running) * same_end[:, :, :, None] * blocked(deltas, pieces)
    )
    inflow = jnp.einsum(
        "scjhp,scjn->schpn",
        to_end[..., None] * blocked(inner, pieces),
        blocked(b_proj, pieces),
        precision=HIGH,
    )
    passing = (
        jnp.exp(running[:, :, -1, :])
        * (seg_blocks[:, :, -1] == before).astype(jnp.float32)[:, :, None]
    )
    return (inflow, passing)


def state_reads(incoming, log_decay, c_proj, inflow, passing, seg_blocks, before):
    pieces = seg_blocks.shape[1]
    running = jnp.cumsum(blocked(log_decay, pieces), axis=2)
    memory = incoming
    entering = [memory]
    memory = passing[:, 0, :, None, None] * memory + inflow[:, 0]
    stacked = jnp.stack(entering, axis=1)
    entry = jnp.exp(running) * (seg_blocks == before[:, :, None]).astype(jnp.float32)[..., None]
    from_state = (
        jnp.einsum("scin,schpn->scihp", blocked(c_proj, pieces), stacked, precision=HIGH)
        * entry[..., None]
    )
    return (from_state, memory)


MESH = pl.DeviceIdType.MESH
BF = jnp.bfloat16
F32 = jnp.float32


def _peers():
    dp, seq, t = lax.axis_index("dp"), lax.axis_index("seq"), lax.axis_index("tensor")
    x, y = lax.rem(dp, 2), lax.div(dp, 2)
    x_dp = dp + 1 - 2 * x
    y_dp = dp + 2 - 4 * y
    d_dp = 3 - dp
    return dp, seq, t, x_dp, y_dp, d_dp


def _dev(dp, seq, t):
    return {"dp": dp, "seq": seq, "tensor": t}


def _plane_barrier(n):
    dp, seq, t, x_dp, y_dp, d_dp = _peers()
    bar = pltpu.get_barrier_semaphore()
    for who in (_dev(dp, 1 - seq, t), _dev(x_dp, seq, t), _dev(y_dp, seq, t)):
        pl.semaphore_signal(bar, inc=1, device_id=who, device_id_type=MESH)

    for step in range(1, n):
        pl.semaphore_signal(
            bar, inc=1, device_id=_dev(dp, seq, lax.rem(t + step, n)), device_id_type=MESH
        )
    pl.semaphore_wait(bar, 3 + n - 1)


class _Line:
    def __init__(self, n, ref, rows, ssem, rsem, own=None):
        self.n, self.ref, self.rows, self.ssem, self.rsem = n, ref, rows, ssem, rsem
        self.own = own

    def block(self, o):
        return self.ref.at[:, pl.ds(pl.multiple_of(o * self.rows, self.rows), self.rows), :]

    def copy(self, o, direction, own=False):
        dp, seq, t = lax.axis_index("dp"), lax.axis_index("seq"), lax.axis_index("tensor")
        return pltpu.make_async_remote_copy(
            src_ref=self.own if own else self.block(o),
            dst_ref=self.block(o),
            send_sem=self.ssem.at[0 if direction > 0 else 1, o],
            recv_sem=self.rsem.at[o],
            device_id=_dev(dp, seq, t + direction),
            device_id_type=MESH,
        )

    def step(self, d):
        n, t = self.n, lax.axis_index("tensor")
        for way in (1, -1):
            o = t - way * d
            here = jnp.logical_and(o >= 0, o < n)
            nxt = jnp.logical_and(t + way >= 0, t + way < n)

            @pl.when(here)
            def _(o=o, way=way, nxt=nxt):
                if d > 0:
                    self.copy(o, way).wait_recv()

                @pl.when(nxt)
                def _():
                    self.copy(o, way, d == 0 and self.own is not None).start()

    def finish(self):
        n, t = self.n, lax.axis_index("tensor")
        for d in range(n):
            for way in (1, -1):
                o = t - way * d
                ok = jnp.logical_and(
                    jnp.logical_and(o >= 0, o < n),
                    jnp.logical_and(t + way >= 0, t + way < n),
                )

                @pl.when(ok)
                def _(o=o, way=way):
                    self.copy(o, way).wait_send()


class _Plane:
    def __init__(self, own, full, ssem, rsem, lsem):
        self.own, self.full, self.ssem, self.rsem, self.lsem = own, full, ssem, rsem, lsem

    def copy(self, src, block, who, s):
        return pltpu.make_async_remote_copy(
            src_ref=src,
            dst_ref=self.full.at[block],
            send_sem=self.ssem.at[s],
            recv_sem=self.rsem.at[s],
            device_id=who,
            device_id_type=MESH,
        )

    def begin(self):
        dp, seq, t, x_dp, y_dp, d_dp = _peers()
        me = dp * 2 + seq
        pltpu.make_async_copy(self.own, self.full.at[me], self.lsem).start()
        self.copy(self.own, me, _dev(x_dp, seq, t), 0).start()
        self.copy(self.own, me, _dev(y_dp, seq, t), 1).start()
        self.copy(self.own, me, _dev(dp, 1 - seq, t), 3).start()

    def forward(self):
        dp, seq, t, x_dp, y_dp, d_dp = _peers()
        bx, by = x_dp * 2 + seq, y_dp * 2 + seq
        self.copy(self.own, bx, _dev(x_dp, seq, t), 0).wait_recv()
        self.copy(self.own, by, _dev(y_dp, seq, t), 1).wait_recv()

        @pl.when(seq == 0)
        def _():
            self.copy(self.full.at[by], by, _dev(x_dp, seq, t), 2).start()

        @pl.when(seq == 1)
        def _():
            self.copy(self.full.at[bx], bx, _dev(y_dp, seq, t), 2).start()

        self.copy(self.full.at[bx], bx, _dev(dp, 1 - seq, t), 4).start()
        self.copy(self.full.at[by], by, _dev(dp, 1 - seq, t), 5).start()

    def share(self):
        dp, seq, t, x_dp, y_dp, d_dp = _peers()
        bd = d_dp * 2 + seq
        self.copy(self.own, bd, _dev(x_dp, seq, t), 2).wait_recv()
        self.copy(self.full.at[bd], bd, _dev(dp, 1 - seq, t), 6).start()

    def arrive(self):
        dp, seq, t, x_dp, y_dp, d_dp = _peers()
        me = dp * 2 + seq
        pltpu.make_async_copy(self.own, self.full.at[me], self.lsem).wait()
        for s in (3, 4, 5, 6):
            self.copy(self.own, me, _dev(dp, 1 - seq, t), s).wait_recv()

    def finish(self):
        dp, seq, t, x_dp, y_dp, d_dp = _peers()
        me = dp * 2 + seq
        for s in range(7):
            self.copy(self.own, me, _dev(dp, 1 - seq, t), s).wait_send()


def gather_kernel(n, tok, gain, wg, wi, ws, wt, normed, fg, fi, fs, ft, zs, zr, ps, pr, ls):
    t = lax.axis_index("tensor")
    rows = tok.shape[1]
    _plane_barrier(n)
    planes = [
        _Plane(own, full, ps.at[i], pr.at[i], ls.at[i])
        for i, (own, full) in enumerate(((ws, fs), (wt, ft), (wi, fi), (wg, fg)))
    ]
    for p in planes[:3]:
        p.begin()
    mine = pl.ds(pl.multiple_of(t * rows, rows), rows)
    for s in range(tok.shape[0]):
        v = tok[s].astype(F32)
        rms = lax.rsqrt(jnp.mean(v * v, axis=-1, keepdims=True) + EPS)
        normed[s, mine, :] = (v * rms * gain[...]).astype(BF)
    a = _Line(n, normed, rows, zs, zr)
    a.step(0)
    planes[3].begin()
    for p in planes[:3]:
        p.forward()
    a.step(1)
    planes[3].forward()
    for p in planes[:3]:
        p.share()
    for d in range(2, n):
        a.step(d)
    planes[3].share()
    for p in planes:
        p.arrive()
    a.finish()
    for p in planes:
        p.finish()


def gather_all(n, tokens, gain, weights):
    seqs, rows, width = tokens.shape
    vm = pl.BlockSpec(memory_space=pltpu.VMEM)
    full = lambda w: jax.ShapeDtypeStruct((8,) + w.shape, w.dtype)
    act = jax.ShapeDtypeStruct((seqs, n * rows, width), BF)
    return pl.pallas_call(
        functools.partial(gather_kernel, n),
        out_shape=(act,) + tuple(full(w) for w in weights),
        in_specs=[vm] * 6,
        out_specs=(vm,) * 5,
        scratch_shapes=[
            pltpu.SemaphoreType.DMA((2, n)),
            pltpu.SemaphoreType.DMA((n,)),
            pltpu.SemaphoreType.DMA((4, 7)),
            pltpu.SemaphoreType.DMA((4, 7)),
            pltpu.SemaphoreType.DMA((4,)),
        ],
        compiler_params=pltpu.CompilerParams(
            collective_id=0, has_side_effects=True, vmem_limit_bytes=28 << 20
        ),
        name="gather_all",
    )(tokens, gain.reshape(1, width), *weights)


def _line_reduce(n, part, left, right, ssem, rsem):
    dp, seq, t = lax.axis_index("dp"), lax.axis_index("seq"), lax.axis_index("tensor")
    rows = left.shape[2]

    def copy(src, box, o, way):
        return pltpu.make_async_remote_copy(
            src_ref=src, dst_ref=box.at[o],
            send_sem=ssem.at[0 if way > 0 else 1, o], recv_sem=rsem.at[0 if way > 0 else 1, o],
            device_id=_dev(dp, seq, t + way), device_id_type=MESH,
        )

    def block(o):
        return part.at[:, pl.ds(pl.multiple_of(o * rows, rows), rows), :]

    def step(k):
        for way, box, place in ((1, left, t), (-1, right, n - 1 - t)):
            target = lambda j: n - 1 - j if way > 0 else j
            if k == 0:
                @pl.when(place == 0)
                def _():
                    for j in range(n - 1):
                        copy(block(target(j)), box, target(j), way).start()
            else:
                @pl.when(jnp.logical_and(place > 0, place <= k))
                def _():
                    o = target(k - place)
                    copy(block(o), box, o, way).wait_recv()
                    for s in range(part.shape[0]):
                        own = part[s, pl.ds(pl.multiple_of(o * rows, rows), rows), :].astype(F32)
                        box[o, s] = (box[o, s].astype(F32) + own).astype(BF)
                    copy(box.at[o], box, o, way).start()

    def final(out):
        mine = pl.ds(pl.multiple_of(t * rows, rows), rows)
        for s in range(part.shape[0]):
            out[s] = part[s, mine, :].astype(F32)

        @pl.when(t > 0)
        def _():
            copy(left.at[0], left, t, 1).wait_recv()
            for s in range(part.shape[0]):
                out[s] = out[s] + left[t, s].astype(F32)

        @pl.when(t < n - 1)
        def _():
            copy(left.at[0], right, t, -1).wait_recv()
            for s in range(part.shape[0]):
                out[s] = out[s] + right[t, s].astype(F32)

    def finish():
        for j in range(n - 1):
            for way, box, o in ((1, left, n - 1 - j), (-1, right, j)):
                sends = (t < o) if way > 0 else (t > o)

                @pl.when(sends)
                def _():
                    copy(box.at[o], box, o, way).wait_send()

    return step, final, finish


class _PlaneReduce:
    def __init__(self, part, pair, box, ssem, rsem):
        self.part, self.pair, self.box, self.ssem, self.rsem = part, pair, box, ssem, rsem

    def copy(self, src, dst, who, s):
        return pltpu.make_async_remote_copy(
            src_ref=src, dst_ref=dst, send_sem=self.ssem.at[s], recv_sem=self.rsem.at[s],
            device_id=who, device_id_type=MESH,
        )

    def begin(self):
        dp, seq, t, x_dp, y_dp, d_dp = _peers()
        for slot, chip in enumerate((d_dp, x_dp, y_dp, dp)):
            self.copy(self.part.at[chip * 2 + 1 - seq], self.pair.at[slot], _dev(dp, 1 - seq, t), slot).start()

    def _paired(self, slot, chip, also=None):
        dp, seq, t, x_dp, y_dp, d_dp = _peers()
        self.copy(self.pair.at[slot], self.pair.at[slot], _dev(dp, 1 - seq, t), slot).wait_recv()
        v = self.part[chip * 2 + seq].astype(F32) + self.pair[slot].astype(F32)
        self.pair[slot] = v.astype(BF)

    def send_far(self):
        dp, seq, t, x_dp, y_dp, d_dp = _peers()
        for slot, chip in enumerate((d_dp, x_dp, y_dp)):
            self._paired(slot, chip)
            if slot == 0:
                @pl.when(seq == 0)
                def _():
                    self.copy(self.pair.at[0], self.box.at[2], _dev(x_dp, seq, t), 4).start()

                @pl.when(seq == 1)
                def _():
                    self.copy(self.pair.at[0], self.box.at[2], _dev(y_dp, seq, t), 4).start()

        @pl.when(seq == 0)
        def _():
            self.copy(self.pair.at[1], self.box.at[0], _dev(x_dp, seq, t), 5).start()

        @pl.when(seq == 1)
        def _():
            self.copy(self.pair.at[2], self.box.at[1], _dev(y_dp, seq, t), 6).start()

    def send_near(self):
        dp, seq, t, x_dp, y_dp, d_dp = _peers()
        self.copy(self.pair.at[0], self.box.at[2], _dev(dp, seq, t), 4).wait_recv()

        @pl.when(seq == 0)
        def _():
            self.box[2] = (self.box[2].astype(F32) + self.pair[2].astype(F32)).astype(BF)
            self.copy(self.box.at[2], self.box.at[1], _dev(y_dp, seq, t), 6).start()

        @pl.when(seq == 1)
        def _():
            self.box[2] = (self.box[2].astype(F32) + self.pair[1].astype(F32)).astype(BF)
            self.copy(self.box.at[2], self.box.at[0], _dev(x_dp, seq, t), 5).start()

    def final(self, out):
        dp, seq, t, x_dp, y_dp, d_dp = _peers()
        self.copy(self.pair.at[3], self.pair.at[3], _dev(dp, seq, t), 3).wait_recv()
        self.copy(self.pair.at[0], self.box.at[0], _dev(dp, seq, t), 5).wait_recv()
        self.copy(self.pair.at[0], self.box.at[1], _dev(dp, seq, t), 6).wait_recv()
        out[...] = (
            self.part[dp * 2 + seq].astype(F32) + self.pair[3].astype(F32)
            + self.box[0].astype(F32) + self.box[1].astype(F32)
        )

    def finish(self):
        dp, seq, t, x_dp, y_dp, d_dp = _peers()
        for s in range(7):
            self.copy(self.pair.at[0], self.box.at[0], _dev(dp, 1 - seq, t), s).wait_send()


class _Smalls:
    def __init__(self, n, box, line, ssem, rsem):
        self.n, self.box, self.line, self.ssem, self.rsem = n, box, line, ssem, rsem

    def copy(self, j, who):
        return pltpu.make_async_remote_copy(
            src_ref=self.box.at[2 * j], dst_ref=self.box.at[2 * j + 1],
            send_sem=self.ssem.at[j], recv_sem=self.rsem.at[j],
            device_id=who, device_id_type=MESH,
        )

    def near(self, j):
        dp, seq, t, x_dp, y_dp, d_dp = _peers()
        return (_dev(dp, 1 - seq, t), _dev(x_dp, seq, t), _dev(y_dp, seq, t))[j]

    def begin(self, value):
        self.box[0] = value
        self.copy(0, self.near(0)).start()

    def step(self, j):
        self.copy(j, self.near(j)).wait_recv()
        total = self.box[2 * j] + self.box[2 * j + 1]
        if j < 2:
            self.box[2 * j + 2] = total
            self.copy(j + 1, self.near(j + 1)).start()
        else:
            t = lax.axis_index("tensor")
            self.line[t] = total
            for o in range(self.n):
                @pl.when(t != o)
                def _(o=o):
                    self.across(t, o).start()

    def across(self, src, who):
        dp, seq, t = lax.axis_index("dp"), lax.axis_index("seq"), lax.axis_index("tensor")
        return pltpu.make_async_remote_copy(
            src_ref=self.line.at[src], dst_ref=self.line.at[src],
            send_sem=self.ssem.at[3 + who], recv_sem=self.rsem.at[3 + src],
            device_id=_dev(dp, seq, who), device_id_type=MESH,
        )

    def final(self):
        t = lax.axis_index("tensor")
        for o in range(self.n):
            @pl.when(t != o)
            def _(o=o):
                self.across(o, o).wait_recv()

    def finish(self):
        t = lax.axis_index("tensor")
        for j in range(3):
            self.copy(j, self.near(j)).wait_send()
        for o in range(self.n):
            @pl.when(t != o)
            def _(o=o):
                self.across(t, o).wait_send()


class _LineSum:
    def __init__(self, n, part, box, out, ssem, rsem):
        self.n, self.part, self.box, self.out, self.ssem, self.rsem = n, part, box, out, ssem, rsem

    def copy(self, phase, src_block, dst_ref, who, origin):
        dp, seq = lax.axis_index("dp"), lax.axis_index("seq")
        return pltpu.make_async_remote_copy(
            src_ref=src_block, dst_ref=dst_ref,
            send_sem=self.ssem.at[phase, who], recv_sem=self.rsem.at[phase, origin],
            device_id=_dev(dp, seq, who), device_id_type=MESH,
        )

    def scatter(self):
        t = lax.axis_index("tensor")
        for o in range(self.n):
            @pl.when(t != o)
            def _(o=o):
                self.copy(0, self.part.at[o], self.box.at[t], o, t).start()

    def gather(self):
        t = lax.axis_index("tensor")
        total = self.part[t].astype(F32)
        for o in range(self.n):
            @pl.when(t != o)
            def _(o=o):
                self.copy(0, self.part.at[o], self.box.at[o], o, o).wait_recv()

            @pl.when(t == o)
            def _(o=o):
                self.box[o] = jnp.zeros(self.box.shape[1:], self.box.dtype)
        for o in range(self.n):
            total = total + self.box[o].astype(F32)
        self.out[t] = total.astype(self.out.dtype)
        for o in range(self.n):
            @pl.when(t != o)
            def _(o=o):
                self.copy(1, self.out.at[t], self.out.at[t], o, t).start()

    def arrive(self):
        t = lax.axis_index("tensor")
        for o in range(self.n):
            @pl.when(t != o)
            def _(o=o):
                self.copy(1, self.out.at[o], self.out.at[o], o, o).wait_recv()

    def finish(self):
        t = lax.axis_index("tensor")
        for o in range(self.n):
            @pl.when(t != o)
            def _(o=o):
                self.copy(0, self.part.at[o], self.box.at[o], o, o).wait_send()
                self.copy(1, self.part.at[o], self.box.at[o], o, o).wait_send()


LANES = 128


def _split(v, parts):
    out = []
    for _ in range(parts):
        b = v.astype(BF)
        out.append(b)
        v = v - b.astype(F32)
    return jnp.concatenate(out, axis=1)


def _dot(a, b, ca=1, cb=0):
    return lax.dot_general(a, b, (((ca,), (cb,)), ((), ())), preferred_element_type=F32)


def _iota(shape, axis):
    return lax.broadcasted_iota(jnp.int32, shape, axis)


def _spreader(rows, p):
    head = lax.rem(_iota((rows, LANES), 0), LANES)
    return (head == 2 * p + lax.div(_iota((rows, LANES), 1), HEAD_DIM)).astype(F32).astype(BF)


def _folder(rows, p):
    chan = lax.rem(_iota((rows, LANES), 0), LANES)
    return (_iota((rows, LANES), 1) == 2 * p + lax.div(chan, HEAD_DIM)).astype(F32).astype(BF)


def _sig(v):
    return 1.0 / (1.0 + jnp.exp(-v))


def _three(v):
    return v[:, :LANES] + v[:, LANES : 2 * LANES] + v[:, 2 * LANES :]


def _head_scalars(raw, hp, marks, length):
    v = raw + hp[0:1, :]
    delta = jnp.maximum(v, 0.0) + jnp.log1p(jnp.exp(-jnp.abs(v)))
    log_decay = -delta * jnp.exp(hp[1:2, :])
    lower = (_iota((length, length), 0) >= _iota((length, length), 1)).astype(F32).astype(BF)
    running = _three(_dot(lower, _split(log_decay, 3)))
    entry = jnp.exp(running) * marks[:, 4:5]
    to_end = jnp.exp(running[length - 1 :, :] - running) * marks[:, 5:6]
    return v, delta, log_decay, running, entry, to_end


def _marks(rows):
    full = jnp.concatenate([rows, jnp.zeros((LANES - rows.shape[0], rows.shape[1]), F32)], axis=0)
    return full.T


def _bias_matrix(rows, marks, length):
    ok = (_iota((length, length), 0) >= _iota((length, length), 1)) & (
        marks[:, 0:1] == rows[0:1, :]
    )
    return jnp.where(ok, 0.0, -1e30)


def _conv(pad, marks, taps, bias, length):
    total = bias + taps[0:1, :] * pad[8 : 8 + length, :]
    for k in range(1, KERNEL):
        total = total + taps[k : k + 1, :] * (pad[8 - k : 8 - k + length, :] * marks[:, k : k + 1])
    return total


def mix_fwd_kernel(n, pre_i, old_i, pre_s, old_s, raw, rows, hp, taps_i, bias_i, taps_s, bias_s,
                   cot, wo, normed, wg, y, u_i, u_s, entry_o, incoming, gate, cot_full, fo,
                   pad, run3, run_t, bias_m, scores, heads_hl, inflow, zs, zr, ps, pr, ls, hs):
    t = lax.axis_index("tensor")
    seqs, length, width = pre_i.shape
    pairs = width // LANES
    _plane_barrier(n)
    line = _Line(n, cot_full, cot.shape[1], zs, zr, cot)
    plane = _Plane(wo, fo, ps, pr, ls.at[0])
    own = pltpu.make_async_copy(cot, line.block(t), ls.at[1])
    own.start()
    line.step(0)
    plane.begin()

    def one(s, _):
        rw = rows[s]
        marks = _marks(rw)
        v, delta, log_decay, running, entry, to_end = _head_scalars(raw[s], hp, marks, length)
        entry_o[s] = entry
        run3[...] = _split(running, 3)
        run_t[...] = running.T
        bias_m[...] = _bias_matrix(rw, marks, length)
        heads_hl[0] = _split(delta, 2)
        heads_hl[1] = _split(to_end, 2)
        maps = []
        for half in range(2):
            ch = slice(half * STATE, (half + 1) * STATE)
            pad[0:8, :] = old_s[s, :, ch].astype(F32)
            pad[8:, :] = pre_s[s, :, ch].astype(F32)
            u = _conv(pad, marks, taps_s[:, ch], bias_s[:, ch], length)
            u_s[s, :, ch] = u
            maps.append((u * _sig(u)).astype(BF))
        b_map, c_map = maps
        scores[...] = _dot(c_map, b_map, 1, 1)

        def pair(p, _):
            @pl.when(jnp.logical_and(s == 1, p == 0))
            def _():
                line.step(1)
                plane.forward()

            @pl.when(jnp.logical_and(s == 1, p == 4))
            def _():
                plane.share()

            ch = pl.ds(pl.multiple_of(p * LANES, LANES), LANES)
            at = pl.ds(pl.multiple_of(t * width + p * LANES, LANES), LANES)
            pad[0:8, :] = old_i[s, :, ch].astype(F32)
            pad[8:, :] = pre_i[s, :, ch].astype(F32)
            u = _conv(pad, marks, taps_i[:, at], bias_i[:, at], length)
            u_i[s, :, ch] = u
            x = u * _sig(u)
            spread = _spreader(2 * LANES, p)
            xd = x * _dot(heads_hl[0], spread)
            inflow[s, :, ch] = _dot(b_map, (xd * _dot(heads_hl[1], spread)).astype(BF), 0, 0).astype(BF)
            skip = _dot(_split(hp[...], 2), spread)[2:3, :]
            total = skip * x
            xb = xd.astype(BF)
            lane = lax.div(_iota(xb.shape, 1), HEAD_DIM)
            for a in range(2):
                h = 2 * p + a
                pick = (lax.rem(_iota((3 * LANES, length), 0), LANES) == h).astype(F32).astype(BF)
                decay = jnp.exp(_dot(run3[...], pick) - run_t[pl.ds(h, 1), :] + bias_m[...])
                mixing = (decay * scores[...]).astype(BF)
                total = total + _dot(mixing, jnp.where(lane == a, xb, jnp.zeros_like(xb)))
            y[s, :, ch] = total
            return 0

        lax.fori_loop(0, pairs, pair, 0)
        return 0

    lax.fori_loop(0, seqs, one, 0)
    dp, seq = lax.axis_index("dp"), lax.axis_index("seq")
    handed = pltpu.make_async_remote_copy(
        src_ref=inflow, dst_ref=incoming, send_sem=hs.at[0], recv_sem=hs.at[1],
        device_id=_dev(dp, 1 - seq, t), device_id_type=MESH,
    )

    @pl.when(seq == 0)
    def _():
        handed.start()
        incoming[...] = jnp.zeros_like(incoming)

    line.step(2)
    flat = normed[...].reshape(seqs * length, normed.shape[2])

    def gate_part(c, _):
        ch = pl.ds(pl.multiple_of(c * 2 * LANES, 2 * LANES), 2 * LANES)
        part = _dot(flat, wg[:, :, ch].reshape(normed.shape[2], 2 * LANES))
        gate[:, :, ch] = part.reshape(seqs, length, 2 * LANES)
        return 0

    lax.fori_loop(0, width // (2 * LANES), gate_part, 0)
    for d in range(3, n):
        line.step(d)
    plane.arrive()
    own.wait()

    @pl.when(seq == 0)
    def _():
        handed.wait_send()

    @pl.when(seq == 1)
    def _():
        handed.wait_recv()

    line.finish()
    plane.finish()


def _mixer_call(kernel, ins, outs, scratch, name, cost, number):
    vm = pl.BlockSpec(memory_space=pltpu.VMEM)
    return pl.pallas_call(
        kernel,
        out_shape=outs,
        in_specs=[vm] * len(ins),
        out_specs=(vm,) * len(outs),
        scratch_shapes=scratch,
        compiler_params=pltpu.CompilerParams(
            collective_id=number, has_side_effects=True, vmem_limit_bytes=28 << 20
        ),
        cost_estimate=pl.CostEstimate(flops=cost, bytes_accessed=1 << 20, transcendentals=0),
        name=name,
    )(*ins)


def mix_fwd(n, pre_i, old_i, pre_s, old_s, raw, rows, hp, taps_i, bias_i, taps_s, bias_s, cot, wo,
            normed, wg):
    seqs, length, width = pre_i.shape
    sd = jax.ShapeDtypeStruct
    return _mixer_call(
        functools.partial(mix_fwd_kernel, n),
        (pre_i, old_i, pre_s, old_s, raw, rows, hp, taps_i, bias_i, taps_s, bias_s, cot, wo,
         normed, wg),
        (
            sd((seqs, length, width), F32),
            sd((seqs, length, width), F32),
            sd((seqs, length, 2 * STATE), F32),
            sd((seqs, length, LANES), F32),
            sd((seqs, STATE, width), BF),
            sd((seqs, length, width), F32),
            sd((seqs, length, cot.shape[2]), BF),
            sd((8,) + wo.shape, BF),
        ),
        [
            pltpu.VMEM((8 + length, LANES), F32),
            pltpu.VMEM((length, 3 * LANES), BF),
            pltpu.VMEM((LANES, length), F32),
            pltpu.VMEM((length, length), F32),
            pltpu.VMEM((length, length), F32),
            pltpu.VMEM((2, length, 2 * LANES), BF),
            pltpu.VMEM((seqs, STATE, width), BF),
            pltpu.SemaphoreType.DMA((2, n)),
            pltpu.SemaphoreType.DMA((n,)),
            pltpu.SemaphoreType.DMA((7,)),
            pltpu.SemaphoreType.DMA((7,)),
            pltpu.SemaphoreType.DMA((2,)),
            pltpu.SemaphoreType.DMA((2,)),
        ],
        "mix_fwd",
        4 * 10**9,
        3,
    )


def gate_kernel(n, y_part, u_s, entry, h0, gate, cot, wo, gain, tokens_in,
                d_mixed, d_gate, lam, po, go, gg, g_gain,
                mixed, gated, grad_gn, normed, local, acc, box, ss, rs, hs):
    dp, seq, t = lax.axis_index("dp"), lax.axis_index("seq"), lax.axis_index("tensor")
    seqs, length, width = y_part.shape
    model = cot.shape[2]
    wide = 2 * LANES
    bar = pltpu.get_barrier_semaphore()
    pl.semaphore_signal(bar, inc=1, device_id=_dev(dp, 1 - seq, t), device_id_type=MESH)
    for step in range(1, n):
        pl.semaphore_signal(
            bar, inc=1, device_id=_dev(dp, seq, lax.rem(t + step, n)), device_id_type=MESH
        )
    acc[...] = jnp.zeros_like(acc)
    g_gain[...] = jnp.zeros_like(g_gain)

    def spread_of(s, c):
        heads = _split(entry[s], 2)
        head = lax.rem(_iota((wide, wide), 0), LANES)
        one = head == 4 * c + lax.div(_iota((wide, wide), 1), HEAD_DIM)
        return _dot(heads, one.astype(F32).astype(BF))

    def maps(s):
        u = u_s[s, :, STATE:]
        return (u * _sig(u)).astype(BF)

    def first(c, _):
        ch = pl.ds(pl.multiple_of(c * wide, wide), wide)
        at = pl.ds(pl.multiple_of(t * width + c * wide, wide), wide)
        w = wo[:, :, ch].reshape(model, wide)
        for s in range(seqs):
            g = _dot(cot[s], w)
            grad_gn[s, :, ch] = g
            m = y_part[s, :, ch] + spread_of(s, c) * _dot(maps(s), h0[s, :, ch])
            z = gate[s, :, ch]
            gd = m * (z * _sig(z))
            mixed[s, :, ch] = m
            gated[s, :, ch] = gd
            sq, ds = gd * gd, g * gain[:, at] * gd
            acc[0, s] += sq[:, :LANES] + sq[:, LANES:]
            acc[1, s] += ds[:, :LANES] + ds[:, LANES:]
        return 0

    lax.fori_loop(0, width // wide, first, 0)
    ones = jnp.ones((8, wide), F32).astype(BF)
    row = _iota((8, length), 0)
    mine = jnp.zeros((8, length), F32)
    for kind in range(2):
        for s in range(seqs):
            sums = _dot(ones, _split(acc[kind, s], 2), 1, 1)
            mine = jnp.where(row == kind * seqs + s, sums, mine)
    box[t] = mine
    pl.semaphore_wait(bar, n)

    def copy(src, who):
        return pltpu.make_async_remote_copy(
            src_ref=box.at[src], dst_ref=box.at[src], send_sem=ss.at[who], recv_sem=rs.at[src],
            device_id=_dev(dp, seq, who), device_id_type=MESH,
        )

    for o in range(n):
        @pl.when(t != o)
        def _(o=o):
            copy(t, o).start()
    for o in range(n):
        @pl.when(t != o)
        def _(o=o):
            copy(o, o).wait_recv()
    full_width = n * width
    cols = _marks(jnp.sum(box[...], axis=0) / full_width)

    def second(c, _):
        ch = pl.ds(pl.multiple_of(c * wide, wide), wide)
        at = pl.ds(pl.multiple_of(t * width + c * wide, wide), wide)
        gn = gain[:, at]
        for s in range(seqs):
            rms = lax.rsqrt(cols[:, s : s + 1] + EPS)
            mean = cols[:, seqs + s : seqs + s + 1]
            g, gd, m, z = grad_gn[s, :, ch], gated[s, :, ch], mixed[s, :, ch], gate[s, :, ch]
            sg = _sig(z)
            scaled = gd * rms
            normed[s, :, ch] = (scaled * gn).astype(BF)
            g_gain[0:1, ch] += jnp.sum(g * scaled, axis=0, keepdims=True)
            d_gd = rms * (g * gn) - scaled * (rms * rms * mean)
            dm = d_gd * (z * sg)
            d_mixed[s, :, ch] = dm
            d_gate[s, :, ch] = (d_gd * m * sg * (1.0 + z * (1.0 - sg))).astype(BF)
            ed = (spread_of(s, c) * dm).astype(BF)
            local[s, :, ch] = _dot(maps(s), ed, 0, 0).astype(BF)
        return 0

    lax.fori_loop(0, width // wide, second, 0)
    handed = pltpu.make_async_remote_copy(
        src_ref=local, dst_ref=lam, send_sem=hs.at[0], recv_sem=hs.at[1],
        device_id=_dev(dp, 1 - seq, t), device_id_type=MESH,
    )

    @pl.when(seq == 1)
    def _():
        handed.start()
        lam[...] = jnp.zeros_like(lam)

    blocks = 2
    rows = blocks * wo.shape[1]

    def third(b, _):
        ch = pl.ds(pl.multiple_of(b * rows, LANES), rows)
        w = wo[pl.ds(b * blocks, blocks)].reshape(rows, width)
        total = None
        for s in range(seqs):
            po[s, :, ch] = _dot(normed[s], w, 1, 1).astype(BF)
            part = _dot(cot[s, :, ch], normed[s], 0, 0)
            total = part if total is None else total + part
        go[pl.ds(b * blocks, blocks)] = total.reshape(blocks, wo.shape[1], width).astype(BF)
        total = None
        for s in range(seqs):
            part = _dot(tokens_in[s, :, ch], d_gate[s], 0, 0)
            total = part if total is None else total + part
        gg[pl.ds(b * blocks, blocks)] = total.reshape(blocks, wo.shape[1], width).astype(BF)
        return 0

    lax.fori_loop(0, model // rows, third, 0)

    @pl.when(seq == 1)
    def _():
        handed.wait_send()

    @pl.when(seq == 0)
    def _():
        handed.wait_recv()

    for o in range(n):
        @pl.when(t != o)
        def _(o=o):
            copy(o, o).wait_send()


def gate_stage(n, y_part, u_s, entry, h0, gate, cot, wo, gain, tokens_in):
    seqs, length, width = y_part.shape
    sd = jax.ShapeDtypeStruct
    whole = pltpu.VMEM((seqs, length, width), F32)
    return _mixer_call(
        functools.partial(gate_kernel, n),
        (y_part, u_s, entry, h0, gate, cot, wo, gain, tokens_in),
        (
            sd((seqs, length, width), F32),
            sd((seqs, length, width), BF),
            sd((seqs, STATE, width), BF),
            sd((seqs, length, cot.shape[2]), BF),
            sd(wo.shape, BF),
            sd(wo.shape, BF),
            sd((8, width), F32),
        ),
        [
            whole, whole, whole,
            pltpu.VMEM((seqs, length, width), BF),
            pltpu.VMEM((seqs, STATE, width), BF),
            pltpu.VMEM((2, seqs, length, LANES), F32),
            pltpu.VMEM((n, 8, length), F32),
            pltpu.SemaphoreType.DMA((n,)),
            pltpu.SemaphoreType.DMA((n,)),
            pltpu.SemaphoreType.DMA((2,)),
        ],
        "gate_stage",
        6 * 10**9,
        2,
    )


def mix_bwd_kernel(n, dy_r, u_i, u_s, pre_i, old_i, pre_s, old_s, raw, rows, h0, lam, hp,
                   taps_i, taps_s, po, go, gg,
                   d_i, d_s, d_raw, sm_i, sm_s, sm_h, o_po, o_go, o_gg,
                   pad, moved, run3, run_t, bias_m, scores, d_scores, heads_hl,
                   acc_r, acc_c, acc_d, acc_q, d_b, d_c, lo, ro, xo, bo, xg, bg,
                   head_i, tail_i, head_s, tail_s, next_i, next_s, zs, zr, ps, pr, hs):
    t = lax.axis_index("tensor")
    seqs, length, width = pre_i.shape
    pairs = width // LANES
    _plane_barrier(n)
    step_o, final_o, finish_o = _line_reduce(n, po, lo, ro, zs, zr)
    planes = (
        _PlaneReduce(go, xo, bo, ps.at[0], pr.at[0]), _PlaneReduce(gg, xg, bg, ps.at[1], pr.at[1])
    )
    step_o(0)
    for plane in planes:
        plane.begin()
    sm_i[...] = jnp.zeros_like(sm_i)
    sm_s[...] = jnp.zeros_like(sm_s)
    sm_h[...] = jnp.zeros_like(sm_h)
    moved[0:8, :] = jnp.zeros((8, LANES), F32)
    moved[8 + length :, :] = jnp.zeros((8, LANES), F32)

    def conv_back(du, marks, taps, s, ch, d_o, head_o, tail_o, sm):
        total = None
        for k in range(KERNEL):
            m = du if k == 0 else du * marks[:, k : k + 1]
            moved[8 : 8 + length, :] = m
            sm[k : k + 1, ch] += jnp.sum(m * pad[8 - k : 8 - k + length, :], axis=0, keepdims=True)
            part = taps[k : k + 1, :] * moved[k : k + 8 + length, :]
            total = part if total is None else total + part
        sm[4:5, ch] += jnp.sum(du, axis=0, keepdims=True)
        head_o[s, :, ch] = total[0:8, :]
        d_o[s, :, ch] = total[8:, :].astype(BF)
        tail_o[s, :, ch] = total[length - 8 :, :]

    def one(s, _):
        rw = rows[s]
        marks = _marks(rw)
        v, delta, log_decay, running, entry, to_end = _head_scalars(raw[s], hp, marks, length)
        run3[...] = _split(running, 3)
        run_t[...] = running.T
        bias_m[...] = _bias_matrix(rw, marks, length)
        heads_hl[0] = _split(delta, 2)
        heads_hl[1] = _split(to_end, 2)
        heads_hl[2] = _split(entry, 2)
        ub, uc = u_s[s, :, :STATE], u_s[s, :, STATE:]
        sb, sc = _sig(ub), _sig(uc)
        b_map, c_map = (ub * sb).astype(BF), (uc * sc).astype(BF)
        scores[...] = _dot(c_map, b_map, 1, 1)
        d_scores[...] = jnp.zeros_like(d_scores)
        for acc in (acc_r, acc_c, acc_d, acc_q, d_b, d_c):
            acc[...] = jnp.zeros_like(acc)

        def pair(p, _):
            @pl.when(jnp.logical_and(s == 0, p == 2))
            def _():
                planes[0].send_far()

            @pl.when(jnp.logical_and(s == 0, p == 3))
            def _():
                planes[1].send_far()

            @pl.when(jnp.logical_and(s == 0, p == 5))
            def _():
                step_o(1)

            @pl.when(jnp.logical_and(s == 1, p == 2))
            def _():
                planes[0].send_near()

            @pl.when(jnp.logical_and(s == 1, p == 5))
            def _():
                planes[1].send_near()

            @pl.when(jnp.logical_and(s == 1, p == 4))
            def _():
                step_o(2)

            ch = pl.ds(pl.multiple_of(p * LANES, LANES), LANES)
            at = pl.ds(pl.multiple_of(t * width + p * LANES, LANES), LANES)
            u = u_i[s, :, ch]
            sg = _sig(u)
            x = u * sg
            dy = dy_r[s, :, ch]
            spread, fold = _spreader(2 * LANES, p), _folder(2 * LANES, p)
            dl = _dot(heads_hl[0], spread)
            q = _dot(heads_hl[1], spread)
            e = _dot(heads_hl[2], spread)
            xd = x * dl
            xb, db = xd.astype(BF), dy.astype(BF)
            h_in, l_in = h0[s, :, ch], lam[s, :, ch]
            c_h = _dot(c_map, h_in)
            b_l = _dot(b_map, l_in)
            qx, ed = q * xd, e * dy
            d_b[...] += _dot(qx.astype(BF), l_in, 1, 1)
            d_c[...] += _dot(ed.astype(BF), h_in, 1, 1)
            late = qx * b_l
            dxd = q * b_l
            lane = lax.div(_iota(xb.shape, 1), HEAD_DIM)
            for a in range(2):
                h = 2 * p + a
                pick = (lax.rem(_iota((3 * LANES, length), 0), LANES) == h).astype(F32).astype(BF)
                decay = jnp.exp(_dot(run3[...], pick) - run_t[pl.ds(h, 1), :] + bias_m[...])
                da = jnp.where(lane == a, db, jnp.zeros_like(db))
                ld = decay * _dot(da, xb, 1, 1)
                d_scores[...] += ld
                both = (ld * scores[...]).astype(BF)
                mixing = (decay * scores[...]).astype(BF)
                dxd = dxd + _dot(mixing, da, 0, 0)
                col = (_iota((length, LANES), 1) == h).astype(F32).astype(BF)
                row = (_iota((LANES, length), 0) == h).astype(F32).astype(BF)
                acc_r[...] += _dot(both, col)
                acc_c[...] += _dot(row, both)
            acc_r[...] += _dot(_split(ed * c_h - late, 2), fold)
            acc_d[...] += _dot(_split(dxd * x, 2), fold)
            total = jnp.broadcast_to(jnp.sum(late, axis=0, keepdims=True), (8, LANES))
            acc_q[...] += _dot(_split(total, 2), fold)
            skip = _dot(_split(hp[...], 2), spread)[2:3, :]
            sm_i[5:6, ch] += jnp.sum(dy * x, axis=0, keepdims=True)
            du = (dxd * dl + skip * dy) * (sg * (1.0 + u * (1.0 - sg)))
            pad[0:8, :] = old_i[s, :, ch].astype(F32)
            pad[8:, :] = pre_i[s, :, ch].astype(F32)
            conv_back(du, marks, taps_i[:, at], s, ch, d_i, head_i, tail_i, sm_i)
            return 0

        lax.fori_loop(0, pairs, pair, 0)
        ds = d_scores[...].astype(BF)
        grads = (d_b[...] + _dot(ds, c_map, 0, 0), d_c[...] + _dot(ds, b_map))
        for half, (g, u, sg) in enumerate(zip(grads, (ub, uc), (sb, sc))):
            ch = slice(half * STATE, (half + 1) * STATE)
            pad[0:8, :] = old_s[s, :, ch].astype(F32)
            pad[8:, :] = pre_s[s, :, ch].astype(F32)
            du = g * (sg * (1.0 + u * (1.0 - sg)))
            conv_back(du, marks, taps_s[:, ch], s, ch, d_s, head_s, tail_s, sm_s)
        d_run = acc_r[...] - acc_c[...].T
        last = _iota(d_run.shape, 0) == length - 1
        d_run = d_run + jnp.where(last, acc_q[0:1, :], 0.0)
        upper = (_iota((length, length), 0) <= _iota((length, length), 1)).astype(F32).astype(BF)
        d_log = _three(_dot(upper, _split(d_run, 3)))
        d_delta = acc_d[...] - d_log * jnp.exp(hp[1:2, :])
        d_step = d_delta * _sig(v)
        d_raw[s] = d_step.astype(BF)
        sm_h[0:1, :] += jnp.sum(d_step, axis=0, keepdims=True)
        sm_h[1:2, :] += jnp.sum(d_log * log_decay, axis=0, keepdims=True)
        return 0

    lax.fori_loop(0, seqs, one, 0)
    for k in range(3, n - 1):
        step_o(k)
    dp, seq = lax.axis_index("dp"), lax.axis_index("seq")
    handed = [
        pltpu.make_async_remote_copy(
            src_ref=a, dst_ref=b, send_sem=hs.at[2 * i], recv_sem=hs.at[2 * i + 1],
            device_id=_dev(dp, 1 - seq, t), device_id_type=MESH,
        )
        for i, (a, b) in enumerate(((head_i, next_i), (head_s, next_s)))
    ]

    @pl.when(seq == 1)
    def _():
        for c in handed:
            c.start()

    planes[0].final(o_go)

    @pl.when(seq == 0)
    def _():
        for c, box, tail, out in zip(handed, (next_i, next_s), (tail_i, tail_s), (d_i, d_s)):
            c.wait_recv()
            for s in range(seqs):
                more = jnp.concatenate([jnp.zeros_like(box[s]), box[s]], axis=0)
                out[s, length - 16 :, :] = (tail[s] + more).astype(BF)

    @pl.when(seq == 1)
    def _():
        for c in handed:
            c.wait_send()

    planes[1].final(o_gg)
    final_o(o_po)
    for plane in planes:
        plane.finish()
    finish_o()


def mix_bwd(n, dy, u_i, u_s, pre_i, old_i, pre_s, old_s, raw, rows, h0, lam, hp, taps_i, taps_s,
            po, go, gg):
    seqs, length, width = pre_i.shape
    model = po.shape[2]
    box = pltpu.VMEM((n, seqs, length // n, model), BF)
    sd = jax.ShapeDtypeStruct
    square = pltpu.VMEM((length, length), F32)
    tall = pltpu.VMEM((length, LANES), F32)
    return _mixer_call(
        functools.partial(mix_bwd_kernel, n),
        (dy, u_i, u_s, pre_i, old_i, pre_s, old_s, raw, rows, h0, lam, hp, taps_i, taps_s, po, go,
         gg),
        (
            sd((seqs, length, width), BF),
            sd((seqs, length, 2 * STATE), BF),
            sd((seqs, length, LANES), BF),
            sd((8, width), F32),
            sd((8, 2 * STATE), F32),
            sd((8, LANES), F32),
            sd((seqs, length // n, model), F32),
            sd(go.shape[1:], F32),
            sd(gg.shape[1:], F32),
        ),
        [
            pltpu.VMEM((8 + length, LANES), F32),
            pltpu.VMEM((16 + length, LANES), F32),
            pltpu.VMEM((length, 3 * LANES), BF),
            pltpu.VMEM((LANES, length), F32),
            square, square, square,
            pltpu.VMEM((3, length, 2 * LANES), BF),
            tall, pltpu.VMEM((LANES, length), F32), tall, pltpu.VMEM((8, LANES), F32), tall, tall,
            box, box,
            pltpu.VMEM((4,) + go.shape[1:], BF),
            pltpu.VMEM((3,) + go.shape[1:], BF),
            pltpu.VMEM((4,) + gg.shape[1:], BF),
            pltpu.VMEM((3,) + gg.shape[1:], BF),
            pltpu.VMEM((seqs, 8, width), F32),
            pltpu.VMEM((seqs, 16, width), F32),
            pltpu.VMEM((seqs, 8, 2 * STATE), F32),
            pltpu.VMEM((seqs, 16, 2 * STATE), F32),
            pltpu.VMEM((seqs, 8, width), F32),
            pltpu.VMEM((seqs, 8, 2 * STATE), F32),
            pltpu.SemaphoreType.DMA((2, n)),
            pltpu.SemaphoreType.DMA((2, n)),
            pltpu.SemaphoreType.DMA((2, 7)),
            pltpu.SemaphoreType.DMA((2, 7)),
            pltpu.SemaphoreType.DMA((4,)),
        ],
        "mix_bwd",
        8 * 10**9,
        4,
    )


def reduce_kernel(n, normed, dg, di, ds, dr, wg, wi, ws, wt, gain, sm_i, sm_s, sm_h, g_gain,
                  o_pg, o_gi, o_gs, o_gt, o_sm,
                  pg, gi, gs, gt, lg, rg, xi, xs, xt, bi, bs, bt, mb,
                  xp, xb, xo2, zs, zr, ps, pr, ms, mr, es, er):
    _plane_barrier(n)
    seqs, length, width = di.shape
    model = normed.shape[2]
    blocks = 2
    rows = blocks * wi.shape[1]
    small = _Smalls(n, mb, o_sm, ms, mr)
    mb[0] = jnp.zeros(mb.shape[1:], F32)
    mb[0, 0:6, :] = sm_i[0:6, :]
    mb[0, 6:7, :] = g_gain[0:1, :]
    for k in range(5):
        at = 256 * (k % 3)
        mb[0, 9 + k // 3 : 10 + k // 3, at : at + 256] = sm_s[k : k + 1, :]
    mb[0, 10:11, 512:640] = sm_h[0:1, :]
    mb[0, 10:11, 640:768] = sm_h[1:2, :]

    for b in range(model // rows):
        ch = slice(b * rows, (b + 1) * rows)
        near = slice(b * blocks, (b + 1) * blocks)
        w = [r[near].reshape(rows, r.shape[2]) for r in (wg, wi, ws, wt)]
        total = None
        for s in range(seqs):
            part = None
            for d, one in zip((dg, di, ds, dr), w):
                more = _dot(d[s], one, 1, 1)
                part = more if part is None else part + more
            pg[s, :, ch] = part.astype(BF)
            part = jnp.sum(part * normed[s, :, ch].astype(F32), axis=0, keepdims=True)
            total = part if total is None else total + part
        mb[0, 7 + b // 2 : 8 + b // 2, (b % 2) * rows : (b % 2 + 1) * rows] = total / gain[:, ch]
    step_g, final_g, finish_g = _line_reduce(n, pg, lg, rg, zs, zr)
    step_g(0)
    small.copy(0, small.near(0)).start()
    planes = [
        _PlaneReduce(part, pair, box, ps.at[i], pr.at[i])
        for i, (part, pair, box) in enumerate(((gs, xs, bs), (gt, xt, bt), (gi, xi, bi)))
    ]

    def weight(d, out):
        def one(b, _):
            ch = pl.ds(pl.multiple_of(b * rows, LANES), rows)
            total = None
            for s in range(seqs):
                part = _dot(normed[s, :, ch], d[s], 0, 0)
                total = part if total is None else total + part
            out[pl.ds(b * blocks, blocks)] = total.reshape(
                blocks, wi.shape[1], d.shape[2]
            ).astype(BF)
            return 0

        lax.fori_loop(0, model // rows, one, 0)

    weight(ds, gs)
    planes[0].begin()
    weight(dr, gt)
    planes[1].begin()
    weight(di, gi)
    planes[2].begin()
    small.step(0)
    step_g(1)
    for p in planes:
        p.send_far()
    small.step(1)
    for p in planes[:2]:
        p.send_near()
    small.step(2)
    step_g(2)
    planes[2].send_near()
    for k in range(3, n - 1):
        step_g(k)
    planes[0].final(o_gs)
    planes[1].final(o_gt)
    quarter = xp.shape[1]
    for o in range(n):
        xp[o] = o_gs[o * quarter : (o + 1) * quarter, :].astype(BF)
    state = _LineSum(n, xp, xb, xo2, es, er)
    state.scatter()
    planes[2].final(o_gi)
    state.gather()
    small.final()
    final_g(o_pg)
    state.arrive()
    for o in range(n):
        o_gs[o * quarter : (o + 1) * quarter, :] = xo2[o].astype(F32)
    for p in planes:
        p.finish()
    state.finish()
    small.finish()
    finish_g()


def reduce_all(n, normed, dg, di, ds, dr, wg, wi, ws, wt, gain, sm_i, sm_s, sm_h, g_gain):
    seqs, length, model = normed.shape
    rows = length // n
    sd = jax.ShapeDtypeStruct
    box = pltpu.VMEM((n, seqs, rows, model), BF)
    quarter = pltpu.VMEM((n, ws.shape[1] // n, ws.shape[2]), BF)
    sums = (16, wi.shape[2])
    return _mixer_call(
        functools.partial(reduce_kernel, n),
        (normed, dg, di, ds, dr, wg, wi, ws, wt, gain, sm_i, sm_s, sm_h, g_gain),
        (sd((seqs, rows, model), F32),)
        + tuple(sd(w.shape[1:], F32) for w in (wi, ws, wt))
        + (sd((n,) + sums, F32),),
        [pltpu.VMEM((seqs, length, model), BF)]
        + [pltpu.VMEM(w.shape, BF) for w in (wi, ws, wt)]
        + [box, box]
        + [pltpu.VMEM((4,) + w.shape[1:], BF) for w in (wi, ws, wt)]
        + [pltpu.VMEM((3,) + w.shape[1:], BF) for w in (wi, ws, wt)]
        + [
            pltpu.VMEM((6,) + sums, F32),
            quarter, quarter, quarter,
            pltpu.SemaphoreType.DMA((2, n)),
            pltpu.SemaphoreType.DMA((2, n)),
            pltpu.SemaphoreType.DMA((3, 7)),
            pltpu.SemaphoreType.DMA((3, 7)),
            pltpu.SemaphoreType.DMA((3 + n,)),
            pltpu.SemaphoreType.DMA((3 + n,)),
            pltpu.SemaphoreType.DMA((2, n)),
            pltpu.SemaphoreType.DMA((2, n)),
        ],
        "reduce_all",
        6 * 10**9,
        1,
    )


def emit_kernel(n, heads, tok, cot, gain, branch, rows, gg, gi, gs, gt, go, sms,
                block_out, g_tok, g_in, o_gg, o_gi, o_gs, o_gt, o_ci, o_ib, o_cs, o_sb,
                o_shift, o_rate, o_skip, o_gain, o_go):
    for s in range(tok.shape[0]):
        v = tok[s].astype(F32)
        rms = lax.rsqrt(jnp.mean(v * v, axis=-1, keepdims=True) + EPS)
        block_out[s] = (v + branch[s]).astype(BF)
        scaled = rows[s] * gain[...]
        mean = jnp.mean(scaled * v, axis=-1, keepdims=True)
        g_tok[s] = cot[s].astype(F32) + rms * scaled - v * (rms * rms * rms * mean)
    o_gg[...] = gg[...]
    o_gi[...] = gi[...]
    o_gs[...] = gs[...]
    o_gt[...] = gt[:, :heads]
    short = jnp.zeros((256 - go.shape[0], go.shape[1]), F32)
    o_go[...] = jnp.concatenate([go[...], short], axis=0).T[:, : go.shape[0]]
    width = sms.shape[2]
    shared = None
    head_rows = None
    for t in range(n):
        ch = slice(t * width, (t + 1) * width)
        o_ci[:, ch] = sms[t, 0:4, :]
        o_ib[:, ch] = sms[t, 4:5, :]
        o_gain[:, ch] = sms[t, 6:7, :]
        block = sms[t, 8:16, :]
        shared = sms[t, 7:11, :] if shared is None else shared + sms[t, 7:11, :]
        lanes = _iota((3 * width, LANES), 0)
        chan = lax.rem(lanes, width)
        to = _iota((3 * width, LANES), 1) == heads * t + lax.div(chan, HEAD_DIM)
        skips = _dot(_split(sms[t, 0:8, :], 3), to.astype(F32).astype(BF))
        lanes = lax.rem(_iota((3 * LANES, LANES), 0), LANES)
        to = (_iota((3 * LANES, LANES), 1) == heads * t + lanes) & (lanes < heads)
        to = to.astype(F32).astype(BF)
        shift = _dot(_split(block[:, 512:640], 3), to)
        rate = _dot(_split(block[:, 640:768], 3), to)
        new = (skips[5:6, :], shift[2:3, :], rate[2:3, :])
        head_rows = new if head_rows is None else tuple(a + b for a, b in zip(head_rows, new))
    every = n * heads
    o_skip[...] = head_rows[0][:, :every]
    o_shift[...] = head_rows[1][:, :every]
    o_rate[...] = head_rows[2][:, :every]
    g_in[:, :width] = shared[0:1, :]
    g_in[:, width:] = shared[1:2, :]
    for k in range(4):
        at = 256 * (k % 3)
        o_cs[k : k + 1, :] = shared[2 + k // 3 : 3 + k // 3, at : at + 256]
    o_sb[...] = shared[3:4, 256:512]


def emit_all(n, heads, tok, cot, gain, branch, rows, gg, gi, gs, gt, go, sms):
    vm = pl.BlockSpec(memory_space=pltpu.VMEM)
    sd = lambda *shape: jax.ShapeDtypeStruct(shape, F32)
    width = sms.shape[2]
    outs = (
        jax.ShapeDtypeStruct(tok.shape, BF), sd(*tok.shape), sd(1, tok.shape[2]),
        sd(*gg.shape), sd(*gi.shape), sd(*gs.shape), sd(gt.shape[0], heads),
        sd(4, n * width), sd(1, n * width), sd(4, 2 * STATE), sd(1, 2 * STATE),
        sd(1, n * heads), sd(1, n * heads), sd(1, n * heads), sd(1, n * width),
        sd(go.shape[1], go.shape[0]),
    )
    return pl.pallas_call(
        functools.partial(emit_kernel, n, heads),
        out_shape=outs,
        in_specs=[vm] * 11,
        out_specs=(vm,) * len(outs),
        compiler_params=pltpu.CompilerParams(vmem_limit_bytes=28 << 20),
        name="emit_all",
    )(tok, cot, gain, branch, rows, gg, gi, gs, gt, go, sms)


def per_device(
    tokens,
    segments,
    input_gain,
    gate_proj,
    inner_proj,
    state_proj,
    step_proj,
    conv_inner,
    inner_bias,
    conv_state,
    state_bias,
    step_bias,
    log_rates,
    skip_gain,
    gated_gain,
    output_proj,
    cotangent,
):
    tensor_count = lax.axis_size("tensor")
    tensor_rank = lax.axis_index("tensor")
    residual = tokens.astype(jnp.float32)
    rms_in = lax.rsqrt(jnp.mean(residual * residual, axis=-1, keepdims=True) + EPS)
    normed_own = (residual * rms_in * input_gain).astype(jnp.bfloat16)
    normed, cot_rows = (
        lax.all_gather(normed_own, "tensor", axis=1, tiled=True),
        lax.all_gather(cotangent, "tensor", axis=1, tiled=True),
    )
    gate_full, inner_full, state_full, step_full, output_full = (
        lax.all_gather(gate_proj, ("dp", "seq"), axis=0, tiled=True),
        lax.all_gather(inner_proj, ("dp", "seq"), axis=0, tiled=True),
        lax.all_gather(state_proj, ("dp", "seq"), axis=0, tiled=True),
        lax.all_gather(step_proj, ("dp", "seq"), axis=0, tiled=True),
        lax.all_gather(output_proj, ("dp", "seq"), axis=1, tiled=True),
    )
    gate_in = jnp.dot(normed, gate_full, preferred_element_type=jnp.float32)
    inner_low = jnp.dot(normed, inner_full, preferred_element_type=jnp.float32).astype(jnp.bfloat16)
    state_low = jnp.dot(normed, state_full, preferred_element_type=jnp.float32).astype(jnp.bfloat16)
    step_raw = jnp.dot(normed, step_full, preferred_element_type=jnp.float32)
    margin = KERNEL - 1
    seg_float = segments.astype(jnp.float32)
    prior_inner, prior_state, prior_seg = passed_along(
        (
            inner_low[:, -margin:],
            state_low[:, -margin:],
            seg_float[:, -margin:].astype(jnp.bfloat16),
        ),
        "seq",
        1,
    )
    padded_inner = jnp.concatenate([prior_inner, inner_low], axis=1).astype(jnp.float32)
    padded_state = jnp.concatenate([prior_state, state_low], axis=1).astype(jnp.float32)
    seg_padded = jnp.concatenate([prior_seg.astype(jnp.float32), seg_float], axis=1)
    pieces = segments.shape[1] // BLOCK
    seg_blocks = blocked(seg_float, pieces)
    before = jnp.concatenate(
        [prior_seg[:, -1:].astype(jnp.float32), seg_blocks[:, :-1, -1]], axis=1
    )
    width_here = inner_full.shape[1]
    heads_here = step_full.shape[1]
    chan_start = tensor_rank * width_here
    head_start = tensor_rank * heads_here
    kernel_here = lax.dynamic_slice_in_dim(conv_inner, chan_start, width_here, 1)
    bias_here = lax.dynamic_slice_in_dim(inner_bias, chan_start, width_here, 0)
    gain_here = lax.dynamic_slice_in_dim(gated_gain, chan_start, width_here, 0)
    shift_here = lax.dynamic_slice_in_dim(step_bias, head_start, heads_here, 0)
    rates_here = lax.dynamic_slice_in_dim(log_rates, head_start, heads_here, 0)
    skip_here = lax.dynamic_slice_in_dim(skip_gain, head_start, heads_here, 0)

    def mixer_front(
        pad_inner, pad_state, raw_steps, kernel_w, kernel_b, state_w, state_b, step_shift, rate_logs
    ):
        inner = jax.nn.silu(causal_mix(pad_inner, seg_padded, kernel_w, kernel_b))
        inner = inner.reshape(inner.shape[0], inner.shape[1], -1, HEAD_DIM)
        both_maps = jax.nn.silu(causal_mix(pad_state, seg_padded, state_w, state_b))
        b_proj = both_maps[:, :, :STATE]
        c_proj = both_maps[:, :, STATE:]
        deltas = jax.nn.softplus(raw_steps + step_shift)
        log_decay = deltas * -jnp.exp(rate_logs)
        inflow, passing = block_sums(inner, deltas, log_decay, b_proj, seg_blocks, before)
        return (inner, deltas, log_decay, b_proj, c_proj, inflow, passing)

    def mixer_rear(inner, deltas, log_decay, b_proj, c_proj, inflow, passing, incoming, skips):
        running = jnp.cumsum(blocked(log_decay, pieces), axis=2)
        places = jnp.arange(running.shape[2])
        allowed = (seg_blocks[:, :, :, None] == seg_blocks[:, :, None, :]) & (
            places[:, None] >= places[None, :]
        )
        inside = allowed[..., None]
        decays = jnp.where(
            inside,
            jnp.exp(jnp.where(inside, running[:, :, :, None, :] - running[:, :, None, :, :], 0.0)),
            0.0,
        )
        scores = jnp.einsum(
            "scin,scjn->scij", blocked(c_proj, pieces), blocked(b_proj, pieces), precision=HIGH
        )
        mixing = decays * scores[..., None] * blocked(deltas, pieces)[:, :, None, :, :]
        direct = jnp.einsum("scijh,scjhp->scihp", mixing, blocked(inner, pieces), precision=HIGH)
        from_state, outgoing = state_reads(
            incoming, log_decay, c_proj, inflow, passing, seg_blocks, before
        )
        heads_out = (direct + from_state).reshape(inner.shape) + skips[:, None] * inner
        return (heads_out.reshape(inner.shape[0], inner.shape[1], -1), outgoing)

    front_args = (
        padded_inner,
        padded_state,
        step_raw,
        kernel_here,
        bias_here,
        conv_state,
        state_bias,
        shift_here,
        rates_here,
    )
    front_vals = mixer_front(*front_args)
    inner, deltas, log_decay, b_proj, c_proj, inflow, passing = front_vals
    span_decay = jnp.ones(passing[:, 0].shape, jnp.float32)
    span_state = jnp.zeros(inflow[:, 0].shape, jnp.float32)
    span_state = passing[:, 0, :, None, None] * span_state + inflow[:, 0]
    span_decay = span_decay * passing[:, 0]
    identity = (jnp.ones_like(span_decay), jnp.zeros_like(span_state))
    incoming = entering_2((span_decay, span_state), "seq", chain_link, identity)[1]
    mixed, outgoing = mixer_rear(*front_vals, incoming, skip_here)
    sigmoid_z = jax.nn.sigmoid(gate_in)
    silu_z = gate_in * sigmoid_z
    gated = mixed * silu_z
    full_width = tensor_count * gated.shape[-1]
    square_sum = lax.psum(jnp.sum(gated * gated, axis=-1), "tensor")
    rms_gate = lax.rsqrt(square_sum / full_width + EPS)[..., None]
    gate_normed = (gated * rms_gate * gain_here).astype(jnp.bfloat16)
    partial_out = jnp.dot(gate_normed, output_full, preferred_element_type=jnp.float32)
    branch_rows = lax.psum_scatter(partial_out, "tensor", scatter_dimension=1, tiled=True)
    block_out = (residual + branch_rows).astype(jnp.bfloat16)
    grad_output = jnp.einsum(
        "srk,srd->kd", gate_normed, cot_rows, preferred_element_type=jnp.float32
    )
    grad_gn = jnp.einsum("srd,kd->srk", cot_rows, output_full, preferred_element_type=jnp.float32)
    scaled = grad_gn * gain_here
    dot_sum = lax.psum(jnp.sum(scaled * gated, axis=-1), "tensor")
    grad_gain_here = jnp.sum(grad_gn * gated * rms_gate, axis=(0, 1))
    grad_gated = rms_gate * scaled - gated * rms_gate**3 * (dot_sum / full_width)[..., None]
    grad_mixed = grad_gated * silu_z
    grad_gate_in = (grad_gated * mixed * sigmoid_z * (1.0 + gate_in * (1.0 - sigmoid_z))).astype(
        jnp.bfloat16
    )
    front_vals, front_back = jax.vjp(mixer_front, *front_args)
    unused_rear, rear_back = jax.vjp(mixer_rear, *front_vals, incoming, skip_here)
    inner, deltas, log_decay, b_proj, c_proj, inflow, passing = front_vals
    grad_blocks = blocked(grad_mixed.reshape(inner.shape), pieces)
    unused_reads, read_back = jax.vjp(
        lambda memory_in: state_reads(
            memory_in, log_decay, c_proj, inflow, passing, seg_blocks, before
        )[0],
        incoming,
    )
    local_grad = read_back(grad_blocks)[0]
    outgoing_grad = carried_in((span_decay, local_grad), "seq", chain_link, identity)[1]
    rear_grads = rear_back((grad_mixed, outgoing_grad))
    grad_skip_here = rear_grads[8]
    (
        pad_grad_inner,
        pad_grad_state,
        grad_step_raw,
        grad_kernel_here,
        grad_bias_here,
        grad_conv_state,
        grad_state_bias,
        grad_shift_here,
        grad_rates_here,
    ) = front_back(tuple(rear_grads[:7]))
    from_next_inner, from_next_state = passed_along(
        (pad_grad_inner[:, :margin], pad_grad_state[:, :margin]), "seq", -1
    )
    grad_inner_pre = jnp.concatenate(
        [pad_grad_inner[:, margin:-margin], pad_grad_inner[:, -margin:] + from_next_inner], axis=1
    )
    grad_state_part = jnp.concatenate(
        [pad_grad_state[:, margin:-margin], pad_grad_state[:, -margin:] + from_next_state], axis=1
    )
    grad_state_pre = lax.psum(grad_state_part, "tensor").astype(jnp.bfloat16)
    grad_inner_low = grad_inner_pre.astype(jnp.bfloat16)
    grad_step_low = grad_step_raw.astype(jnp.bfloat16)
    grad_normed = jnp.einsum(
        "srk,dk->srd", grad_gate_in, gate_full, preferred_element_type=jnp.float32
    )
    grad_normed = grad_normed + jnp.einsum(
        "srk,dk->srd", grad_inner_low, inner_full, preferred_element_type=jnp.float32
    )
    grad_normed = grad_normed + jnp.einsum(
        "srk,dk->srd", grad_step_low, step_full, preferred_element_type=jnp.float32
    )
    grad_rows = lax.psum_scatter(grad_normed, "tensor", scatter_dimension=1, tiled=True)
    own_rows = tokens.shape[1]
    state_mine = lax.dynamic_slice_in_dim(grad_state_pre, tensor_rank * own_rows, own_rows, 1)
    grad_rows = grad_rows + jnp.einsum(
        "srk,dk->srd", state_mine, state_full, preferred_element_type=jnp.float32
    )
    grad_gate_w = jnp.einsum(
        "srd,srk->dk", normed, grad_gate_in, preferred_element_type=jnp.float32
    )
    grad_inner_w = jnp.einsum(
        "srd,srk->dk", normed, grad_inner_low, preferred_element_type=jnp.float32
    )
    grad_state_w = jnp.einsum(
        "srd,srk->dk", normed, grad_state_pre, preferred_element_type=jnp.float32
    )
    grad_step_w = jnp.einsum(
        "srd,srk->dk", normed, grad_step_low, preferred_element_type=jnp.float32
    )
    shard_gate, shard_inner, shard_state, shard_step, shard_output = (
        lax.psum_scatter(grad_gate_w, ("dp", "seq"), scatter_dimension=0, tiled=True),
        lax.psum_scatter(grad_inner_w, ("dp", "seq"), scatter_dimension=0, tiled=True),
        lax.psum_scatter(grad_state_w, ("dp", "seq"), scatter_dimension=0, tiled=True),
        lax.psum_scatter(grad_step_w, ("dp", "seq"), scatter_dimension=0, tiled=True),
        lax.psum_scatter(grad_output, ("dp", "seq"), scatter_dimension=1, tiled=True),
    )
    scaled_in = grad_rows * input_gain
    grad_input_gain = jnp.sum(grad_rows * residual * rms_in, axis=(0, 1))
    grad_tokens = (
        cotangent.astype(jnp.float32)
        + rms_in * scaled_in
        - residual * rms_in**3 * jnp.mean(scaled_in * residual, axis=-1, keepdims=True)
    )

    def placed(whole, piece_grad, start, axis_number):
        return lax.dynamic_update_slice_in_dim(
            jnp.zeros_like(whole), piece_grad, start, axis_number
        )

    smalls = lax.psum(
        (
            grad_input_gain,
            placed(conv_inner, grad_kernel_here, chan_start, 1),
            placed(inner_bias, grad_bias_here, chan_start, 0),
            grad_conv_state,
            grad_state_bias,
            placed(step_bias, grad_shift_here, head_start, 0),
            placed(log_rates, grad_rates_here, head_start, 0),
            placed(skip_gain, grad_skip_here, head_start, 0),
            placed(gated_gain, grad_gain_here, chan_start, 0),
        ),
        ("dp", "seq", "tensor"),
    )
    return (
        block_out,
        grad_tokens,
        smalls[0],
        shard_gate,
        shard_inner,
        shard_state,
        shard_step,
        smalls[1],
        smalls[2],
        smalls[3],
        smalls[4],
        smalls[5],
        smalls[6],
        smalls[7],
        smalls[8],
        shard_output,
    )


def per_device_fast(
    tokens,
    segments,
    input_gain,
    gate_proj,
    inner_proj,
    state_proj,
    step_proj,
    conv_inner,
    inner_bias,
    conv_state,
    state_bias,
    step_bias,
    log_rates,
    skip_gain,
    gated_gain,
    output_proj,
    cotangent,
):
    tensor_count = lax.axis_size("tensor")
    tensor_rank = lax.axis_index("tensor")
    heads = step_proj.shape[1]
    step_wide = jnp.pad(step_proj, ((0, 0), (0, 128 - heads)))
    normed, g8, i8, s8, t8 = gather_all(
        tensor_count,
        tokens,
        input_gain,
        (gate_proj, inner_proj, state_proj, step_wide),
    )
    width = tokens.shape[2]
    inner_full = i8.reshape(width, -1)
    state_full = s8.reshape(width, -1)
    step_full = t8.reshape(width, -1)
    width_here = inner_full.shape[1]
    heads_here = heads
    head_start = tensor_rank * heads_here
    margin = 8
    inner_low = jnp.dot(normed, inner_full, preferred_element_type=jnp.float32).astype(jnp.bfloat16)
    state_low = jnp.dot(normed, state_full, preferred_element_type=jnp.float32).astype(jnp.bfloat16)
    prior_inner, prior_state = passed_along(
        (inner_low[:, -margin:], state_low[:, -margin:]), "seq", 1
    )
    step_raw = jnp.dot(normed, step_full, preferred_element_type=jnp.float32)
    prior_seg = passed_along(segments[:, 1 - KERNEL :], "seq", 1)
    seg_padded = jnp.concatenate([prior_seg, segments], axis=1)
    length = segments.shape[1]
    same = [
        seg_padded[:, KERNEL - 1 - k : KERNEL - 1 - k + length] == segments for k in range(1, KERNEL)
    ]
    same += [segments == prior_seg[:, -1:], segments == segments[:, -1:]]
    rows = jnp.stack(
        [segments.astype(jnp.float32)]
        + [m.astype(jnp.float32) for m in same]
        + [jnp.zeros(segments.shape, jnp.float32)] * 2,
        axis=1,
    )
    heads_param = jnp.pad(
        lax.dynamic_slice_in_dim(
            jnp.stack([step_bias, log_rates, skip_gain]), head_start, heads_here, 1
        ),
        ((0, 5), (0, LANES - heads_here)),
    )
    y_part, u_inner, u_state, entry, incoming, gate_in, cot_rows, o8 = mix_fwd(
        tensor_count, inner_low, prior_inner, state_low, prior_state, step_raw, rows, heads_param,
        conv_inner, inner_bias[None], conv_state, state_bias[None], cotangent, output_proj.T,
        normed, g8,
    )
    grad_mixed, grad_gate_in, outgoing_grad, partial_out, grad_output, grad_gate, grad_gain = gate_stage(
        tensor_count, y_part, u_state, entry, incoming, gate_in, cot_rows, o8, gated_gain[None], normed
    )
    (
        d_inner, d_state, d_step, sm_i, sm_s, sm_h, branch_rows, shard_output, shard_gate
    ) = mix_bwd(
        tensor_count, grad_mixed, u_inner, u_state, inner_low, prior_inner, state_low, prior_state,
        step_raw, rows, incoming, outgoing_grad, heads_param, conv_inner, conv_state,
        partial_out, grad_output, grad_gate,
    )
    gain_row = input_gain[None]
    grad_rows, shard_inner, shard_state, shard_step, sms = reduce_all(
        tensor_count, normed, grad_gate_in, d_inner, d_state, d_step, g8, i8, s8, t8, gain_row,
        sm_i, sm_s, sm_h, grad_gain,
    )
    outs = emit_all(
        tensor_count, heads, tokens, cotangent, gain_row, branch_rows, grad_rows,
        shard_gate, shard_inner, shard_state, shard_step, shard_output, sms,
    )
    flat = (2, 8, 10, 11, 12, 13, 14)
    return tuple(o[0] if i in flat else o for i, o in enumerate(outs))


def solution(mesh):
    fast = mesh.shape["dp"] == 4 and mesh.shape["seq"] == 2
    placed = (
        P("dp", ("seq", "tensor"), None),
        P("dp", "seq"),
        P(),
        P(("dp", "seq"), "tensor"),
        P(("dp", "seq"), "tensor"),
        P(("dp", "seq"), None),
        P(("dp", "seq"), "tensor"),
        P(),
        P(),
        P(),
        P(),
        P(),
        P(),
        P(),
        P(),
        P("tensor", ("dp", "seq")),
        P("dp", ("seq", "tensor"), None),
    )
    return jax.shard_map(
        per_device_fast if fast else per_device,
        mesh=mesh,
        in_specs=placed,
        out_specs=(
            P("dp", ("seq", "tensor"), None),
            P("dp", ("seq", "tensor"), None),
            P(),
            P(("dp", "seq"), "tensor"),
            P(("dp", "seq"), "tensor"),
            P(("dp", "seq"), None),
            P(("dp", "seq"), "tensor"),
            P(),
            P(),
            P(),
            P(),
            P(),
            P(),
            P(),
            P(),
            P("tensor", ("dp", "seq")),
        ),
        check_vma=False,
    )
```

```python
import functools

import jax
import jax.numpy as jnp
from jax import lax
from jax.experimental import pallas as pl
from jax.experimental.pallas import tpu as pltpu
from jax.sharding import PartitionSpec as P

HEAD_DIM = 64
STATE = 128
KERNEL = 4
BLOCK = 256


EPS = 1e-05
HIGH = lax.Precision.HIGHEST


def passed_along(block, axis, distance):
    devices = range(lax.axis_size(axis))
    route = [(i - distance, i) for i in devices if i - distance in devices]
    return lax.ppermute(block, axis, route)


def entering_2(shard, axis, join, neutral):
    place = lax.axis_index(axis)
    gathered = jax.tree.map(
        lambda a, kind: lax.all_gather(a.astype(kind), axis), shard, (jnp.bfloat16, jnp.bfloat16)
    )
    state = jax.tree.map(lambda a, e: jnp.zeros_like(a) + jnp.asarray(e, a.dtype), shard, neutral)

    def one(hop, state):
        return join(
            state,
            jax.tree.map(
                lambda a, own: lax.dynamic_index_in_dim(a, hop, 0, False).astype(own.dtype),
                gathered,
                shard,
            ),
        )

    return lax.fori_loop(0, place, one, state)


def carried_in(shard, axis, combine, identity):
    length, here = (lax.axis_size(axis), lax.axis_index(axis))
    everything = jax.tree.map(
        lambda part, kind: lax.all_gather(part.astype(kind), axis),
        shard,
        jax.tree.map(lambda a: jnp.bfloat16 if a.dtype == jnp.float32 else a.dtype, shard),
    )
    start = jax.tree.map(
        lambda part, zero: jnp.broadcast_to(jnp.asarray(zero, part.dtype), part.shape),
        shard,
        identity,
    )

    def hop(k, before):
        at = length - 1 - k
        reached = at > here
        new = combine(
            before, jax.tree.map(lambda part, own: part[at].astype(own.dtype), everything, shard)
        )
        return jax.tree.map(lambda a, b: jnp.where(reached, a, b), new, before)

    return lax.fori_loop(0, length, hop, start)


def chain_link(earlier, later):
    return (earlier[0] * later[0], later[0][:, :, None, None] * earlier[1] + later[1])


def causal_mix(padded, seg_padded, kernel_w, kernel_b):
    margin = KERNEL - 1
    length = padded.shape[1] - margin
    seg_now = seg_padded[:, margin:]
    result = kernel_b + kernel_w[0] * padded[:, margin:]
    for offset in range(1, KERNEL):
        moved = padded[:, margin - offset : margin - offset + length]
        same_doc = (seg_padded[:, margin - offset : margin - offset + length] == seg_now).astype(
            jnp.float32
        )
        result = result + kernel_w[offset] * moved * same_doc[:, :, None]
    return result


def blocked(values, pieces):
    return values.reshape((values.shape[0], pieces, values.shape[1] // pieces) + values.shape[2:])


def block_sums(inner, deltas, log_decay, b_proj, seg_blocks, before):
    pieces = seg_blocks.shape[1]
    running = jnp.cumsum(blocked(log_decay, pieces), axis=2)
    same_end = (seg_blocks == seg_blocks[:, :, -1:]).astype(jnp.float32)
    to_end = (
        jnp.exp(running[:, :, -1:, :] - running) * same_end[:, :, :, None] * blocked(deltas, pieces)
    )
    inflow = jnp.einsum(
        "scjhp,scjn->schpn",
        to_end[..., None] * blocked(inner, pieces),
        blocked(b_proj, pieces),
        precision=HIGH,
    )
    passing = (
        jnp.exp(running[:, :, -1, :])
        * (seg_blocks[:, :, -1] == before).astype(jnp.float32)[:, :, None]
    )
    return (inflow, passing)


def state_reads(incoming, log_decay, c_proj, inflow, passing, seg_blocks, before):
    pieces = seg_blocks.shape[1]
    running = jnp.cumsum(blocked(log_decay, pieces), axis=2)
    memory = incoming
    entering = [memory]
    memory = passing[:, 0, :, None, None] * memory + inflow[:, 0]
    stacked = jnp.stack(entering, axis=1)
    entry = jnp.exp(running) * (seg_blocks == before[:, :, None]).astype(jnp.float32)[..., None]
    from_state = (
        jnp.einsum("scin,schpn->scihp", blocked(c_proj, pieces), stacked, precision=HIGH)
        * entry[..., None]
    )
    return (from_state, memory)


MESH = pl.DeviceIdType.MESH
BF = jnp.bfloat16
F32 = jnp.float32


def _peers():
    dp, seq, t = lax.axis_index("dp"), lax.axis_index("seq"), lax.axis_index("tensor")
    x, y = lax.rem(dp, 2), lax.div(dp, 2)
    x_dp = dp + 1 - 2 * x
    y_dp = dp + 2 - 4 * y
    d_dp = 3 - dp
    return dp, seq, t, x_dp, y_dp, d_dp


def _dev(dp, seq, t):
    return {"dp": dp, "seq": seq, "tensor": t}


def _plane_barrier(n):
    dp, seq, t, x_dp, y_dp, d_dp = _peers()
    bar = pltpu.get_barrier_semaphore()
    for who in (_dev(dp, 1 - seq, t), _dev(x_dp, seq, t), _dev(y_dp, seq, t)):
        pl.semaphore_signal(bar, inc=1, device_id=who, device_id_type=MESH)

    for step in range(1, n):
        pl.semaphore_signal(
            bar, inc=1, device_id=_dev(dp, seq, lax.rem(t + step, n)), device_id_type=MESH
        )
    pl.semaphore_wait(bar, 3 + n - 1)


class _Line:
    def __init__(self, n, ref, rows, ssem, rsem, own=None):
        self.n, self.ref, self.rows, self.ssem, self.rsem = n, ref, rows, ssem, rsem
        self.own = own

    def block(self, o):
        return self.ref.at[:, pl.ds(pl.multiple_of(o * self.rows, self.rows), self.rows), :]

    def copy(self, o, direction, own=False):
        dp, seq, t = lax.axis_index("dp"), lax.axis_index("seq"), lax.axis_index("tensor")
        return pltpu.make_async_remote_copy(
            src_ref=self.own if own else self.block(o),
            dst_ref=self.block(o),
            send_sem=self.ssem.at[0 if direction > 0 else 1, o],
            recv_sem=self.rsem.at[o],
            device_id=_dev(dp, seq, t + direction),
            device_id_type=MESH,
        )

    def step(self, d):
        n, t = self.n, lax.axis_index("tensor")
        for way in (1, -1):
            o = t - way * d
            here = jnp.logical_and(o >= 0, o < n)
            nxt = jnp.logical_and(t + way >= 0, t + way < n)

            @pl.when(here)
            def _(o=o, way=way, nxt=nxt):
                if d > 0:
                    self.copy(o, way).wait_recv()

                @pl.when(nxt)
                def _():
                    self.copy(o, way, d == 0 and self.own is not None).start()

    def finish(self):
        n, t = self.n, lax.axis_index("tensor")
        for d in range(n):
            for way in (1, -1):
                o = t - way * d
                ok = jnp.logical_and(
                    jnp.logical_and(o >= 0, o < n),
                    jnp.logical_and(t + way >= 0, t + way < n),
                )

                @pl.when(ok)
                def _(o=o, way=way):
                    self.copy(o, way).wait_send()


class _Plane:
    def __init__(self, own, full, ssem, rsem, lsem):
        self.own, self.full, self.ssem, self.rsem, self.lsem = own, full, ssem, rsem, lsem

    def copy(self, src, block, who, s):
        return pltpu.make_async_remote_copy(
            src_ref=src,
            dst_ref=self.full.at[block],
            send_sem=self.ssem.at[s],
            recv_sem=self.rsem.at[s],
            device_id=who,
            device_id_type=MESH,
        )

    def begin(self):
        dp, seq, t, x_dp, y_dp, d_dp = _peers()
        me = dp * 2 + seq
        pltpu.make_async_copy(self.own, self.full.at[me], self.lsem).start()
        self.copy(self.own, me, _dev(x_dp, seq, t), 0).start()
        self.copy(self.own, me, _dev(y_dp, seq, t), 1).start()
        self.copy(self.own, me, _dev(dp, 1 - seq, t), 3).start()

    def forward(self):
        dp, seq, t, x_dp, y_dp, d_dp = _peers()
        bx, by = x_dp * 2 + seq, y_dp * 2 + seq
        self.copy(self.own, bx, _dev(x_dp, seq, t), 0).wait_recv()
        self.copy(self.own, by, _dev(y_dp, seq, t), 1).wait_recv()

        @pl.when(seq == 0)
        def _():
            self.copy(self.full.at[by], by, _dev(x_dp, seq, t), 2).start()

        @pl.when(seq == 1)
        def _():
            self.copy(self.full.at[bx], bx, _dev(y_dp, seq, t), 2).start()

        self.copy(self.full.at[bx], bx, _dev(dp, 1 - seq, t), 4).start()
        self.copy(self.full.at[by], by, _dev(dp, 1 - seq, t), 5).start()

    def share(self):
        dp, seq, t, x_dp, y_dp, d_dp = _peers()
        bd = d_dp * 2 + seq
        self.copy(self.own, bd, _dev(x_dp, seq, t), 2).wait_recv()
        self.copy(self.full.at[bd], bd, _dev(dp, 1 - seq, t), 6).start()

    def arrive(self):
        dp, seq, t, x_dp, y_dp, d_dp = _peers()
        me = dp * 2 + seq
        pltpu.make_async_copy(self.own, self.full.at[me], self.lsem).wait()
        for s in (3, 4, 5, 6):
            self.copy(self.own, me, _dev(dp, 1 - seq, t), s).wait_recv()

    def finish(self):
        dp, seq, t, x_dp, y_dp, d_dp = _peers()
        me = dp * 2 + seq
        for s in range(7):
            self.copy(self.own, me, _dev(dp, 1 - seq, t), s).wait_send()


def gather_kernel(n, tok, gain, wg, wi, ws, wt, normed, fg, fi, fs, ft, zs, zr, ps, pr, ls):
    t = lax.axis_index("tensor")
    rows = tok.shape[1]
    _plane_barrier(n)
    planes = [
        _Plane(own, full, ps.at[i], pr.at[i], ls.at[i])
        for i, (own, full) in enumerate(((ws, fs), (wt, ft), (wi, fi), (wg, fg)))
    ]
    for p in planes[:3]:
        p.begin()
    mine = pl.ds(pl.multiple_of(t * rows, rows), rows)
    for s in range(tok.shape[0]):
        v = tok[s].astype(F32)
        rms = lax.rsqrt(jnp.mean(v * v, axis=-1, keepdims=True) + EPS)
        normed[s, mine, :] = (v * rms * gain[...]).astype(BF)
    a = _Line(n, normed, rows, zs, zr)
    a.step(0)
    planes[3].begin()
    for p in planes[:3]:
        p.forward()
    a.step(1)
    planes[3].forward()
    for p in planes[:3]:
        p.share()
    for d in range(2, n):
        a.step(d)
    planes[3].share()
    for p in planes:
        p.arrive()
    a.finish()
    for p in planes:
        p.finish()


def gather_all(n, tokens, gain, weights):
    seqs, rows, width = tokens.shape
    vm = pl.BlockSpec(memory_space=pltpu.VMEM)
    full = lambda w: jax.ShapeDtypeStruct((8,) + w.shape, w.dtype)
    act = jax.ShapeDtypeStruct((seqs, n * rows, width), BF)
    return pl.pallas_call(
        functools.partial(gather_kernel, n),
        out_shape=(act,) + tuple(full(w) for w in weights),
        in_specs=[vm] * 6,
        out_specs=(vm,) * 5,
        scratch_shapes=[
            pltpu.SemaphoreType.DMA((2, n)),
            pltpu.SemaphoreType.DMA((n,)),
            pltpu.SemaphoreType.DMA((4, 7)),
            pltpu.SemaphoreType.DMA((4, 7)),
            pltpu.SemaphoreType.DMA((4,)),
        ],
        compiler_params=pltpu.CompilerParams(
            collective_id=0, has_side_effects=True, vmem_limit_bytes=28 << 20
        ),
        name="gather_all",
    )(tokens, gain.reshape(1, width), *weights)


def _line_reduce(n, part, left, right, ssem, rsem):
    dp, seq, t = lax.axis_index("dp"), lax.axis_index("seq"), lax.axis_index("tensor")
    rows = left.shape[2]

    def copy(src, box, o, way):
        return pltpu.make_async_remote_copy(
            src_ref=src, dst_ref=box.at[o],
            send_sem=ssem.at[0 if way > 0 else 1, o], recv_sem=rsem.at[0 if way > 0 else 1, o],
            device_id=_dev(dp, seq, t + way), device_id_type=MESH,
        )

    def block(o):
        return part.at[:, pl.ds(pl.multiple_of(o * rows, rows), rows), :]

    def step(k):
        for way, box, place in ((1, left, t), (-1, right, n - 1 - t)):
            target = lambda j: n - 1 - j if way > 0 else j
            if k == 0:
                @pl.when(place == 0)
                def _():
                    for j in range(n - 1):
                        copy(block(target(j)), box, target(j), way).start()
            else:
                @pl.when(jnp.logical_and(place > 0, place <= k))
                def _():
                    o = target(k - place)
                    copy(block(o), box, o, way).wait_recv()
                    for s in range(part.shape[0]):
                        own = part[s, pl.ds(pl.multiple_of(o * rows, rows), rows), :].astype(F32)
                        box[o, s] = (box[o, s].astype(F32) + own).astype(BF)
                    copy(box.at[o], box, o, way).start()

    def final(out):
        mine = pl.ds(pl.multiple_of(t * rows, rows), rows)
        for s in range(part.shape[0]):
            out[s] = part[s, mine, :].astype(F32)

        @pl.when(t > 0)
        def _():
            copy(left.at[0], left, t, 1).wait_recv()
            for s in range(part.shape[0]):
                out[s] = out[s] + left[t, s].astype(F32)

        @pl.when(t < n - 1)
        def _():
            copy(left.at[0], right, t, -1).wait_recv()
            for s in range(part.shape[0]):
                out[s] = out[s] + right[t, s].astype(F32)

    def finish():
        for j in range(n - 1):
            for way, box, o in ((1, left, n - 1 - j), (-1, right, j)):
                sends = (t < o) if way > 0 else (t > o)

                @pl.when(sends)
                def _():
                    copy(box.at[o], box, o, way).wait_send()

    return step, final, finish


def _line_reduces(n, part, left, right, ssem, rsem):
    one = lambda s: pl.ds(s, 1)
    return [
        _line_reduce(
            n, part.at[one(s)], left.at[:, one(s)], right.at[:, one(s)], ssem.at[s], rsem.at[s]
        )
        for s in range(part.shape[0])
    ]


class _PlaneReduce:
    def __init__(self, part, pair, box, ssem, rsem):
        self.part, self.pair, self.box, self.ssem, self.rsem = part, pair, box, ssem, rsem

    def copy(self, src, dst, who, s):
        return pltpu.make_async_remote_copy(
            src_ref=src, dst_ref=dst, send_sem=self.ssem.at[s], recv_sem=self.rsem.at[s],
            device_id=who, device_id_type=MESH,
        )

    def begin(self):
        dp, seq, t, x_dp, y_dp, d_dp = _peers()
        for slot, chip in enumerate((d_dp, x_dp, y_dp, dp)):
            self.copy(self.part.at[chip * 2 + 1 - seq], self.pair.at[slot], _dev(dp, 1 - seq, t), slot).start()

    def _paired(self, slot, chip, also=None):
        dp, seq, t, x_dp, y_dp, d_dp = _peers()
        self.copy(self.pair.at[slot], self.pair.at[slot], _dev(dp, 1 - seq, t), slot).wait_recv()
        v = self.part[chip * 2 + seq].astype(F32) + self.pair[slot].astype(F32)
        self.pair[slot] = v.astype(BF)

    def send_far(self):
        dp, seq, t, x_dp, y_dp, d_dp = _peers()
        for slot, chip in enumerate((d_dp, x_dp, y_dp)):
            self._paired(slot, chip)
            if slot == 0:
                @pl.when(seq == 0)
                def _():
                    self.copy(self.pair.at[0], self.box.at[2], _dev(x_dp, seq, t), 4).start()

                @pl.when(seq == 1)
                def _():
                    self.copy(self.pair.at[0], self.box.at[2], _dev(y_dp, seq, t), 4).start()

        @pl.when(seq == 0)
        def _():
            self.copy(self.pair.at[1], self.box.at[0], _dev(x_dp, seq, t), 5).start()

        @pl.when(seq == 1)
        def _():
            self.copy(self.pair.at[2], self.box.at[1], _dev(y_dp, seq, t), 6).start()

    def send_near(self):
        dp, seq, t, x_dp, y_dp, d_dp = _peers()
        self.copy(self.pair.at[0], self.box.at[2], _dev(dp, seq, t), 4).wait_recv()

        @pl.when(seq == 0)
        def _():
            self.box[2] = (self.box[2].astype(F32) + self.pair[2].astype(F32)).astype(BF)
            self.copy(self.box.at[2], self.box.at[1], _dev(y_dp, seq, t), 6).start()

        @pl.when(seq == 1)
        def _():
            self.box[2] = (self.box[2].astype(F32) + self.pair[1].astype(F32)).astype(BF)
            self.copy(self.box.at[2], self.box.at[0], _dev(x_dp, seq, t), 5).start()

    def final(self, out):
        dp, seq, t, x_dp, y_dp, d_dp = _peers()
        self.copy(self.pair.at[3], self.pair.at[3], _dev(dp, seq, t), 3).wait_recv()
        self.copy(self.pair.at[0], self.box.at[0], _dev(dp, seq, t), 5).wait_recv()
        self.copy(self.pair.at[0], self.box.at[1], _dev(dp, seq, t), 6).wait_recv()
        out[...] = (
            self.part[dp * 2 + seq].astype(F32) + self.pair[3].astype(F32)
            + self.box[0].astype(F32) + self.box[1].astype(F32)
        )

    def finish(self):
        dp, seq, t, x_dp, y_dp, d_dp = _peers()
        for s in range(7):
            self.copy(self.pair.at[0], self.box.at[0], _dev(dp, 1 - seq, t), s).wait_send()


class _Smalls:
    def __init__(self, n, box, line, ssem, rsem):
        self.n, self.box, self.line, self.ssem, self.rsem = n, box, line, ssem, rsem

    def copy(self, j, who):
        return pltpu.make_async_remote_copy(
            src_ref=self.box.at[2 * j], dst_ref=self.box.at[2 * j + 1],
            send_sem=self.ssem.at[j], recv_sem=self.rsem.at[j],
            device_id=who, device_id_type=MESH,
        )

    def near(self, j):
        dp, seq, t, x_dp, y_dp, d_dp = _peers()
        return (_dev(dp, 1 - seq, t), _dev(x_dp, seq, t), _dev(y_dp, seq, t))[j]

    def begin(self, value):
        self.box[0] = value
        self.copy(0, self.near(0)).start()

    def step(self, j):
        self.copy(j, self.near(j)).wait_recv()
        total = self.box[2 * j] + self.box[2 * j + 1]
        if j < 2:
            self.box[2 * j + 2] = total
            self.copy(j + 1, self.near(j + 1)).start()
        else:
            t = lax.axis_index("tensor")
            self.line[t] = total
            for o in range(self.n):
                @pl.when(t != o)
                def _(o=o):
                    self.across(t, o).start()

    def across(self, src, who):
        dp, seq, t = lax.axis_index("dp"), lax.axis_index("seq"), lax.axis_index("tensor")
        return pltpu.make_async_remote_copy(
            src_ref=self.line.at[src], dst_ref=self.line.at[src],
            send_sem=self.ssem.at[3 + who], recv_sem=self.rsem.at[3 + src],
            device_id=_dev(dp, seq, who), device_id_type=MESH,
        )

    def final(self):
        t = lax.axis_index("tensor")
        for o in range(self.n):
            @pl.when(t != o)
            def _(o=o):
                self.across(o, o).wait_recv()

    def finish(self):
        t = lax.axis_index("tensor")
        for j in range(3):
            self.copy(j, self.near(j)).wait_send()
        for o in range(self.n):
            @pl.when(t != o)
            def _(o=o):
                self.across(t, o).wait_send()


class _LineSum:
    def __init__(self, n, part, box, out, ssem, rsem):
        self.n, self.part, self.box, self.out, self.ssem, self.rsem = n, part, box, out, ssem, rsem

    def copy(self, phase, src_block, dst_ref, who, origin):
        dp, seq = lax.axis_index("dp"), lax.axis_index("seq")
        return pltpu.make_async_remote_copy(
            src_ref=src_block, dst_ref=dst_ref,
            send_sem=self.ssem.at[phase, who], recv_sem=self.rsem.at[phase, origin],
            device_id=_dev(dp, seq, who), device_id_type=MESH,
        )

    def scatter(self):
        t = lax.axis_index("tensor")
        for o in range(self.n):
            @pl.when(t != o)
            def _(o=o):
                self.copy(0, self.part.at[o], self.box.at[t], o, t).start()

    def gather(self):
        t = lax.axis_index("tensor")
        total = self.part[t].astype(F32)
        for o in range(self.n):
            @pl.when(t != o)
            def _(o=o):
                self.copy(0, self.part.at[o], self.box.at[o], o, o).wait_recv()

            @pl.when(t == o)
            def _(o=o):
                self.box[o] = jnp.zeros(self.box.shape[1:], self.box.dtype)
        for o in range(self.n):
            total = total + self.box[o].astype(F32)
        self.out[t] = total.astype(self.out.dtype)
        for o in range(self.n):
            @pl.when(t != o)
            def _(o=o):
                self.copy(1, self.out.at[t], self.out.at[t], o, t).start()

    def arrive(self):
        t = lax.axis_index("tensor")
        for o in range(self.n):
            @pl.when(t != o)
            def _(o=o):
                self.copy(1, self.out.at[o], self.out.at[o], o, o).wait_recv()

    def finish(self):
        t = lax.axis_index("tensor")
        for o in range(self.n):
            @pl.when(t != o)
            def _(o=o):
                self.copy(0, self.part.at[o], self.box.at[o], o, o).wait_send()
                self.copy(1, self.part.at[o], self.box.at[o], o, o).wait_send()


LANES = 128


def _split(v, parts):
    out = []
    for _ in range(parts):
        b = v.astype(BF)
        out.append(b)
        v = v - b.astype(F32)
    return jnp.concatenate(out, axis=1)


def _dot(a, b, ca=1, cb=0):
    return lax.dot_general(a, b, (((ca,), (cb,)), ((), ())), preferred_element_type=F32)


def _iota(shape, axis):
    return lax.broadcasted_iota(jnp.int32, shape, axis)


def _spreader(rows, p):
    head = lax.rem(_iota((rows, LANES), 0), LANES)
    return (head == 2 * p + lax.div(_iota((rows, LANES), 1), HEAD_DIM)).astype(F32).astype(BF)


def _folder(rows, p):
    chan = lax.rem(_iota((rows, LANES), 0), LANES)
    return (_iota((rows, LANES), 1) == 2 * p + lax.div(chan, HEAD_DIM)).astype(F32).astype(BF)


def _sig(v):
    return 1.0 / (1.0 + jnp.exp(-v))


def _three(v):
    return v[:, :LANES] + v[:, LANES : 2 * LANES] + v[:, 2 * LANES :]


def _head_scalars(raw, hp, marks, length):
    v = raw + hp[0:1, :]
    delta = jnp.maximum(v, 0.0) + jnp.log1p(jnp.exp(-jnp.abs(v)))
    log_decay = -delta * jnp.exp(hp[1:2, :])
    lower = (_iota((length, length), 0) >= _iota((length, length), 1)).astype(F32).astype(BF)
    running = _three(_dot(lower, _split(log_decay, 3)))
    entry = jnp.exp(running) * marks[:, 4:5]
    to_end = jnp.exp(running[length - 1 :, :] - running) * marks[:, 5:6]
    return v, delta, log_decay, running, entry, to_end


def _marks(rows):
    full = jnp.concatenate([rows, jnp.zeros((LANES - rows.shape[0], rows.shape[1]), F32)], axis=0)
    return full.T


def _bias_matrix(rows, marks, length):
    ok = (_iota((length, length), 0) >= _iota((length, length), 1)) & (
        marks[:, 0:1] == rows[0:1, :]
    )
    return jnp.where(ok, 0.0, -1e30)


def _conv(pad, marks, taps, bias, length):
    total = bias + taps[0:1, :] * pad[8 : 8 + length, :]
    for k in range(1, KERNEL):
        total = total + taps[k : k + 1, :] * (pad[8 - k : 8 - k + length, :] * marks[:, k : k + 1])
    return total


def mix_fwd_kernel(n, pre_i, old_i, pre_s, old_s, raw, rows, hp, taps_i, bias_i, taps_s, bias_s,
                   cot, wo, normed, wg, y, u_i, u_s, entry_o, incoming, gate, cot_full, fo,
                   pad, run3, run_t, bias_m, scores, heads_hl, inflow, zs, zr, ps, pr, ls, hs):
    t = lax.axis_index("tensor")
    seqs, length, width = pre_i.shape
    pairs = width // LANES
    _plane_barrier(n)
    line = _Line(n, cot_full, cot.shape[1], zs, zr, cot)
    plane = _Plane(wo, fo, ps, pr, ls.at[0])
    own = pltpu.make_async_copy(cot, line.block(t), ls.at[1])
    own.start()
    line.step(0)
    plane.begin()

    def one(s, _):
        rw = rows[s]
        marks = _marks(rw)
        v, delta, log_decay, running, entry, to_end = _head_scalars(raw[s], hp, marks, length)
        entry_o[s] = entry
        run3[...] = _split(running, 3)
        run_t[...] = running.T
        bias_m[...] = _bias_matrix(rw, marks, length)
        heads_hl[0] = _split(delta, 2)
        heads_hl[1] = _split(to_end, 2)
        maps = []
        for half in range(2):
            ch = slice(half * STATE, (half + 1) * STATE)
            pad[0:8, :] = old_s[s, :, ch].astype(F32)
            pad[8:, :] = pre_s[s, :, ch].astype(F32)
            u = _conv(pad, marks, taps_s[:, ch], bias_s[:, ch], length)
            u_s[s, :, ch] = u
            maps.append((u * _sig(u)).astype(BF))
        b_map, c_map = maps
        scores[...] = _dot(c_map, b_map, 1, 1)

        def pair(p, _):
            @pl.when(jnp.logical_and(s == 1, p == 0))
            def _():
                line.step(1)
                plane.forward()

            @pl.when(jnp.logical_and(s == 1, p == 4))
            def _():
                plane.share()

            ch = pl.ds(pl.multiple_of(p * LANES, LANES), LANES)
            at = pl.ds(pl.multiple_of(t * width + p * LANES, LANES), LANES)
            pad[0:8, :] = old_i[s, :, ch].astype(F32)
            pad[8:, :] = pre_i[s, :, ch].astype(F32)
            u = _conv(pad, marks, taps_i[:, at], bias_i[:, at], length)
            u_i[s, :, ch] = u
            x = u * _sig(u)
            spread = _spreader(2 * LANES, p)
            xd = x * _dot(heads_hl[0], spread)
            inflow[s, :, ch] = _dot(b_map, (xd * _dot(heads_hl[1], spread)).astype(BF), 0, 0).astype(BF)
            skip = _dot(_split(hp[...], 2), spread)[2:3, :]
            total = skip * x
            xb = xd.astype(BF)
            lane = lax.div(_iota(xb.shape, 1), HEAD_DIM)
            for a in range(2):
                h = 2 * p + a
                pick = (lax.rem(_iota((3 * LANES, length), 0), LANES) == h).astype(F32).astype(BF)
                decay = jnp.exp(_dot(run3[...], pick) - run_t[pl.ds(h, 1), :] + bias_m[...])
                mixing = (decay * scores[...]).astype(BF)
                total = total + _dot(mixing, jnp.where(lane == a, xb, jnp.zeros_like(xb)))
            y[s, :, ch] = total
            return 0

        lax.fori_loop(0, pairs, pair, 0)
        return 0

    lax.fori_loop(0, seqs, one, 0)
    dp, seq = lax.axis_index("dp"), lax.axis_index("seq")
    handed = pltpu.make_async_remote_copy(
        src_ref=inflow, dst_ref=incoming, send_sem=hs.at[0], recv_sem=hs.at[1],
        device_id=_dev(dp, 1 - seq, t), device_id_type=MESH,
    )

    @pl.when(seq == 0)
    def _():
        handed.start()
        incoming[...] = jnp.zeros_like(incoming)

    line.step(2)
    flat = normed[...].reshape(seqs * length, normed.shape[2])

    def gate_part(c, _):
        ch = pl.ds(pl.multiple_of(c * 2 * LANES, 2 * LANES), 2 * LANES)
        part = _dot(flat, wg[:, :, ch].reshape(normed.shape[2], 2 * LANES))
        gate[:, :, ch] = part.reshape(seqs, length, 2 * LANES)
        return 0

    lax.fori_loop(0, width // (2 * LANES), gate_part, 0)
    for d in range(3, n):
        line.step(d)
    plane.arrive()
    own.wait()

    @pl.when(seq == 0)
    def _():
        handed.wait_send()

    @pl.when(seq == 1)
    def _():
        handed.wait_recv()

    line.finish()
    plane.finish()


def _mixer_call(kernel, ins, outs, scratch, name, cost, number):
    vm = pl.BlockSpec(memory_space=pltpu.VMEM)
    return pl.pallas_call(
        kernel,
        out_shape=outs,
        in_specs=[vm] * len(ins),
        out_specs=(vm,) * len(outs),
        scratch_shapes=scratch,
        compiler_params=pltpu.CompilerParams(
            collective_id=number, has_side_effects=True, vmem_limit_bytes=28 << 20
        ),
        cost_estimate=pl.CostEstimate(flops=cost, bytes_accessed=1 << 20, transcendentals=0),
        name=name,
    )(*ins)


def mix_fwd(n, pre_i, old_i, pre_s, old_s, raw, rows, hp, taps_i, bias_i, taps_s, bias_s, cot, wo,
            normed, wg):
    seqs, length, width = pre_i.shape
    sd = jax.ShapeDtypeStruct
    return _mixer_call(
        functools.partial(mix_fwd_kernel, n),
        (pre_i, old_i, pre_s, old_s, raw, rows, hp, taps_i, bias_i, taps_s, bias_s, cot, wo,
         normed, wg),
        (
            sd((seqs, length, width), F32),
            sd((seqs, length, width), F32),
            sd((seqs, length, 2 * STATE), F32),
            sd((seqs, length, LANES), F32),
            sd((seqs, STATE, width), BF),
            sd((seqs, length, width), F32),
            sd((seqs, length, cot.shape[2]), BF),
            sd((8,) + wo.shape, BF),
        ),
        [
            pltpu.VMEM((8 + length, LANES), F32),
            pltpu.VMEM((length, 3 * LANES), BF),
            pltpu.VMEM((LANES, length), F32),
            pltpu.VMEM((length, length), F32),
            pltpu.VMEM((length, length), F32),
            pltpu.VMEM((2, length, 2 * LANES), BF),
            pltpu.VMEM((seqs, STATE, width), BF),
            pltpu.SemaphoreType.DMA((2, n)),
            pltpu.SemaphoreType.DMA((n,)),
            pltpu.SemaphoreType.DMA((7,)),
            pltpu.SemaphoreType.DMA((7,)),
            pltpu.SemaphoreType.DMA((2,)),
            pltpu.SemaphoreType.DMA((2,)),
        ],
        "mix_fwd",
        4 * 10**9,
        3,
    )


def gate_kernel(n, y_part, u_s, entry, h0, gate, cot, wo, gain, tokens_in,
                d_mixed, d_gate, lam, po, go, gg, g_gain,
                mixed, gated, grad_gn, normed, local, acc, box, ss, rs, hs):
    dp, seq, t = lax.axis_index("dp"), lax.axis_index("seq"), lax.axis_index("tensor")
    seqs, length, width = y_part.shape
    model = cot.shape[2]
    wide = 2 * LANES
    bar = pltpu.get_barrier_semaphore()
    pl.semaphore_signal(bar, inc=1, device_id=_dev(dp, 1 - seq, t), device_id_type=MESH)
    for step in range(1, n):
        pl.semaphore_signal(
            bar, inc=1, device_id=_dev(dp, seq, lax.rem(t + step, n)), device_id_type=MESH
        )
    acc[...] = jnp.zeros_like(acc)
    g_gain[...] = jnp.zeros_like(g_gain)

    def spread_of(s, c):
        heads = _split(entry[s], 2)
        head = lax.rem(_iota((wide, wide), 0), LANES)
        one = head == 4 * c + lax.div(_iota((wide, wide), 1), HEAD_DIM)
        return _dot(heads, one.astype(F32).astype(BF))

    def maps(s):
        u = u_s[s, :, STATE:]
        return (u * _sig(u)).astype(BF)

    def first(c, _):
        ch = pl.ds(pl.multiple_of(c * wide, wide), wide)
        at = pl.ds(pl.multiple_of(t * width + c * wide, wide), wide)
        w = wo[:, :, ch].reshape(model, wide)
        for s in range(seqs):
            g = _dot(cot[s], w)
            grad_gn[s, :, ch] = g
            m = y_part[s, :, ch] + spread_of(s, c) * _dot(maps(s), h0[s, :, ch])
            z = gate[s, :, ch]
            gd = m * (z * _sig(z))
            mixed[s, :, ch] = m
            gated[s, :, ch] = gd
            sq, ds = gd * gd, g * gain[:, at] * gd
            acc[0, s] += sq[:, :LANES] + sq[:, LANES:]
            acc[1, s] += ds[:, :LANES] + ds[:, LANES:]
        return 0

    lax.fori_loop(0, width // wide, first, 0)
    ones = jnp.ones((8, wide), F32).astype(BF)
    row = _iota((8, length), 0)
    mine = jnp.zeros((8, length), F32)
    for kind in range(2):
        for s in range(seqs):
            sums = _dot(ones, _split(acc[kind, s], 2), 1, 1)
            mine = jnp.where(row == kind * seqs + s, sums, mine)
    box[t] = mine
    pl.semaphore_wait(bar, n)

    def copy(src, who):
        return pltpu.make_async_remote_copy(
            src_ref=box.at[src], dst_ref=box.at[src], send_sem=ss.at[who], recv_sem=rs.at[src],
            device_id=_dev(dp, seq, who), device_id_type=MESH,
        )

    for o in range(n):
        @pl.when(t != o)
        def _(o=o):
            copy(t, o).start()
    for o in range(n):
        @pl.when(t != o)
        def _(o=o):
            copy(o, o).wait_recv()
    full_width = n * width
    cols = _marks(jnp.sum(box[...], axis=0) / full_width)

    def second(c, _):
        ch = pl.ds(pl.multiple_of(c * wide, wide), wide)
        at = pl.ds(pl.multiple_of(t * width + c * wide, wide), wide)
        gn = gain[:, at]
        for s in range(seqs):
            rms = lax.rsqrt(cols[:, s : s + 1] + EPS)
            mean = cols[:, seqs + s : seqs + s + 1]
            g, gd, m, z = grad_gn[s, :, ch], gated[s, :, ch], mixed[s, :, ch], gate[s, :, ch]
            sg = _sig(z)
            scaled = gd * rms
            normed[s, :, ch] = (scaled * gn).astype(BF)
            g_gain[0:1, ch] += jnp.sum(g * scaled, axis=0, keepdims=True)
            d_gd = rms * (g * gn) - scaled * (rms * rms * mean)
            dm = d_gd * (z * sg)
            d_mixed[s, :, ch] = dm
            d_gate[s, :, ch] = (d_gd * m * sg * (1.0 + z * (1.0 - sg))).astype(BF)
            ed = (spread_of(s, c) * dm).astype(BF)
            local[s, :, ch] = _dot(maps(s), ed, 0, 0).astype(BF)
        return 0

    lax.fori_loop(0, width // wide, second, 0)
    handed = pltpu.make_async_remote_copy(
        src_ref=local, dst_ref=lam, send_sem=hs.at[0], recv_sem=hs.at[1],
        device_id=_dev(dp, 1 - seq, t), device_id_type=MESH,
    )

    @pl.when(seq == 1)
    def _():
        handed.start()
        lam[...] = jnp.zeros_like(lam)

    blocks = 2
    rows = blocks * wo.shape[1]

    def third(b, _):
        ch = pl.ds(pl.multiple_of(b * rows, LANES), rows)
        w = wo[pl.ds(b * blocks, blocks)].reshape(rows, width)
        total = None
        for s in range(seqs):
            po[s, :, ch] = _dot(normed[s], w, 1, 1).astype(BF)
            part = _dot(cot[s, :, ch], normed[s], 0, 0)
            total = part if total is None else total + part
        go[pl.ds(b * blocks, blocks)] = total.reshape(blocks, wo.shape[1], width).astype(BF)
        total = None
        for s in range(seqs):
            part = _dot(tokens_in[s, :, ch], d_gate[s], 0, 0)
            total = part if total is None else total + part
        gg[pl.ds(b * blocks, blocks)] = total.reshape(blocks, wo.shape[1], width).astype(BF)
        return 0

    lax.fori_loop(0, model // rows, third, 0)

    @pl.when(seq == 1)
    def _():
        handed.wait_send()

    @pl.when(seq == 0)
    def _():
        handed.wait_recv()

    for o in range(n):
        @pl.when(t != o)
        def _(o=o):
            copy(o, o).wait_send()


def gate_stage(n, y_part, u_s, entry, h0, gate, cot, wo, gain, tokens_in):
    seqs, length, width = y_part.shape
    sd = jax.ShapeDtypeStruct
    whole = pltpu.VMEM((seqs, length, width), F32)
    return _mixer_call(
        functools.partial(gate_kernel, n),
        (y_part, u_s, entry, h0, gate, cot, wo, gain, tokens_in),
        (
            sd((seqs, length, width), F32),
            sd((seqs, length, width), BF),
            sd((seqs, STATE, width), BF),
            sd((seqs, length, cot.shape[2]), BF),
            sd(wo.shape, BF),
            sd(wo.shape, BF),
            sd((8, width), F32),
        ),
        [
            whole, whole, whole,
            pltpu.VMEM((seqs, length, width), BF),
            pltpu.VMEM((seqs, STATE, width), BF),
            pltpu.VMEM((2, seqs, length, LANES), F32),
            pltpu.VMEM((n, 8, length), F32),
            pltpu.SemaphoreType.DMA((n,)),
            pltpu.SemaphoreType.DMA((n,)),
            pltpu.SemaphoreType.DMA((2,)),
        ],
        "gate_stage",
        6 * 10**9,
        2,
    )


def mix_bwd_kernel(n, dy_r, u_i, u_s, pre_i, old_i, pre_s, old_s, raw, rows, h0, lam, hp,
                   taps_i, taps_s, po, go, gg,
                   d_i, d_s, d_raw, sm_i, sm_s, sm_h, o_po, o_go, o_gg,
                   pad, moved, run3, run_t, bias_m, scores, d_scores, heads_hl,
                   acc_r, acc_c, acc_d, acc_q, d_b, d_c, lo, ro, xo, bo, xg, bg,
                   head_i, tail_i, head_s, tail_s, next_i, next_s, zs, zr, ps, pr, hs):
    t = lax.axis_index("tensor")
    seqs, length, width = pre_i.shape
    pairs = width // LANES
    _plane_barrier(n)
    lines = _line_reduces(n, po, lo, ro, zs, zr)
    planes = (
        _PlaneReduce(go, xo, bo, ps.at[0], pr.at[0]), _PlaneReduce(gg, xg, bg, ps.at[1], pr.at[1])
    )
    for step, _, _ in lines:
        step(0)
    for plane in planes:
        plane.begin()
    sm_i[...] = jnp.zeros_like(sm_i)
    sm_s[...] = jnp.zeros_like(sm_s)
    sm_h[...] = jnp.zeros_like(sm_h)
    moved[0:8, :] = jnp.zeros((8, LANES), F32)
    moved[8 + length :, :] = jnp.zeros((8, LANES), F32)

    def conv_back(du, marks, taps, s, ch, d_o, head_o, tail_o, sm):
        total = None
        for k in range(KERNEL):
            m = du if k == 0 else du * marks[:, k : k + 1]
            moved[8 : 8 + length, :] = m
            sm[k : k + 1, ch] += jnp.sum(m * pad[8 - k : 8 - k + length, :], axis=0, keepdims=True)
            part = taps[k : k + 1, :] * moved[k : k + 8 + length, :]
            total = part if total is None else total + part
        sm[4:5, ch] += jnp.sum(du, axis=0, keepdims=True)
        head_o[s, :, ch] = total[0:8, :]
        d_o[s, :, ch] = total[8:, :].astype(BF)
        tail_o[s, :, ch] = total[length - 8 :, :]

    def one(s, _):
        rw = rows[s]
        marks = _marks(rw)
        v, delta, log_decay, running, entry, to_end = _head_scalars(raw[s], hp, marks, length)
        run3[...] = _split(running, 3)
        run_t[...] = running.T
        bias_m[...] = _bias_matrix(rw, marks, length)
        heads_hl[0] = _split(delta, 2)
        heads_hl[1] = _split(to_end, 2)
        heads_hl[2] = _split(entry, 2)
        ub, uc = u_s[s, :, :STATE], u_s[s, :, STATE:]
        sb, sc = _sig(ub), _sig(uc)
        b_map, c_map = (ub * sb).astype(BF), (uc * sc).astype(BF)
        scores[...] = _dot(c_map, b_map, 1, 1)
        d_scores[...] = jnp.zeros_like(d_scores)
        for acc in (acc_r, acc_c, acc_d, acc_q, d_b, d_c):
            acc[...] = jnp.zeros_like(acc)

        def pair(p, _):
            @pl.when(jnp.logical_and(s == 0, p == 2))
            def _():
                planes[0].send_far()

            @pl.when(jnp.logical_and(s == 0, p == 3))
            def _():
                lines[0][0](1)
                planes[1].send_far()

            @pl.when(jnp.logical_and(s == 0, p == 5))
            def _():
                lines[0][0](2)

            @pl.when(jnp.logical_and(s == 1, p == 2))
            def _():
                planes[0].send_near()

            @pl.when(jnp.logical_and(s == 1, p == 5))
            def _():
                planes[1].send_near()

            @pl.when(jnp.logical_and(s == 1, p == 4))
            def _():
                lines[1][0](1)

            ch = pl.ds(pl.multiple_of(p * LANES, LANES), LANES)
            at = pl.ds(pl.multiple_of(t * width + p * LANES, LANES), LANES)
            u = u_i[s, :, ch]
            sg = _sig(u)
            x = u * sg
            dy = dy_r[s, :, ch]
            spread, fold = _spreader(2 * LANES, p), _folder(2 * LANES, p)
            dl = _dot(heads_hl[0], spread)
            q = _dot(heads_hl[1], spread)
            e = _dot(heads_hl[2], spread)
            xd = x * dl
            xb, db = xd.astype(BF), dy.astype(BF)
            h_in, l_in = h0[s, :, ch], lam[s, :, ch]
            c_h = _dot(c_map, h_in)
            b_l = _dot(b_map, l_in)
            qx, ed = q * xd, e * dy
            d_b[...] += _dot(qx.astype(BF), l_in, 1, 1)
            d_c[...] += _dot(ed.astype(BF), h_in, 1, 1)
            late = qx * b_l
            dxd = q * b_l
            lane = lax.div(_iota(xb.shape, 1), HEAD_DIM)
            for a in range(2):
                h = 2 * p + a
                pick = (lax.rem(_iota((3 * LANES, length), 0), LANES) == h).astype(F32).astype(BF)
                decay = jnp.exp(_dot(run3[...], pick) - run_t[pl.ds(h, 1), :] + bias_m[...])
                da = jnp.where(lane == a, db, jnp.zeros_like(db))
                ld = decay * _dot(da, xb, 1, 1)
                d_scores[...] += ld
                both = (ld * scores[...]).astype(BF)
                mixing = (decay * scores[...]).astype(BF)
                dxd = dxd + _dot(mixing, da, 0, 0)
                col = (_iota((length, LANES), 1) == h).astype(F32).astype(BF)
                row = (_iota((LANES, length), 0) == h).astype(F32).astype(BF)
                acc_r[...] += _dot(both, col)
                acc_c[...] += _dot(row, both)
            acc_r[...] += _dot(_split(ed * c_h - late, 2), fold)
            acc_d[...] += _dot(_split(dxd * x, 2), fold)
            total = jnp.broadcast_to(jnp.sum(late, axis=0, keepdims=True), (8, LANES))
            acc_q[...] += _dot(_split(total, 2), fold)
            skip = _dot(_split(hp[...], 2), spread)[2:3, :]
            sm_i[5:6, ch] += jnp.sum(dy * x, axis=0, keepdims=True)
            du = (dxd * dl + skip * dy) * (sg * (1.0 + u * (1.0 - sg)))
            pad[0:8, :] = old_i[s, :, ch].astype(F32)
            pad[8:, :] = pre_i[s, :, ch].astype(F32)
            conv_back(du, marks, taps_i[:, at], s, ch, d_i, head_i, tail_i, sm_i)
            return 0

        lax.fori_loop(0, pairs, pair, 0)
        ds = d_scores[...].astype(BF)
        grads = (d_b[...] + _dot(ds, c_map, 0, 0), d_c[...] + _dot(ds, b_map))
        for half, (g, u, sg) in enumerate(zip(grads, (ub, uc), (sb, sc))):
            ch = slice(half * STATE, (half + 1) * STATE)
            pad[0:8, :] = old_s[s, :, ch].astype(F32)
            pad[8:, :] = pre_s[s, :, ch].astype(F32)
            du = g * (sg * (1.0 + u * (1.0 - sg)))
            conv_back(du, marks, taps_s[:, ch], s, ch, d_s, head_s, tail_s, sm_s)
        d_run = acc_r[...] - acc_c[...].T
        last = _iota(d_run.shape, 0) == length - 1
        d_run = d_run + jnp.where(last, acc_q[0:1, :], 0.0)
        upper = (_iota((length, length), 0) <= _iota((length, length), 1)).astype(F32).astype(BF)
        d_log = _three(_dot(upper, _split(d_run, 3)))
        d_delta = acc_d[...] - d_log * jnp.exp(hp[1:2, :])
        d_step = d_delta * _sig(v)
        d_raw[s] = d_step.astype(BF)
        sm_h[0:1, :] += jnp.sum(d_step, axis=0, keepdims=True)
        sm_h[1:2, :] += jnp.sum(d_log * log_decay, axis=0, keepdims=True)
        return 0

    lax.fori_loop(0, seqs, one, 0)
    lines[1][0](2)
    dp, seq = lax.axis_index("dp"), lax.axis_index("seq")
    handed = [
        pltpu.make_async_remote_copy(
            src_ref=a, dst_ref=b, send_sem=hs.at[2 * i], recv_sem=hs.at[2 * i + 1],
            device_id=_dev(dp, 1 - seq, t), device_id_type=MESH,
        )
        for i, (a, b) in enumerate(((head_i, next_i), (head_s, next_s)))
    ]

    @pl.when(seq == 1)
    def _():
        for c in handed:
            c.start()

    planes[0].final(o_go)

    @pl.when(seq == 0)
    def _():
        for c, box, tail, out in zip(handed, (next_i, next_s), (tail_i, tail_s), (d_i, d_s)):
            c.wait_recv()
            for s in range(seqs):
                more = jnp.concatenate([jnp.zeros_like(box[s]), box[s]], axis=0)
                out[s, length - 16 :, :] = (tail[s] + more).astype(BF)

    @pl.when(seq == 1)
    def _():
        for c in handed:
            c.wait_send()

    planes[1].final(o_gg)
    for s, (_, final, _) in enumerate(lines):
        final(o_po.at[pl.ds(s, 1)])
    for plane in planes:
        plane.finish()
    for _, _, finish in lines:
        finish()


def mix_bwd(n, dy, u_i, u_s, pre_i, old_i, pre_s, old_s, raw, rows, h0, lam, hp, taps_i, taps_s,
            po, go, gg):
    seqs, length, width = pre_i.shape
    model = po.shape[2]
    box = pltpu.VMEM((n, seqs, length // n, model), BF)
    sd = jax.ShapeDtypeStruct
    square = pltpu.VMEM((length, length), F32)
    tall = pltpu.VMEM((length, LANES), F32)
    return _mixer_call(
        functools.partial(mix_bwd_kernel, n),
        (dy, u_i, u_s, pre_i, old_i, pre_s, old_s, raw, rows, h0, lam, hp, taps_i, taps_s, po, go,
         gg),
        (
            sd((seqs, length, width), BF),
            sd((seqs, length, 2 * STATE), BF),
            sd((seqs, length, LANES), BF),
            sd((8, width), F32),
            sd((8, 2 * STATE), F32),
            sd((8, LANES), F32),
            sd((seqs, length // n, model), F32),
            sd(go.shape[1:], F32),
            sd(gg.shape[1:], F32),
        ),
        [
            pltpu.VMEM((8 + length, LANES), F32),
            pltpu.VMEM((16 + length, LANES), F32),
            pltpu.VMEM((length, 3 * LANES), BF),
            pltpu.VMEM((LANES, length), F32),
            square, square, square,
            pltpu.VMEM((3, length, 2 * LANES), BF),
            tall, pltpu.VMEM((LANES, length), F32), tall, pltpu.VMEM((8, LANES), F32), tall, tall,
            box, box,
            pltpu.VMEM((4,) + go.shape[1:], BF),
            pltpu.VMEM((3,) + go.shape[1:], BF),
            pltpu.VMEM((4,) + gg.shape[1:], BF),
            pltpu.VMEM((3,) + gg.shape[1:], BF),
            pltpu.VMEM((seqs, 8, width), F32),
            pltpu.VMEM((seqs, 16, width), F32),
            pltpu.VMEM((seqs, 8, 2 * STATE), F32),
            pltpu.VMEM((seqs, 16, 2 * STATE), F32),
            pltpu.VMEM((seqs, 8, width), F32),
            pltpu.VMEM((seqs, 8, 2 * STATE), F32),
            pltpu.SemaphoreType.DMA((seqs, 2, n)),
            pltpu.SemaphoreType.DMA((seqs, 2, n)),
            pltpu.SemaphoreType.DMA((2, 7)),
            pltpu.SemaphoreType.DMA((2, 7)),
            pltpu.SemaphoreType.DMA((4,)),
        ],
        "mix_bwd",
        8 * 10**9,
        4,
    )


def reduce_kernel(n, normed, dg, di, ds, dr, wg, wi, ws, wt, gain, sm_i, sm_s, sm_h, g_gain,
                  o_pg, o_gi, o_gs, o_gt, o_sm,
                  pg, gi, gs, gt, lg, rg, xi, xs, xt, bi, bs, bt, mb,
                  xp, xb, xo2, zs, zr, ps, pr, ms, mr, es, er):
    _plane_barrier(n)
    seqs, length, width = di.shape
    model = normed.shape[2]
    blocks = 2
    rows = blocks * wi.shape[1]
    small = _Smalls(n, mb, o_sm, ms, mr)
    mb[0] = jnp.zeros(mb.shape[1:], F32)
    mb[0, 0:6, :] = sm_i[0:6, :]
    mb[0, 6:7, :] = g_gain[0:1, :]
    for k in range(5):
        at = 256 * (k % 3)
        mb[0, 9 + k // 3 : 10 + k // 3, at : at + 256] = sm_s[k : k + 1, :]
    mb[0, 10:11, 512:640] = sm_h[0:1, :]
    mb[0, 10:11, 640:768] = sm_h[1:2, :]

    lines = _line_reduces(n, pg, lg, rg, zs, zr)
    totals = [None] * (model // rows)
    for s in range(seqs):
        for b in range(model // rows):
            ch = slice(b * rows, (b + 1) * rows)
            near = slice(b * blocks, (b + 1) * blocks)
            part = None
            for d, w in zip((dg, di, ds, dr), (wg, wi, ws, wt)):
                more = _dot(d[s], w[near].reshape(rows, w.shape[2]), 1, 1)
                part = more if part is None else part + more
            pg[s, :, ch] = part.astype(BF)
            part = jnp.sum(part * normed[s, :, ch].astype(F32), axis=0, keepdims=True)
            totals[b] = part if totals[b] is None else totals[b] + part
        lines[s][0](0)
    for b, total in enumerate(totals):
        ch = slice(b * rows, (b + 1) * rows)
        mb[0, 7 + b // 2 : 8 + b // 2, (b % 2) * rows : (b % 2 + 1) * rows] = total / gain[:, ch]
    small.copy(0, small.near(0)).start()
    planes = [
        _PlaneReduce(part, pair, box, ps.at[i], pr.at[i])
        for i, (part, pair, box) in enumerate(((gs, xs, bs), (gt, xt, bt), (gi, xi, bi)))
    ]

    def weight(d, out):
        def one(b, _):
            ch = pl.ds(pl.multiple_of(b * rows, LANES), rows)
            total = None
            for s in range(seqs):
                part = _dot(normed[s, :, ch], d[s], 0, 0)
                total = part if total is None else total + part
            out[pl.ds(b * blocks, blocks)] = total.reshape(
                blocks, wi.shape[1], d.shape[2]
            ).astype(BF)
            return 0

        lax.fori_loop(0, model // rows, one, 0)

    weight(ds, gs)
    planes[0].begin()
    weight(dr, gt)
    planes[1].begin()
    weight(di, gi)
    planes[2].begin()
    lines[0][0](1)
    small.step(0)
    for p in planes:
        p.send_far()
    small.step(1)
    lines[0][0](2)
    for p in planes[:2]:
        p.send_near()
    small.step(2)
    lines[1][0](1)
    planes[2].send_near()
    planes[0].final(o_gs)
    planes[1].final(o_gt)
    quarter = xp.shape[1]
    for o in range(n):
        xp[o] = o_gs[o * quarter : (o + 1) * quarter, :].astype(BF)
    state = _LineSum(n, xp, xb, xo2, es, er)
    state.scatter()
    lines[1][0](2)
    state.gather()
    planes[2].final(o_gi)
    small.final()
    for s, (_, final, _) in enumerate(lines):
        final(o_pg.at[pl.ds(s, 1)])
    state.arrive()
    for o in range(n):
        o_gs[o * quarter : (o + 1) * quarter, :] = xo2[o].astype(F32)
    for p in planes:
        p.finish()
    state.finish()
    small.finish()
    for _, _, finish in lines:
        finish()


def reduce_all(n, normed, dg, di, ds, dr, wg, wi, ws, wt, gain, sm_i, sm_s, sm_h, g_gain):
    seqs, length, model = normed.shape
    rows = length // n
    sd = jax.ShapeDtypeStruct
    box = pltpu.VMEM((n, seqs, rows, model), BF)
    quarter = pltpu.VMEM((n, ws.shape[1] // n, ws.shape[2]), BF)
    sums = (16, wi.shape[2])
    return _mixer_call(
        functools.partial(reduce_kernel, n),
        (normed, dg, di, ds, dr, wg, wi, ws, wt, gain, sm_i, sm_s, sm_h, g_gain),
        (sd((seqs, rows, model), F32),)
        + tuple(sd(w.shape[1:], F32) for w in (wi, ws, wt))
        + (sd((n,) + sums, F32),),
        [pltpu.VMEM((seqs, length, model), BF)]
        + [pltpu.VMEM(w.shape, BF) for w in (wi, ws, wt)]
        + [box, box]
        + [pltpu.VMEM((4,) + w.shape[1:], BF) for w in (wi, ws, wt)]
        + [pltpu.VMEM((3,) + w.shape[1:], BF) for w in (wi, ws, wt)]
        + [
            pltpu.VMEM((6,) + sums, F32),
            quarter, quarter, quarter,
            pltpu.SemaphoreType.DMA((seqs, 2, n)),
            pltpu.SemaphoreType.DMA((seqs, 2, n)),
            pltpu.SemaphoreType.DMA((3, 7)),
            pltpu.SemaphoreType.DMA((3, 7)),
            pltpu.SemaphoreType.DMA((3 + n,)),
            pltpu.SemaphoreType.DMA((3 + n,)),
            pltpu.SemaphoreType.DMA((2, n)),
            pltpu.SemaphoreType.DMA((2, n)),
        ],
        "reduce_all",
        6 * 10**9,
        1,
    )


def emit_kernel(n, heads, tok, cot, gain, branch, rows, gg, gi, gs, gt, go, sms,
                block_out, g_tok, g_in, o_gg, o_gi, o_gs, o_gt, o_ci, o_ib, o_cs, o_sb,
                o_shift, o_rate, o_skip, o_gain, o_go):
    for s in range(tok.shape[0]):
        v = tok[s].astype(F32)
        rms = lax.rsqrt(jnp.mean(v * v, axis=-1, keepdims=True) + EPS)
        block_out[s] = (v + branch[s]).astype(BF)
        scaled = rows[s] * gain[...]
        mean = jnp.mean(scaled * v, axis=-1, keepdims=True)
        g_tok[s] = cot[s].astype(F32) + rms * scaled - v * (rms * rms * rms * mean)
    o_gg[...] = gg[...]
    o_gi[...] = gi[...]
    o_gs[...] = gs[...]
    o_gt[...] = gt[:, :heads]
    short = jnp.zeros((256 - go.shape[0], go.shape[1]), F32)
    o_go[...] = jnp.concatenate([go[...], short], axis=0).T[:, : go.shape[0]]
    width = sms.shape[2]
    shared = None
    head_rows = None
    for t in range(n):
        ch = slice(t * width, (t + 1) * width)
        o_ci[:, ch] = sms[t, 0:4, :]
        o_ib[:, ch] = sms[t, 4:5, :]
        o_gain[:, ch] = sms[t, 6:7, :]
        block = sms[t, 8:16, :]
        shared = sms[t, 7:11, :] if shared is None else shared + sms[t, 7:11, :]
        lanes = _iota((3 * width, LANES), 0)
        chan = lax.rem(lanes, width)
        to = _iota((3 * width, LANES), 1) == heads * t + lax.div(chan, HEAD_DIM)
        skips = _dot(_split(sms[t, 0:8, :], 3), to.astype(F32).astype(BF))
        lanes = lax.rem(_iota((3 * LANES, LANES), 0), LANES)
        to = (_iota((3 * LANES, LANES), 1) == heads * t + lanes) & (lanes < heads)
        to = to.astype(F32).astype(BF)
        shift = _dot(_split(block[:, 512:640], 3), to)
        rate = _dot(_split(block[:, 640:768], 3), to)
        new = (skips[5:6, :], shift[2:3, :], rate[2:3, :])
        head_rows = new if head_rows is None else tuple(a + b for a, b in zip(head_rows, new))
    every = n * heads
    o_skip[...] = head_rows[0][:, :every]
    o_shift[...] = head_rows[1][:, :every]
    o_rate[...] = head_rows[2][:, :every]
    g_in[:, :width] = shared[0:1, :]
    g_in[:, width:] = shared[1:2, :]
    for k in range(4):
        at = 256 * (k % 3)
        o_cs[k : k + 1, :] = shared[2 + k // 3 : 3 + k // 3, at : at + 256]
    o_sb[...] = shared[3:4, 256:512]


def emit_all(n, heads, tok, cot, gain, branch, rows, gg, gi, gs, gt, go, sms):
    vm = pl.BlockSpec(memory_space=pltpu.VMEM)
    sd = lambda *shape: jax.ShapeDtypeStruct(shape, F32)
    width = sms.shape[2]
    outs = (
        jax.ShapeDtypeStruct(tok.shape, BF), sd(*tok.shape), sd(1, tok.shape[2]),
        sd(*gg.shape), sd(*gi.shape), sd(*gs.shape), sd(gt.shape[0], heads),
        sd(4, n * width), sd(1, n * width), sd(4, 2 * STATE), sd(1, 2 * STATE),
        sd(1, n * heads), sd(1, n * heads), sd(1, n * heads), sd(1, n * width),
        sd(go.shape[1], go.shape[0]),
    )
    return pl.pallas_call(
        functools.partial(emit_kernel, n, heads),
        out_shape=outs,
        in_specs=[vm] * 11,
        out_specs=(vm,) * len(outs),
        compiler_params=pltpu.CompilerParams(vmem_limit_bytes=28 << 20),
        name="emit_all",
    )(tok, cot, gain, branch, rows, gg, gi, gs, gt, go, sms)


def per_device(
    tokens,
    segments,
    input_gain,
    gate_proj,
    inner_proj,
    state_proj,
    step_proj,
    conv_inner,
    inner_bias,
    conv_state,
    state_bias,
    step_bias,
    log_rates,
    skip_gain,
    gated_gain,
    output_proj,
    cotangent,
):
    tensor_count = lax.axis_size("tensor")
    tensor_rank = lax.axis_index("tensor")
    residual = tokens.astype(jnp.float32)
    rms_in = lax.rsqrt(jnp.mean(residual * residual, axis=-1, keepdims=True) + EPS)
    normed_own = (residual * rms_in * input_gain).astype(jnp.bfloat16)
    normed, cot_rows = (
        lax.all_gather(normed_own, "tensor", axis=1, tiled=True),
        lax.all_gather(cotangent, "tensor", axis=1, tiled=True),
    )
    gate_full, inner_full, state_full, step_full, output_full = (
        lax.all_gather(gate_proj, ("dp", "seq"), axis=0, tiled=True),
        lax.all_gather(inner_proj, ("dp", "seq"), axis=0, tiled=True),
        lax.all_gather(state_proj, ("dp", "seq"), axis=0, tiled=True),
        lax.all_gather(step_proj, ("dp", "seq"), axis=0, tiled=True),
        lax.all_gather(output_proj, ("dp", "seq"), axis=1, tiled=True),
    )
    gate_in = jnp.dot(normed, gate_full, preferred_element_type=jnp.float32)
    inner_low = jnp.dot(normed, inner_full, preferred_element_type=jnp.float32).astype(jnp.bfloat16)
    state_low = jnp.dot(normed, state_full, preferred_element_type=jnp.float32).astype(jnp.bfloat16)
    step_raw = jnp.dot(normed, step_full, preferred_element_type=jnp.float32)
    margin = KERNEL - 1
    seg_float = segments.astype(jnp.float32)
    prior_inner, prior_state, prior_seg = passed_along(
        (
            inner_low[:, -margin:],
            state_low[:, -margin:],
            seg_float[:, -margin:].astype(jnp.bfloat16),
        ),
        "seq",
        1,
    )
    padded_inner = jnp.concatenate([prior_inner, inner_low], axis=1).astype(jnp.float32)
    padded_state = jnp.concatenate([prior_state, state_low], axis=1).astype(jnp.float32)
    seg_padded = jnp.concatenate([prior_seg.astype(jnp.float32), seg_float], axis=1)
    pieces = segments.shape[1] // BLOCK
    seg_blocks = blocked(seg_float, pieces)
    before = jnp.concatenate(
        [prior_seg[:, -1:].astype(jnp.float32), seg_blocks[:, :-1, -1]], axis=1
    )
    width_here = inner_full.shape[1]
    heads_here = step_full.shape[1]
    chan_start = tensor_rank * width_here
    head_start = tensor_rank * heads_here
    kernel_here = lax.dynamic_slice_in_dim(conv_inner, chan_start, width_here, 1)
    bias_here = lax.dynamic_slice_in_dim(inner_bias, chan_start, width_here, 0)
    gain_here = lax.dynamic_slice_in_dim(gated_gain, chan_start, width_here, 0)
    shift_here = lax.dynamic_slice_in_dim(step_bias, head_start, heads_here, 0)
    rates_here = lax.dynamic_slice_in_dim(log_rates, head_start, heads_here, 0)
    skip_here = lax.dynamic_slice_in_dim(skip_gain, head_start, heads_here, 0)

    def mixer_front(
        pad_inner, pad_state, raw_steps, kernel_w, kernel_b, state_w, state_b, step_shift, rate_logs
    ):
        inner = jax.nn.silu(causal_mix(pad_inner, seg_padded, kernel_w, kernel_b))
        inner = inner.reshape(inner.shape[0], inner.shape[1], -1, HEAD_DIM)
        both_maps = jax.nn.silu(causal_mix(pad_state, seg_padded, state_w, state_b))
        b_proj = both_maps[:, :, :STATE]
        c_proj = both_maps[:, :, STATE:]
        deltas = jax.nn.softplus(raw_steps + step_shift)
        log_decay = deltas * -jnp.exp(rate_logs)
        inflow, passing = block_sums(inner, deltas, log_decay, b_proj, seg_blocks, before)
        return (inner, deltas, log_decay, b_proj, c_proj, inflow, passing)

    def mixer_rear(inner, deltas, log_decay, b_proj, c_proj, inflow, passing, incoming, skips):
        running = jnp.cumsum(blocked(log_decay, pieces), axis=2)
        places = jnp.arange(running.shape[2])
        allowed = (seg_blocks[:, :, :, None] == seg_blocks[:, :, None, :]) & (
            places[:, None] >= places[None, :]
        )
        inside = allowed[..., None]
        decays = jnp.where(
            inside,
            jnp.exp(jnp.where(inside, running[:, :, :, None, :] - running[:, :, None, :, :], 0.0)),
            0.0,
        )
        scores = jnp.einsum(
            "scin,scjn->scij", blocked(c_proj, pieces), blocked(b_proj, pieces), precision=HIGH
        )
        mixing = decays * scores[..., None] * blocked(deltas, pieces)[:, :, None, :, :]
        direct = jnp.einsum("scijh,scjhp->scihp", mixing, blocked(inner, pieces), precision=HIGH)
        from_state, outgoing = state_reads(
            incoming, log_decay, c_proj, inflow, passing, seg_blocks, before
        )
        heads_out = (direct + from_state).reshape(inner.shape) + skips[:, None] * inner
        return (heads_out.reshape(inner.shape[0], inner.shape[1], -1), outgoing)

    front_args = (
        padded_inner,
        padded_state,
        step_raw,
        kernel_here,
        bias_here,
        conv_state,
        state_bias,
        shift_here,
        rates_here,
    )
    front_vals = mixer_front(*front_args)
    inner, deltas, log_decay, b_proj, c_proj, inflow, passing = front_vals
    span_decay = jnp.ones(passing[:, 0].shape, jnp.float32)
    span_state = jnp.zeros(inflow[:, 0].shape, jnp.float32)
    span_state = passing[:, 0, :, None, None] * span_state + inflow[:, 0]
    span_decay = span_decay * passing[:, 0]
    identity = (jnp.ones_like(span_decay), jnp.zeros_like(span_state))
    incoming = entering_2((span_decay, span_state), "seq", chain_link, identity)[1]
    mixed, outgoing = mixer_rear(*front_vals, incoming, skip_here)
    sigmoid_z = jax.nn.sigmoid(gate_in)
    silu_z = gate_in * sigmoid_z
    gated = mixed * silu_z
    full_width = tensor_count * gated.shape[-1]
    square_sum = lax.psum(jnp.sum(gated * gated, axis=-1), "tensor")
    rms_gate = lax.rsqrt(square_sum / full_width + EPS)[..., None]
    gate_normed = (gated * rms_gate * gain_here).astype(jnp.bfloat16)
    partial_out = jnp.dot(gate_normed, output_full, preferred_element_type=jnp.float32)
    branch_rows = lax.psum_scatter(partial_out, "tensor", scatter_dimension=1, tiled=True)
    block_out = (residual + branch_rows).astype(jnp.bfloat16)
    grad_output = jnp.einsum(
        "srk,srd->kd", gate_normed, cot_rows, preferred_element_type=jnp.float32
    )
    grad_gn = jnp.einsum("srd,kd->srk", cot_rows, output_full, preferred_element_type=jnp.float32)
    scaled = grad_gn * gain_here
    dot_sum = lax.psum(jnp.sum(scaled * gated, axis=-1), "tensor")
    grad_gain_here = jnp.sum(grad_gn * gated * rms_gate, axis=(0, 1))
    grad_gated = rms_gate * scaled - gated * rms_gate**3 * (dot_sum / full_width)[..., None]
    grad_mixed = grad_gated * silu_z
    grad_gate_in = (grad_gated * mixed * sigmoid_z * (1.0 + gate_in * (1.0 - sigmoid_z))).astype(
        jnp.bfloat16
    )
    front_vals, front_back = jax.vjp(mixer_front, *front_args)
    unused_rear, rear_back = jax.vjp(mixer_rear, *front_vals, incoming, skip_here)
    inner, deltas, log_decay, b_proj, c_proj, inflow, passing = front_vals
    grad_blocks = blocked(grad_mixed.reshape(inner.shape), pieces)
    unused_reads, read_back = jax.vjp(
        lambda memory_in: state_reads(
            memory_in, log_decay, c_proj, inflow, passing, seg_blocks, before
        )[0],
        incoming,
    )
    local_grad = read_back(grad_blocks)[0]
    outgoing_grad = carried_in((span_decay, local_grad), "seq", chain_link, identity)[1]
    rear_grads = rear_back((grad_mixed, outgoing_grad))
    grad_skip_here = rear_grads[8]
    (
        pad_grad_inner,
        pad_grad_state,
        grad_step_raw,
        grad_kernel_here,
        grad_bias_here,
        grad_conv_state,
        grad_state_bias,
        grad_shift_here,
        grad_rates_here,
    ) = front_back(tuple(rear_grads[:7]))
    from_next_inner, from_next_state = passed_along(
        (pad_grad_inner[:, :margin], pad_grad_state[:, :margin]), "seq", -1
    )
    grad_inner_pre = jnp.concatenate(
        [pad_grad_inner[:, margin:-margin], pad_grad_inner[:, -margin:] + from_next_inner], axis=1
    )
    grad_state_part = jnp.concatenate(
        [pad_grad_state[:, margin:-margin], pad_grad_state[:, -margin:] + from_next_state], axis=1
    )
    grad_state_pre = lax.psum(grad_state_part, "tensor").astype(jnp.bfloat16)
    grad_inner_low = grad_inner_pre.astype(jnp.bfloat16)
    grad_step_low = grad_step_raw.astype(jnp.bfloat16)
    grad_normed = jnp.einsum(
        "srk,dk->srd", grad_gate_in, gate_full, preferred_element_type=jnp.float32
    )
    grad_normed = grad_normed + jnp.einsum(
        "srk,dk->srd", grad_inner_low, inner_full, preferred_element_type=jnp.float32
    )
    grad_normed = grad_normed + jnp.einsum(
        "srk,dk->srd", grad_step_low, step_full, preferred_element_type=jnp.float32
    )
    grad_rows = lax.psum_scatter(grad_normed, "tensor", scatter_dimension=1, tiled=True)
    own_rows = tokens.shape[1]
    state_mine = lax.dynamic_slice_in_dim(grad_state_pre, tensor_rank * own_rows, own_rows, 1)
    grad_rows = grad_rows + jnp.einsum(
        "srk,dk->srd", state_mine, state_full, preferred_element_type=jnp.float32
    )
    grad_gate_w = jnp.einsum(
        "srd,srk->dk", normed, grad_gate_in, preferred_element_type=jnp.float32
    )
    grad_inner_w = jnp.einsum(
        "srd,srk->dk", normed, grad_inner_low, preferred_element_type=jnp.float32
    )
    grad_state_w = jnp.einsum(
        "srd,srk->dk", normed, grad_state_pre, preferred_element_type=jnp.float32
    )
    grad_step_w = jnp.einsum(
        "srd,srk->dk", normed, grad_step_low, preferred_element_type=jnp.float32
    )
    shard_gate, shard_inner, shard_state, shard_step, shard_output = (
        lax.psum_scatter(grad_gate_w, ("dp", "seq"), scatter_dimension=0, tiled=True),
        lax.psum_scatter(grad_inner_w, ("dp", "seq"), scatter_dimension=0, tiled=True),
        lax.psum_scatter(grad_state_w, ("dp", "seq"), scatter_dimension=0, tiled=True),
        lax.psum_scatter(grad_step_w, ("dp", "seq"), scatter_dimension=0, tiled=True),
        lax.psum_scatter(grad_output, ("dp", "seq"), scatter_dimension=1, tiled=True),
    )
    scaled_in = grad_rows * input_gain
    grad_input_gain = jnp.sum(grad_rows * residual * rms_in, axis=(0, 1))
    grad_tokens = (
        cotangent.astype(jnp.float32)
        + rms_in * scaled_in
        - residual * rms_in**3 * jnp.mean(scaled_in * residual, axis=-1, keepdims=True)
    )

    def placed(whole, piece_grad, start, axis_number):
        return lax.dynamic_update_slice_in_dim(
            jnp.zeros_like(whole), piece_grad, start, axis_number
        )

    smalls = lax.psum(
        (
            grad_input_gain,
            placed(conv_inner, grad_kernel_here, chan_start, 1),
            placed(inner_bias, grad_bias_here, chan_start, 0),
            grad_conv_state,
            grad_state_bias,
            placed(step_bias, grad_shift_here, head_start, 0),
            placed(log_rates, grad_rates_here, head_start, 0),
            placed(skip_gain, grad_skip_here, head_start, 0),
            placed(gated_gain, grad_gain_here, chan_start, 0),
        ),
        ("dp", "seq", "tensor"),
    )
    return (
        block_out,
        grad_tokens,
        smalls[0],
        shard_gate,
        shard_inner,
        shard_state,
        shard_step,
        smalls[1],
        smalls[2],
        smalls[3],
        smalls[4],
        smalls[5],
        smalls[6],
        smalls[7],
        smalls[8],
        shard_output,
    )


def per_device_fast(
    tokens,
    segments,
    input_gain,
    gate_proj,
    inner_proj,
    state_proj,
    step_proj,
    conv_inner,
    inner_bias,
    conv_state,
    state_bias,
    step_bias,
    log_rates,
    skip_gain,
    gated_gain,
    output_proj,
    cotangent,
):
    tensor_count = lax.axis_size("tensor")
    tensor_rank = lax.axis_index("tensor")
    heads = step_proj.shape[1]
    step_wide = jnp.pad(step_proj, ((0, 0), (0, 128 - heads)))
    normed, g8, i8, s8, t8 = gather_all(
        tensor_count,
        tokens,
        input_gain,
        (gate_proj, inner_proj, state_proj, step_wide),
    )
    width = tokens.shape[2]
    inner_full = i8.reshape(width, -1)
    state_full = s8.reshape(width, -1)
    step_full = t8.reshape(width, -1)
    width_here = inner_full.shape[1]
    heads_here = heads
    head_start = tensor_rank * heads_here
    margin = 8
    inner_low = jnp.dot(normed, inner_full, preferred_element_type=jnp.float32).astype(jnp.bfloat16)
    state_low = jnp.dot(normed, state_full, preferred_element_type=jnp.float32).astype(jnp.bfloat16)
    prior_inner, prior_state = passed_along(
        (inner_low[:, -margin:], state_low[:, -margin:]), "seq", 1
    )
    step_raw = jnp.dot(normed, step_full, preferred_element_type=jnp.float32)
    prior_seg = passed_along(segments[:, 1 - KERNEL :], "seq", 1)
    seg_padded = jnp.concatenate([prior_seg, segments], axis=1)
    length = segments.shape[1]
    same = [
        seg_padded[:, KERNEL - 1 - k : KERNEL - 1 - k + length] == segments for k in range(1, KERNEL)
    ]
    same += [segments == prior_seg[:, -1:], segments == segments[:, -1:]]
    rows = jnp.stack(
        [segments.astype(jnp.float32)]
        + [m.astype(jnp.float32) for m in same]
        + [jnp.zeros(segments.shape, jnp.float32)] * 2,
        axis=1,
    )
    heads_param = jnp.pad(
        lax.dynamic_slice_in_dim(
            jnp.stack([step_bias, log_rates, skip_gain]), head_start, heads_here, 1
        ),
        ((0, 5), (0, LANES - heads_here)),
    )
    y_part, u_inner, u_state, entry, incoming, gate_in, cot_rows, o8 = mix_fwd(
        tensor_count, inner_low, prior_inner, state_low, prior_state, step_raw, rows, heads_param,
        conv_inner, inner_bias[None], conv_state, state_bias[None], cotangent, output_proj.T,
        normed, g8,
    )
    grad_mixed, grad_gate_in, outgoing_grad, partial_out, grad_output, grad_gate, grad_gain = gate_stage(
        tensor_count, y_part, u_state, entry, incoming, gate_in, cot_rows, o8, gated_gain[None], normed
    )
    (
        d_inner, d_state, d_step, sm_i, sm_s, sm_h, branch_rows, shard_output, shard_gate
    ) = mix_bwd(
        tensor_count, grad_mixed, u_inner, u_state, inner_low, prior_inner, state_low, prior_state,
        step_raw, rows, incoming, outgoing_grad, heads_param, conv_inner, conv_state,
        partial_out, grad_output, grad_gate,
    )
    gain_row = input_gain[None]
    grad_rows, shard_inner, shard_state, shard_step, sms = reduce_all(
        tensor_count, normed, grad_gate_in, d_inner, d_state, d_step, g8, i8, s8, t8, gain_row,
        sm_i, sm_s, sm_h, grad_gain,
    )
    outs = emit_all(
        tensor_count, heads, tokens, cotangent, gain_row, branch_rows, grad_rows,
        shard_gate, shard_inner, shard_state, shard_step, shard_output, sms,
    )
    flat = (2, 8, 10, 11, 12, 13, 14)
    return tuple(o[0] if i in flat else o for i, o in enumerate(outs))


def solution(mesh):
    fast = mesh.shape["dp"] == 4 and mesh.shape["seq"] == 2
    placed = (
        P("dp", ("seq", "tensor"), None),
        P("dp", "seq"),
        P(),
        P(("dp", "seq"), "tensor"),
        P(("dp", "seq"), "tensor"),
        P(("dp", "seq"), None),
        P(("dp", "seq"), "tensor"),
        P(),
        P(),
        P(),
        P(),
        P(),
        P(),
        P(),
        P(),
        P("tensor", ("dp", "seq")),
        P("dp", ("seq", "tensor"), None),
    )
    return jax.shard_map(
        per_device_fast if fast else per_device,
        mesh=mesh,
        in_specs=placed,
        out_specs=(
            P("dp", ("seq", "tensor"), None),
            P("dp", ("seq", "tensor"), None),
            P(),
            P(("dp", "seq"), "tensor"),
            P(("dp", "seq"), "tensor"),
            P(("dp", "seq"), None),
            P(("dp", "seq"), "tensor"),
            P(),
            P(),
            P(),
            P(),
            P(),
            P(),
            P(),
            P(),
            P("tensor", ("dp", "seq")),
        ),
        check_vma=False,
    )
```

```python
import functools

import jax
import jax.numpy as jnp
from jax import lax
from jax.experimental import pallas as pl
from jax.experimental.pallas import tpu as pltpu
from jax.sharding import PartitionSpec as P

HEAD_DIM = 64
STATE = 128
KERNEL = 4
BLOCK = 256


EPS = 1e-05
HIGH = lax.Precision.HIGHEST


def passed_along(block, axis, distance):
    devices = range(lax.axis_size(axis))
    route = [(i - distance, i) for i in devices if i - distance in devices]
    return lax.ppermute(block, axis, route)


def entering_2(shard, axis, join, neutral):
    place = lax.axis_index(axis)
    gathered = jax.tree.map(
        lambda a, kind: lax.all_gather(a.astype(kind), axis), shard, (jnp.bfloat16, jnp.bfloat16)
    )
    state = jax.tree.map(lambda a, e: jnp.zeros_like(a) + jnp.asarray(e, a.dtype), shard, neutral)

    def one(hop, state):
        return join(
            state,
            jax.tree.map(
                lambda a, own: lax.dynamic_index_in_dim(a, hop, 0, False).astype(own.dtype),
                gathered,
                shard,
            ),
        )

    return lax.fori_loop(0, place, one, state)


def carried_in(shard, axis, combine, identity):
    length, here = (lax.axis_size(axis), lax.axis_index(axis))
    everything = jax.tree.map(
        lambda part, kind: lax.all_gather(part.astype(kind), axis),
        shard,
        jax.tree.map(lambda a: jnp.bfloat16 if a.dtype == jnp.float32 else a.dtype, shard),
    )
    start = jax.tree.map(
        lambda part, zero: jnp.broadcast_to(jnp.asarray(zero, part.dtype), part.shape),
        shard,
        identity,
    )

    def hop(k, before):
        at = length - 1 - k
        reached = at > here
        new = combine(
            before, jax.tree.map(lambda part, own: part[at].astype(own.dtype), everything, shard)
        )
        return jax.tree.map(lambda a, b: jnp.where(reached, a, b), new, before)

    return lax.fori_loop(0, length, hop, start)


def chain_link(earlier, later):
    return (earlier[0] * later[0], later[0][:, :, None, None] * earlier[1] + later[1])


def causal_mix(padded, seg_padded, kernel_w, kernel_b):
    margin = KERNEL - 1
    length = padded.shape[1] - margin
    seg_now = seg_padded[:, margin:]
    result = kernel_b + kernel_w[0] * padded[:, margin:]
    for offset in range(1, KERNEL):
        moved = padded[:, margin - offset : margin - offset + length]
        same_doc = (seg_padded[:, margin - offset : margin - offset + length] == seg_now).astype(
            jnp.float32
        )
        result = result + kernel_w[offset] * moved * same_doc[:, :, None]
    return result


def blocked(values, pieces):
    return values.reshape((values.shape[0], pieces, values.shape[1] // pieces) + values.shape[2:])


def block_sums(inner, deltas, log_decay, b_proj, seg_blocks, before):
    pieces = seg_blocks.shape[1]
    running = jnp.cumsum(blocked(log_decay, pieces), axis=2)
    same_end = (seg_blocks == seg_blocks[:, :, -1:]).astype(jnp.float32)
    to_end = (
        jnp.exp(running[:, :, -1:, :] - running) * same_end[:, :, :, None] * blocked(deltas, pieces)
    )
    inflow = jnp.einsum(
        "scjhp,scjn->schpn",
        to_end[..., None] * blocked(inner, pieces),
        blocked(b_proj, pieces),
        precision=HIGH,
    )
    passing = (
        jnp.exp(running[:, :, -1, :])
        * (seg_blocks[:, :, -1] == before).astype(jnp.float32)[:, :, None]
    )
    return (inflow, passing)


def state_reads(incoming, log_decay, c_proj, inflow, passing, seg_blocks, before):
    pieces = seg_blocks.shape[1]
    running = jnp.cumsum(blocked(log_decay, pieces), axis=2)
    memory = incoming
    entering = [memory]
    memory = passing[:, 0, :, None, None] * memory + inflow[:, 0]
    stacked = jnp.stack(entering, axis=1)
    entry = jnp.exp(running) * (seg_blocks == before[:, :, None]).astype(jnp.float32)[..., None]
    from_state = (
        jnp.einsum("scin,schpn->scihp", blocked(c_proj, pieces), stacked, precision=HIGH)
        * entry[..., None]
    )
    return (from_state, memory)


MESH = pl.DeviceIdType.MESH
BF = jnp.bfloat16
F32 = jnp.float32


def _peers():
    dp, seq, t = lax.axis_index("dp"), lax.axis_index("seq"), lax.axis_index("tensor")
    x, y = lax.rem(dp, 2), lax.div(dp, 2)
    x_dp = dp + 1 - 2 * x
    y_dp = dp + 2 - 4 * y
    d_dp = 3 - dp
    return dp, seq, t, x_dp, y_dp, d_dp


def _dev(dp, seq, t):
    return {"dp": dp, "seq": seq, "tensor": t}


def _plane_barrier(n):
    dp, seq, t, x_dp, y_dp, d_dp = _peers()
    bar = pltpu.get_barrier_semaphore()
    for who in (_dev(dp, 1 - seq, t), _dev(x_dp, seq, t), _dev(y_dp, seq, t)):
        pl.semaphore_signal(bar, inc=1, device_id=who, device_id_type=MESH)

    for step in range(1, n):
        pl.semaphore_signal(
            bar, inc=1, device_id=_dev(dp, seq, lax.rem(t + step, n)), device_id_type=MESH
        )
    pl.semaphore_wait(bar, 3 + n - 1)


class _Line:
    def __init__(self, n, ref, rows, ssem, rsem, own=None):
        self.n, self.ref, self.rows, self.ssem, self.rsem = n, ref, rows, ssem, rsem
        self.own = own

    def block(self, o):
        return self.ref.at[:, pl.ds(pl.multiple_of(o * self.rows, self.rows), self.rows), :]

    def copy(self, o, direction, own=False):
        dp, seq, t = lax.axis_index("dp"), lax.axis_index("seq"), lax.axis_index("tensor")
        return pltpu.make_async_remote_copy(
            src_ref=self.own if own else self.block(o),
            dst_ref=self.block(o),
            send_sem=self.ssem.at[0 if direction > 0 else 1, o],
            recv_sem=self.rsem.at[o],
            device_id=_dev(dp, seq, t + direction),
            device_id_type=MESH,
        )

    def step(self, d):
        n, t = self.n, lax.axis_index("tensor")
        for way in (1, -1):
            o = t - way * d
            here = jnp.logical_and(o >= 0, o < n)
            nxt = jnp.logical_and(t + way >= 0, t + way < n)

            @pl.when(here)
            def _(o=o, way=way, nxt=nxt):
                if d > 0:
                    self.copy(o, way).wait_recv()

                @pl.when(nxt)
                def _():
                    self.copy(o, way, d == 0 and self.own is not None).start()

    def finish(self):
        n, t = self.n, lax.axis_index("tensor")
        for d in range(n):
            for way in (1, -1):
                o = t - way * d
                ok = jnp.logical_and(
                    jnp.logical_and(o >= 0, o < n),
                    jnp.logical_and(t + way >= 0, t + way < n),
                )

                @pl.when(ok)
                def _(o=o, way=way):
                    self.copy(o, way).wait_send()


class _Plane:
    def __init__(self, own, full, ssem, rsem, lsem):
        self.own, self.full, self.ssem, self.rsem, self.lsem = own, full, ssem, rsem, lsem

    def copy(self, src, block, who, s):
        return pltpu.make_async_remote_copy(
            src_ref=src,
            dst_ref=self.full.at[block],
            send_sem=self.ssem.at[s],
            recv_sem=self.rsem.at[s],
            device_id=who,
            device_id_type=MESH,
        )

    def begin(self):
        dp, seq, t, x_dp, y_dp, d_dp = _peers()
        me = dp * 2 + seq
        pltpu.make_async_copy(self.own, self.full.at[me], self.lsem).start()
        self.copy(self.own, me, _dev(x_dp, seq, t), 0).start()
        self.copy(self.own, me, _dev(y_dp, seq, t), 1).start()
        self.copy(self.own, me, _dev(dp, 1 - seq, t), 3).start()

    def forward(self):
        dp, seq, t, x_dp, y_dp, d_dp = _peers()
        bx, by = x_dp * 2 + seq, y_dp * 2 + seq
        self.copy(self.own, bx, _dev(x_dp, seq, t), 0).wait_recv()
        self.copy(self.own, by, _dev(y_dp, seq, t), 1).wait_recv()

        @pl.when(seq == 0)
        def _():
            self.copy(self.full.at[by], by, _dev(x_dp, seq, t), 2).start()

        @pl.when(seq == 1)
        def _():
            self.copy(self.full.at[bx], bx, _dev(y_dp, seq, t), 2).start()

        self.copy(self.full.at[bx], bx, _dev(dp, 1 - seq, t), 4).start()
        self.copy(self.full.at[by], by, _dev(dp, 1 - seq, t), 5).start()

    def share(self):
        dp, seq, t, x_dp, y_dp, d_dp = _peers()
        bd = d_dp * 2 + seq
        self.copy(self.own, bd, _dev(x_dp, seq, t), 2).wait_recv()
        self.copy(self.full.at[bd], bd, _dev(dp, 1 - seq, t), 6).start()

    def arrive(self):
        dp, seq, t, x_dp, y_dp, d_dp = _peers()
        me = dp * 2 + seq
        pltpu.make_async_copy(self.own, self.full.at[me], self.lsem).wait()
        for s in (3, 4, 5, 6):
            self.copy(self.own, me, _dev(dp, 1 - seq, t), s).wait_recv()

    def finish(self):
        dp, seq, t, x_dp, y_dp, d_dp = _peers()
        me = dp * 2 + seq
        for s in range(7):
            self.copy(self.own, me, _dev(dp, 1 - seq, t), s).wait_send()


def gather_kernel(n, tok_far, gain, seg, ws, wt, wi, normed, seg_old, fs, ft, fi,
                  tok, zs, zr, ps, pr, ls, hs):
    dp, seq, t = lax.axis_index("dp"), lax.axis_index("seq"), lax.axis_index("tensor")
    rows = tok.shape[1]
    near = pltpu.make_async_copy(tok_far, tok, ls.at[3])
    near.start()
    _plane_barrier(n)
    planes = [
        _Plane(own, full, ps.at[i], pr.at[i], ls.at[i])
        for i, (own, full) in enumerate(((ws, fs), (wt, ft), (wi, fi)))
    ]
    handed = pltpu.make_async_remote_copy(
        src_ref=seg, dst_ref=seg_old, send_sem=hs.at[0], recv_sem=hs.at[1],
        device_id=_dev(dp, 1 - seq, t), device_id_type=MESH,
    )

    @pl.when(seq == 0)
    def _():
        handed.start()
        seg_old[...] = jnp.zeros_like(seg_old)

    for p in planes:
        p.begin()
    near.wait()
    mine = pl.ds(pl.multiple_of(t * rows, rows), rows)
    lines = []
    for s in range(tok.shape[0]):
        v = tok[s].astype(F32)
        rms = lax.rsqrt(jnp.mean(v * v, axis=-1, keepdims=True) + EPS)
        normed[s, mine, :] = (v * rms * gain[...]).astype(BF)
        lines.append(_Line(n, normed.at[pl.ds(s, 1)], rows, zs.at[s], zr.at[s]))
        lines[s].step(0)
    for line in lines:
        line.step(1)
    for p in planes:
        p.forward()
    lines[0].step(2)
    for p in planes:
        p.share()
    for line in lines[1:]:
        line.step(2)
    for d in range(3, n):
        for line in lines:
            line.step(d)
    for p in planes:
        p.arrive()

    @pl.when(seq == 0)
    def _():
        handed.wait_send()

    @pl.when(seq == 1)
    def _():
        handed.wait_recv()

    for line in lines:
        line.finish()
    for p in planes:
        p.finish()


def gather_all(n, tokens, gain, seg, weights):
    seqs, rows, width = tokens.shape
    vm = pl.BlockSpec(memory_space=pltpu.VMEM)
    far = pl.BlockSpec(memory_space=pltpu.HBM)
    full = lambda w: jax.ShapeDtypeStruct((8,) + w.shape, w.dtype)
    act = jax.ShapeDtypeStruct((seqs, n * rows, width), BF)
    return pl.pallas_call(
        functools.partial(gather_kernel, n),
        out_shape=(act, jax.ShapeDtypeStruct(seg.shape, seg.dtype)) + tuple(full(w) for w in weights),
        in_specs=[far, vm, vm, far, vm, far],
        out_specs=(vm,) * 5,
        scratch_shapes=[
            pltpu.VMEM(tokens.shape, tokens.dtype),
            pltpu.SemaphoreType.DMA((seqs, 2, n)),
            pltpu.SemaphoreType.DMA((seqs, n)),
            pltpu.SemaphoreType.DMA((3, 7)),
            pltpu.SemaphoreType.DMA((3, 7)),
            pltpu.SemaphoreType.DMA((4,)),
            pltpu.SemaphoreType.DMA((2,)),
        ],
        compiler_params=pltpu.CompilerParams(
            collective_id=0, has_side_effects=True, vmem_limit_bytes=16 << 20
        ),
        cost_estimate=pl.CostEstimate(flops=30 * 10**9, bytes_accessed=1 << 20, transcendentals=0),
        name="gather_all",
    )(tokens, gain, seg, *weights)


def _line_reduce(n, part, left, right, ssem, rsem):
    dp, seq, t = lax.axis_index("dp"), lax.axis_index("seq"), lax.axis_index("tensor")
    rows = left.shape[2]

    def copy(src, box, o, way):
        return pltpu.make_async_remote_copy(
            src_ref=src, dst_ref=box.at[o],
            send_sem=ssem.at[0 if way > 0 else 1, o], recv_sem=rsem.at[0 if way > 0 else 1, o],
            device_id=_dev(dp, seq, t + way), device_id_type=MESH,
        )

    def block(o):
        return part.at[:, pl.ds(pl.multiple_of(o * rows, rows), rows), :]

    def step(k):
        for way, box, place in ((1, left, t), (-1, right, n - 1 - t)):
            target = lambda j: n - 1 - j if way > 0 else j
            if k == 0:
                @pl.when(place == 0)
                def _():
                    for j in range(n - 1):
                        copy(block(target(j)), box, target(j), way).start()
            else:
                @pl.when(jnp.logical_and(place > 0, place <= k))
                def _():
                    o = target(k - place)
                    copy(block(o), box, o, way).wait_recv()
                    for s in range(part.shape[0]):
                        own = part[s, pl.ds(pl.multiple_of(o * rows, rows), rows), :].astype(F32)
                        box[o, s] = (box[o, s].astype(F32) + own).astype(BF)
                    copy(box.at[o], box, o, way).start()

    def final(out):
        mine = pl.ds(pl.multiple_of(t * rows, rows), rows)
        for s in range(part.shape[0]):
            out[s] = part[s, mine, :].astype(F32)

        @pl.when(t > 0)
        def _():
            copy(left.at[0], left, t, 1).wait_recv()
            for s in range(part.shape[0]):
                out[s] = out[s] + left[t, s].astype(F32)

        @pl.when(t < n - 1)
        def _():
            copy(left.at[0], right, t, -1).wait_recv()
            for s in range(part.shape[0]):
                out[s] = out[s] + right[t, s].astype(F32)

    def finish():
        for j in range(n - 1):
            for way, box, o in ((1, left, n - 1 - j), (-1, right, j)):
                sends = (t < o) if way > 0 else (t > o)

                @pl.when(sends)
                def _():
                    copy(box.at[o], box, o, way).wait_send()

    return step, final, finish


def _line_reduces(n, part, left, right, ssem, rsem):
    one = lambda s: pl.ds(s, 1)
    return [
        _line_reduce(
            n, part.at[one(s)], left.at[:, one(s)], right.at[:, one(s)], ssem.at[s], rsem.at[s]
        )
        for s in range(part.shape[0])
    ]


class _PlaneReduce:
    def __init__(self, part, pair, box, ssem, rsem):
        self.part, self.pair, self.box, self.ssem, self.rsem = part, pair, box, ssem, rsem

    def copy(self, src, dst, who, s):
        return pltpu.make_async_remote_copy(
            src_ref=src, dst_ref=dst, send_sem=self.ssem.at[s], recv_sem=self.rsem.at[s],
            device_id=who, device_id_type=MESH,
        )

    def begin(self):
        dp, seq, t, x_dp, y_dp, d_dp = _peers()
        for slot, chip in enumerate((d_dp, x_dp, y_dp, dp)):
            self.copy(self.part.at[chip * 2 + 1 - seq], self.pair.at[slot], _dev(dp, 1 - seq, t), slot).start()

    def _paired(self, slot, chip, also=None):
        dp, seq, t, x_dp, y_dp, d_dp = _peers()
        self.copy(self.pair.at[slot], self.pair.at[slot], _dev(dp, 1 - seq, t), slot).wait_recv()
        v = self.part[chip * 2 + seq].astype(F32) + self.pair[slot].astype(F32)
        self.pair[slot] = v.astype(BF)

    def send_far(self):
        dp, seq, t, x_dp, y_dp, d_dp = _peers()
        for slot, chip in enumerate((d_dp, x_dp, y_dp)):
            self._paired(slot, chip)
            if slot == 0:
                @pl.when(seq == 0)
                def _():
                    self.copy(self.pair.at[0], self.box.at[2], _dev(x_dp, seq, t), 4).start()

                @pl.when(seq == 1)
                def _():
                    self.copy(self.pair.at[0], self.box.at[2], _dev(y_dp, seq, t), 4).start()

        @pl.when(seq == 0)
        def _():
            self.copy(self.pair.at[1], self.box.at[0], _dev(x_dp, seq, t), 5).start()

        @pl.when(seq == 1)
        def _():
            self.copy(self.pair.at[2], self.box.at[1], _dev(y_dp, seq, t), 6).start()

    def send_near(self):
        dp, seq, t, x_dp, y_dp, d_dp = _peers()
        self.copy(self.pair.at[0], self.box.at[2], _dev(dp, seq, t), 4).wait_recv()

        @pl.when(seq == 0)
        def _():
            self.box[2] = (self.box[2].astype(F32) + self.pair[2].astype(F32)).astype(BF)
            self.copy(self.box.at[2], self.box.at[1], _dev(y_dp, seq, t), 6).start()

        @pl.when(seq == 1)
        def _():
            self.box[2] = (self.box[2].astype(F32) + self.pair[1].astype(F32)).astype(BF)
            self.copy(self.box.at[2], self.box.at[0], _dev(x_dp, seq, t), 5).start()

    def final(self, out):
        dp, seq, t, x_dp, y_dp, d_dp = _peers()
        self.copy(self.pair.at[3], self.pair.at[3], _dev(dp, seq, t), 3).wait_recv()
        self.copy(self.pair.at[0], self.box.at[0], _dev(dp, seq, t), 5).wait_recv()
        self.copy(self.pair.at[0], self.box.at[1], _dev(dp, seq, t), 6).wait_recv()
        out[...] = (
            self.part[dp * 2 + seq].astype(F32) + self.pair[3].astype(F32)
            + self.box[0].astype(F32) + self.box[1].astype(F32)
        )

    def finish(self):
        dp, seq, t, x_dp, y_dp, d_dp = _peers()
        for s in range(7):
            self.copy(self.pair.at[0], self.box.at[0], _dev(dp, 1 - seq, t), s).wait_send()


class _Smalls:
    def __init__(self, n, box, line, ssem, rsem):
        self.n, self.box, self.line, self.ssem, self.rsem = n, box, line, ssem, rsem

    def copy(self, j, who):
        return pltpu.make_async_remote_copy(
            src_ref=self.box.at[2 * j], dst_ref=self.box.at[2 * j + 1],
            send_sem=self.ssem.at[j], recv_sem=self.rsem.at[j],
            device_id=who, device_id_type=MESH,
        )

    def near(self, j):
        dp, seq, t, x_dp, y_dp, d_dp = _peers()
        return (_dev(dp, 1 - seq, t), _dev(x_dp, seq, t), _dev(y_dp, seq, t))[j]

    def begin(self, value):
        self.box[0] = value
        self.copy(0, self.near(0)).start()

    def step(self, j):
        self.copy(j, self.near(j)).wait_recv()
        total = self.box[2 * j] + self.box[2 * j + 1]
        if j < 2:
            self.box[2 * j + 2] = total
            self.copy(j + 1, self.near(j + 1)).start()
        else:
            t = lax.axis_index("tensor")
            self.line[t] = total
            for o in range(self.n):
                @pl.when(t != o)
                def _(o=o):
                    self.across(t, o).start()

    def across(self, src, who):
        dp, seq, t = lax.axis_index("dp"), lax.axis_index("seq"), lax.axis_index("tensor")
        return pltpu.make_async_remote_copy(
            src_ref=self.line.at[src], dst_ref=self.line.at[src],
            send_sem=self.ssem.at[3 + who], recv_sem=self.rsem.at[3 + src],
            device_id=_dev(dp, seq, who), device_id_type=MESH,
        )

    def final(self):
        t = lax.axis_index("tensor")
        for o in range(self.n):
            @pl.when(t != o)
            def _(o=o):
                self.across(o, o).wait_recv()

    def finish(self):
        t = lax.axis_index("tensor")
        for j in range(3):
            self.copy(j, self.near(j)).wait_send()
        for o in range(self.n):
            @pl.when(t != o)
            def _(o=o):
                self.across(t, o).wait_send()


class _LineSum:
    def __init__(self, n, part, box, out, ssem, rsem):
        self.n, self.part, self.box, self.out, self.ssem, self.rsem = n, part, box, out, ssem, rsem

    def copy(self, phase, src_block, dst_ref, who, origin):
        dp, seq = lax.axis_index("dp"), lax.axis_index("seq")
        return pltpu.make_async_remote_copy(
            src_ref=src_block, dst_ref=dst_ref,
            send_sem=self.ssem.at[phase, who], recv_sem=self.rsem.at[phase, origin],
            device_id=_dev(dp, seq, who), device_id_type=MESH,
        )

    def scatter(self):
        t = lax.axis_index("tensor")
        for o in range(self.n):
            @pl.when(t != o)
            def _(o=o):
                self.copy(0, self.part.at[o], self.box.at[t], o, t).start()

    def gather(self):
        t = lax.axis_index("tensor")
        total = self.part[t].astype(F32)
        for o in range(self.n):
            @pl.when(t != o)
            def _(o=o):
                self.copy(0, self.part.at[o], self.box.at[o], o, o).wait_recv()

            @pl.when(t == o)
            def _(o=o):
                self.box[o] = jnp.zeros(self.box.shape[1:], self.box.dtype)
        for o in range(self.n):
            total = total + self.box[o].astype(F32)
        self.out[t] = total.astype(self.out.dtype)
        for o in range(self.n):
            @pl.when(t != o)
            def _(o=o):
                self.copy(1, self.out.at[t], self.out.at[t], o, t).start()

    def arrive(self):
        t = lax.axis_index("tensor")
        for o in range(self.n):
            @pl.when(t != o)
            def _(o=o):
                self.copy(1, self.out.at[o], self.out.at[o], o, o).wait_recv()

    def finish(self):
        t = lax.axis_index("tensor")
        for o in range(self.n):
            @pl.when(t != o)
            def _(o=o):
                self.copy(0, self.part.at[o], self.box.at[o], o, o).wait_send()
                self.copy(1, self.part.at[o], self.box.at[o], o, o).wait_send()


LANES = 128


def _split(v, parts):
    out = []
    for _ in range(parts):
        b = v.astype(BF)
        out.append(b)
        v = v - b.astype(F32)
    return jnp.concatenate(out, axis=1)


def _dot(a, b, ca=1, cb=0):
    return lax.dot_general(a, b, (((ca,), (cb,)), ((), ())), preferred_element_type=F32)


def _iota(shape, axis):
    return lax.broadcasted_iota(jnp.int32, shape, axis)


def _spreader(rows, p):
    head = lax.rem(_iota((rows, LANES), 0), LANES)
    return (head == 2 * p + lax.div(_iota((rows, LANES), 1), HEAD_DIM)).astype(F32).astype(BF)


def _folder(rows, p):
    chan = lax.rem(_iota((rows, LANES), 0), LANES)
    return (_iota((rows, LANES), 1) == 2 * p + lax.div(chan, HEAD_DIM)).astype(F32).astype(BF)


def _sig(v):
    return 1.0 / (1.0 + jnp.exp(-v))


def _three(v):
    return v[:, :LANES] + v[:, LANES : 2 * LANES] + v[:, 2 * LANES :]


def _head_scalars(raw, hp, marks, length):
    v = raw + hp[0:1, :]
    delta = jnp.maximum(v, 0.0) + jnp.log1p(jnp.exp(-jnp.abs(v)))
    log_decay = -delta * jnp.exp(hp[1:2, :])
    lower = (_iota((length, length), 0) >= _iota((length, length), 1)).astype(F32).astype(BF)
    running = _three(_dot(lower, _split(log_decay, 3)))
    entry = jnp.exp(running) * marks[:, 4:5]
    to_end = jnp.exp(running[length - 1 :, :] - running) * marks[:, 5:6]
    return v, delta, log_decay, running, entry, to_end


def _marks(rows):
    full = jnp.concatenate([rows, jnp.zeros((LANES - rows.shape[0], rows.shape[1]), F32)], axis=0)
    return full.T


def _bias_matrix(rows, marks, length):
    ok = (_iota((length, length), 0) >= _iota((length, length), 1)) & (
        marks[:, 0:1] == rows[0:1, :]
    )
    return jnp.where(ok, 0.0, -1e30)


def _conv(pad, marks, taps, bias, length):
    total = bias + taps[0:1, :] * pad[8 : 8 + length, :]
    for k in range(1, KERNEL):
        total = total + taps[k : k + 1, :] * (pad[8 - k : 8 - k + length, :] * marks[:, k : k + 1])
    return total


def mix_fwd_kernel(n, seg, seg_old, hp, taps_i, bias_i, taps_s, bias_s, cot, wo, wg, normed, wi, ws, wt,
                   y, u_i, u_s, entry_o, incoming, gate, cot_full, fo, fg,
                   pre_i, pre_s, old_i, old_s, raw, rows,
                   pad, run3, run_t, bias_m, scores, heads_hl, inflow, zs, zr, ps, pr, ls, hs):
    dp, seq, t = lax.axis_index("dp"), lax.axis_index("seq"), lax.axis_index("tensor")
    seqs, length, width = pre_i.shape
    model = normed.shape[2]
    pairs = width // LANES
    wide = 2 * LANES
    _plane_barrier(n)
    lines = [
        _Line(n, cot_full.at[pl.ds(s, 1)], cot.shape[1], zs.at[s], zr.at[s], cot.at[pl.ds(s, 1)])
        for s in range(seqs)
    ]
    planes = (_Plane(wg, fg, ps.at[0], pr.at[0], ls.at[0]), _Plane(wo, fo, ps.at[1], pr.at[1], ls.at[1]))
    whole = _Line(n, cot_full, cot.shape[1], zs, zr)
    own = pltpu.make_async_copy(cot, whole.block(t), ls.at[2])
    own.start()
    for line in lines:
        line.step(0)
    for plane in planes:
        plane.begin()
    flat = normed[...].reshape(seqs * length, model)
    pre_s[...] = _dot(flat, ws[...].reshape(model, ws.shape[2])).astype(BF).reshape(pre_s.shape)

    def inner_part(c, _):
        ch = pl.ds(pl.multiple_of(c * wide, wide), wide)
        part = _dot(flat, wi[:, :, ch].reshape(model, wide))
        pre_i[:, :, ch] = part.astype(BF).reshape(seqs, length, wide)
        return 0

    lax.fori_loop(0, width // wide, inner_part, 0)
    ends = [
        pltpu.make_async_remote_copy(
            src_ref=a.at[:, pl.ds(length - 16, 16), :], dst_ref=b,
            send_sem=hs.at[2 + i], recv_sem=hs.at[4 + i],
            device_id=_dev(dp, 1 - seq, t), device_id_type=MESH,
        )
        for i, (a, b) in enumerate(((pre_i, old_i), (pre_s, old_s)))
    ]

    @pl.when(seq == 0)
    def _():
        for c in ends:
            c.start()
        old_i[...] = jnp.zeros_like(old_i)
        old_s[...] = jnp.zeros_like(old_s)

    raw[...] = _dot(flat, wt[...].reshape(model, LANES)).reshape(raw.shape)
    for s in range(seqs):
        now = seg[s : s + 1, :].astype(F32)
        old = seg_old[s : s + 1, :].astype(F32)
        both = jnp.broadcast_to(jnp.concatenate([old, now], axis=1), (8, 2 * length))
        here = jnp.broadcast_to(now, (8, length))
        place = _iota((8, length), 0)
        block = jnp.where(place == 0, here, 0.0)
        others = [pltpu.roll(both, k, 1)[:, length:] for k in range(1, KERNEL)]
        others += [both[:, length - 1 : length], both[:, 2 * length - 1 :]]
        for k, other in enumerate(others):
            block = jnp.where((place == k + 1) & (here == other), 1.0, block)
        rows[s] = block

    lines[0].step(1)

    @pl.when(seq == 1)
    def _():
        for c in ends:
            c.wait_recv()

    def one(s, _):
        rw = rows[s]
        marks = _marks(rw)
        v, delta, log_decay, running, entry, to_end = _head_scalars(raw[s], hp, marks, length)
        entry_o[s] = entry
        run3[...] = _split(running, 3)
        run_t[...] = running.T
        bias_m[...] = _bias_matrix(rw, marks, length)
        heads_hl[0] = _split(delta, 2)
        heads_hl[1] = _split(to_end, 2)
        maps = []
        for half in range(2):
            ch = slice(half * STATE, (half + 1) * STATE)
            pad[0:8, :] = old_s[s, :, ch].astype(F32)[8:16, :]
            pad[8:, :] = pre_s[s, :, ch].astype(F32)
            u = _conv(pad, marks, taps_s[:, ch], bias_s[:, ch], length)
            u_s[s, :, ch] = u
            maps.append((u * _sig(u)).astype(BF))
        b_map, c_map = maps
        scores[...] = _dot(c_map, b_map, 1, 1)

        def pair(p, _):
            @pl.when(jnp.logical_and(s == 0, p == 4))
            def _():
                lines[1].step(1)

            @pl.when(jnp.logical_and(s == 1, p == 0))
            def _():
                for plane in planes:
                    plane.forward()

            @pl.when(jnp.logical_and(s == 1, p == 1))
            def _():
                lines[0].step(2)

            @pl.when(jnp.logical_and(s == 1, p == 5))
            def _():
                lines[1].step(2)
                planes[0].share()

            ch = pl.ds(pl.multiple_of(p * LANES, LANES), LANES)
            at = pl.ds(pl.multiple_of(t * width + p * LANES, LANES), LANES)
            pad[0:8, :] = old_i[s, :, ch].astype(F32)[8:16, :]
            pad[8:, :] = pre_i[s, :, ch].astype(F32)
            u = _conv(pad, marks, taps_i[:, at], bias_i[:, at], length)
            u_i[s, :, ch] = u
            x = u * _sig(u)
            spread = _spreader(2 * LANES, p)
            xd = x * _dot(heads_hl[0], spread)
            inflow[s, :, ch] = _dot(b_map, (xd * _dot(heads_hl[1], spread)).astype(BF), 0, 0).astype(BF)
            skip = _dot(_split(hp[...], 2), spread)[2:3, :]
            total = skip * x
            xb = xd.astype(BF)
            lane = lax.div(_iota(xb.shape, 1), HEAD_DIM)
            for a in range(2):
                h = 2 * p + a
                pick = (lax.rem(_iota((3 * LANES, length), 0), LANES) == h).astype(F32).astype(BF)
                decay = jnp.exp(_dot(run3[...], pick) - run_t[pl.ds(h, 1), :] + bias_m[...])
                mixing = (decay * scores[...]).astype(BF)
                total = total + _dot(mixing, jnp.where(lane == a, xb, jnp.zeros_like(xb)))
            y[s, :, ch] = total
            return 0

        lax.fori_loop(0, pairs, pair, 0)
        return 0

    lax.fori_loop(0, seqs, one, 0)
    handed = pltpu.make_async_remote_copy(
        src_ref=inflow, dst_ref=incoming, send_sem=hs.at[0], recv_sem=hs.at[1],
        device_id=_dev(dp, 1 - seq, t), device_id_type=MESH,
    )

    @pl.when(seq == 0)
    def _():
        handed.start()
        incoming[...] = jnp.zeros_like(incoming)

    planes[1].share()
    for d in range(3, n):
        lines[0].step(d)
    planes[0].arrive()

    def gate_part(c, _):
        ch = pl.ds(pl.multiple_of(c * wide, wide), wide)
        part = _dot(flat, fg[:, :, ch].reshape(model, wide))
        gate[:, :, ch] = part.reshape(seqs, length, wide)
        return 0

    lax.fori_loop(0, width // wide, gate_part, 0)
    for d in range(3, n):
        lines[1].step(d)
    planes[1].arrive()
    own.wait()

    @pl.when(seq == 0)
    def _():
        handed.wait_send()
        for c in ends:
            c.wait_send()

    @pl.when(seq == 1)
    def _():
        handed.wait_recv()

    for line in lines:
        line.finish()
    for plane in planes:
        plane.finish()


def _mixer_call(kernel, ins, outs, scratch, name, cost, number, far=()):
    vm = pl.BlockSpec(memory_space=pltpu.VMEM)
    return pl.pallas_call(
        kernel,
        out_shape=outs,
        in_specs=[
            pl.BlockSpec(memory_space=pltpu.HBM if i in far else pltpu.VMEM) for i in range(len(ins))
        ],
        out_specs=(vm,) * len(outs),
        scratch_shapes=scratch,
        compiler_params=pltpu.CompilerParams(
            collective_id=number, has_side_effects=True, vmem_limit_bytes=28 << 20
        ),
        cost_estimate=pl.CostEstimate(flops=cost, bytes_accessed=1 << 20, transcendentals=0),
        name=name,
    )(*ins)


def mix_fwd(n, seg, seg_old, hp, taps_i, bias_i, taps_s, bias_s, cot, wo, wg, normed, wi, ws, wt):
    seqs, length, model = normed.shape
    width = wi.shape[2]
    sd = jax.ShapeDtypeStruct
    return _mixer_call(
        functools.partial(mix_fwd_kernel, n),
        (seg, seg_old, hp, taps_i, bias_i, taps_s, bias_s, cot, wo, wg, normed, wi, ws, wt),
        (
            sd((seqs, length, width), F32),
            sd((seqs, length, width), F32),
            sd((seqs, length, 2 * STATE), F32),
            sd((seqs, length, LANES), F32),
            sd((seqs, STATE, width), BF),
            sd((seqs, length, width), F32),
            sd((seqs, length, model), BF),
            sd((8,) + wo.shape, BF),
            sd((8,) + wg.shape, BF),
            sd((seqs, length, width), BF),
            sd((seqs, length, 2 * STATE), BF),
            sd((seqs, 16, width), BF),
            sd((seqs, 16, 2 * STATE), BF),
            sd((seqs, length, LANES), F32),
            sd((seqs, 8, length), F32),
        ),
        [
            pltpu.VMEM((8 + length, LANES), F32),
            pltpu.VMEM((length, 3 * LANES), BF),
            pltpu.VMEM((LANES, length), F32),
            pltpu.VMEM((length, length), F32),
            pltpu.VMEM((length, length), F32),
            pltpu.VMEM((2, length, 2 * LANES), BF),
            pltpu.VMEM((seqs, STATE, width), BF),
            pltpu.SemaphoreType.DMA((seqs, 2, n)),
            pltpu.SemaphoreType.DMA((seqs, n)),
            pltpu.SemaphoreType.DMA((2, 7)),
            pltpu.SemaphoreType.DMA((2, 7)),
            pltpu.SemaphoreType.DMA((3,)),
            pltpu.SemaphoreType.DMA((6,)),
        ],
        "mix_fwd",
        30 * 10**9,
        3,
        (7, 8, 9),
    )


def gate_kernel(n, y_part, u_s, entry, h0, gate, cot, wo, gain, tokens_in,
                d_mixed, d_gate, lam, po, go, gg, g_gain,
                mixed, gated, grad_gn, normed, local, acc, box, ss, rs, hs):
    dp, seq, t = lax.axis_index("dp"), lax.axis_index("seq"), lax.axis_index("tensor")
    seqs, length, width = y_part.shape
    model = cot.shape[2]
    wide = 2 * LANES
    bar = pltpu.get_barrier_semaphore()
    pl.semaphore_signal(bar, inc=1, device_id=_dev(dp, 1 - seq, t), device_id_type=MESH)
    for step in range(1, n):
        pl.semaphore_signal(
            bar, inc=1, device_id=_dev(dp, seq, lax.rem(t + step, n)), device_id_type=MESH
        )
    acc[...] = jnp.zeros_like(acc)
    g_gain[...] = jnp.zeros_like(g_gain)

    def spread_of(s, c):
        heads = _split(entry[s], 2)
        head = lax.rem(_iota((wide, wide), 0), LANES)
        one = head == 4 * c + lax.div(_iota((wide, wide), 1), HEAD_DIM)
        return _dot(heads, one.astype(F32).astype(BF))

    def maps(s):
        u = u_s[s, :, STATE:]
        return (u * _sig(u)).astype(BF)

    def first(c, _):
        ch = pl.ds(pl.multiple_of(c * wide, wide), wide)
        at = pl.ds(pl.multiple_of(t * width + c * wide, wide), wide)
        w = wo[:, :, ch].reshape(model, wide)
        for s in range(seqs):
            g = _dot(cot[s], w)
            grad_gn[s, :, ch] = g
            m = y_part[s, :, ch] + spread_of(s, c) * _dot(maps(s), h0[s, :, ch])
            z = gate[s, :, ch]
            gd = m * (z * _sig(z))
            mixed[s, :, ch] = m
            gated[s, :, ch] = gd
            sq, ds = gd * gd, g * gain[:, at] * gd
            acc[0, s] += sq[:, :LANES] + sq[:, LANES:]
            acc[1, s] += ds[:, :LANES] + ds[:, LANES:]
        return 0

    lax.fori_loop(0, width // wide, first, 0)
    ones = jnp.ones((8, wide), F32).astype(BF)
    row = _iota((8, length), 0)
    mine = jnp.zeros((8, length), F32)
    for kind in range(2):
        for s in range(seqs):
            sums = _dot(ones, _split(acc[kind, s], 2), 1, 1)
            mine = jnp.where(row == kind * seqs + s, sums, mine)
    box[t] = mine
    pl.semaphore_wait(bar, n)

    def copy(src, who):
        return pltpu.make_async_remote_copy(
            src_ref=box.at[src], dst_ref=box.at[src], send_sem=ss.at[who], recv_sem=rs.at[src],
            device_id=_dev(dp, seq, who), device_id_type=MESH,
        )

    for o in range(n):
        @pl.when(t != o)
        def _(o=o):
            copy(t, o).start()
    for o in range(n):
        @pl.when(t != o)
        def _(o=o):
            copy(o, o).wait_recv()
    full_width = n * width
    cols = _marks(jnp.sum(box[...], axis=0) / full_width)

    def second(c, _):
        ch = pl.ds(pl.multiple_of(c * wide, wide), wide)
        at = pl.ds(pl.multiple_of(t * width + c * wide, wide), wide)
        gn = gain[:, at]
        for s in range(seqs):
            rms = lax.rsqrt(cols[:, s : s + 1] + EPS)
            mean = cols[:, seqs + s : seqs + s + 1]
            g, gd, m, z = grad_gn[s, :, ch], gated[s, :, ch], mixed[s, :, ch], gate[s, :, ch]
            sg = _sig(z)
            scaled = gd * rms
            normed[s, :, ch] = (scaled * gn).astype(BF)
            g_gain[0:1, ch] += jnp.sum(g * scaled, axis=0, keepdims=True)
            d_gd = rms * (g * gn) - scaled * (rms * rms * mean)
            dm = d_gd * (z * sg)
            d_mixed[s, :, ch] = dm
            d_gate[s, :, ch] = (d_gd * m * sg * (1.0 + z * (1.0 - sg))).astype(BF)
            ed = (spread_of(s, c) * dm).astype(BF)
            local[s, :, ch] = _dot(maps(s), ed, 0, 0).astype(BF)
        return 0

    lax.fori_loop(0, width // wide, second, 0)
    handed = pltpu.make_async_remote_copy(
        src_ref=local, dst_ref=lam, send_sem=hs.at[0], recv_sem=hs.at[1],
        device_id=_dev(dp, 1 - seq, t), device_id_type=MESH,
    )

    @pl.when(seq == 1)
    def _():
        handed.start()
        lam[...] = jnp.zeros_like(lam)

    blocks = 2
    rows = blocks * wo.shape[1]

    def third(b, _):
        ch = pl.ds(pl.multiple_of(b * rows, LANES), rows)
        w = wo[pl.ds(b * blocks, blocks)].reshape(rows, width)
        total = None
        for s in range(seqs):
            po[s, :, ch] = _dot(normed[s], w, 1, 1).astype(BF)
            part = _dot(cot[s, :, ch], normed[s], 0, 0)
            total = part if total is None else total + part
        go[pl.ds(b * blocks, blocks)] = total.reshape(blocks, wo.shape[1], width).astype(BF)
        total = None
        for s in range(seqs):
            part = _dot(tokens_in[s, :, ch], d_gate[s], 0, 0)
            total = part if total is None else total + part
        gg[pl.ds(b * blocks, blocks)] = total.reshape(blocks, wo.shape[1], width).astype(BF)
        return 0

    lax.fori_loop(0, model // rows, third, 0)

    @pl.when(seq == 1)
    def _():
        handed.wait_send()

    @pl.when(seq == 0)
    def _():
        handed.wait_recv()

    for o in range(n):
        @pl.when(t != o)
        def _(o=o):
            copy(o, o).wait_send()


def gate_stage(n, y_part, u_s, entry, h0, gate, cot, wo, gain, tokens_in):
    seqs, length, width = y_part.shape
    sd = jax.ShapeDtypeStruct
    whole = pltpu.VMEM((seqs, length, width), F32)
    return _mixer_call(
        functools.partial(gate_kernel, n),
        (y_part, u_s, entry, h0, gate, cot, wo, gain, tokens_in),
        (
            sd((seqs, length, width), F32),
            sd((seqs, length, width), BF),
            sd((seqs, STATE, width), BF),
            sd((seqs, length, cot.shape[2]), BF),
            sd(wo.shape, BF),
            sd(wo.shape, BF),
            sd((8, width), F32),
        ),
        [
            whole, whole, whole,
            pltpu.VMEM((seqs, length, width), BF),
            pltpu.VMEM((seqs, STATE, width), BF),
            pltpu.VMEM((2, seqs, length, LANES), F32),
            pltpu.VMEM((n, 8, length), F32),
            pltpu.SemaphoreType.DMA((n,)),
            pltpu.SemaphoreType.DMA((n,)),
            pltpu.SemaphoreType.DMA((2,)),
        ],
        "gate_stage",
        6 * 10**9,
        2,
    )


def mix_bwd_kernel(n, dy_r, u_i, u_s, pre_i, old_i, pre_s, old_s, raw, rows, h0, lam, hp,
                   taps_i, taps_s, po, go, gg,
                   d_i, d_s, d_raw, sm_i, sm_s, sm_h, o_po, o_go, o_gg,
                   pad, moved, run3, run_t, bias_m, scores, d_scores, heads_hl,
                   acc_r, acc_c, acc_d, acc_q, d_b, d_c, lo, ro, xo, bo, xg, bg,
                   head_i, tail_i, head_s, tail_s, next_i, next_s, zs, zr, ps, pr, hs):
    t = lax.axis_index("tensor")
    seqs, length, width = pre_i.shape
    pairs = width // LANES
    _plane_barrier(n)
    lines = _line_reduces(n, po, lo, ro, zs, zr)
    planes = (
        _PlaneReduce(go, xo, bo, ps.at[0], pr.at[0]), _PlaneReduce(gg, xg, bg, ps.at[1], pr.at[1])
    )
    for step, _, _ in lines:
        step(0)
    for plane in planes:
        plane.begin()
    sm_i[...] = jnp.zeros_like(sm_i)
    sm_s[...] = jnp.zeros_like(sm_s)
    sm_h[...] = jnp.zeros_like(sm_h)
    moved[0:8, :] = jnp.zeros((8, LANES), F32)
    moved[8 + length :, :] = jnp.zeros((8, LANES), F32)

    def conv_back(du, marks, taps, s, ch, d_o, head_o, tail_o, sm):
        total = None
        for k in range(KERNEL):
            m = du if k == 0 else du * marks[:, k : k + 1]
            moved[8 : 8 + length, :] = m
            sm[k : k + 1, ch] += jnp.sum(m * pad[8 - k : 8 - k + length, :], axis=0, keepdims=True)
            part = taps[k : k + 1, :] * moved[k : k + 8 + length, :]
            total = part if total is None else total + part
        sm[4:5, ch] += jnp.sum(du, axis=0, keepdims=True)
        head_o[s, :, ch] = total[0:8, :]
        d_o[s, :, ch] = total[8:, :].astype(BF)
        tail_o[s, :, ch] = total[length - 8 :, :]

    def one(s, _):
        rw = rows[s]
        marks = _marks(rw)
        v, delta, log_decay, running, entry, to_end = _head_scalars(raw[s], hp, marks, length)
        run3[...] = _split(running, 3)
        run_t[...] = running.T
        bias_m[...] = _bias_matrix(rw, marks, length)
        heads_hl[0] = _split(delta, 2)
        heads_hl[1] = _split(to_end, 2)
        heads_hl[2] = _split(entry, 2)
        ub, uc = u_s[s, :, :STATE], u_s[s, :, STATE:]
        sb, sc = _sig(ub), _sig(uc)
        b_map, c_map = (ub * sb).astype(BF), (uc * sc).astype(BF)
        scores[...] = _dot(c_map, b_map, 1, 1)
        d_scores[...] = jnp.zeros_like(d_scores)
        for acc in (acc_r, acc_c, acc_d, acc_q, d_b, d_c):
            acc[...] = jnp.zeros_like(acc)

        def pair(p, _):
            @pl.when(jnp.logical_and(s == 0, p == 2))
            def _():
                planes[0].send_far()

            @pl.when(jnp.logical_and(s == 0, p == 3))
            def _():
                planes[1].send_far()
                lines[0][0](1)

            @pl.when(jnp.logical_and(s == 0, p == 5))
            def _():
                lines[0][0](2)

            @pl.when(jnp.logical_and(s == 1, p == 2))
            def _():
                planes[0].send_near()

            @pl.when(jnp.logical_and(s == 1, p == 5))
            def _():
                planes[1].send_near()

            @pl.when(jnp.logical_and(s == 1, p == 4))
            def _():
                lines[1][0](1)

            ch = pl.ds(pl.multiple_of(p * LANES, LANES), LANES)
            at = pl.ds(pl.multiple_of(t * width + p * LANES, LANES), LANES)
            u = u_i[s, :, ch]
            sg = _sig(u)
            x = u * sg
            dy = dy_r[s, :, ch]
            spread, fold = _spreader(2 * LANES, p), _folder(2 * LANES, p)
            dl = _dot(heads_hl[0], spread)
            q = _dot(heads_hl[1], spread)
            e = _dot(heads_hl[2], spread)
            xd = x * dl
            xb, db = xd.astype(BF), dy.astype(BF)
            h_in, l_in = h0[s, :, ch], lam[s, :, ch]
            c_h = _dot(c_map, h_in)
            b_l = _dot(b_map, l_in)
            qx, ed = q * xd, e * dy
            d_b[...] += _dot(qx.astype(BF), l_in, 1, 1)
            d_c[...] += _dot(ed.astype(BF), h_in, 1, 1)
            late = qx * b_l
            dxd = q * b_l
            lane = lax.div(_iota(xb.shape, 1), HEAD_DIM)
            for a in range(2):
                h = 2 * p + a
                pick = (lax.rem(_iota((3 * LANES, length), 0), LANES) == h).astype(F32).astype(BF)
                decay = jnp.exp(_dot(run3[...], pick) - run_t[pl.ds(h, 1), :] + bias_m[...])
                da = jnp.where(lane == a, db, jnp.zeros_like(db))
                ld = decay * _dot(da, xb, 1, 1)
                d_scores[...] += ld
                both = (ld * scores[...]).astype(BF)
                mixing = (decay * scores[...]).astype(BF)
                dxd = dxd + _dot(mixing, da, 0, 0)
                col = (_iota((length, LANES), 1) == h).astype(F32).astype(BF)
                row = (_iota((LANES, length), 0) == h).astype(F32).astype(BF)
                acc_r[...] += _dot(both, col)
                acc_c[...] += _dot(row, both)
            acc_r[...] += _dot(_split(ed * c_h - late, 2), fold)
            acc_d[...] += _dot(_split(dxd * x, 2), fold)
            total = jnp.broadcast_to(jnp.sum(late, axis=0, keepdims=True), (8, LANES))
            acc_q[...] += _dot(_split(total, 2), fold)
            skip = _dot(_split(hp[...], 2), spread)[2:3, :]
            sm_i[5:6, ch] += jnp.sum(dy * x, axis=0, keepdims=True)
            du = (dxd * dl + skip * dy) * (sg * (1.0 + u * (1.0 - sg)))
            pad[0:8, :] = old_i[s, :, ch].astype(F32)[8:16, :]
            pad[8:, :] = pre_i[s, :, ch].astype(F32)
            conv_back(du, marks, taps_i[:, at], s, ch, d_i, head_i, tail_i, sm_i)
            return 0

        lax.fori_loop(0, pairs, pair, 0)
        ds = d_scores[...].astype(BF)
        grads = (d_b[...] + _dot(ds, c_map, 0, 0), d_c[...] + _dot(ds, b_map))
        for half, (g, u, sg) in enumerate(zip(grads, (ub, uc), (sb, sc))):
            ch = slice(half * STATE, (half + 1) * STATE)
            pad[0:8, :] = old_s[s, :, ch].astype(F32)[8:16, :]
            pad[8:, :] = pre_s[s, :, ch].astype(F32)
            du = g * (sg * (1.0 + u * (1.0 - sg)))
            conv_back(du, marks, taps_s[:, ch], s, ch, d_s, head_s, tail_s, sm_s)
        d_run = acc_r[...] - acc_c[...].T
        last = _iota(d_run.shape, 0) == length - 1
        d_run = d_run + jnp.where(last, acc_q[0:1, :], 0.0)
        upper = (_iota((length, length), 0) <= _iota((length, length), 1)).astype(F32).astype(BF)
        d_log = _three(_dot(upper, _split(d_run, 3)))
        d_delta = acc_d[...] - d_log * jnp.exp(hp[1:2, :])
        d_step = d_delta * _sig(v)
        d_raw[s] = d_step.astype(BF)
        sm_h[0:1, :] += jnp.sum(d_step, axis=0, keepdims=True)
        sm_h[1:2, :] += jnp.sum(d_log * log_decay, axis=0, keepdims=True)
        return 0

    lax.fori_loop(0, seqs, one, 0)
    lines[1][0](2)
    dp, seq = lax.axis_index("dp"), lax.axis_index("seq")
    handed = [
        pltpu.make_async_remote_copy(
            src_ref=a, dst_ref=b, send_sem=hs.at[2 * i], recv_sem=hs.at[2 * i + 1],
            device_id=_dev(dp, 1 - seq, t), device_id_type=MESH,
        )
        for i, (a, b) in enumerate(((head_i, next_i), (head_s, next_s)))
    ]

    @pl.when(seq == 1)
    def _():
        for c in handed:
            c.start()

    planes[0].final(o_go)

    @pl.when(seq == 0)
    def _():
        for c, box, tail, out in zip(handed, (next_i, next_s), (tail_i, tail_s), (d_i, d_s)):
            c.wait_recv()
            for s in range(seqs):
                more = jnp.concatenate([jnp.zeros_like(box[s]), box[s]], axis=0)
                out[s, length - 16 :, :] = (tail[s] + more).astype(BF)

    @pl.when(seq == 1)
    def _():
        for c in handed:
            c.wait_send()

    planes[1].final(o_gg)
    for s, (_, final, _) in enumerate(lines):
        final(o_po.at[pl.ds(s, 1)])
    for plane in planes:
        plane.finish()
    for _, _, finish in lines:
        finish()


def mix_bwd(n, dy, u_i, u_s, pre_i, old_i, pre_s, old_s, raw, rows, h0, lam, hp, taps_i, taps_s,
            po, go, gg):
    seqs, length, width = pre_i.shape
    model = po.shape[2]
    box = pltpu.VMEM((n, seqs, length // n, model), BF)
    sd = jax.ShapeDtypeStruct
    square = pltpu.VMEM((length, length), F32)
    tall = pltpu.VMEM((length, LANES), F32)
    return _mixer_call(
        functools.partial(mix_bwd_kernel, n),
        (dy, u_i, u_s, pre_i, old_i, pre_s, old_s, raw, rows, h0, lam, hp, taps_i, taps_s, po, go,
         gg),
        (
            sd((seqs, length, width), BF),
            sd((seqs, length, 2 * STATE), BF),
            sd((seqs, length, LANES), BF),
            sd((8, width), F32),
            sd((8, 2 * STATE), F32),
            sd((8, LANES), F32),
            sd((seqs, length // n, model), F32),
            sd(go.shape[1:], F32),
            sd(gg.shape[1:], F32),
        ),
        [
            pltpu.VMEM((8 + length, LANES), F32),
            pltpu.VMEM((16 + length, LANES), F32),
            pltpu.VMEM((length, 3 * LANES), BF),
            pltpu.VMEM((LANES, length), F32),
            square, square, square,
            pltpu.VMEM((3, length, 2 * LANES), BF),
            tall, pltpu.VMEM((LANES, length), F32), tall, pltpu.VMEM((8, LANES), F32), tall, tall,
            box, box,
            pltpu.VMEM((4,) + go.shape[1:], BF),
            pltpu.VMEM((3,) + go.shape[1:], BF),
            pltpu.VMEM((4,) + gg.shape[1:], BF),
            pltpu.VMEM((3,) + gg.shape[1:], BF),
            pltpu.VMEM((seqs, 8, width), F32),
            pltpu.VMEM((seqs, 16, width), F32),
            pltpu.VMEM((seqs, 8, 2 * STATE), F32),
            pltpu.VMEM((seqs, 16, 2 * STATE), F32),
            pltpu.VMEM((seqs, 8, width), F32),
            pltpu.VMEM((seqs, 8, 2 * STATE), F32),
            pltpu.SemaphoreType.DMA((seqs, 2, n)),
            pltpu.SemaphoreType.DMA((seqs, 2, n)),
            pltpu.SemaphoreType.DMA((2, 7)),
            pltpu.SemaphoreType.DMA((2, 7)),
            pltpu.SemaphoreType.DMA((4,)),
        ],
        "mix_bwd",
        8 * 10**9,
        4,
    )


def reduce_kernel(n, normed, dg, di, ds, dr, wg, wi, ws, wt, gain, sm_i, sm_s, sm_h, g_gain,
                  o_pg, o_gi, o_gs, o_gt, o_sm,
                  pg, gi, gs, gt, lg, rg, xi, xs, xt, bi, bs, bt, mb,
                  xp, xb, xo2, zs, zr, ps, pr, ms, mr, es, er):
    _plane_barrier(n)
    seqs, length, width = di.shape
    model = normed.shape[2]
    blocks = 2
    rows = blocks * wi.shape[1]
    small = _Smalls(n, mb, o_sm, ms, mr)
    mb[0] = jnp.zeros(mb.shape[1:], F32)
    mb[0, 0:6, :] = sm_i[0:6, :]
    mb[0, 6:7, :] = g_gain[0:1, :]
    for k in range(5):
        at = 256 * (k % 3)
        mb[0, 9 + k // 3 : 10 + k // 3, at : at + 256] = sm_s[k : k + 1, :]
    mb[0, 10:11, 512:640] = sm_h[0:1, :]
    mb[0, 10:11, 640:768] = sm_h[1:2, :]

    planes = [
        _PlaneReduce(part, pair, box, ps.at[i], pr.at[i])
        for i, (part, pair, box) in enumerate(((gs, xs, bs), (gt, xt, bt), (gi, xi, bi)))
    ]

    def weight(d, out):
        def one(b, _):
            ch = pl.ds(pl.multiple_of(b * rows, LANES), rows)
            total = None
            for s in range(seqs):
                part = _dot(normed[s, :, ch], d[s], 0, 0)
                total = part if total is None else total + part
            out[pl.ds(b * blocks, blocks)] = total.reshape(
                blocks, wi.shape[1], d.shape[2]
            ).astype(BF)
            return 0

        lax.fori_loop(0, model // rows, one, 0)

    weight(ds, gs)
    planes[0].begin()
    weight(dr, gt)
    planes[1].begin()
    weight(di, gi)
    planes[2].begin()
    lines = _line_reduces(n, pg, lg, rg, zs, zr)
    totals = [None] * (model // rows)
    for s in range(seqs):
        for b in range(model // rows):
            ch = slice(b * rows, (b + 1) * rows)
            near = slice(b * blocks, (b + 1) * blocks)
            part = None
            for d, w in zip((dg, di, ds, dr), (wg, wi, ws, wt)):
                more = _dot(d[s], w[near].reshape(rows, w.shape[2]), 1, 1)
                part = more if part is None else part + more
            pg[s, :, ch] = part.astype(BF)
            part = jnp.sum(part * normed[s, :, ch].astype(F32), axis=0, keepdims=True)
            totals[b] = part if totals[b] is None else totals[b] + part
        lines[s][0](0)
    for b, total in enumerate(totals):
        ch = slice(b * rows, (b + 1) * rows)
        mb[0, 7 + b // 2 : 8 + b // 2, (b % 2) * rows : (b % 2 + 1) * rows] = total / gain[:, ch]
    small.copy(0, small.near(0)).start()
    lines[0][0](1)
    small.step(0)
    for p in planes:
        p.send_far()
    small.step(1)
    lines[0][0](2)
    for p in planes[:2]:
        p.send_near()
    small.step(2)
    lines[1][0](1)
    planes[2].send_near()
    planes[0].final(o_gs)
    planes[1].final(o_gt)
    quarter = xp.shape[1]
    for o in range(n):
        xp[o] = o_gs[o * quarter : (o + 1) * quarter, :].astype(BF)
    state = _LineSum(n, xp, xb, xo2, es, er)
    state.scatter()
    lines[1][0](2)
    state.gather()
    planes[2].final(o_gi)
    small.final()
    for s, (_, final, _) in enumerate(lines):
        final(o_pg.at[pl.ds(s, 1)])
    state.arrive()
    for o in range(n):
        o_gs[o * quarter : (o + 1) * quarter, :] = xo2[o].astype(F32)
    for p in planes:
        p.finish()
    state.finish()
    small.finish()
    for _, _, finish in lines:
        finish()


def reduce_all(n, normed, dg, di, ds, dr, wg, wi, ws, wt, gain, sm_i, sm_s, sm_h, g_gain):
    seqs, length, model = normed.shape
    rows = length // n
    sd = jax.ShapeDtypeStruct
    box = pltpu.VMEM((n, seqs, rows, model), BF)
    quarter = pltpu.VMEM((n, ws.shape[1] // n, ws.shape[2]), BF)
    sums = (16, wi.shape[2])
    return _mixer_call(
        functools.partial(reduce_kernel, n),
        (normed, dg, di, ds, dr, wg, wi, ws, wt, gain, sm_i, sm_s, sm_h, g_gain),
        (sd((seqs, rows, model), F32),)
        + tuple(sd(w.shape[1:], F32) for w in (wi, ws, wt))
        + (sd((n,) + sums, F32),),
        [pltpu.VMEM((seqs, length, model), BF)]
        + [pltpu.VMEM(w.shape, BF) for w in (wi, ws, wt)]
        + [box, box]
        + [pltpu.VMEM((4,) + w.shape[1:], BF) for w in (wi, ws, wt)]
        + [pltpu.VMEM((3,) + w.shape[1:], BF) for w in (wi, ws, wt)]
        + [
            pltpu.VMEM((6,) + sums, F32),
            quarter, quarter, quarter,
            pltpu.SemaphoreType.DMA((seqs, 2, n)),
            pltpu.SemaphoreType.DMA((seqs, 2, n)),
            pltpu.SemaphoreType.DMA((3, 7)),
            pltpu.SemaphoreType.DMA((3, 7)),
            pltpu.SemaphoreType.DMA((3 + n,)),
            pltpu.SemaphoreType.DMA((3 + n,)),
            pltpu.SemaphoreType.DMA((2, n)),
            pltpu.SemaphoreType.DMA((2, n)),
        ],
        "reduce_all",
        6 * 10**9,
        1,
    )


def emit_kernel(n, heads, tok, cot, gain, branch, rows, gg, gi, gs, gt, go, sms,
                block_out, g_tok, g_in, o_gg, o_gi, o_gs, o_gt, o_ci, o_ib, o_cs, o_sb,
                o_shift, o_rate, o_skip, o_gain, o_go):
    for s in range(tok.shape[0]):
        v = tok[s].astype(F32)
        rms = lax.rsqrt(jnp.mean(v * v, axis=-1, keepdims=True) + EPS)
        block_out[s] = (v + branch[s]).astype(BF)
        scaled = rows[s] * gain[...]
        mean = jnp.mean(scaled * v, axis=-1, keepdims=True)
        g_tok[s] = cot[s].astype(F32) + rms * scaled - v * (rms * rms * rms * mean)
    o_gg[...] = gg[...]
    o_gi[...] = gi[...]
    o_gs[...] = gs[...]
    o_gt[...] = gt[:, :heads]
    short = jnp.zeros((256 - go.shape[0], go.shape[1]), F32)
    o_go[...] = jnp.concatenate([go[...], short], axis=0).T[:, : go.shape[0]]
    width = sms.shape[2]
    shared = None
    head_rows = None
    for t in range(n):
        ch = slice(t * width, (t + 1) * width)
        o_ci[:, ch] = sms[t, 0:4, :]
        o_ib[:, ch] = sms[t, 4:5, :]
        o_gain[:, ch] = sms[t, 6:7, :]
        block = sms[t, 8:16, :]
        shared = sms[t, 7:11, :] if shared is None else shared + sms[t, 7:11, :]
        lanes = _iota((3 * width, LANES), 0)
        chan = lax.rem(lanes, width)
        to = _iota((3 * width, LANES), 1) == heads * t + lax.div(chan, HEAD_DIM)
        skips = _dot(_split(sms[t, 0:8, :], 3), to.astype(F32).astype(BF))
        lanes = lax.rem(_iota((3 * LANES, LANES), 0), LANES)
        to = (_iota((3 * LANES, LANES), 1) == heads * t + lanes) & (lanes < heads)
        to = to.astype(F32).astype(BF)
        shift = _dot(_split(block[:, 512:640], 3), to)
        rate = _dot(_split(block[:, 640:768], 3), to)
        new = (skips[5:6, :], shift[2:3, :], rate[2:3, :])
        head_rows = new if head_rows is None else tuple(a + b for a, b in zip(head_rows, new))
    every = n * heads
    o_skip[...] = head_rows[0][:, :every]
    o_shift[...] = head_rows[1][:, :every]
    o_rate[...] = head_rows[2][:, :every]
    g_in[:, :width] = shared[0:1, :]
    g_in[:, width:] = shared[1:2, :]
    for k in range(4):
        at = 256 * (k % 3)
        o_cs[k : k + 1, :] = shared[2 + k // 3 : 3 + k // 3, at : at + 256]
    o_sb[...] = shared[3:4, 256:512]


def emit_all(n, heads, tok, cot, gain, branch, rows, gg, gi, gs, gt, go, sms):
    vm = pl.BlockSpec(memory_space=pltpu.VMEM)
    sd = lambda *shape: jax.ShapeDtypeStruct(shape, F32)
    width = sms.shape[2]
    outs = (
        jax.ShapeDtypeStruct(tok.shape, BF), sd(*tok.shape), sd(1, tok.shape[2]),
        sd(*gg.shape), sd(*gi.shape), sd(*gs.shape), sd(gt.shape[0], heads),
        sd(4, n * width), sd(1, n * width), sd(4, 2 * STATE), sd(1, 2 * STATE),
        sd(1, n * heads), sd(1, n * heads), sd(1, n * heads), sd(1, n * width),
        sd(go.shape[1], go.shape[0]),
    )
    return pl.pallas_call(
        functools.partial(emit_kernel, n, heads),
        out_shape=outs,
        in_specs=[vm] * 11,
        out_specs=(vm,) * len(outs),
        compiler_params=pltpu.CompilerParams(vmem_limit_bytes=28 << 20),
        name="emit_all",
    )(tok, cot, gain, branch, rows, gg, gi, gs, gt, go, sms)


def per_device(
    tokens,
    segments,
    input_gain,
    gate_proj,
    inner_proj,
    state_proj,
    step_proj,
    conv_inner,
    inner_bias,
    conv_state,
    state_bias,
    step_bias,
    log_rates,
    skip_gain,
    gated_gain,
    output_proj,
    cotangent,
):
    tensor_count = lax.axis_size("tensor")
    tensor_rank = lax.axis_index("tensor")
    residual = tokens.astype(jnp.float32)
    rms_in = lax.rsqrt(jnp.mean(residual * residual, axis=-1, keepdims=True) + EPS)
    normed_own = (residual * rms_in * input_gain).astype(jnp.bfloat16)
    normed, cot_rows = (
        lax.all_gather(normed_own, "tensor", axis=1, tiled=True),
        lax.all_gather(cotangent, "tensor", axis=1, tiled=True),
    )
    gate_full, inner_full, state_full, step_full, output_full = (
        lax.all_gather(gate_proj, ("dp", "seq"), axis=0, tiled=True),
        lax.all_gather(inner_proj, ("dp", "seq"), axis=0, tiled=True),
        lax.all_gather(state_proj, ("dp", "seq"), axis=0, tiled=True),
        lax.all_gather(step_proj, ("dp", "seq"), axis=0, tiled=True),
        lax.all_gather(output_proj, ("dp", "seq"), axis=1, tiled=True),
    )
    gate_in = jnp.dot(normed, gate_full, preferred_element_type=jnp.float32)
    inner_low = jnp.dot(normed, inner_full, preferred_element_type=jnp.float32).astype(jnp.bfloat16)
    state_low = jnp.dot(normed, state_full, preferred_element_type=jnp.float32).astype(jnp.bfloat16)
    step_raw = jnp.dot(normed, step_full, preferred_element_type=jnp.float32)
    margin = KERNEL - 1
    seg_float = segments.astype(jnp.float32)
    prior_inner, prior_state, prior_seg = passed_along(
        (
            inner_low[:, -margin:],
            state_low[:, -margin:],
            seg_float[:, -margin:].astype(jnp.bfloat16),
        ),
        "seq",
        1,
    )
    padded_inner = jnp.concatenate([prior_inner, inner_low], axis=1).astype(jnp.float32)
    padded_state = jnp.concatenate([prior_state, state_low], axis=1).astype(jnp.float32)
    seg_padded = jnp.concatenate([prior_seg.astype(jnp.float32), seg_float], axis=1)
    pieces = segments.shape[1] // BLOCK
    seg_blocks = blocked(seg_float, pieces)
    before = jnp.concatenate(
        [prior_seg[:, -1:].astype(jnp.float32), seg_blocks[:, :-1, -1]], axis=1
    )
    width_here = inner_full.shape[1]
    heads_here = step_full.shape[1]
    chan_start = tensor_rank * width_here
    head_start = tensor_rank * heads_here
    kernel_here = lax.dynamic_slice_in_dim(conv_inner, chan_start, width_here, 1)
    bias_here = lax.dynamic_slice_in_dim(inner_bias, chan_start, width_here, 0)
    gain_here = lax.dynamic_slice_in_dim(gated_gain, chan_start, width_here, 0)
    shift_here = lax.dynamic_slice_in_dim(step_bias, head_start, heads_here, 0)
    rates_here = lax.dynamic_slice_in_dim(log_rates, head_start, heads_here, 0)
    skip_here = lax.dynamic_slice_in_dim(skip_gain, head_start, heads_here, 0)

    def mixer_front(
        pad_inner, pad_state, raw_steps, kernel_w, kernel_b, state_w, state_b, step_shift, rate_logs
    ):
        inner = jax.nn.silu(causal_mix(pad_inner, seg_padded, kernel_w, kernel_b))
        inner = inner.reshape(inner.shape[0], inner.shape[1], -1, HEAD_DIM)
        both_maps = jax.nn.silu(causal_mix(pad_state, seg_padded, state_w, state_b))
        b_proj = both_maps[:, :, :STATE]
        c_proj = both_maps[:, :, STATE:]
        deltas = jax.nn.softplus(raw_steps + step_shift)
        log_decay = deltas * -jnp.exp(rate_logs)
        inflow, passing = block_sums(inner, deltas, log_decay, b_proj, seg_blocks, before)
        return (inner, deltas, log_decay, b_proj, c_proj, inflow, passing)

    def mixer_rear(inner, deltas, log_decay, b_proj, c_proj, inflow, passing, incoming, skips):
        running = jnp.cumsum(blocked(log_decay, pieces), axis=2)
        places = jnp.arange(running.shape[2])
        allowed = (seg_blocks[:, :, :, None] == seg_blocks[:, :, None, :]) & (
            places[:, None] >= places[None, :]
        )
        inside = allowed[..., None]
        decays = jnp.where(
            inside,
            jnp.exp(jnp.where(inside, running[:, :, :, None, :] - running[:, :, None, :, :], 0.0)),
            0.0,
        )
        scores = jnp.einsum(
            "scin,scjn->scij", blocked(c_proj, pieces), blocked(b_proj, pieces), precision=HIGH
        )
        mixing = decays * scores[..., None] * blocked(deltas, pieces)[:, :, None, :, :]
        direct = jnp.einsum("scijh,scjhp->scihp", mixing, blocked(inner, pieces), precision=HIGH)
        from_state, outgoing = state_reads(
            incoming, log_decay, c_proj, inflow, passing, seg_blocks, before
        )
        heads_out = (direct + from_state).reshape(inner.shape) + skips[:, None] * inner
        return (heads_out.reshape(inner.shape[0], inner.shape[1], -1), outgoing)

    front_args = (
        padded_inner,
        padded_state,
        step_raw,
        kernel_here,
        bias_here,
        conv_state,
        state_bias,
        shift_here,
        rates_here,
    )
    front_vals = mixer_front(*front_args)
    inner, deltas, log_decay, b_proj, c_proj, inflow, passing = front_vals
    span_decay = jnp.ones(passing[:, 0].shape, jnp.float32)
    span_state = jnp.zeros(inflow[:, 0].shape, jnp.float32)
    span_state = passing[:, 0, :, None, None] * span_state + inflow[:, 0]
    span_decay = span_decay * passing[:, 0]
    identity = (jnp.ones_like(span_decay), jnp.zeros_like(span_state))
    incoming = entering_2((span_decay, span_state), "seq", chain_link, identity)[1]
    mixed, outgoing = mixer_rear(*front_vals, incoming, skip_here)
    sigmoid_z = jax.nn.sigmoid(gate_in)
    silu_z = gate_in * sigmoid_z
    gated = mixed * silu_z
    full_width = tensor_count * gated.shape[-1]
    square_sum = lax.psum(jnp.sum(gated * gated, axis=-1), "tensor")
    rms_gate = lax.rsqrt(square_sum / full_width + EPS)[..., None]
    gate_normed = (gated * rms_gate * gain_here).astype(jnp.bfloat16)
    partial_out = jnp.dot(gate_normed, output_full, preferred_element_type=jnp.float32)
    branch_rows = lax.psum_scatter(partial_out, "tensor", scatter_dimension=1, tiled=True)
    block_out = (residual + branch_rows).astype(jnp.bfloat16)
    grad_output = jnp.einsum(
        "srk,srd->kd", gate_normed, cot_rows, preferred_element_type=jnp.float32
    )
    grad_gn = jnp.einsum("srd,kd->srk", cot_rows, output_full, preferred_element_type=jnp.float32)
    scaled = grad_gn * gain_here
    dot_sum = lax.psum(jnp.sum(scaled * gated, axis=-1), "tensor")
    grad_gain_here = jnp.sum(grad_gn * gated * rms_gate, axis=(0, 1))
    grad_gated = rms_gate * scaled - gated * rms_gate**3 * (dot_sum / full_width)[..., None]
    grad_mixed = grad_gated * silu_z
    grad_gate_in = (grad_gated * mixed * sigmoid_z * (1.0 + gate_in * (1.0 - sigmoid_z))).astype(
        jnp.bfloat16
    )
    front_vals, front_back = jax.vjp(mixer_front, *front_args)
    unused_rear, rear_back = jax.vjp(mixer_rear, *front_vals, incoming, skip_here)
    inner, deltas, log_decay, b_proj, c_proj, inflow, passing = front_vals
    grad_blocks = blocked(grad_mixed.reshape(inner.shape), pieces)
    unused_reads, read_back = jax.vjp(
        lambda memory_in: state_reads(
            memory_in, log_decay, c_proj, inflow, passing, seg_blocks, before
        )[0],
        incoming,
    )
    local_grad = read_back(grad_blocks)[0]
    outgoing_grad = carried_in((span_decay, local_grad), "seq", chain_link, identity)[1]
    rear_grads = rear_back((grad_mixed, outgoing_grad))
    grad_skip_here = rear_grads[8]
    (
        pad_grad_inner,
        pad_grad_state,
        grad_step_raw,
        grad_kernel_here,
        grad_bias_here,
        grad_conv_state,
        grad_state_bias,
        grad_shift_here,
        grad_rates_here,
    ) = front_back(tuple(rear_grads[:7]))
    from_next_inner, from_next_state = passed_along(
        (pad_grad_inner[:, :margin], pad_grad_state[:, :margin]), "seq", -1
    )
    grad_inner_pre = jnp.concatenate(
        [pad_grad_inner[:, margin:-margin], pad_grad_inner[:, -margin:] + from_next_inner], axis=1
    )
    grad_state_part = jnp.concatenate(
        [pad_grad_state[:, margin:-margin], pad_grad_state[:, -margin:] + from_next_state], axis=1
    )
    grad_state_pre = lax.psum(grad_state_part, "tensor").astype(jnp.bfloat16)
    grad_inner_low = grad_inner_pre.astype(jnp.bfloat16)
    grad_step_low = grad_step_raw.astype(jnp.bfloat16)
    grad_normed = jnp.einsum(
        "srk,dk->srd", grad_gate_in, gate_full, preferred_element_type=jnp.float32
    )
    grad_normed = grad_normed + jnp.einsum(
        "srk,dk->srd", grad_inner_low, inner_full, preferred_element_type=jnp.float32
    )
    grad_normed = grad_normed + jnp.einsum(
        "srk,dk->srd", grad_step_low, step_full, preferred_element_type=jnp.float32
    )
    grad_rows = lax.psum_scatter(grad_normed, "tensor", scatter_dimension=1, tiled=True)
    own_rows = tokens.shape[1]
    state_mine = lax.dynamic_slice_in_dim(grad_state_pre, tensor_rank * own_rows, own_rows, 1)
    grad_rows = grad_rows + jnp.einsum(
        "srk,dk->srd", state_mine, state_full, preferred_element_type=jnp.float32
    )
    grad_gate_w = jnp.einsum(
        "srd,srk->dk", normed, grad_gate_in, preferred_element_type=jnp.float32
    )
    grad_inner_w = jnp.einsum(
        "srd,srk->dk", normed, grad_inner_low, preferred_element_type=jnp.float32
    )
    grad_state_w = jnp.einsum(
        "srd,srk->dk", normed, grad_state_pre, preferred_element_type=jnp.float32
    )
    grad_step_w = jnp.einsum(
        "srd,srk->dk", normed, grad_step_low, preferred_element_type=jnp.float32
    )
    shard_gate, shard_inner, shard_state, shard_step, shard_output = (
        lax.psum_scatter(grad_gate_w, ("dp", "seq"), scatter_dimension=0, tiled=True),
        lax.psum_scatter(grad_inner_w, ("dp", "seq"), scatter_dimension=0, tiled=True),
        lax.psum_scatter(grad_state_w, ("dp", "seq"), scatter_dimension=0, tiled=True),
        lax.psum_scatter(grad_step_w, ("dp", "seq"), scatter_dimension=0, tiled=True),
        lax.psum_scatter(grad_output, ("dp", "seq"), scatter_dimension=1, tiled=True),
    )
    scaled_in = grad_rows * input_gain
    grad_input_gain = jnp.sum(grad_rows * residual * rms_in, axis=(0, 1))
    grad_tokens = (
        cotangent.astype(jnp.float32)
        + rms_in * scaled_in
        - residual * rms_in**3 * jnp.mean(scaled_in * residual, axis=-1, keepdims=True)
    )

    def placed(whole, piece_grad, start, axis_number):
        return lax.dynamic_update_slice_in_dim(
            jnp.zeros_like(whole), piece_grad, start, axis_number
        )

    smalls = lax.psum(
        (
            grad_input_gain,
            placed(conv_inner, grad_kernel_here, chan_start, 1),
            placed(inner_bias, grad_bias_here, chan_start, 0),
            grad_conv_state,
            grad_state_bias,
            placed(step_bias, grad_shift_here, head_start, 0),
            placed(log_rates, grad_rates_here, head_start, 0),
            placed(skip_gain, grad_skip_here, head_start, 0),
            placed(gated_gain, grad_gain_here, chan_start, 0),
        ),
        ("dp", "seq", "tensor"),
    )
    return (
        block_out,
        grad_tokens,
        smalls[0],
        shard_gate,
        shard_inner,
        shard_state,
        shard_step,
        smalls[1],
        smalls[2],
        smalls[3],
        smalls[4],
        smalls[5],
        smalls[6],
        smalls[7],
        smalls[8],
        shard_output,
    )


def per_device_fast(
    tokens,
    segments,
    input_gain,
    gate_proj,
    inner_proj,
    state_proj,
    step_proj,
    conv_inner,
    inner_bias,
    conv_state,
    state_bias,
    step_bias,
    log_rates,
    skip_gain,
    gated_gain,
    output_proj,
    cotangent,
):
    tensor_count = lax.axis_size("tensor")
    tensor_rank = lax.axis_index("tensor")
    heads = step_proj.shape[1]
    step_wide = jnp.pad(step_proj, ((0, 0), (0, 128 - heads)))
    gain_row = input_gain[None]
    normed, seg_old, s8, t8, i8 = gather_all(
        tensor_count, tokens, gain_row, segments, (state_proj, step_wide, inner_proj)
    )
    heads_param = jnp.pad(
        lax.dynamic_slice_in_dim(
            jnp.stack([step_bias, log_rates, skip_gain]), tensor_rank * heads, heads, 1
        ),
        ((0, 5), (0, LANES - heads)),
    )
    (
        y_part, u_inner, u_state, entry, incoming, gate_in, cot_rows, o8, g8,
        inner_low, state_low, prior_inner, prior_state, step_raw, rows,
    ) = mix_fwd(
        tensor_count, segments, seg_old, heads_param,
        conv_inner, inner_bias[None], conv_state, state_bias[None],
        cotangent, output_proj.T, gate_proj, normed, i8, s8, t8,
    )
    grad_mixed, grad_gate_in, outgoing_grad, partial_out, grad_output, grad_gate, grad_gain = gate_stage(
        tensor_count, y_part, u_state, entry, incoming, gate_in, cot_rows, o8, gated_gain[None], normed
    )
    (
        d_inner, d_state, d_step, sm_i, sm_s, sm_h, branch_rows, shard_output, shard_gate
    ) = mix_bwd(
        tensor_count, grad_mixed, u_inner, u_state, inner_low, prior_inner, state_low, prior_state,
        step_raw, rows, incoming, outgoing_grad, heads_param, conv_inner, conv_state,
        partial_out, grad_output, grad_gate,
    )
    grad_rows, shard_inner, shard_state, shard_step, sms = reduce_all(
        tensor_count, normed, grad_gate_in, d_inner, d_state, d_step, g8, i8, s8, t8, gain_row,
        sm_i, sm_s, sm_h, grad_gain,
    )
    outs = emit_all(
        tensor_count, heads, tokens, cotangent, gain_row, branch_rows, grad_rows,
        shard_gate, shard_inner, shard_state, shard_step, shard_output, sms,
    )
    flat = (2, 8, 10, 11, 12, 13, 14)
    return tuple(o[0] if i in flat else o for i, o in enumerate(outs))


def solution(mesh):
    fast = mesh.shape["dp"] == 4 and mesh.shape["seq"] == 2
    placed = (
        P("dp", ("seq", "tensor"), None),
        P("dp", "seq"),
        P(),
        P(("dp", "seq"), "tensor"),
        P(("dp", "seq"), "tensor"),
        P(("dp", "seq"), None),
        P(("dp", "seq"), "tensor"),
        P(),
        P(),
        P(),
        P(),
        P(),
        P(),
        P(),
        P(),
        P("tensor", ("dp", "seq")),
        P("dp", ("seq", "tensor"), None),
    )
    return jax.shard_map(
        per_device_fast if fast else per_device,
        mesh=mesh,
        in_specs=placed,
        out_specs=(
            P("dp", ("seq", "tensor"), None),
            P("dp", ("seq", "tensor"), None),
            P(),
            P(("dp", "seq"), "tensor"),
            P(("dp", "seq"), "tensor"),
            P(("dp", "seq"), None),
            P(("dp", "seq"), "tensor"),
            P(),
            P(),
            P(),
            P(),
            P(),
            P(),
            P(),
            P(),
            P("tensor", ("dp", "seq")),
        ),
        check_vma=False,
    )
```

```python
import functools

import jax
import jax.numpy as jnp
from jax import lax
from jax.experimental import pallas as pl
from jax.experimental.pallas import tpu as pltpu
from jax.sharding import PartitionSpec as P

HEAD_DIM = 64
STATE = 128
KERNEL = 4
BLOCK = 256


EPS = 1e-05
HIGH = lax.Precision.HIGHEST


def passed_along(block, axis, distance):
    devices = range(lax.axis_size(axis))
    route = [(i - distance, i) for i in devices if i - distance in devices]
    return lax.ppermute(block, axis, route)


def entering_2(shard, axis, join, neutral):
    place = lax.axis_index(axis)
    gathered = jax.tree.map(
        lambda a, kind: lax.all_gather(a.astype(kind), axis), shard, (jnp.bfloat16, jnp.bfloat16)
    )
    state = jax.tree.map(lambda a, e: jnp.zeros_like(a) + jnp.asarray(e, a.dtype), shard, neutral)

    def one(hop, state):
        return join(
            state,
            jax.tree.map(
                lambda a, own: lax.dynamic_index_in_dim(a, hop, 0, False).astype(own.dtype),
                gathered,
                shard,
            ),
        )

    return lax.fori_loop(0, place, one, state)


def carried_in(shard, axis, combine, identity):
    length, here = (lax.axis_size(axis), lax.axis_index(axis))
    everything = jax.tree.map(
        lambda part, kind: lax.all_gather(part.astype(kind), axis),
        shard,
        jax.tree.map(lambda a: jnp.bfloat16 if a.dtype == jnp.float32 else a.dtype, shard),
    )
    start = jax.tree.map(
        lambda part, zero: jnp.broadcast_to(jnp.asarray(zero, part.dtype), part.shape),
        shard,
        identity,
    )

    def hop(k, before):
        at = length - 1 - k
        reached = at > here
        new = combine(
            before, jax.tree.map(lambda part, own: part[at].astype(own.dtype), everything, shard)
        )
        return jax.tree.map(lambda a, b: jnp.where(reached, a, b), new, before)

    return lax.fori_loop(0, length, hop, start)


def chain_link(earlier, later):
    return (earlier[0] * later[0], later[0][:, :, None, None] * earlier[1] + later[1])


def causal_mix(padded, seg_padded, kernel_w, kernel_b):
    margin = KERNEL - 1
    length = padded.shape[1] - margin
    seg_now = seg_padded[:, margin:]
    result = kernel_b + kernel_w[0] * padded[:, margin:]
    for offset in range(1, KERNEL):
        moved = padded[:, margin - offset : margin - offset + length]
        same_doc = (seg_padded[:, margin - offset : margin - offset + length] == seg_now).astype(
            jnp.float32
        )
        result = result + kernel_w[offset] * moved * same_doc[:, :, None]
    return result


def blocked(values, pieces):
    return values.reshape((values.shape[0], pieces, values.shape[1] // pieces) + values.shape[2:])


def block_sums(inner, deltas, log_decay, b_proj, seg_blocks, before):
    pieces = seg_blocks.shape[1]
    running = jnp.cumsum(blocked(log_decay, pieces), axis=2)
    same_end = (seg_blocks == seg_blocks[:, :, -1:]).astype(jnp.float32)
    to_end = (
        jnp.exp(running[:, :, -1:, :] - running) * same_end[:, :, :, None] * blocked(deltas, pieces)
    )
    inflow = jnp.einsum(
        "scjhp,scjn->schpn",
        to_end[..., None] * blocked(inner, pieces),
        blocked(b_proj, pieces),
        precision=HIGH,
    )
    passing = (
        jnp.exp(running[:, :, -1, :])
        * (seg_blocks[:, :, -1] == before).astype(jnp.float32)[:, :, None]
    )
    return (inflow, passing)


def state_reads(incoming, log_decay, c_proj, inflow, passing, seg_blocks, before):
    pieces = seg_blocks.shape[1]
    running = jnp.cumsum(blocked(log_decay, pieces), axis=2)
    memory = incoming
    entering = [memory]
    memory = passing[:, 0, :, None, None] * memory + inflow[:, 0]
    stacked = jnp.stack(entering, axis=1)
    entry = jnp.exp(running) * (seg_blocks == before[:, :, None]).astype(jnp.float32)[..., None]
    from_state = (
        jnp.einsum("scin,schpn->scihp", blocked(c_proj, pieces), stacked, precision=HIGH)
        * entry[..., None]
    )
    return (from_state, memory)


MESH = pl.DeviceIdType.MESH
BF = jnp.bfloat16
F32 = jnp.float32


def _peers():
    dp, seq, t = lax.axis_index("dp"), lax.axis_index("seq"), lax.axis_index("tensor")
    x, y = lax.rem(dp, 2), lax.div(dp, 2)
    x_dp = dp + 1 - 2 * x
    y_dp = dp + 2 - 4 * y
    d_dp = 3 - dp
    return dp, seq, t, x_dp, y_dp, d_dp


def _dev(dp, seq, t):
    return {"dp": dp, "seq": seq, "tensor": t}


def _plane_barrier(n):
    dp, seq, t, x_dp, y_dp, d_dp = _peers()
    bar = pltpu.get_barrier_semaphore()
    for who in (_dev(dp, 1 - seq, t), _dev(x_dp, seq, t), _dev(y_dp, seq, t)):
        pl.semaphore_signal(bar, inc=1, device_id=who, device_id_type=MESH)

    for step in range(1, n):
        pl.semaphore_signal(
            bar, inc=1, device_id=_dev(dp, seq, lax.rem(t + step, n)), device_id_type=MESH
        )
    pl.semaphore_wait(bar, 3 + n - 1)


class _Line:
    def __init__(self, n, ref, rows, ssem, rsem, own=None):
        self.n, self.ref, self.rows, self.ssem, self.rsem = n, ref, rows, ssem, rsem
        self.own = own

    def block(self, o):
        return self.ref.at[:, pl.ds(pl.multiple_of(o * self.rows, self.rows), self.rows), :]

    def copy(self, o, direction, own=False):
        dp, seq, t = lax.axis_index("dp"), lax.axis_index("seq"), lax.axis_index("tensor")
        return pltpu.make_async_remote_copy(
            src_ref=self.own if own else self.block(o),
            dst_ref=self.block(o),
            send_sem=self.ssem.at[0 if direction > 0 else 1, o],
            recv_sem=self.rsem.at[o],
            device_id=_dev(dp, seq, t + direction),
            device_id_type=MESH,
        )

    def step(self, d):
        n, t = self.n, lax.axis_index("tensor")
        for way in (1, -1):
            o = t - way * d
            here = jnp.logical_and(o >= 0, o < n)
            nxt = jnp.logical_and(t + way >= 0, t + way < n)

            @pl.when(here)
            def _(o=o, way=way, nxt=nxt):
                if d > 0:
                    self.copy(o, way).wait_recv()

                @pl.when(nxt)
                def _():
                    self.copy(o, way, d == 0 and self.own is not None).start()

    def finish(self):
        n, t = self.n, lax.axis_index("tensor")
        for d in range(n):
            for way in (1, -1):
                o = t - way * d
                ok = jnp.logical_and(
                    jnp.logical_and(o >= 0, o < n),
                    jnp.logical_and(t + way >= 0, t + way < n),
                )

                @pl.when(ok)
                def _(o=o, way=way):
                    self.copy(o, way).wait_send()


class _Plane:
    def __init__(self, own, full, ssem, rsem, lsem):
        self.own, self.full, self.ssem, self.rsem, self.lsem = own, full, ssem, rsem, lsem

    def copy(self, src, block, who, s):
        return pltpu.make_async_remote_copy(
            src_ref=src,
            dst_ref=self.full.at[block],
            send_sem=self.ssem.at[s],
            recv_sem=self.rsem.at[s],
            device_id=who,
            device_id_type=MESH,
        )

    def begin(self):
        dp, seq, t, x_dp, y_dp, d_dp = _peers()
        me = dp * 2 + seq
        pltpu.make_async_copy(self.own, self.full.at[me], self.lsem).start()
        self.copy(self.own, me, _dev(x_dp, seq, t), 0).start()
        self.copy(self.own, me, _dev(y_dp, seq, t), 1).start()
        self.copy(self.own, me, _dev(dp, 1 - seq, t), 3).start()

    def forward(self):
        dp, seq, t, x_dp, y_dp, d_dp = _peers()
        bx, by = x_dp * 2 + seq, y_dp * 2 + seq
        self.copy(self.own, bx, _dev(x_dp, seq, t), 0).wait_recv()
        self.copy(self.own, by, _dev(y_dp, seq, t), 1).wait_recv()

        @pl.when(seq == 0)
        def _():
            self.copy(self.full.at[by], by, _dev(x_dp, seq, t), 2).start()

        @pl.when(seq == 1)
        def _():
            self.copy(self.full.at[bx], bx, _dev(y_dp, seq, t), 2).start()

        self.copy(self.full.at[bx], bx, _dev(dp, 1 - seq, t), 4).start()
        self.copy(self.full.at[by], by, _dev(dp, 1 - seq, t), 5).start()

    def share(self):
        dp, seq, t, x_dp, y_dp, d_dp = _peers()
        bd = d_dp * 2 + seq
        self.copy(self.own, bd, _dev(x_dp, seq, t), 2).wait_recv()
        self.copy(self.full.at[bd], bd, _dev(dp, 1 - seq, t), 6).start()

    def arrive(self):
        dp, seq, t, x_dp, y_dp, d_dp = _peers()
        me = dp * 2 + seq
        pltpu.make_async_copy(self.own, self.full.at[me], self.lsem).wait()
        for s in (3, 4, 5, 6):
            self.copy(self.own, me, _dev(dp, 1 - seq, t), s).wait_recv()

    def finish(self):
        dp, seq, t, x_dp, y_dp, d_dp = _peers()
        me = dp * 2 + seq
        for s in range(7):
            self.copy(self.own, me, _dev(dp, 1 - seq, t), s).wait_send()


def gather_kernel(n, tok_far, gain, seg, ws, wt_t, wi, normed, seg_old, fs, ft, fi,
                  tok, wt, zs, zr, ps, pr, ls, hs):
    dp, seq, t = lax.axis_index("dp"), lax.axis_index("seq"), lax.axis_index("tensor")
    rows = tok.shape[1]
    near = pltpu.make_async_copy(tok_far, tok, ls.at[3])
    near.start()
    v = wt_t[...].astype(F32)
    v = jnp.concatenate([v, jnp.zeros((LANES - v.shape[0], v.shape[1]), F32)], axis=0)
    v = jnp.concatenate([v, jnp.zeros((LANES, 256 - v.shape[1]), F32)], axis=1)
    wt[...] = v.T[: wt.shape[0], :].astype(BF)
    _plane_barrier(n)
    planes = [
        _Plane(own, full, ps.at[i], pr.at[i], ls.at[i])
        for i, (own, full) in enumerate(((ws, fs), (wt, ft), (wi, fi)))
    ]
    handed = pltpu.make_async_remote_copy(
        src_ref=seg, dst_ref=seg_old, send_sem=hs.at[0], recv_sem=hs.at[1],
        device_id=_dev(dp, 1 - seq, t), device_id_type=MESH,
    )

    @pl.when(seq == 0)
    def _():
        handed.start()
        seg_old[...] = jnp.zeros_like(seg_old)

    for p in planes:
        p.begin()
    near.wait()
    mine = pl.ds(pl.multiple_of(t * rows, rows), rows)
    lines = []
    for s in range(tok.shape[0]):
        v = tok[s].astype(F32)
        rms = lax.rsqrt(jnp.mean(v * v, axis=-1, keepdims=True) + EPS)
        normed[s, mine, :] = (v * rms * gain[...]).astype(BF)
        lines.append(_Line(n, normed.at[pl.ds(s, 1)], rows, zs.at[s], zr.at[s]))
        lines[s].step(0)
    for line in lines:
        line.step(1)
    for p in planes:
        p.forward()
    lines[0].step(2)
    for p in planes:
        p.share()
    for line in lines[1:]:
        line.step(2)
    for d in range(3, n):
        for line in lines:
            line.step(d)
    for p in planes:
        p.arrive()

    @pl.when(seq == 0)
    def _():
        handed.wait_send()

    @pl.when(seq == 1)
    def _():
        handed.wait_recv()

    for line in lines:
        line.finish()
    for p in planes:
        p.finish()


def gather_all(n, tokens, gain, seg, weights):
    seqs, rows, width = tokens.shape
    vm = pl.BlockSpec(memory_space=pltpu.VMEM)
    far = pl.BlockSpec(memory_space=pltpu.HBM)
    wide = (weights[1].shape[1], LANES)
    full = lambda *shape: jax.ShapeDtypeStruct((8,) + shape, BF)
    act = jax.ShapeDtypeStruct((seqs, n * rows, width), BF)
    return pl.pallas_call(
        functools.partial(gather_kernel, n),
        out_shape=(
            act, jax.ShapeDtypeStruct(seg.shape, seg.dtype),
            full(*weights[0].shape), full(*wide), full(*weights[2].shape),
        ),
        in_specs=[far, vm, vm, far, vm, far],
        out_specs=(vm,) * 5,
        scratch_shapes=[
            pltpu.VMEM(tokens.shape, tokens.dtype),
            pltpu.VMEM(wide, BF),
            pltpu.SemaphoreType.DMA((seqs, 2, n)),
            pltpu.SemaphoreType.DMA((seqs, n)),
            pltpu.SemaphoreType.DMA((3, 7)),
            pltpu.SemaphoreType.DMA((3, 7)),
            pltpu.SemaphoreType.DMA((4,)),
            pltpu.SemaphoreType.DMA((2,)),
        ],
        compiler_params=pltpu.CompilerParams(
            collective_id=0, has_side_effects=True, vmem_limit_bytes=16 << 20
        ),
        cost_estimate=pl.CostEstimate(flops=30 * 10**9, bytes_accessed=1 << 20, transcendentals=0),
        name="gather_all",
    )(tokens, gain, seg, *weights)


def _line_reduce(n, part, left, right, ssem, rsem):
    dp, seq, t = lax.axis_index("dp"), lax.axis_index("seq"), lax.axis_index("tensor")
    rows = left.shape[2]

    def copy(src, box, o, way):
        return pltpu.make_async_remote_copy(
            src_ref=src, dst_ref=box.at[o],
            send_sem=ssem.at[0 if way > 0 else 1, o], recv_sem=rsem.at[0 if way > 0 else 1, o],
            device_id=_dev(dp, seq, t + way), device_id_type=MESH,
        )

    def block(o):
        return part.at[:, pl.ds(pl.multiple_of(o * rows, rows), rows), :]

    def step(k):
        for way, box, place in ((1, left, t), (-1, right, n - 1 - t)):
            target = lambda j: n - 1 - j if way > 0 else j
            if k == 0:
                @pl.when(place == 0)
                def _():
                    for j in range(n - 1):
                        copy(block(target(j)), box, target(j), way).start()
            else:
                @pl.when(jnp.logical_and(place > 0, place <= k))
                def _():
                    o = target(k - place)
                    copy(block(o), box, o, way).wait_recv()
                    for s in range(part.shape[0]):
                        own = part[s, pl.ds(pl.multiple_of(o * rows, rows), rows), :].astype(F32)
                        box[o, s] = (box[o, s].astype(F32) + own).astype(BF)
                    copy(box.at[o], box, o, way).start()

    def final(out):
        mine = pl.ds(pl.multiple_of(t * rows, rows), rows)
        for s in range(part.shape[0]):
            out[s] = part[s, mine, :].astype(F32)

        @pl.when(t > 0)
        def _():
            copy(left.at[0], left, t, 1).wait_recv()
            for s in range(part.shape[0]):
                out[s] = out[s] + left[t, s].astype(F32)

        @pl.when(t < n - 1)
        def _():
            copy(left.at[0], right, t, -1).wait_recv()
            for s in range(part.shape[0]):
                out[s] = out[s] + right[t, s].astype(F32)

    def finish():
        for j in range(n - 1):
            for way, box, o in ((1, left, n - 1 - j), (-1, right, j)):
                sends = (t < o) if way > 0 else (t > o)

                @pl.when(sends)
                def _():
                    copy(box.at[o], box, o, way).wait_send()

    return step, final, finish


def _line_reduces(n, part, left, right, ssem, rsem):
    one = lambda s: pl.ds(s, 1)
    return [
        _line_reduce(
            n, part.at[one(s)], left.at[:, one(s)], right.at[:, one(s)], ssem.at[s], rsem.at[s]
        )
        for s in range(part.shape[0])
    ]


class _PlaneReduce:
    def __init__(self, part, pair, box, ssem, rsem):
        self.part, self.pair, self.box, self.ssem, self.rsem = part, pair, box, ssem, rsem

    def copy(self, src, dst, who, s):
        return pltpu.make_async_remote_copy(
            src_ref=src, dst_ref=dst, send_sem=self.ssem.at[s], recv_sem=self.rsem.at[s],
            device_id=who, device_id_type=MESH,
        )

    def begin(self):
        dp, seq, t, x_dp, y_dp, d_dp = _peers()
        for slot, chip in enumerate((d_dp, x_dp, y_dp, dp)):
            self.copy(self.part.at[chip * 2 + 1 - seq], self.pair.at[slot], _dev(dp, 1 - seq, t), slot).start()

    def _paired(self, slot, chip, also=None):
        dp, seq, t, x_dp, y_dp, d_dp = _peers()
        self.copy(self.pair.at[slot], self.pair.at[slot], _dev(dp, 1 - seq, t), slot).wait_recv()
        v = self.part[chip * 2 + seq].astype(F32) + self.pair[slot].astype(F32)
        self.pair[slot] = v.astype(BF)

    def send_far(self):
        dp, seq, t, x_dp, y_dp, d_dp = _peers()
        for slot, chip in enumerate((d_dp, x_dp, y_dp)):
            self._paired(slot, chip)
            if slot == 0:
                @pl.when(seq == 0)
                def _():
                    self.copy(self.pair.at[0], self.box.at[2], _dev(x_dp, seq, t), 4).start()

                @pl.when(seq == 1)
                def _():
                    self.copy(self.pair.at[0], self.box.at[2], _dev(y_dp, seq, t), 4).start()

        @pl.when(seq == 0)
        def _():
            self.copy(self.pair.at[1], self.box.at[0], _dev(x_dp, seq, t), 5).start()

        @pl.when(seq == 1)
        def _():
            self.copy(self.pair.at[2], self.box.at[1], _dev(y_dp, seq, t), 6).start()

    def send_near(self):
        dp, seq, t, x_dp, y_dp, d_dp = _peers()
        self.copy(self.pair.at[0], self.box.at[2], _dev(dp, seq, t), 4).wait_recv()

        @pl.when(seq == 0)
        def _():
            self.box[2] = (self.box[2].astype(F32) + self.pair[2].astype(F32)).astype(BF)
            self.copy(self.box.at[2], self.box.at[1], _dev(y_dp, seq, t), 6).start()

        @pl.when(seq == 1)
        def _():
            self.box[2] = (self.box[2].astype(F32) + self.pair[1].astype(F32)).astype(BF)
            self.copy(self.box.at[2], self.box.at[0], _dev(x_dp, seq, t), 5).start()

    def final(self, out):
        dp, seq, t, x_dp, y_dp, d_dp = _peers()
        self.copy(self.pair.at[3], self.pair.at[3], _dev(dp, seq, t), 3).wait_recv()
        self.copy(self.pair.at[0], self.box.at[0], _dev(dp, seq, t), 5).wait_recv()
        self.copy(self.pair.at[0], self.box.at[1], _dev(dp, seq, t), 6).wait_recv()
        out[...] = (
            self.part[dp * 2 + seq].astype(F32) + self.pair[3].astype(F32)
            + self.box[0].astype(F32) + self.box[1].astype(F32)
        )

    def finish(self):
        dp, seq, t, x_dp, y_dp, d_dp = _peers()
        for s in range(7):
            self.copy(self.pair.at[0], self.box.at[0], _dev(dp, 1 - seq, t), s).wait_send()


class _Smalls:
    def __init__(self, n, box, line, ssem, rsem):
        self.n, self.box, self.line, self.ssem, self.rsem = n, box, line, ssem, rsem

    def copy(self, j, who):
        return pltpu.make_async_remote_copy(
            src_ref=self.box.at[2 * j], dst_ref=self.box.at[2 * j + 1],
            send_sem=self.ssem.at[j], recv_sem=self.rsem.at[j],
            device_id=who, device_id_type=MESH,
        )

    def near(self, j):
        dp, seq, t, x_dp, y_dp, d_dp = _peers()
        return (_dev(dp, 1 - seq, t), _dev(x_dp, seq, t), _dev(y_dp, seq, t))[j]

    def begin(self, value):
        self.box[0] = value
        self.copy(0, self.near(0)).start()

    def step(self, j):
        self.copy(j, self.near(j)).wait_recv()
        total = self.box[2 * j] + self.box[2 * j + 1]
        if j < 2:
            self.box[2 * j + 2] = total
            self.copy(j + 1, self.near(j + 1)).start()
        else:
            t = lax.axis_index("tensor")
            self.line[t] = total
            for o in range(self.n):
                @pl.when(t != o)
                def _(o=o):
                    self.across(t, o).start()

    def across(self, src, who):
        dp, seq, t = lax.axis_index("dp"), lax.axis_index("seq"), lax.axis_index("tensor")
        return pltpu.make_async_remote_copy(
            src_ref=self.line.at[src], dst_ref=self.line.at[src],
            send_sem=self.ssem.at[3 + who], recv_sem=self.rsem.at[3 + src],
            device_id=_dev(dp, seq, who), device_id_type=MESH,
        )

    def final(self):
        t = lax.axis_index("tensor")
        for o in range(self.n):
            @pl.when(t != o)
            def _(o=o):
                self.across(o, o).wait_recv()

    def finish(self):
        t = lax.axis_index("tensor")
        for j in range(3):
            self.copy(j, self.near(j)).wait_send()
        for o in range(self.n):
            @pl.when(t != o)
            def _(o=o):
                self.across(t, o).wait_send()


class _LineSum:
    def __init__(self, n, part, box, out, ssem, rsem):
        self.n, self.part, self.box, self.out, self.ssem, self.rsem = n, part, box, out, ssem, rsem

    def copy(self, phase, src_block, dst_ref, who, origin):
        dp, seq = lax.axis_index("dp"), lax.axis_index("seq")
        return pltpu.make_async_remote_copy(
            src_ref=src_block, dst_ref=dst_ref,
            send_sem=self.ssem.at[phase, who], recv_sem=self.rsem.at[phase, origin],
            device_id=_dev(dp, seq, who), device_id_type=MESH,
        )

    def scatter(self):
        t = lax.axis_index("tensor")
        for o in range(self.n):
            @pl.when(t != o)
            def _(o=o):
                self.copy(0, self.part.at[o], self.box.at[t], o, t).start()

    def gather(self):
        t = lax.axis_index("tensor")
        total = self.part[t].astype(F32)
        for o in range(self.n):
            @pl.when(t != o)
            def _(o=o):
                self.copy(0, self.part.at[o], self.box.at[o], o, o).wait_recv()

            @pl.when(t == o)
            def _(o=o):
                self.box[o] = jnp.zeros(self.box.shape[1:], self.box.dtype)
        for o in range(self.n):
            total = total + self.box[o].astype(F32)
        self.out[t] = total.astype(self.out.dtype)
        for o in range(self.n):
            @pl.when(t != o)
            def _(o=o):
                self.copy(1, self.out.at[t], self.out.at[t], o, t).start()

    def arrive(self):
        t = lax.axis_index("tensor")
        for o in range(self.n):
            @pl.when(t != o)
            def _(o=o):
                self.copy(1, self.out.at[o], self.out.at[o], o, o).wait_recv()

    def finish(self):
        t = lax.axis_index("tensor")
        for o in range(self.n):
            @pl.when(t != o)
            def _(o=o):
                self.copy(0, self.part.at[o], self.box.at[o], o, o).wait_send()
                self.copy(1, self.part.at[o], self.box.at[o], o, o).wait_send()


LANES = 128


def _split(v, parts):
    out = []
    for _ in range(parts):
        b = v.astype(BF)
        out.append(b)
        v = v - b.astype(F32)
    return jnp.concatenate(out, axis=1)


def _dot(a, b, ca=1, cb=0):
    return lax.dot_general(a, b, (((ca,), (cb,)), ((), ())), preferred_element_type=F32)


def _iota(shape, axis):
    return lax.broadcasted_iota(jnp.int32, shape, axis)


def _spreader(rows, p):
    head = lax.rem(_iota((rows, LANES), 0), LANES)
    return (head == 2 * p + lax.div(_iota((rows, LANES), 1), HEAD_DIM)).astype(F32).astype(BF)


def _folder(rows, p):
    chan = lax.rem(_iota((rows, LANES), 0), LANES)
    return (_iota((rows, LANES), 1) == 2 * p + lax.div(chan, HEAD_DIM)).astype(F32).astype(BF)


def _sig(v):
    return 1.0 / (1.0 + jnp.exp(-v))


def _three(v):
    return v[:, :LANES] + v[:, LANES : 2 * LANES] + v[:, 2 * LANES :]


def _head_scalars(raw, hp, marks, length):
    v = raw + hp[0:1, :]
    delta = jnp.maximum(v, 0.0) + jnp.log1p(jnp.exp(-jnp.abs(v)))
    log_decay = -delta * jnp.exp(hp[1:2, :])
    lower = (_iota((length, length), 0) >= _iota((length, length), 1)).astype(F32).astype(BF)
    running = _three(_dot(lower, _split(log_decay, 3)))
    entry = jnp.exp(running) * marks[:, 4:5]
    to_end = jnp.exp(running[length - 1 :, :] - running) * marks[:, 5:6]
    return v, delta, log_decay, running, entry, to_end


def _marks(rows):
    full = jnp.concatenate([rows, jnp.zeros((LANES - rows.shape[0], rows.shape[1]), F32)], axis=0)
    return full.T


def _bias_matrix(rows, marks, length):
    ok = (_iota((length, length), 0) >= _iota((length, length), 1)) & (
        marks[:, 0:1] == rows[0:1, :]
    )
    return jnp.where(ok, 0.0, -1e30)


def _conv(pad, marks, taps, bias, length):
    total = bias + taps[0:1, :] * pad[8 : 8 + length, :]
    for k in range(1, KERNEL):
        total = total + taps[k : k + 1, :] * (pad[8 - k : 8 - k + length, :] * marks[:, k : k + 1])
    return total


def mix_fwd_kernel(n, seg, seg_old, hp, taps_i, bias_i, taps_s, bias_s, cot, wo, wg, normed, wi, ws, wt,
                   y, u_i, u_s, entry_o, incoming, gate, cot_full, fo, fg,
                   pre_i, pre_s, old_i, old_s, raw, rows,
                   pad, run3, run_t, bias_m, scores, heads_hl, inflow, zs, zr, ps, pr, ls, hs):
    dp, seq, t = lax.axis_index("dp"), lax.axis_index("seq"), lax.axis_index("tensor")
    seqs, length, width = pre_i.shape
    model = normed.shape[2]
    pairs = width // LANES
    wide = 2 * LANES
    _plane_barrier(n)
    lines = [
        _Line(n, cot_full.at[pl.ds(s, 1)], cot.shape[1], zs.at[s], zr.at[s], cot.at[pl.ds(s, 1)])
        for s in range(seqs)
    ]
    planes = (_Plane(wg, fg, ps.at[0], pr.at[0], ls.at[0]), _Plane(wo, fo, ps.at[1], pr.at[1], ls.at[1]))
    whole = _Line(n, cot_full, cot.shape[1], zs, zr)
    own = pltpu.make_async_copy(cot, whole.block(t), ls.at[2])
    own.start()
    for line in lines:
        line.step(0)
    for plane in planes:
        plane.begin()
    flat = normed[...].reshape(seqs * length, model)
    pre_s[...] = _dot(flat, ws[...].reshape(model, ws.shape[2])).astype(BF).reshape(pre_s.shape)

    def inner_part(c, _):
        ch = pl.ds(pl.multiple_of(c * wide, wide), wide)
        part = _dot(flat, wi[:, :, ch].reshape(model, wide))
        pre_i[:, :, ch] = part.astype(BF).reshape(seqs, length, wide)
        return 0

    lax.fori_loop(0, width // wide, inner_part, 0)
    ends = [
        pltpu.make_async_remote_copy(
            src_ref=a.at[:, pl.ds(length - 16, 16), :], dst_ref=b,
            send_sem=hs.at[2 + i], recv_sem=hs.at[4 + i],
            device_id=_dev(dp, 1 - seq, t), device_id_type=MESH,
        )
        for i, (a, b) in enumerate(((pre_i, old_i), (pre_s, old_s)))
    ]

    @pl.when(seq == 0)
    def _():
        for c in ends:
            c.start()
        old_i[...] = jnp.zeros_like(old_i)
        old_s[...] = jnp.zeros_like(old_s)

    raw[...] = _dot(flat, wt[...].reshape(model, LANES)).reshape(raw.shape)
    for s in range(seqs):
        now = seg[s : s + 1, :].astype(F32)
        old = seg_old[s : s + 1, :].astype(F32)
        both = jnp.broadcast_to(jnp.concatenate([old, now], axis=1), (8, 2 * length))
        here = jnp.broadcast_to(now, (8, length))
        place = _iota((8, length), 0)
        block = jnp.where(place == 0, here, 0.0)
        others = [pltpu.roll(both, k, 1)[:, length:] for k in range(1, KERNEL)]
        others += [both[:, length - 1 : length], both[:, 2 * length - 1 :]]
        for k, other in enumerate(others):
            block = jnp.where((place == k + 1) & (here == other), 1.0, block)
        rows[s] = block

    lines[0].step(1)

    @pl.when(seq == 1)
    def _():
        for c in ends:
            c.wait_recv()

    def one(s, _):
        rw = rows[s]
        marks = _marks(rw)
        v, delta, log_decay, running, entry, to_end = _head_scalars(raw[s], hp, marks, length)
        entry_o[s] = entry
        run3[...] = _split(running, 3)
        run_t[...] = running.T
        bias_m[...] = _bias_matrix(rw, marks, length)
        heads_hl[0] = _split(delta, 2)
        heads_hl[1] = _split(to_end, 2)
        maps = []
        for half in range(2):
            ch = slice(half * STATE, (half + 1) * STATE)
            pad[0:8, :] = old_s[s, :, ch].astype(F32)[8:16, :]
            pad[8:, :] = pre_s[s, :, ch].astype(F32)
            u = _conv(pad, marks, taps_s[:, ch], bias_s[:, ch], length)
            u_s[s, :, ch] = u
            maps.append((u * _sig(u)).astype(BF))
        b_map, c_map = maps
        scores[...] = _dot(c_map, b_map, 1, 1)

        def pair(p, _):
            @pl.when(jnp.logical_and(s == 0, p == 4))
            def _():
                lines[1].step(1)

            @pl.when(jnp.logical_and(s == 1, p == 0))
            def _():
                for plane in planes:
                    plane.forward()

            @pl.when(jnp.logical_and(s == 1, p == 1))
            def _():
                lines[0].step(2)

            @pl.when(jnp.logical_and(s == 1, p == 5))
            def _():
                lines[1].step(2)
                planes[0].share()

            ch = pl.ds(pl.multiple_of(p * LANES, LANES), LANES)
            at = pl.ds(pl.multiple_of(t * width + p * LANES, LANES), LANES)
            pad[0:8, :] = old_i[s, :, ch].astype(F32)[8:16, :]
            pad[8:, :] = pre_i[s, :, ch].astype(F32)
            u = _conv(pad, marks, taps_i[:, at], bias_i[:, at], length)
            u_i[s, :, ch] = u
            x = u * _sig(u)
            spread = _spreader(2 * LANES, p)
            xd = x * _dot(heads_hl[0], spread)
            inflow[s, :, ch] = _dot(b_map, (xd * _dot(heads_hl[1], spread)).astype(BF), 0, 0).astype(BF)
            skip = _dot(_split(hp[...], 2), spread)[2:3, :]
            total = skip * x
            xb = xd.astype(BF)
            lane = lax.div(_iota(xb.shape, 1), HEAD_DIM)
            for a in range(2):
                h = 2 * p + a
                pick = (lax.rem(_iota((3 * LANES, length), 0), LANES) == h).astype(F32).astype(BF)
                decay = jnp.exp(_dot(run3[...], pick) - run_t[pl.ds(h, 1), :] + bias_m[...])
                mixing = (decay * scores[...]).astype(BF)
                total = total + _dot(mixing, jnp.where(lane == a, xb, jnp.zeros_like(xb)))
            y[s, :, ch] = total
            return 0

        lax.fori_loop(0, pairs, pair, 0)
        return 0

    lax.fori_loop(0, seqs, one, 0)
    handed = pltpu.make_async_remote_copy(
        src_ref=inflow, dst_ref=incoming, send_sem=hs.at[0], recv_sem=hs.at[1],
        device_id=_dev(dp, 1 - seq, t), device_id_type=MESH,
    )

    @pl.when(seq == 0)
    def _():
        handed.start()
        incoming[...] = jnp.zeros_like(incoming)

    planes[1].share()
    for d in range(3, n):
        lines[0].step(d)
    planes[0].arrive()

    def gate_part(c, _):
        ch = pl.ds(pl.multiple_of(c * wide, wide), wide)
        part = _dot(flat, fg[:, :, ch].reshape(model, wide))
        gate[:, :, ch] = part.reshape(seqs, length, wide)
        return 0

    lax.fori_loop(0, width // wide, gate_part, 0)
    for d in range(3, n):
        lines[1].step(d)
    planes[1].arrive()
    own.wait()

    @pl.when(seq == 0)
    def _():
        handed.wait_send()
        for c in ends:
            c.wait_send()

    @pl.when(seq == 1)
    def _():
        handed.wait_recv()

    for line in lines:
        line.finish()
    for plane in planes:
        plane.finish()


def _mixer_call(kernel, ins, outs, scratch, name, cost, number, far=()):
    vm = pl.BlockSpec(memory_space=pltpu.VMEM)
    return pl.pallas_call(
        kernel,
        out_shape=outs,
        in_specs=[
            pl.BlockSpec(memory_space=pltpu.HBM if i in far else pltpu.VMEM) for i in range(len(ins))
        ],
        out_specs=(vm,) * len(outs),
        scratch_shapes=scratch,
        compiler_params=pltpu.CompilerParams(
            collective_id=number, has_side_effects=True, vmem_limit_bytes=28 << 20
        ),
        cost_estimate=pl.CostEstimate(flops=cost, bytes_accessed=1 << 20, transcendentals=0),
        name=name,
    )(*ins)


def mix_fwd(n, seg, seg_old, hp, taps_i, bias_i, taps_s, bias_s, cot, wo, wg, normed, wi, ws, wt):
    seqs, length, model = normed.shape
    width = wi.shape[2]
    sd = jax.ShapeDtypeStruct
    return _mixer_call(
        functools.partial(mix_fwd_kernel, n),
        (seg, seg_old, hp, taps_i, bias_i, taps_s, bias_s, cot, wo, wg, normed, wi, ws, wt),
        (
            sd((seqs, length, width), F32),
            sd((seqs, length, width), F32),
            sd((seqs, length, 2 * STATE), F32),
            sd((seqs, length, LANES), F32),
            sd((seqs, STATE, width), BF),
            sd((seqs, length, width), F32),
            sd((seqs, length, model), BF),
            sd((8,) + wo.shape, BF),
            sd((8,) + wg.shape, BF),
            sd((seqs, length, width), BF),
            sd((seqs, length, 2 * STATE), BF),
            sd((seqs, 16, width), BF),
            sd((seqs, 16, 2 * STATE), BF),
            sd((seqs, length, LANES), F32),
            sd((seqs, 8, length), F32),
        ),
        [
            pltpu.VMEM((8 + length, LANES), F32),
            pltpu.VMEM((length, 3 * LANES), BF),
            pltpu.VMEM((LANES, length), F32),
            pltpu.VMEM((length, length), F32),
            pltpu.VMEM((length, length), F32),
            pltpu.VMEM((2, length, 2 * LANES), BF),
            pltpu.VMEM((seqs, STATE, width), BF),
            pltpu.SemaphoreType.DMA((seqs, 2, n)),
            pltpu.SemaphoreType.DMA((seqs, n)),
            pltpu.SemaphoreType.DMA((2, 7)),
            pltpu.SemaphoreType.DMA((2, 7)),
            pltpu.SemaphoreType.DMA((3,)),
            pltpu.SemaphoreType.DMA((6,)),
        ],
        "mix_fwd",
        30 * 10**9,
        3,
        (7, 8, 9),
    )


def gate_kernel(n, y_part, u_s, entry, h0, gate, cot, wo, gain, tokens_in,
                d_mixed, d_gate, lam, po, go, gg, g_gain,
                mixed, gated, grad_gn, normed, local, acc, box, ss, rs, hs):
    dp, seq, t = lax.axis_index("dp"), lax.axis_index("seq"), lax.axis_index("tensor")
    seqs, length, width = y_part.shape
    model = cot.shape[2]
    wide = 2 * LANES
    bar = pltpu.get_barrier_semaphore()
    pl.semaphore_signal(bar, inc=1, device_id=_dev(dp, 1 - seq, t), device_id_type=MESH)
    for step in range(1, n):
        pl.semaphore_signal(
            bar, inc=1, device_id=_dev(dp, seq, lax.rem(t + step, n)), device_id_type=MESH
        )
    acc[...] = jnp.zeros_like(acc)
    g_gain[...] = jnp.zeros_like(g_gain)

    def spread_of(s, c):
        heads = _split(entry[s], 2)
        head = lax.rem(_iota((wide, wide), 0), LANES)
        one = head == 4 * c + lax.div(_iota((wide, wide), 1), HEAD_DIM)
        return _dot(heads, one.astype(F32).astype(BF))

    def maps(s):
        u = u_s[s, :, STATE:]
        return (u * _sig(u)).astype(BF)

    def first(c, _):
        ch = pl.ds(pl.multiple_of(c * wide, wide), wide)
        at = pl.ds(pl.multiple_of(t * width + c * wide, wide), wide)
        w = wo[:, :, ch].reshape(model, wide)
        for s in range(seqs):
            g = _dot(cot[s], w)
            grad_gn[s, :, ch] = g
            m = y_part[s, :, ch] + spread_of(s, c) * _dot(maps(s), h0[s, :, ch])
            z = gate[s, :, ch]
            gd = m * (z * _sig(z))
            mixed[s, :, ch] = m
            gated[s, :, ch] = gd
            sq, ds = gd * gd, g * gain[:, at] * gd
            acc[0, s] += sq[:, :LANES] + sq[:, LANES:]
            acc[1, s] += ds[:, :LANES] + ds[:, LANES:]
        return 0

    lax.fori_loop(0, width // wide, first, 0)
    ones = jnp.ones((8, wide), F32).astype(BF)
    row = _iota((8, length), 0)
    mine = jnp.zeros((8, length), F32)
    for kind in range(2):
        for s in range(seqs):
            sums = _dot(ones, _split(acc[kind, s], 2), 1, 1)
            mine = jnp.where(row == kind * seqs + s, sums, mine)
    box[t] = mine
    pl.semaphore_wait(bar, n)

    def copy(src, who):
        return pltpu.make_async_remote_copy(
            src_ref=box.at[src], dst_ref=box.at[src], send_sem=ss.at[who], recv_sem=rs.at[src],
            device_id=_dev(dp, seq, who), device_id_type=MESH,
        )

    for o in range(n):
        @pl.when(t != o)
        def _(o=o):
            copy(t, o).start()
    for o in range(n):
        @pl.when(t != o)
        def _(o=o):
            copy(o, o).wait_recv()
    full_width = n * width
    cols = _marks(jnp.sum(box[...], axis=0) / full_width)

    def second(c, _):
        ch = pl.ds(pl.multiple_of(c * wide, wide), wide)
        at = pl.ds(pl.multiple_of(t * width + c * wide, wide), wide)
        gn = gain[:, at]
        for s in range(seqs):
            rms = lax.rsqrt(cols[:, s : s + 1] + EPS)
            mean = cols[:, seqs + s : seqs + s + 1]
            g, gd, m, z = grad_gn[s, :, ch], gated[s, :, ch], mixed[s, :, ch], gate[s, :, ch]
            sg = _sig(z)
            scaled = gd * rms
            normed[s, :, ch] = (scaled * gn).astype(BF)
            g_gain[0:1, ch] += jnp.sum(g * scaled, axis=0, keepdims=True)
            d_gd = rms * (g * gn) - scaled * (rms * rms * mean)
            dm = d_gd * (z * sg)
            d_mixed[s, :, ch] = dm
            d_gate[s, :, ch] = (d_gd * m * sg * (1.0 + z * (1.0 - sg))).astype(BF)
            ed = (spread_of(s, c) * dm).astype(BF)
            local[s, :, ch] = _dot(maps(s), ed, 0, 0).astype(BF)
        return 0

    lax.fori_loop(0, width // wide, second, 0)
    handed = pltpu.make_async_remote_copy(
        src_ref=local, dst_ref=lam, send_sem=hs.at[0], recv_sem=hs.at[1],
        device_id=_dev(dp, 1 - seq, t), device_id_type=MESH,
    )

    @pl.when(seq == 1)
    def _():
        handed.start()
        lam[...] = jnp.zeros_like(lam)

    blocks = 2
    rows = blocks * wo.shape[1]

    def third(b, _):
        ch = pl.ds(pl.multiple_of(b * rows, LANES), rows)
        w = wo[pl.ds(b * blocks, blocks)].reshape(rows, width)
        total = None
        for s in range(seqs):
            po[s, :, ch] = _dot(normed[s], w, 1, 1).astype(BF)
            part = _dot(cot[s, :, ch], normed[s], 0, 0)
            total = part if total is None else total + part
        go[pl.ds(b * blocks, blocks)] = total.reshape(blocks, wo.shape[1], width).astype(BF)
        total = None
        for s in range(seqs):
            part = _dot(tokens_in[s, :, ch], d_gate[s], 0, 0)
            total = part if total is None else total + part
        gg[pl.ds(b * blocks, blocks)] = total.reshape(blocks, wo.shape[1], width).astype(BF)
        return 0

    lax.fori_loop(0, model // rows, third, 0)

    @pl.when(seq == 1)
    def _():
        handed.wait_send()

    @pl.when(seq == 0)
    def _():
        handed.wait_recv()

    for o in range(n):
        @pl.when(t != o)
        def _(o=o):
            copy(o, o).wait_send()


def gate_stage(n, y_part, u_s, entry, h0, gate, cot, wo, gain, tokens_in):
    seqs, length, width = y_part.shape
    sd = jax.ShapeDtypeStruct
    whole = pltpu.VMEM((seqs, length, width), F32)
    return _mixer_call(
        functools.partial(gate_kernel, n),
        (y_part, u_s, entry, h0, gate, cot, wo, gain, tokens_in),
        (
            sd((seqs, length, width), F32),
            sd((seqs, length, width), BF),
            sd((seqs, STATE, width), BF),
            sd((seqs, length, cot.shape[2]), BF),
            sd(wo.shape, BF),
            sd(wo.shape, BF),
            sd((8, width), F32),
        ),
        [
            whole, whole, whole,
            pltpu.VMEM((seqs, length, width), BF),
            pltpu.VMEM((seqs, STATE, width), BF),
            pltpu.VMEM((2, seqs, length, LANES), F32),
            pltpu.VMEM((n, 8, length), F32),
            pltpu.SemaphoreType.DMA((n,)),
            pltpu.SemaphoreType.DMA((n,)),
            pltpu.SemaphoreType.DMA((2,)),
        ],
        "gate_stage",
        6 * 10**9,
        2,
    )


def mix_bwd_kernel(n, dy_r, u_i, u_s, pre_i, old_i, pre_s, old_s, raw, rows, h0, lam, hp,
                   taps_i, taps_s, po, go, gg,
                   d_i, d_s, d_raw, sm_i, sm_s, sm_h, o_po, o_go, o_gg,
                   pad, moved, run3, run_t, bias_m, scores, d_scores, heads_hl,
                   acc_r, acc_c, acc_d, acc_q, d_b, d_c, lo, ro, xo, bo, xg, bg,
                   head_i, tail_i, head_s, tail_s, next_i, next_s, zs, zr, ps, pr, hs):
    t = lax.axis_index("tensor")
    seqs, length, width = pre_i.shape
    pairs = width // LANES
    _plane_barrier(n)
    lines = _line_reduces(n, po, lo, ro, zs, zr)
    planes = (
        _PlaneReduce(go, xo, bo, ps.at[0], pr.at[0]), _PlaneReduce(gg, xg, bg, ps.at[1], pr.at[1])
    )
    for step, _, _ in lines:
        step(0)
    for plane in planes:
        plane.begin()
    sm_i[...] = jnp.zeros_like(sm_i)
    sm_s[...] = jnp.zeros_like(sm_s)
    sm_h[...] = jnp.zeros_like(sm_h)
    moved[0:8, :] = jnp.zeros((8, LANES), F32)
    moved[8 + length :, :] = jnp.zeros((8, LANES), F32)

    def conv_back(du, marks, taps, s, ch, d_o, head_o, tail_o, sm):
        total = None
        for k in range(KERNEL):
            m = du if k == 0 else du * marks[:, k : k + 1]
            moved[8 : 8 + length, :] = m
            sm[k : k + 1, ch] += jnp.sum(m * pad[8 - k : 8 - k + length, :], axis=0, keepdims=True)
            part = taps[k : k + 1, :] * moved[k : k + 8 + length, :]
            total = part if total is None else total + part
        sm[4:5, ch] += jnp.sum(du, axis=0, keepdims=True)
        head_o[s, :, ch] = total[0:8, :]
        d_o[s, :, ch] = total[8:, :].astype(BF)
        tail_o[s, :, ch] = total[length - 8 :, :]

    def one(s, _):
        rw = rows[s]
        marks = _marks(rw)
        v, delta, log_decay, running, entry, to_end = _head_scalars(raw[s], hp, marks, length)
        run3[...] = _split(running, 3)
        run_t[...] = running.T
        bias_m[...] = _bias_matrix(rw, marks, length)
        heads_hl[0] = _split(delta, 2)
        heads_hl[1] = _split(to_end, 2)
        heads_hl[2] = _split(entry, 2)
        ub, uc = u_s[s, :, :STATE], u_s[s, :, STATE:]
        sb, sc = _sig(ub), _sig(uc)
        b_map, c_map = (ub * sb).astype(BF), (uc * sc).astype(BF)
        scores[...] = _dot(c_map, b_map, 1, 1)
        d_scores[...] = jnp.zeros_like(d_scores)
        for acc in (acc_r, acc_c, acc_d, acc_q, d_b, d_c):
            acc[...] = jnp.zeros_like(acc)

        def pair(p, _):
            @pl.when(jnp.logical_and(s == 0, p == 3))
            def _():
                lines[0][0](1)

            @pl.when(jnp.logical_and(s == 0, p == 4))
            def _():
                for plane in planes:
                    plane.send_far()

            @pl.when(jnp.logical_and(s == 1, p == 0))
            def _():
                lines[0][0](2)

            @pl.when(jnp.logical_and(s == 1, p == 3))
            def _():
                for plane in planes:
                    plane.send_near()

            @pl.when(jnp.logical_and(s == 1, p == 4))
            def _():
                lines[1][0](1)

            ch = pl.ds(pl.multiple_of(p * LANES, LANES), LANES)
            at = pl.ds(pl.multiple_of(t * width + p * LANES, LANES), LANES)
            u = u_i[s, :, ch]
            sg = _sig(u)
            x = u * sg
            dy = dy_r[s, :, ch]
            spread, fold = _spreader(2 * LANES, p), _folder(2 * LANES, p)
            dl = _dot(heads_hl[0], spread)
            q = _dot(heads_hl[1], spread)
            e = _dot(heads_hl[2], spread)
            xd = x * dl
            xb, db = xd.astype(BF), dy.astype(BF)
            h_in, l_in = h0[s, :, ch], lam[s, :, ch]
            c_h = _dot(c_map, h_in)
            b_l = _dot(b_map, l_in)
            qx, ed = q * xd, e * dy
            d_b[...] += _dot(qx.astype(BF), l_in, 1, 1)
            d_c[...] += _dot(ed.astype(BF), h_in, 1, 1)
            late = qx * b_l
            dxd = q * b_l
            lane = lax.div(_iota(xb.shape, 1), HEAD_DIM)
            for a in range(2):
                h = 2 * p + a
                pick = (lax.rem(_iota((3 * LANES, length), 0), LANES) == h).astype(F32).astype(BF)
                decay = jnp.exp(_dot(run3[...], pick) - run_t[pl.ds(h, 1), :] + bias_m[...])
                da = jnp.where(lane == a, db, jnp.zeros_like(db))
                ld = decay * _dot(da, xb, 1, 1)
                d_scores[...] += ld
                both = (ld * scores[...]).astype(BF)
                mixing = (decay * scores[...]).astype(BF)
                dxd = dxd + _dot(mixing, da, 0, 0)
                col = (_iota((length, LANES), 1) == h).astype(F32).astype(BF)
                row = (_iota((LANES, length), 0) == h).astype(F32).astype(BF)
                acc_r[...] += _dot(both, col)
                acc_c[...] += _dot(row, both)
            acc_r[...] += _dot(_split(ed * c_h - late, 2), fold)
            acc_d[...] += _dot(_split(dxd * x, 2), fold)
            total = jnp.broadcast_to(jnp.sum(late, axis=0, keepdims=True), (8, LANES))
            acc_q[...] += _dot(_split(total, 2), fold)
            skip = _dot(_split(hp[...], 2), spread)[2:3, :]
            sm_i[5:6, ch] += jnp.sum(dy * x, axis=0, keepdims=True)
            du = (dxd * dl + skip * dy) * (sg * (1.0 + u * (1.0 - sg)))
            pad[0:8, :] = old_i[s, :, ch].astype(F32)[8:16, :]
            pad[8:, :] = pre_i[s, :, ch].astype(F32)
            conv_back(du, marks, taps_i[:, at], s, ch, d_i, head_i, tail_i, sm_i)
            return 0

        lax.fori_loop(0, pairs, pair, 0)
        ds = d_scores[...].astype(BF)
        grads = (d_b[...] + _dot(ds, c_map, 0, 0), d_c[...] + _dot(ds, b_map))
        for half, (g, u, sg) in enumerate(zip(grads, (ub, uc), (sb, sc))):
            ch = slice(half * STATE, (half + 1) * STATE)
            pad[0:8, :] = old_s[s, :, ch].astype(F32)[8:16, :]
            pad[8:, :] = pre_s[s, :, ch].astype(F32)
            du = g * (sg * (1.0 + u * (1.0 - sg)))
            conv_back(du, marks, taps_s[:, ch], s, ch, d_s, head_s, tail_s, sm_s)
        d_run = acc_r[...] - acc_c[...].T
        last = _iota(d_run.shape, 0) == length - 1
        d_run = d_run + jnp.where(last, acc_q[0:1, :], 0.0)
        upper = (_iota((length, length), 0) <= _iota((length, length), 1)).astype(F32).astype(BF)
        d_log = _three(_dot(upper, _split(d_run, 3)))
        d_delta = acc_d[...] - d_log * jnp.exp(hp[1:2, :])
        d_step = d_delta * _sig(v)
        d_raw[s] = d_step.astype(BF)
        sm_h[0:1, :] += jnp.sum(d_step, axis=0, keepdims=True)
        sm_h[1:2, :] += jnp.sum(d_log * log_decay, axis=0, keepdims=True)
        return 0

    lax.fori_loop(0, seqs, one, 0)
    lines[1][0](2)
    dp, seq = lax.axis_index("dp"), lax.axis_index("seq")
    handed = [
        pltpu.make_async_remote_copy(
            src_ref=a, dst_ref=b, send_sem=hs.at[2 * i], recv_sem=hs.at[2 * i + 1],
            device_id=_dev(dp, 1 - seq, t), device_id_type=MESH,
        )
        for i, (a, b) in enumerate(((head_i, next_i), (head_s, next_s)))
    ]

    @pl.when(seq == 1)
    def _():
        for c in handed:
            c.start()

    planes[0].final(o_go)

    @pl.when(seq == 0)
    def _():
        for c, box, tail, out in zip(handed, (next_i, next_s), (tail_i, tail_s), (d_i, d_s)):
            c.wait_recv()
            for s in range(seqs):
                more = jnp.concatenate([jnp.zeros_like(box[s]), box[s]], axis=0)
                out[s, length - 16 :, :] = (tail[s] + more).astype(BF)

    @pl.when(seq == 1)
    def _():
        for c in handed:
            c.wait_send()

    planes[1].final(o_gg)
    for s, (_, final, _) in enumerate(lines):
        final(o_po.at[pl.ds(s, 1)])
    for plane in planes:
        plane.finish()
    for _, _, finish in lines:
        finish()


def mix_bwd(n, dy, u_i, u_s, pre_i, old_i, pre_s, old_s, raw, rows, h0, lam, hp, taps_i, taps_s,
            po, go, gg):
    seqs, length, width = pre_i.shape
    model = po.shape[2]
    box = pltpu.VMEM((n, seqs, length // n, model), BF)
    sd = jax.ShapeDtypeStruct
    square = pltpu.VMEM((length, length), F32)
    tall = pltpu.VMEM((length, LANES), F32)
    return _mixer_call(
        functools.partial(mix_bwd_kernel, n),
        (dy, u_i, u_s, pre_i, old_i, pre_s, old_s, raw, rows, h0, lam, hp, taps_i, taps_s, po, go,
         gg),
        (
            sd((seqs, length, width), BF),
            sd((seqs, length, 2 * STATE), BF),
            sd((seqs, length, LANES), BF),
            sd((8, width), F32),
            sd((8, 2 * STATE), F32),
            sd((8, LANES), F32),
            sd((seqs, length // n, model), F32),
            sd(go.shape[1:], F32),
            sd(gg.shape[1:], F32),
        ),
        [
            pltpu.VMEM((8 + length, LANES), F32),
            pltpu.VMEM((16 + length, LANES), F32),
            pltpu.VMEM((length, 3 * LANES), BF),
            pltpu.VMEM((LANES, length), F32),
            square, square, square,
            pltpu.VMEM((3, length, 2 * LANES), BF),
            tall, pltpu.VMEM((LANES, length), F32), tall, pltpu.VMEM((8, LANES), F32), tall, tall,
            box, box,
            pltpu.VMEM((4,) + go.shape[1:], BF),
            pltpu.VMEM((3,) + go.shape[1:], BF),
            pltpu.VMEM((4,) + gg.shape[1:], BF),
            pltpu.VMEM((3,) + gg.shape[1:], BF),
            pltpu.VMEM((seqs, 8, width), F32),
            pltpu.VMEM((seqs, 16, width), F32),
            pltpu.VMEM((seqs, 8, 2 * STATE), F32),
            pltpu.VMEM((seqs, 16, 2 * STATE), F32),
            pltpu.VMEM((seqs, 8, width), F32),
            pltpu.VMEM((seqs, 8, 2 * STATE), F32),
            pltpu.SemaphoreType.DMA((seqs, 2, n)),
            pltpu.SemaphoreType.DMA((seqs, 2, n)),
            pltpu.SemaphoreType.DMA((2, 7)),
            pltpu.SemaphoreType.DMA((2, 7)),
            pltpu.SemaphoreType.DMA((4,)),
        ],
        "mix_bwd",
        8 * 10**9,
        4,
    )


def reduce_kernel(n, normed, dg, di, ds, dr, wg, wi, ws, wt, gain, sm_i, sm_s, sm_h, g_gain,
                  o_pg, o_gi, o_gs, o_gt, o_sm,
                  pg, gi, gs, gt, lg, rg, xi, xs, xt, bi, bs, bt, mb,
                  xp, xb, xo2, zs, zr, ps, pr, ms, mr, es, er):
    _plane_barrier(n)
    seqs, length, width = di.shape
    model = normed.shape[2]
    blocks = 2
    rows = blocks * wi.shape[1]
    small = _Smalls(n, mb, o_sm, ms, mr)
    mb[0] = jnp.zeros(mb.shape[1:], F32)
    mb[0, 0:6, :] = sm_i[0:6, :]
    mb[0, 6:7, :] = g_gain[0:1, :]
    for k in range(5):
        at = 256 * (k % 3)
        mb[0, 9 + k // 3 : 10 + k // 3, at : at + 256] = sm_s[k : k + 1, :]
    mb[0, 10:11, 512:640] = sm_h[0:1, :]
    mb[0, 10:11, 640:768] = sm_h[1:2, :]

    lines = _line_reduces(n, pg, lg, rg, zs, zr)
    totals = [None] * (model // rows)
    for s in range(seqs):
        for b in range(model // rows):
            ch = slice(b * rows, (b + 1) * rows)
            near = slice(b * blocks, (b + 1) * blocks)
            part = None
            for d, w in zip((dg, di, ds, dr), (wg, wi, ws, wt)):
                more = _dot(d[s], w[near].reshape(rows, w.shape[2]), 1, 1)
                part = more if part is None else part + more
            pg[s, :, ch] = part.astype(BF)
            part = jnp.sum(part * normed[s, :, ch].astype(F32), axis=0, keepdims=True)
            totals[b] = part if totals[b] is None else totals[b] + part
        if s == 0:
            lines[s][0](0)
    for b, total in enumerate(totals):
        ch = slice(b * rows, (b + 1) * rows)
        mb[0, 7 + b // 2 : 8 + b // 2, (b % 2) * rows : (b % 2 + 1) * rows] = total / gain[:, ch]
    small.copy(0, small.near(0)).start()
    planes = [
        _PlaneReduce(part, pair, box, ps.at[i], pr.at[i])
        for i, (part, pair, box) in enumerate(((gs, xs, bs), (gt, xt, bt), (gi, xi, bi)))
    ]

    def weight(d, out):
        def one(b, _):
            ch = pl.ds(pl.multiple_of(b * rows, LANES), rows)
            total = None
            for s in range(seqs):
                part = _dot(normed[s, :, ch], d[s], 0, 0)
                total = part if total is None else total + part
            out[pl.ds(b * blocks, blocks)] = total.reshape(
                blocks, wi.shape[1], d.shape[2]
            ).astype(BF)
            return 0

        lax.fori_loop(0, model // rows, one, 0)

    weight(ds, gs)
    planes[0].begin()
    weight(dr, gt)
    planes[1].begin()
    small.step(0)
    weight(di, gi)
    planes[2].begin()
    small.step(1)
    lines[0][0](1)
    small.step(2)
    for line in lines[1:]:
        line[0](0)
    for p in planes:
        p.send_far()
    lines[0][0](2)
    for p in planes[:2]:
        p.send_near()
    planes[0].final(o_gs)
    planes[1].final(o_gt)
    quarter = xp.shape[1]
    for o in range(n):
        xp[o] = o_gs[o * quarter : (o + 1) * quarter, :].astype(BF)
    state = _LineSum(n, xp, xb, xo2, es, er)
    state.scatter()
    lines[1][0](1)
    planes[2].send_near()
    lines[1][0](2)
    state.gather()
    planes[2].final(o_gi)
    small.final()
    for s, (_, final, _) in enumerate(lines):
        final(o_pg.at[pl.ds(s, 1)])
    state.arrive()
    for o in range(n):
        o_gs[o * quarter : (o + 1) * quarter, :] = xo2[o].astype(F32)
    for p in planes:
        p.finish()
    state.finish()
    small.finish()
    for _, _, finish in lines:
        finish()


def reduce_all(n, normed, dg, di, ds, dr, wg, wi, ws, wt, gain, sm_i, sm_s, sm_h, g_gain):
    seqs, length, model = normed.shape
    rows = length // n
    sd = jax.ShapeDtypeStruct
    box = pltpu.VMEM((n, seqs, rows, model), BF)
    quarter = pltpu.VMEM((n, ws.shape[1] // n, ws.shape[2]), BF)
    sums = (16, wi.shape[2])
    return _mixer_call(
        functools.partial(reduce_kernel, n),
        (normed, dg, di, ds, dr, wg, wi, ws, wt, gain, sm_i, sm_s, sm_h, g_gain),
        (sd((seqs, rows, model), F32),)
        + tuple(sd(w.shape[1:], F32) for w in (wi, ws, wt))
        + (sd((n,) + sums, F32),),
        [pltpu.VMEM((seqs, length, model), BF)]
        + [pltpu.VMEM(w.shape, BF) for w in (wi, ws, wt)]
        + [box, box]
        + [pltpu.VMEM((4,) + w.shape[1:], BF) for w in (wi, ws, wt)]
        + [pltpu.VMEM((3,) + w.shape[1:], BF) for w in (wi, ws, wt)]
        + [
            pltpu.VMEM((6,) + sums, F32),
            quarter, quarter, quarter,
            pltpu.SemaphoreType.DMA((seqs, 2, n)),
            pltpu.SemaphoreType.DMA((seqs, 2, n)),
            pltpu.SemaphoreType.DMA((3, 7)),
            pltpu.SemaphoreType.DMA((3, 7)),
            pltpu.SemaphoreType.DMA((3 + n,)),
            pltpu.SemaphoreType.DMA((3 + n,)),
            pltpu.SemaphoreType.DMA((2, n)),
            pltpu.SemaphoreType.DMA((2, n)),
        ],
        "reduce_all",
        6 * 10**9,
        1,
    )


def emit_kernel(n, heads, tok, cot, gain, branch, rows, gg, gi, gs, gt, go, sms,
                block_out, g_tok, g_in, o_gg, o_gi, o_gs, o_gt, o_ci, o_ib, o_cs, o_sb,
                o_shift, o_rate, o_skip, o_gain, o_go):
    for s in range(tok.shape[0]):
        v = tok[s].astype(F32)
        rms = lax.rsqrt(jnp.mean(v * v, axis=-1, keepdims=True) + EPS)
        block_out[s] = (v + branch[s]).astype(BF)
        scaled = rows[s] * gain[...]
        mean = jnp.mean(scaled * v, axis=-1, keepdims=True)
        g_tok[s] = cot[s].astype(F32) + rms * scaled - v * (rms * rms * rms * mean)
    o_gg[...] = gg[...]
    o_gi[...] = gi[...]
    o_gs[...] = gs[...]
    short = jnp.zeros((256 - gt.shape[0], LANES), F32)
    o_gt[...] = jnp.concatenate([gt[...], short], axis=0).T[:heads, : gt.shape[0]]
    o_go[...] = go[...]
    width = sms.shape[2]
    shared = None
    head_rows = None
    for t in range(n):
        ch = slice(t * width, (t + 1) * width)
        o_ci[:, ch] = sms[t, 0:4, :]
        o_ib[:, ch] = sms[t, 4:5, :]
        o_gain[:, ch] = sms[t, 6:7, :]
        block = sms[t, 8:16, :]
        shared = sms[t, 7:11, :] if shared is None else shared + sms[t, 7:11, :]
        lanes = _iota((3 * width, LANES), 0)
        chan = lax.rem(lanes, width)
        to = _iota((3 * width, LANES), 1) == heads * t + lax.div(chan, HEAD_DIM)
        skips = _dot(_split(sms[t, 0:8, :], 3), to.astype(F32).astype(BF))
        lanes = lax.rem(_iota((3 * LANES, LANES), 0), LANES)
        to = (_iota((3 * LANES, LANES), 1) == heads * t + lanes) & (lanes < heads)
        to = to.astype(F32).astype(BF)
        shift = _dot(_split(block[:, 512:640], 3), to)
        rate = _dot(_split(block[:, 640:768], 3), to)
        new = (skips[5:6, :], shift[2:3, :], rate[2:3, :])
        head_rows = new if head_rows is None else tuple(a + b for a, b in zip(head_rows, new))
    every = n * heads
    o_skip[...] = head_rows[0][:, :every]
    o_shift[...] = head_rows[1][:, :every]
    o_rate[...] = head_rows[2][:, :every]
    g_in[:, :width] = shared[0:1, :]
    g_in[:, width:] = shared[1:2, :]
    for k in range(4):
        at = 256 * (k % 3)
        o_cs[k : k + 1, :] = shared[2 + k // 3 : 3 + k // 3, at : at + 256]
    o_sb[...] = shared[3:4, 256:512]


def emit_all(n, heads, tok, cot, gain, branch, rows, gg, gi, gs, gt, go, sms):
    vm = pl.BlockSpec(memory_space=pltpu.VMEM)
    sd = lambda *shape: jax.ShapeDtypeStruct(shape, F32)
    width = sms.shape[2]
    outs = (
        jax.ShapeDtypeStruct(tok.shape, BF), sd(*tok.shape), sd(1, tok.shape[2]),
        sd(*gg.shape), sd(*gi.shape), sd(*gs.shape), sd(heads, gt.shape[0]),
        sd(4, n * width), sd(1, n * width), sd(4, 2 * STATE), sd(1, 2 * STATE),
        sd(1, n * heads), sd(1, n * heads), sd(1, n * heads), sd(1, n * width),
        sd(*go.shape),
    )
    return pl.pallas_call(
        functools.partial(emit_kernel, n, heads),
        out_shape=outs,
        in_specs=[vm] * 11,
        out_specs=(vm,) * len(outs),
        compiler_params=pltpu.CompilerParams(vmem_limit_bytes=28 << 20),
        name="emit_all",
    )(tok, cot, gain, branch, rows, gg, gi, gs, gt, go, sms)


def per_device(
    tokens,
    segments,
    input_gain,
    gate_proj,
    inner_proj,
    state_proj,
    step_proj,
    conv_inner,
    inner_bias,
    conv_state,
    state_bias,
    step_bias,
    log_rates,
    skip_gain,
    gated_gain,
    output_proj,
    cotangent,
):
    tensor_count = lax.axis_size("tensor")
    tensor_rank = lax.axis_index("tensor")
    residual = tokens.astype(jnp.float32)
    rms_in = lax.rsqrt(jnp.mean(residual * residual, axis=-1, keepdims=True) + EPS)
    normed_own = (residual * rms_in * input_gain).astype(jnp.bfloat16)
    normed, cot_rows = (
        lax.all_gather(normed_own, "tensor", axis=1, tiled=True),
        lax.all_gather(cotangent, "tensor", axis=1, tiled=True),
    )
    gate_full, inner_full, state_full, step_full, output_full = (
        lax.all_gather(gate_proj, ("dp", "seq"), axis=0, tiled=True),
        lax.all_gather(inner_proj, ("dp", "seq"), axis=0, tiled=True),
        lax.all_gather(state_proj, ("dp", "seq"), axis=0, tiled=True),
        lax.all_gather(step_proj, ("dp", "seq"), axis=0, tiled=True),
        lax.all_gather(output_proj, ("dp", "seq"), axis=1, tiled=True),
    )
    gate_in = jnp.dot(normed, gate_full, preferred_element_type=jnp.float32)
    inner_low = jnp.dot(normed, inner_full, preferred_element_type=jnp.float32).astype(jnp.bfloat16)
    state_low = jnp.dot(normed, state_full, preferred_element_type=jnp.float32).astype(jnp.bfloat16)
    step_raw = jnp.dot(normed, step_full, preferred_element_type=jnp.float32)
    margin = KERNEL - 1
    seg_float = segments.astype(jnp.float32)
    prior_inner, prior_state, prior_seg = passed_along(
        (
            inner_low[:, -margin:],
            state_low[:, -margin:],
            seg_float[:, -margin:].astype(jnp.bfloat16),
        ),
        "seq",
        1,
    )
    padded_inner = jnp.concatenate([prior_inner, inner_low], axis=1).astype(jnp.float32)
    padded_state = jnp.concatenate([prior_state, state_low], axis=1).astype(jnp.float32)
    seg_padded = jnp.concatenate([prior_seg.astype(jnp.float32), seg_float], axis=1)
    pieces = segments.shape[1] // BLOCK
    seg_blocks = blocked(seg_float, pieces)
    before = jnp.concatenate(
        [prior_seg[:, -1:].astype(jnp.float32), seg_blocks[:, :-1, -1]], axis=1
    )
    width_here = inner_full.shape[1]
    heads_here = step_full.shape[1]
    chan_start = tensor_rank * width_here
    head_start = tensor_rank * heads_here
    kernel_here = lax.dynamic_slice_in_dim(conv_inner, chan_start, width_here, 1)
    bias_here = lax.dynamic_slice_in_dim(inner_bias, chan_start, width_here, 0)
    gain_here = lax.dynamic_slice_in_dim(gated_gain, chan_start, width_here, 0)
    shift_here = lax.dynamic_slice_in_dim(step_bias, head_start, heads_here, 0)
    rates_here = lax.dynamic_slice_in_dim(log_rates, head_start, heads_here, 0)
    skip_here = lax.dynamic_slice_in_dim(skip_gain, head_start, heads_here, 0)

    def mixer_front(
        pad_inner, pad_state, raw_steps, kernel_w, kernel_b, state_w, state_b, step_shift, rate_logs
    ):
        inner = jax.nn.silu(causal_mix(pad_inner, seg_padded, kernel_w, kernel_b))
        inner = inner.reshape(inner.shape[0], inner.shape[1], -1, HEAD_DIM)
        both_maps = jax.nn.silu(causal_mix(pad_state, seg_padded, state_w, state_b))
        b_proj = both_maps[:, :, :STATE]
        c_proj = both_maps[:, :, STATE:]
        deltas = jax.nn.softplus(raw_steps + step_shift)
        log_decay = deltas * -jnp.exp(rate_logs)
        inflow, passing = block_sums(inner, deltas, log_decay, b_proj, seg_blocks, before)
        return (inner, deltas, log_decay, b_proj, c_proj, inflow, passing)

    def mixer_rear(inner, deltas, log_decay, b_proj, c_proj, inflow, passing, incoming, skips):
        running = jnp.cumsum(blocked(log_decay, pieces), axis=2)
        places = jnp.arange(running.shape[2])
        allowed = (seg_blocks[:, :, :, None] == seg_blocks[:, :, None, :]) & (
            places[:, None] >= places[None, :]
        )
        inside = allowed[..., None]
        decays = jnp.where(
            inside,
            jnp.exp(jnp.where(inside, running[:, :, :, None, :] - running[:, :, None, :, :], 0.0)),
            0.0,
        )
        scores = jnp.einsum(
            "scin,scjn->scij", blocked(c_proj, pieces), blocked(b_proj, pieces), precision=HIGH
        )
        mixing = decays * scores[..., None] * blocked(deltas, pieces)[:, :, None, :, :]
        direct = jnp.einsum("scijh,scjhp->scihp", mixing, blocked(inner, pieces), precision=HIGH)
        from_state, outgoing = state_reads(
            incoming, log_decay, c_proj, inflow, passing, seg_blocks, before
        )
        heads_out = (direct + from_state).reshape(inner.shape) + skips[:, None] * inner
        return (heads_out.reshape(inner.shape[0], inner.shape[1], -1), outgoing)

    front_args = (
        padded_inner,
        padded_state,
        step_raw,
        kernel_here,
        bias_here,
        conv_state,
        state_bias,
        shift_here,
        rates_here,
    )
    front_vals = mixer_front(*front_args)
    inner, deltas, log_decay, b_proj, c_proj, inflow, passing = front_vals
    span_decay = jnp.ones(passing[:, 0].shape, jnp.float32)
    span_state = jnp.zeros(inflow[:, 0].shape, jnp.float32)
    span_state = passing[:, 0, :, None, None] * span_state + inflow[:, 0]
    span_decay = span_decay * passing[:, 0]
    identity = (jnp.ones_like(span_decay), jnp.zeros_like(span_state))
    incoming = entering_2((span_decay, span_state), "seq", chain_link, identity)[1]
    mixed, outgoing = mixer_rear(*front_vals, incoming, skip_here)
    sigmoid_z = jax.nn.sigmoid(gate_in)
    silu_z = gate_in * sigmoid_z
    gated = mixed * silu_z
    full_width = tensor_count * gated.shape[-1]
    square_sum = lax.psum(jnp.sum(gated * gated, axis=-1), "tensor")
    rms_gate = lax.rsqrt(square_sum / full_width + EPS)[..., None]
    gate_normed = (gated * rms_gate * gain_here).astype(jnp.bfloat16)
    partial_out = jnp.dot(gate_normed, output_full, preferred_element_type=jnp.float32)
    branch_rows = lax.psum_scatter(partial_out, "tensor", scatter_dimension=1, tiled=True)
    block_out = (residual + branch_rows).astype(jnp.bfloat16)
    grad_output = jnp.einsum(
        "srk,srd->kd", gate_normed, cot_rows, preferred_element_type=jnp.float32
    )
    grad_gn = jnp.einsum("srd,kd->srk", cot_rows, output_full, preferred_element_type=jnp.float32)
    scaled = grad_gn * gain_here
    dot_sum = lax.psum(jnp.sum(scaled * gated, axis=-1), "tensor")
    grad_gain_here = jnp.sum(grad_gn * gated * rms_gate, axis=(0, 1))
    grad_gated = rms_gate * scaled - gated * rms_gate**3 * (dot_sum / full_width)[..., None]
    grad_mixed = grad_gated * silu_z
    grad_gate_in = (grad_gated * mixed * sigmoid_z * (1.0 + gate_in * (1.0 - sigmoid_z))).astype(
        jnp.bfloat16
    )
    front_vals, front_back = jax.vjp(mixer_front, *front_args)
    unused_rear, rear_back = jax.vjp(mixer_rear, *front_vals, incoming, skip_here)
    inner, deltas, log_decay, b_proj, c_proj, inflow, passing = front_vals
    grad_blocks = blocked(grad_mixed.reshape(inner.shape), pieces)
    unused_reads, read_back = jax.vjp(
        lambda memory_in: state_reads(
            memory_in, log_decay, c_proj, inflow, passing, seg_blocks, before
        )[0],
        incoming,
    )
    local_grad = read_back(grad_blocks)[0]
    outgoing_grad = carried_in((span_decay, local_grad), "seq", chain_link, identity)[1]
    rear_grads = rear_back((grad_mixed, outgoing_grad))
    grad_skip_here = rear_grads[8]
    (
        pad_grad_inner,
        pad_grad_state,
        grad_step_raw,
        grad_kernel_here,
        grad_bias_here,
        grad_conv_state,
        grad_state_bias,
        grad_shift_here,
        grad_rates_here,
    ) = front_back(tuple(rear_grads[:7]))
    from_next_inner, from_next_state = passed_along(
        (pad_grad_inner[:, :margin], pad_grad_state[:, :margin]), "seq", -1
    )
    grad_inner_pre = jnp.concatenate(
        [pad_grad_inner[:, margin:-margin], pad_grad_inner[:, -margin:] + from_next_inner], axis=1
    )
    grad_state_part = jnp.concatenate(
        [pad_grad_state[:, margin:-margin], pad_grad_state[:, -margin:] + from_next_state], axis=1
    )
    grad_state_pre = lax.psum(grad_state_part, "tensor").astype(jnp.bfloat16)
    grad_inner_low = grad_inner_pre.astype(jnp.bfloat16)
    grad_step_low = grad_step_raw.astype(jnp.bfloat16)
    grad_normed = jnp.einsum(
        "srk,dk->srd", grad_gate_in, gate_full, preferred_element_type=jnp.float32
    )
    grad_normed = grad_normed + jnp.einsum(
        "srk,dk->srd", grad_inner_low, inner_full, preferred_element_type=jnp.float32
    )
    grad_normed = grad_normed + jnp.einsum(
        "srk,dk->srd", grad_step_low, step_full, preferred_element_type=jnp.float32
    )
    grad_rows = lax.psum_scatter(grad_normed, "tensor", scatter_dimension=1, tiled=True)
    own_rows = tokens.shape[1]
    state_mine = lax.dynamic_slice_in_dim(grad_state_pre, tensor_rank * own_rows, own_rows, 1)
    grad_rows = grad_rows + jnp.einsum(
        "srk,dk->srd", state_mine, state_full, preferred_element_type=jnp.float32
    )
    grad_gate_w = jnp.einsum(
        "srd,srk->dk", normed, grad_gate_in, preferred_element_type=jnp.float32
    )
    grad_inner_w = jnp.einsum(
        "srd,srk->dk", normed, grad_inner_low, preferred_element_type=jnp.float32
    )
    grad_state_w = jnp.einsum(
        "srd,srk->dk", normed, grad_state_pre, preferred_element_type=jnp.float32
    )
    grad_step_w = jnp.einsum(
        "srd,srk->dk", normed, grad_step_low, preferred_element_type=jnp.float32
    )
    shard_gate, shard_inner, shard_state, shard_step, shard_output = (
        lax.psum_scatter(grad_gate_w, ("dp", "seq"), scatter_dimension=0, tiled=True),
        lax.psum_scatter(grad_inner_w, ("dp", "seq"), scatter_dimension=0, tiled=True),
        lax.psum_scatter(grad_state_w, ("dp", "seq"), scatter_dimension=0, tiled=True),
        lax.psum_scatter(grad_step_w, ("dp", "seq"), scatter_dimension=0, tiled=True),
        lax.psum_scatter(grad_output, ("dp", "seq"), scatter_dimension=1, tiled=True),
    )
    scaled_in = grad_rows * input_gain
    grad_input_gain = jnp.sum(grad_rows * residual * rms_in, axis=(0, 1))
    grad_tokens = (
        cotangent.astype(jnp.float32)
        + rms_in * scaled_in
        - residual * rms_in**3 * jnp.mean(scaled_in * residual, axis=-1, keepdims=True)
    )

    def placed(whole, piece_grad, start, axis_number):
        return lax.dynamic_update_slice_in_dim(
            jnp.zeros_like(whole), piece_grad, start, axis_number
        )

    smalls = lax.psum(
        (
            grad_input_gain,
            placed(conv_inner, grad_kernel_here, chan_start, 1),
            placed(inner_bias, grad_bias_here, chan_start, 0),
            grad_conv_state,
            grad_state_bias,
            placed(step_bias, grad_shift_here, head_start, 0),
            placed(log_rates, grad_rates_here, head_start, 0),
            placed(skip_gain, grad_skip_here, head_start, 0),
            placed(gated_gain, grad_gain_here, chan_start, 0),
        ),
        ("dp", "seq", "tensor"),
    )
    return (
        block_out,
        grad_tokens,
        smalls[0],
        shard_gate,
        shard_inner,
        shard_state,
        shard_step,
        smalls[1],
        smalls[2],
        smalls[3],
        smalls[4],
        smalls[5],
        smalls[6],
        smalls[7],
        smalls[8],
        shard_output,
    )


def per_device_fast(
    tokens,
    segments,
    input_gain,
    gate_proj,
    inner_proj,
    state_proj,
    step_proj,
    conv_inner,
    inner_bias,
    conv_state,
    state_bias,
    step_bias,
    log_rates,
    skip_gain,
    gated_gain,
    output_proj,
    cotangent,
):
    tensor_count = lax.axis_size("tensor")
    tensor_rank = lax.axis_index("tensor")
    heads = step_proj.shape[1]
    gain_row = input_gain[None]
    normed, seg_old, s8, t8, i8 = gather_all(
        tensor_count, tokens, gain_row, segments, (state_proj, step_proj.T, inner_proj)
    )
    heads_param = jnp.pad(
        lax.dynamic_slice_in_dim(
            jnp.stack([step_bias, log_rates, skip_gain]), tensor_rank * heads, heads, 1
        ),
        ((0, 5), (0, LANES - heads)),
    )
    (
        y_part, u_inner, u_state, entry, incoming, gate_in, cot_rows, o8, g8,
        inner_low, state_low, prior_inner, prior_state, step_raw, rows,
    ) = mix_fwd(
        tensor_count, segments, seg_old, heads_param,
        conv_inner, inner_bias[None], conv_state, state_bias[None],
        cotangent, output_proj.T, gate_proj, normed, i8, s8, t8,
    )
    grad_mixed, grad_gate_in, outgoing_grad, partial_out, grad_output, grad_gate, grad_gain = gate_stage(
        tensor_count, y_part, u_state, entry, incoming, gate_in, cot_rows, o8, gated_gain[None], normed
    )
    (
        d_inner, d_state, d_step, sm_i, sm_s, sm_h, branch_rows, shard_output, shard_gate
    ) = mix_bwd(
        tensor_count, grad_mixed, u_inner, u_state, inner_low, prior_inner, state_low, prior_state,
        step_raw, rows, incoming, outgoing_grad, heads_param, conv_inner, conv_state,
        partial_out, grad_output, grad_gate,
    )
    grad_rows, shard_inner, shard_state, shard_step, sms = reduce_all(
        tensor_count, normed, grad_gate_in, d_inner, d_state, d_step, g8, i8, s8, t8, gain_row,
        sm_i, sm_s, sm_h, grad_gain,
    )
    outs = emit_all(
        tensor_count, heads, tokens, cotangent, gain_row, branch_rows, grad_rows,
        shard_gate, shard_inner, shard_state, shard_step, shard_output, sms,
    )
    flat = (2, 8, 10, 11, 12, 13, 14)
    return tuple(
        o[0] if i in flat else o.T if i in (6, 15) else o for i, o in enumerate(outs)
    )


def solution(mesh):
    fast = mesh.shape["dp"] == 4 and mesh.shape["seq"] == 2
    placed = (
        P("dp", ("seq", "tensor"), None),
        P("dp", "seq"),
        P(),
        P(("dp", "seq"), "tensor"),
        P(("dp", "seq"), "tensor"),
        P(("dp", "seq"), None),
        P(("dp", "seq"), "tensor"),
        P(),
        P(),
        P(),
        P(),
        P(),
        P(),
        P(),
        P(),
        P("tensor", ("dp", "seq")),
        P("dp", ("seq", "tensor"), None),
    )
    return jax.shard_map(
        per_device_fast if fast else per_device,
        mesh=mesh,
        in_specs=placed,
        out_specs=(
            P("dp", ("seq", "tensor"), None),
            P("dp", ("seq", "tensor"), None),
            P(),
            P(("dp", "seq"), "tensor"),
            P(("dp", "seq"), "tensor"),
            P(("dp", "seq"), None),
            P(("dp", "seq"), "tensor"),
            P(),
            P(),
            P(),
            P(),
            P(),
            P(),
            P(),
            P(),
            P("tensor", ("dp", "seq")),
        ),
        check_vma=False,
    )
```

```python
import functools

import jax
import jax.numpy as jnp
from jax import lax
from jax.experimental import pallas as pl
from jax.experimental.pallas import tpu as pltpu
from jax.sharding import PartitionSpec as P

HEAD_DIM = 64
STATE = 128
KERNEL = 4
BLOCK = 256


EPS = 1e-05
HIGH = lax.Precision.HIGHEST


def passed_along(block, axis, distance):
    devices = range(lax.axis_size(axis))
    route = [(i - distance, i) for i in devices if i - distance in devices]
    return lax.ppermute(block, axis, route)


def entering_2(shard, axis, join, neutral):
    place = lax.axis_index(axis)
    gathered = jax.tree.map(
        lambda a, kind: lax.all_gather(a.astype(kind), axis), shard, (jnp.bfloat16, jnp.bfloat16)
    )
    state = jax.tree.map(lambda a, e: jnp.zeros_like(a) + jnp.asarray(e, a.dtype), shard, neutral)

    def one(hop, state):
        return join(
            state,
            jax.tree.map(
                lambda a, own: lax.dynamic_index_in_dim(a, hop, 0, False).astype(own.dtype),
                gathered,
                shard,
            ),
        )

    return lax.fori_loop(0, place, one, state)


def carried_in(shard, axis, combine, identity):
    length, here = (lax.axis_size(axis), lax.axis_index(axis))
    everything = jax.tree.map(
        lambda part, kind: lax.all_gather(part.astype(kind), axis),
        shard,
        jax.tree.map(lambda a: jnp.bfloat16 if a.dtype == jnp.float32 else a.dtype, shard),
    )
    start = jax.tree.map(
        lambda part, zero: jnp.broadcast_to(jnp.asarray(zero, part.dtype), part.shape),
        shard,
        identity,
    )

    def hop(k, before):
        at = length - 1 - k
        reached = at > here
        new = combine(
            before, jax.tree.map(lambda part, own: part[at].astype(own.dtype), everything, shard)
        )
        return jax.tree.map(lambda a, b: jnp.where(reached, a, b), new, before)

    return lax.fori_loop(0, length, hop, start)


def chain_link(earlier, later):
    return (earlier[0] * later[0], later[0][:, :, None, None] * earlier[1] + later[1])


def causal_mix(padded, seg_padded, kernel_w, kernel_b):
    margin = KERNEL - 1
    length = padded.shape[1] - margin
    seg_now = seg_padded[:, margin:]
    result = kernel_b + kernel_w[0] * padded[:, margin:]
    for offset in range(1, KERNEL):
        moved = padded[:, margin - offset : margin - offset + length]
        same_doc = (seg_padded[:, margin - offset : margin - offset + length] == seg_now).astype(
            jnp.float32
        )
        result = result + kernel_w[offset] * moved * same_doc[:, :, None]
    return result


def blocked(values, pieces):
    return values.reshape((values.shape[0], pieces, values.shape[1] // pieces) + values.shape[2:])


def block_sums(inner, deltas, log_decay, b_proj, seg_blocks, before):
    pieces = seg_blocks.shape[1]
    running = jnp.cumsum(blocked(log_decay, pieces), axis=2)
    same_end = (seg_blocks == seg_blocks[:, :, -1:]).astype(jnp.float32)
    to_end = (
        jnp.exp(running[:, :, -1:, :] - running) * same_end[:, :, :, None] * blocked(deltas, pieces)
    )
    inflow = jnp.einsum(
        "scjhp,scjn->schpn",
        to_end[..., None] * blocked(inner, pieces),
        blocked(b_proj, pieces),
        precision=HIGH,
    )
    passing = (
        jnp.exp(running[:, :, -1, :])
        * (seg_blocks[:, :, -1] == before).astype(jnp.float32)[:, :, None]
    )
    return (inflow, passing)


def state_reads(incoming, log_decay, c_proj, inflow, passing, seg_blocks, before):
    pieces = seg_blocks.shape[1]
    running = jnp.cumsum(blocked(log_decay, pieces), axis=2)
    memory = incoming
    entering = [memory]
    memory = passing[:, 0, :, None, None] * memory + inflow[:, 0]
    stacked = jnp.stack(entering, axis=1)
    entry = jnp.exp(running) * (seg_blocks == before[:, :, None]).astype(jnp.float32)[..., None]
    from_state = (
        jnp.einsum("scin,schpn->scihp", blocked(c_proj, pieces), stacked, precision=HIGH)
        * entry[..., None]
    )
    return (from_state, memory)


MESH = pl.DeviceIdType.MESH
BF = jnp.bfloat16
F32 = jnp.float32


def _peers():
    dp, seq, t = lax.axis_index("dp"), lax.axis_index("seq"), lax.axis_index("tensor")
    x, y = lax.rem(dp, 2), lax.div(dp, 2)
    x_dp = dp + 1 - 2 * x
    y_dp = dp + 2 - 4 * y
    d_dp = 3 - dp
    return dp, seq, t, x_dp, y_dp, d_dp


def _dev(dp, seq, t):
    return {"dp": dp, "seq": seq, "tensor": t}


def _plane_barrier(n):
    dp, seq, t, x_dp, y_dp, d_dp = _peers()
    bar = pltpu.get_barrier_semaphore()
    for who in (_dev(dp, 1 - seq, t), _dev(x_dp, seq, t), _dev(y_dp, seq, t)):
        pl.semaphore_signal(bar, inc=1, device_id=who, device_id_type=MESH)

    for step in range(1, n):
        pl.semaphore_signal(
            bar, inc=1, device_id=_dev(dp, seq, lax.rem(t + step, n)), device_id_type=MESH
        )
    pl.semaphore_wait(bar, 3 + n - 1)


class _Line:
    def __init__(self, n, ref, rows, ssem, rsem, own=None):
        self.n, self.ref, self.rows, self.ssem, self.rsem = n, ref, rows, ssem, rsem
        self.own = own

    def block(self, o):
        return self.ref.at[:, pl.ds(pl.multiple_of(o * self.rows, self.rows), self.rows), :]

    def copy(self, o, direction, own=False):
        dp, seq, t = lax.axis_index("dp"), lax.axis_index("seq"), lax.axis_index("tensor")
        return pltpu.make_async_remote_copy(
            src_ref=self.own if own else self.block(o),
            dst_ref=self.block(o),
            send_sem=self.ssem.at[0 if direction > 0 else 1, o],
            recv_sem=self.rsem.at[o],
            device_id=_dev(dp, seq, t + direction),
            device_id_type=MESH,
        )

    def step(self, d):
        n, t = self.n, lax.axis_index("tensor")
        for way in (1, -1):
            o = t - way * d
            here = jnp.logical_and(o >= 0, o < n)
            nxt = jnp.logical_and(t + way >= 0, t + way < n)

            @pl.when(here)
            def _(o=o, way=way, nxt=nxt):
                if d > 0:
                    self.copy(o, way).wait_recv()

                @pl.when(nxt)
                def _():
                    self.copy(o, way, d == 0 and self.own is not None).start()

    def finish(self):
        n, t = self.n, lax.axis_index("tensor")
        for d in range(n):
            for way in (1, -1):
                o = t - way * d
                ok = jnp.logical_and(
                    jnp.logical_and(o >= 0, o < n),
                    jnp.logical_and(t + way >= 0, t + way < n),
                )

                @pl.when(ok)
                def _(o=o, way=way):
                    self.copy(o, way).wait_send()


class _Plane:
    def __init__(self, own, full, ssem, rsem, lsem):
        self.own, self.full, self.ssem, self.rsem, self.lsem = own, full, ssem, rsem, lsem

    def copy(self, src, block, who, s):
        return pltpu.make_async_remote_copy(
            src_ref=src,
            dst_ref=self.full.at[block],
            send_sem=self.ssem.at[s],
            recv_sem=self.rsem.at[s],
            device_id=who,
            device_id_type=MESH,
        )

    def begin(self):
        dp, seq, t, x_dp, y_dp, d_dp = _peers()
        me = dp * 2 + seq
        pltpu.make_async_copy(self.own, self.full.at[me], self.lsem).start()
        self.copy(self.own, me, _dev(x_dp, seq, t), 0).start()
        self.copy(self.own, me, _dev(y_dp, seq, t), 1).start()
        self.copy(self.own, me, _dev(dp, 1 - seq, t), 3).start()

    def forward(self):
        dp, seq, t, x_dp, y_dp, d_dp = _peers()
        bx, by = x_dp * 2 + seq, y_dp * 2 + seq
        self.copy(self.own, bx, _dev(x_dp, seq, t), 0).wait_recv()
        self.copy(self.own, by, _dev(y_dp, seq, t), 1).wait_recv()

        @pl.when(seq == 0)
        def _():
            self.copy(self.full.at[by], by, _dev(x_dp, seq, t), 2).start()

        @pl.when(seq == 1)
        def _():
            self.copy(self.full.at[bx], bx, _dev(y_dp, seq, t), 2).start()

        self.copy(self.full.at[bx], bx, _dev(dp, 1 - seq, t), 4).start()
        self.copy(self.full.at[by], by, _dev(dp, 1 - seq, t), 5).start()

    def share(self):
        dp, seq, t, x_dp, y_dp, d_dp = _peers()
        bd = d_dp * 2 + seq
        self.copy(self.own, bd, _dev(x_dp, seq, t), 2).wait_recv()
        self.copy(self.full.at[bd], bd, _dev(dp, 1 - seq, t), 6).start()

    def arrive(self):
        dp, seq, t, x_dp, y_dp, d_dp = _peers()
        me = dp * 2 + seq
        pltpu.make_async_copy(self.own, self.full.at[me], self.lsem).wait()
        for s in (3, 4, 5, 6):
            self.copy(self.own, me, _dev(dp, 1 - seq, t), s).wait_recv()

    def finish(self):
        dp, seq, t, x_dp, y_dp, d_dp = _peers()
        me = dp * 2 + seq
        for s in range(7):
            self.copy(self.own, me, _dev(dp, 1 - seq, t), s).wait_send()


def gather_kernel(n, tok_far, gain, seg, ws, wt_t, wi, normed, seg_old, fs, ft, fi,
                  tok, wt, zs, zr, ps, pr, ls, hs):
    dp, seq, t = lax.axis_index("dp"), lax.axis_index("seq"), lax.axis_index("tensor")
    rows = tok.shape[1]
    near = pltpu.make_async_copy(tok_far, tok, ls.at[3])
    near.start()
    v = wt_t[...].astype(F32)
    v = jnp.concatenate([v, jnp.zeros((LANES - v.shape[0], v.shape[1]), F32)], axis=0)
    v = jnp.concatenate([v, jnp.zeros((LANES, 256 - v.shape[1]), F32)], axis=1)
    wt[...] = v.T[: wt.shape[0], :].astype(BF)
    _plane_barrier(n)
    planes = [
        _Plane(own, full, ps.at[i], pr.at[i], ls.at[i])
        for i, (own, full) in enumerate(((ws, fs), (wt, ft), (wi, fi)))
    ]
    handed = pltpu.make_async_remote_copy(
        src_ref=seg, dst_ref=seg_old, send_sem=hs.at[0], recv_sem=hs.at[1],
        device_id=_dev(dp, 1 - seq, t), device_id_type=MESH,
    )

    @pl.when(seq == 0)
    def _():
        handed.start()
        seg_old[...] = jnp.zeros_like(seg_old)

    for p in planes:
        p.begin()
    near.wait()
    mine = pl.ds(pl.multiple_of(t * rows, rows), rows)
    lines = []
    for s in range(tok.shape[0]):
        v = tok[s].astype(F32)
        rms = lax.rsqrt(jnp.mean(v * v, axis=-1, keepdims=True) + EPS)
        normed[s, mine, :] = (v * rms * gain[...]).astype(BF)
        lines.append(_Line(n, normed.at[pl.ds(s, 1)], rows, zs.at[s], zr.at[s]))
        lines[s].step(0)
    for line in lines:
        line.step(1)
    for p in planes:
        p.forward()
    lines[0].step(2)
    for p in planes:
        p.share()
    for line in lines[1:]:
        line.step(2)
    for d in range(3, n):
        for line in lines:
            line.step(d)
    for p in planes:
        p.arrive()

    @pl.when(seq == 0)
    def _():
        handed.wait_send()

    @pl.when(seq == 1)
    def _():
        handed.wait_recv()

    for line in lines:
        line.finish()
    for p in planes:
        p.finish()


def gather_all(n, tokens, gain, seg, weights):
    seqs, rows, width = tokens.shape
    vm = pl.BlockSpec(memory_space=pltpu.VMEM)
    far = pl.BlockSpec(memory_space=pltpu.HBM)
    wide = (weights[1].shape[1], LANES)
    full = lambda *shape: jax.ShapeDtypeStruct((8,) + shape, BF)
    act = jax.ShapeDtypeStruct((seqs, n * rows, width), BF)
    return pl.pallas_call(
        functools.partial(gather_kernel, n),
        out_shape=(
            act, jax.ShapeDtypeStruct(seg.shape, seg.dtype),
            full(*weights[0].shape), full(*wide), full(*weights[2].shape),
        ),
        in_specs=[far, vm, vm, far, vm, far],
        out_specs=(vm,) * 5,
        scratch_shapes=[
            pltpu.VMEM(tokens.shape, tokens.dtype),
            pltpu.VMEM(wide, BF),
            pltpu.SemaphoreType.DMA((seqs, 2, n)),
            pltpu.SemaphoreType.DMA((seqs, n)),
            pltpu.SemaphoreType.DMA((3, 7)),
            pltpu.SemaphoreType.DMA((3, 7)),
            pltpu.SemaphoreType.DMA((4,)),
            pltpu.SemaphoreType.DMA((2,)),
        ],
        compiler_params=pltpu.CompilerParams(
            collective_id=0, has_side_effects=True, vmem_limit_bytes=16 << 20
        ),
        cost_estimate=pl.CostEstimate(flops=30 * 10**9, bytes_accessed=1 << 20, transcendentals=0),
        name="gather_all",
    )(tokens, gain, seg, *weights)


def _line_reduce(n, part, left, right, ssem, rsem):
    dp, seq, t = lax.axis_index("dp"), lax.axis_index("seq"), lax.axis_index("tensor")
    rows = left.shape[2]

    def copy(src, box, o, way):
        return pltpu.make_async_remote_copy(
            src_ref=src, dst_ref=box.at[o],
            send_sem=ssem.at[0 if way > 0 else 1, o], recv_sem=rsem.at[0 if way > 0 else 1, o],
            device_id=_dev(dp, seq, t + way), device_id_type=MESH,
        )

    def block(o):
        return part.at[:, pl.ds(pl.multiple_of(o * rows, rows), rows), :]

    def begin(j):
        for way, box, place, o in ((1, left, t, n - 1 - j), (-1, right, n - 1 - t, j)):
            @pl.when(place == 0)
            def _():
                copy(block(o), box, o, way).start()

    def step(k):
        for way, box, place in ((1, left, t), (-1, right, n - 1 - t)):
            @pl.when(jnp.logical_and(place > 0, place <= k))
            def _():
                o = n - 1 - (k - place) if way > 0 else k - place
                copy(block(o), box, o, way).wait_recv()
                for s in range(part.shape[0]):
                    own = part[s, pl.ds(pl.multiple_of(o * rows, rows), rows), :].astype(F32)
                    box[o, s] = (box[o, s].astype(F32) + own).astype(BF)
                copy(box.at[o], box, o, way).start()

    def final(out):
        mine = pl.ds(pl.multiple_of(t * rows, rows), rows)
        for s in range(part.shape[0]):
            out[s] = part[s, mine, :].astype(F32)

        @pl.when(t > 0)
        def _():
            copy(left.at[0], left, t, 1).wait_recv()
            for s in range(part.shape[0]):
                out[s] = out[s] + left[t, s].astype(F32)

        @pl.when(t < n - 1)
        def _():
            copy(left.at[0], right, t, -1).wait_recv()
            for s in range(part.shape[0]):
                out[s] = out[s] + right[t, s].astype(F32)

    def finish():
        for j in range(n - 1):
            for way, box, o in ((1, left, n - 1 - j), (-1, right, j)):
                sends = (t < o) if way > 0 else (t > o)

                @pl.when(sends)
                def _():
                    copy(box.at[o], box, o, way).wait_send()

    return begin, step, final, finish


def _line_reduces(n, part, left, right, ssem, rsem):
    one = lambda s: pl.ds(s, 1)
    return [
        _line_reduce(
            n, part.at[one(s)], left.at[:, one(s)], right.at[:, one(s)], ssem.at[s], rsem.at[s]
        )
        for s in range(part.shape[0])
    ]


class _PlaneReduce:
    def __init__(self, part, pair, box, ssem, rsem):
        self.part, self.pair, self.box, self.ssem, self.rsem = part, pair, box, ssem, rsem

    def copy(self, src, dst, who, s):
        return pltpu.make_async_remote_copy(
            src_ref=src, dst_ref=dst, send_sem=self.ssem.at[s], recv_sem=self.rsem.at[s],
            device_id=who, device_id_type=MESH,
        )

    def begin(self):
        dp, seq, t, x_dp, y_dp, d_dp = _peers()
        for slot, chip in enumerate((d_dp, x_dp, y_dp, dp)):
            self.copy(self.part.at[chip * 2 + 1 - seq], self.pair.at[slot], _dev(dp, 1 - seq, t), slot).start()

    def _paired(self, slot, chip, also=None):
        dp, seq, t, x_dp, y_dp, d_dp = _peers()
        self.copy(self.pair.at[slot], self.pair.at[slot], _dev(dp, 1 - seq, t), slot).wait_recv()
        v = self.part[chip * 2 + seq].astype(F32) + self.pair[slot].astype(F32)
        self.pair[slot] = v.astype(BF)

    def send_far(self):
        dp, seq, t, x_dp, y_dp, d_dp = _peers()
        for slot, chip in enumerate((d_dp, x_dp, y_dp)):
            self._paired(slot, chip)
            if slot == 0:
                @pl.when(seq == 0)
                def _():
                    self.copy(self.pair.at[0], self.box.at[2], _dev(x_dp, seq, t), 4).start()

                @pl.when(seq == 1)
                def _():
                    self.copy(self.pair.at[0], self.box.at[2], _dev(y_dp, seq, t), 4).start()

        @pl.when(seq == 0)
        def _():
            self.copy(self.pair.at[1], self.box.at[0], _dev(x_dp, seq, t), 5).start()

        @pl.when(seq == 1)
        def _():
            self.copy(self.pair.at[2], self.box.at[1], _dev(y_dp, seq, t), 6).start()

    def send_near(self):
        dp, seq, t, x_dp, y_dp, d_dp = _peers()
        self.copy(self.pair.at[0], self.box.at[2], _dev(dp, seq, t), 4).wait_recv()

        @pl.when(seq == 0)
        def _():
            self.box[2] = (self.box[2].astype(F32) + self.pair[2].astype(F32)).astype(BF)
            self.copy(self.box.at[2], self.box.at[1], _dev(y_dp, seq, t), 6).start()

        @pl.when(seq == 1)
        def _():
            self.box[2] = (self.box[2].astype(F32) + self.pair[1].astype(F32)).astype(BF)
            self.copy(self.box.at[2], self.box.at[0], _dev(x_dp, seq, t), 5).start()

    def final(self, out):
        dp, seq, t, x_dp, y_dp, d_dp = _peers()
        self.copy(self.pair.at[3], self.pair.at[3], _dev(dp, seq, t), 3).wait_recv()
        self.copy(self.pair.at[0], self.box.at[0], _dev(dp, seq, t), 5).wait_recv()
        self.copy(self.pair.at[0], self.box.at[1], _dev(dp, seq, t), 6).wait_recv()
        out[...] = (
            self.part[dp * 2 + seq].astype(F32) + self.pair[3].astype(F32)
            + self.box[0].astype(F32) + self.box[1].astype(F32)
        )

    def finish(self):
        dp, seq, t, x_dp, y_dp, d_dp = _peers()
        for s in range(7):
            self.copy(self.pair.at[0], self.box.at[0], _dev(dp, 1 - seq, t), s).wait_send()


class _Smalls:
    def __init__(self, n, box, line, ssem, rsem):
        self.n, self.box, self.line, self.ssem, self.rsem = n, box, line, ssem, rsem

    def copy(self, j, who):
        return pltpu.make_async_remote_copy(
            src_ref=self.box.at[2 * j], dst_ref=self.box.at[2 * j + 1],
            send_sem=self.ssem.at[j], recv_sem=self.rsem.at[j],
            device_id=who, device_id_type=MESH,
        )

    def near(self, j):
        dp, seq, t, x_dp, y_dp, d_dp = _peers()
        return (_dev(dp, 1 - seq, t), _dev(x_dp, seq, t), _dev(y_dp, seq, t))[j]

    def begin(self, value):
        self.box[0] = value
        self.copy(0, self.near(0)).start()

    def step(self, j):
        self.copy(j, self.near(j)).wait_recv()
        total = self.box[2 * j] + self.box[2 * j + 1]
        if j < 2:
            self.box[2 * j + 2] = total
            self.copy(j + 1, self.near(j + 1)).start()
        else:
            t = lax.axis_index("tensor")
            self.line[t] = total
            for o in range(self.n):
                @pl.when(t != o)
                def _(o=o):
                    self.across(t, o).start()

    def across(self, src, who):
        dp, seq, t = lax.axis_index("dp"), lax.axis_index("seq"), lax.axis_index("tensor")
        return pltpu.make_async_remote_copy(
            src_ref=self.line.at[src], dst_ref=self.line.at[src],
            send_sem=self.ssem.at[3 + who], recv_sem=self.rsem.at[3 + src],
            device_id=_dev(dp, seq, who), device_id_type=MESH,
        )

    def final(self):
        t = lax.axis_index("tensor")
        for o in range(self.n):
            @pl.when(t != o)
            def _(o=o):
                self.across(o, o).wait_recv()

    def finish(self):
        t = lax.axis_index("tensor")
        for j in range(3):
            self.copy(j, self.near(j)).wait_send()
        for o in range(self.n):
            @pl.when(t != o)
            def _(o=o):
                self.across(t, o).wait_send()


class _LineSum:
    def __init__(self, n, part, box, out, ssem, rsem):
        self.n, self.part, self.box, self.out, self.ssem, self.rsem = n, part, box, out, ssem, rsem

    def copy(self, phase, src_block, dst_ref, who, origin):
        dp, seq = lax.axis_index("dp"), lax.axis_index("seq")
        return pltpu.make_async_remote_copy(
            src_ref=src_block, dst_ref=dst_ref,
            send_sem=self.ssem.at[phase, who], recv_sem=self.rsem.at[phase, origin],
            device_id=_dev(dp, seq, who), device_id_type=MESH,
        )

    def scatter(self):
        t = lax.axis_index("tensor")
        for o in range(self.n):
            @pl.when(t != o)
            def _(o=o):
                self.copy(0, self.part.at[o], self.box.at[t], o, t).start()

    def gather(self):
        t = lax.axis_index("tensor")
        total = self.part[t].astype(F32)
        for o in range(self.n):
            @pl.when(t != o)
            def _(o=o):
                self.copy(0, self.part.at[o], self.box.at[o], o, o).wait_recv()

            @pl.when(t == o)
            def _(o=o):
                self.box[o] = jnp.zeros(self.box.shape[1:], self.box.dtype)
        for o in range(self.n):
            total = total + self.box[o].astype(F32)
        self.out[t] = total.astype(self.out.dtype)
        for o in range(self.n):
            @pl.when(t != o)
            def _(o=o):
                self.copy(1, self.out.at[t], self.out.at[t], o, t).start()

    def arrive(self):
        t = lax.axis_index("tensor")
        for o in range(self.n):
            @pl.when(t != o)
            def _(o=o):
                self.copy(1, self.out.at[o], self.out.at[o], o, o).wait_recv()

    def finish(self):
        t = lax.axis_index("tensor")
        for o in range(self.n):
            @pl.when(t != o)
            def _(o=o):
                self.copy(0, self.part.at[o], self.box.at[o], o, o).wait_send()
                self.copy(1, self.part.at[o], self.box.at[o], o, o).wait_send()


LANES = 128


def _split(v, parts):
    out = []
    for _ in range(parts):
        b = v.astype(BF)
        out.append(b)
        v = v - b.astype(F32)
    return jnp.concatenate(out, axis=1)


def _dot(a, b, ca=1, cb=0):
    return lax.dot_general(a, b, (((ca,), (cb,)), ((), ())), preferred_element_type=F32)


def _iota(shape, axis):
    return lax.broadcasted_iota(jnp.int32, shape, axis)


def _spreader(rows, p):
    head = lax.rem(_iota((rows, LANES), 0), LANES)
    return (head == 2 * p + lax.div(_iota((rows, LANES), 1), HEAD_DIM)).astype(F32).astype(BF)


def _folder(rows, p):
    chan = lax.rem(_iota((rows, LANES), 0), LANES)
    return (_iota((rows, LANES), 1) == 2 * p + lax.div(chan, HEAD_DIM)).astype(F32).astype(BF)


def _sig(v):
    return 1.0 / (1.0 + jnp.exp(-v))


def _three(v):
    return v[:, :LANES] + v[:, LANES : 2 * LANES] + v[:, 2 * LANES :]


def _head_scalars(raw, hp, marks, length):
    v = raw + hp[0:1, :]
    delta = jnp.maximum(v, 0.0) + jnp.log1p(jnp.exp(-jnp.abs(v)))
    log_decay = -delta * jnp.exp(hp[1:2, :])
    lower = (_iota((length, length), 0) >= _iota((length, length), 1)).astype(F32).astype(BF)
    running = _three(_dot(lower, _split(log_decay, 3)))
    entry = jnp.exp(running) * marks[:, 4:5]
    to_end = jnp.exp(running[length - 1 :, :] - running) * marks[:, 5:6]
    return v, delta, log_decay, running, entry, to_end


def _marks(rows):
    full = jnp.concatenate([rows, jnp.zeros((LANES - rows.shape[0], rows.shape[1]), F32)], axis=0)
    return full.T


def _bias_matrix(rows, marks, length):
    ok = (_iota((length, length), 0) >= _iota((length, length), 1)) & (
        marks[:, 0:1] == rows[0:1, :]
    )
    return jnp.where(ok, 0.0, -1e30)


def _conv(pad, marks, taps, bias, length):
    total = bias + taps[0:1, :] * pad[8 : 8 + length, :]
    for k in range(1, KERNEL):
        total = total + taps[k : k + 1, :] * (pad[8 - k : 8 - k + length, :] * marks[:, k : k + 1])
    return total


def mix_fwd_kernel(n, seg, seg_old, hp, taps_i, bias_i, taps_s, bias_s, cot, wo, wg, normed, wi, ws, wt,
                   y, u_i, u_s, entry_o, incoming, gate, cot_full, fo, fg,
                   pre_i, pre_s, old_i, old_s, raw, rows,
                   pad, run3, run_t, bias_m, scores, heads_hl, inflow, zs, zr, ps, pr, ls, hs):
    dp, seq, t = lax.axis_index("dp"), lax.axis_index("seq"), lax.axis_index("tensor")
    seqs, length, width = pre_i.shape
    model = normed.shape[2]
    pairs = width // LANES
    wide = 2 * LANES
    _plane_barrier(n)
    lines = [
        _Line(n, cot_full.at[pl.ds(s, 1)], cot.shape[1], zs.at[s], zr.at[s], cot.at[pl.ds(s, 1)])
        for s in range(seqs)
    ]
    planes = (_Plane(wg, fg, ps.at[0], pr.at[0], ls.at[0]), _Plane(wo, fo, ps.at[1], pr.at[1], ls.at[1]))
    whole = _Line(n, cot_full, cot.shape[1], zs, zr)
    own = pltpu.make_async_copy(cot, whole.block(t), ls.at[2])
    own.start()
    for line in lines:
        line.step(0)
    for plane in planes:
        plane.begin()
    flat = normed[...].reshape(seqs * length, model)
    pre_s[...] = _dot(flat, ws[...].reshape(model, ws.shape[2])).astype(BF).reshape(pre_s.shape)

    def inner_part(c, _):
        ch = pl.ds(pl.multiple_of(c * wide, wide), wide)
        part = _dot(flat, wi[:, :, ch].reshape(model, wide))
        pre_i[:, :, ch] = part.astype(BF).reshape(seqs, length, wide)
        return 0

    lax.fori_loop(0, width // wide, inner_part, 0)
    ends = [
        pltpu.make_async_remote_copy(
            src_ref=a.at[:, pl.ds(length - 16, 16), :], dst_ref=b,
            send_sem=hs.at[2 + i], recv_sem=hs.at[4 + i],
            device_id=_dev(dp, 1 - seq, t), device_id_type=MESH,
        )
        for i, (a, b) in enumerate(((pre_i, old_i), (pre_s, old_s)))
    ]

    @pl.when(seq == 0)
    def _():
        for c in ends:
            c.start()
        old_i[...] = jnp.zeros_like(old_i)
        old_s[...] = jnp.zeros_like(old_s)

    raw[...] = _dot(flat, wt[...].reshape(model, LANES)).reshape(raw.shape)
    for s in range(seqs):
        now = seg[s : s + 1, :].astype(F32)
        old = seg_old[s : s + 1, :].astype(F32)
        both = jnp.broadcast_to(jnp.concatenate([old, now], axis=1), (8, 2 * length))
        here = jnp.broadcast_to(now, (8, length))
        place = _iota((8, length), 0)
        block = jnp.where(place == 0, here, 0.0)
        others = [pltpu.roll(both, k, 1)[:, length:] for k in range(1, KERNEL)]
        others += [both[:, length - 1 : length], both[:, 2 * length - 1 :]]
        for k, other in enumerate(others):
            block = jnp.where((place == k + 1) & (here == other), 1.0, block)
        rows[s] = block

    lines[0].step(1)

    @pl.when(seq == 1)
    def _():
        for c in ends:
            c.wait_recv()

    def one(s, _):
        rw = rows[s]
        marks = _marks(rw)
        v, delta, log_decay, running, entry, to_end = _head_scalars(raw[s], hp, marks, length)
        entry_o[s] = entry
        run3[...] = _split(running, 3)
        run_t[...] = running.T
        bias_m[...] = _bias_matrix(rw, marks, length)
        heads_hl[0] = _split(delta, 2)
        heads_hl[1] = _split(to_end, 2)
        maps = []
        for half in range(2):
            ch = slice(half * STATE, (half + 1) * STATE)
            pad[0:8, :] = old_s[s, :, ch].astype(F32)[8:16, :]
            pad[8:, :] = pre_s[s, :, ch].astype(F32)
            u = _conv(pad, marks, taps_s[:, ch], bias_s[:, ch], length)
            u_s[s, :, ch] = u
            maps.append((u * _sig(u)).astype(BF))
        b_map, c_map = maps
        scores[...] = _dot(c_map, b_map, 1, 1)

        def pair(p, _):
            @pl.when(jnp.logical_and(s == 0, p == 4))
            def _():
                lines[1].step(1)

            @pl.when(jnp.logical_and(s == 1, p == 0))
            def _():
                for plane in planes:
                    plane.forward()

            @pl.when(jnp.logical_and(s == 1, p == 1))
            def _():
                lines[0].step(2)

            @pl.when(jnp.logical_and(s == 1, p == 5))
            def _():
                lines[1].step(2)
                planes[0].share()

            ch = pl.ds(pl.multiple_of(p * LANES, LANES), LANES)
            at = pl.ds(pl.multiple_of(t * width + p * LANES, LANES), LANES)
            pad[0:8, :] = old_i[s, :, ch].astype(F32)[8:16, :]
            pad[8:, :] = pre_i[s, :, ch].astype(F32)
            u = _conv(pad, marks, taps_i[:, at], bias_i[:, at], length)
            u_i[s, :, ch] = u
            x = u * _sig(u)
            spread = _spreader(2 * LANES, p)
            xd = x * _dot(heads_hl[0], spread)
            inflow[s, :, ch] = _dot(b_map, (xd * _dot(heads_hl[1], spread)).astype(BF), 0, 0).astype(BF)
            skip = _dot(_split(hp[...], 2), spread)[2:3, :]
            total = skip * x
            xb = xd.astype(BF)
            lane = lax.div(_iota(xb.shape, 1), HEAD_DIM)
            for a in range(2):
                h = 2 * p + a
                pick = (lax.rem(_iota((3 * LANES, length), 0), LANES) == h).astype(F32).astype(BF)
                decay = jnp.exp(_dot(run3[...], pick) - run_t[pl.ds(h, 1), :] + bias_m[...])
                mixing = (decay * scores[...]).astype(BF)
                total = total + _dot(mixing, jnp.where(lane == a, xb, jnp.zeros_like(xb)))
            y[s, :, ch] = total
            return 0

        lax.fori_loop(0, pairs, pair, 0)
        return 0

    lax.fori_loop(0, seqs, one, 0)
    handed = pltpu.make_async_remote_copy(
        src_ref=inflow, dst_ref=incoming, send_sem=hs.at[0], recv_sem=hs.at[1],
        device_id=_dev(dp, 1 - seq, t), device_id_type=MESH,
    )

    @pl.when(seq == 0)
    def _():
        handed.start()
        incoming[...] = jnp.zeros_like(incoming)

    planes[1].share()
    for d in range(3, n):
        lines[0].step(d)
    planes[0].arrive()

    def gate_part(c, _):
        ch = pl.ds(pl.multiple_of(c * wide, wide), wide)
        part = _dot(flat, fg[:, :, ch].reshape(model, wide))
        gate[:, :, ch] = part.reshape(seqs, length, wide)
        return 0

    lax.fori_loop(0, width // wide, gate_part, 0)
    for d in range(3, n):
        lines[1].step(d)
    planes[1].arrive()
    own.wait()

    @pl.when(seq == 0)
    def _():
        handed.wait_send()
        for c in ends:
            c.wait_send()

    @pl.when(seq == 1)
    def _():
        handed.wait_recv()

    for line in lines:
        line.finish()
    for plane in planes:
        plane.finish()


def _mixer_call(kernel, ins, outs, scratch, name, cost, number, far=()):
    vm = pl.BlockSpec(memory_space=pltpu.VMEM)
    return pl.pallas_call(
        kernel,
        out_shape=outs,
        in_specs=[
            pl.BlockSpec(memory_space=pltpu.HBM if i in far else pltpu.VMEM) for i in range(len(ins))
        ],
        out_specs=(vm,) * len(outs),
        scratch_shapes=scratch,
        compiler_params=pltpu.CompilerParams(
            collective_id=number, has_side_effects=True, vmem_limit_bytes=28 << 20
        ),
        cost_estimate=pl.CostEstimate(flops=cost, bytes_accessed=1 << 20, transcendentals=0),
        name=name,
    )(*ins)


def mix_fwd(n, seg, seg_old, hp, taps_i, bias_i, taps_s, bias_s, cot, wo, wg, normed, wi, ws, wt):
    seqs, length, model = normed.shape
    width = wi.shape[2]
    sd = jax.ShapeDtypeStruct
    return _mixer_call(
        functools.partial(mix_fwd_kernel, n),
        (seg, seg_old, hp, taps_i, bias_i, taps_s, bias_s, cot, wo, wg, normed, wi, ws, wt),
        (
            sd((seqs, length, width), F32),
            sd((seqs, length, width), F32),
            sd((seqs, length, 2 * STATE), F32),
            sd((seqs, length, LANES), F32),
            sd((seqs, STATE, width), BF),
            sd((seqs, length, width), F32),
            sd((seqs, length, model), BF),
            sd((8,) + wo.shape, BF),
            sd((8,) + wg.shape, BF),
            sd((seqs, length, width), BF),
            sd((seqs, length, 2 * STATE), BF),
            sd((seqs, 16, width), BF),
            sd((seqs, 16, 2 * STATE), BF),
            sd((seqs, length, LANES), F32),
            sd((seqs, 8, length), F32),
        ),
        [
            pltpu.VMEM((8 + length, LANES), F32),
            pltpu.VMEM((length, 3 * LANES), BF),
            pltpu.VMEM((LANES, length), F32),
            pltpu.VMEM((length, length), F32),
            pltpu.VMEM((length, length), F32),
            pltpu.VMEM((2, length, 2 * LANES), BF),
            pltpu.VMEM((seqs, STATE, width), BF),
            pltpu.SemaphoreType.DMA((seqs, 2, n)),
            pltpu.SemaphoreType.DMA((seqs, n)),
            pltpu.SemaphoreType.DMA((2, 7)),
            pltpu.SemaphoreType.DMA((2, 7)),
            pltpu.SemaphoreType.DMA((3,)),
            pltpu.SemaphoreType.DMA((6,)),
        ],
        "mix_fwd",
        30 * 10**9,
        3,
        (7, 8, 9),
    )


def gate_kernel(n, y_part, u_s, entry, h0, gate, cot, wo, gain, tokens_in,
                d_mixed, d_gate, lam, po, go, gg, g_gain,
                mixed, gated, grad_gn, normed, local, acc, box, ss, rs, hs):
    dp, seq, t = lax.axis_index("dp"), lax.axis_index("seq"), lax.axis_index("tensor")
    seqs, length, width = y_part.shape
    model = cot.shape[2]
    wide = 2 * LANES
    bar = pltpu.get_barrier_semaphore()
    pl.semaphore_signal(bar, inc=1, device_id=_dev(dp, 1 - seq, t), device_id_type=MESH)
    for step in range(1, n):
        pl.semaphore_signal(
            bar, inc=1, device_id=_dev(dp, seq, lax.rem(t + step, n)), device_id_type=MESH
        )
    acc[...] = jnp.zeros_like(acc)
    g_gain[...] = jnp.zeros_like(g_gain)

    def spread_of(s, c):
        heads = _split(entry[s], 2)
        head = lax.rem(_iota((wide, wide), 0), LANES)
        one = head == 4 * c + lax.div(_iota((wide, wide), 1), HEAD_DIM)
        return _dot(heads, one.astype(F32).astype(BF))

    def maps(s):
        u = u_s[s, :, STATE:]
        return (u * _sig(u)).astype(BF)

    def first(c, _):
        ch = pl.ds(pl.multiple_of(c * wide, wide), wide)
        at = pl.ds(pl.multiple_of(t * width + c * wide, wide), wide)
        w = wo[:, :, ch].reshape(model, wide)
        for s in range(seqs):
            g = _dot(cot[s], w)
            grad_gn[s, :, ch] = g
            m = y_part[s, :, ch] + spread_of(s, c) * _dot(maps(s), h0[s, :, ch])
            z = gate[s, :, ch]
            gd = m * (z * _sig(z))
            mixed[s, :, ch] = m
            gated[s, :, ch] = gd
            sq, ds = gd * gd, g * gain[:, at] * gd
            acc[0, s] += sq[:, :LANES] + sq[:, LANES:]
            acc[1, s] += ds[:, :LANES] + ds[:, LANES:]
        return 0

    lax.fori_loop(0, width // wide, first, 0)
    ones = jnp.ones((8, wide), F32).astype(BF)
    row = _iota((8, length), 0)
    mine = jnp.zeros((8, length), F32)
    for kind in range(2):
        for s in range(seqs):
            sums = _dot(ones, _split(acc[kind, s], 2), 1, 1)
            mine = jnp.where(row == kind * seqs + s, sums, mine)
    box[t] = mine
    pl.semaphore_wait(bar, n)

    def copy(src, who):
        return pltpu.make_async_remote_copy(
            src_ref=box.at[src], dst_ref=box.at[src], send_sem=ss.at[who], recv_sem=rs.at[src],
            device_id=_dev(dp, seq, who), device_id_type=MESH,
        )

    for o in range(n):
        @pl.when(t != o)
        def _(o=o):
            copy(t, o).start()
    for o in range(n):
        @pl.when(t != o)
        def _(o=o):
            copy(o, o).wait_recv()
    full_width = n * width
    cols = _marks(jnp.sum(box[...], axis=0) / full_width)

    def second(c, _):
        ch = pl.ds(pl.multiple_of(c * wide, wide), wide)
        at = pl.ds(pl.multiple_of(t * width + c * wide, wide), wide)
        gn = gain[:, at]
        for s in range(seqs):
            rms = lax.rsqrt(cols[:, s : s + 1] + EPS)
            mean = cols[:, seqs + s : seqs + s + 1]
            g, gd, m, z = grad_gn[s, :, ch], gated[s, :, ch], mixed[s, :, ch], gate[s, :, ch]
            sg = _sig(z)
            scaled = gd * rms
            normed[s, :, ch] = (scaled * gn).astype(BF)
            g_gain[0:1, ch] += jnp.sum(g * scaled, axis=0, keepdims=True)
            d_gd = rms * (g * gn) - scaled * (rms * rms * mean)
            dm = d_gd * (z * sg)
            d_mixed[s, :, ch] = dm
            d_gate[s, :, ch] = (d_gd * m * sg * (1.0 + z * (1.0 - sg))).astype(BF)
            ed = (spread_of(s, c) * dm).astype(BF)
            local[s, :, ch] = _dot(maps(s), ed, 0, 0).astype(BF)
        return 0

    lax.fori_loop(0, width // wide, second, 0)
    handed = pltpu.make_async_remote_copy(
        src_ref=local, dst_ref=lam, send_sem=hs.at[0], recv_sem=hs.at[1],
        device_id=_dev(dp, 1 - seq, t), device_id_type=MESH,
    )

    @pl.when(seq == 1)
    def _():
        handed.start()
        lam[...] = jnp.zeros_like(lam)

    blocks = 2
    rows = blocks * wo.shape[1]

    def third(b, _):
        ch = pl.ds(pl.multiple_of(b * rows, LANES), rows)
        w = wo[pl.ds(b * blocks, blocks)].reshape(rows, width)
        total = None
        for s in range(seqs):
            po[s, :, ch] = _dot(normed[s], w, 1, 1).astype(BF)
            part = _dot(cot[s, :, ch], normed[s], 0, 0)
            total = part if total is None else total + part
        go[pl.ds(b * blocks, blocks)] = total.reshape(blocks, wo.shape[1], width).astype(BF)
        total = None
        for s in range(seqs):
            part = _dot(tokens_in[s, :, ch], d_gate[s], 0, 0)
            total = part if total is None else total + part
        gg[pl.ds(b * blocks, blocks)] = total.reshape(blocks, wo.shape[1], width).astype(BF)
        return 0

    lax.fori_loop(0, model // rows, third, 0)

    @pl.when(seq == 1)
    def _():
        handed.wait_send()

    @pl.when(seq == 0)
    def _():
        handed.wait_recv()

    for o in range(n):
        @pl.when(t != o)
        def _(o=o):
            copy(o, o).wait_send()


def gate_stage(n, y_part, u_s, entry, h0, gate, cot, wo, gain, tokens_in):
    seqs, length, width = y_part.shape
    sd = jax.ShapeDtypeStruct
    whole = pltpu.VMEM((seqs, length, width), F32)
    return _mixer_call(
        functools.partial(gate_kernel, n),
        (y_part, u_s, entry, h0, gate, cot, wo, gain, tokens_in),
        (
            sd((seqs, length, width), F32),
            sd((seqs, length, width), BF),
            sd((seqs, STATE, width), BF),
            sd((seqs, length, cot.shape[2]), BF),
            sd(wo.shape, BF),
            sd(wo.shape, BF),
            sd((8, width), F32),
        ),
        [
            whole, whole, whole,
            pltpu.VMEM((seqs, length, width), BF),
            pltpu.VMEM((seqs, STATE, width), BF),
            pltpu.VMEM((2, seqs, length, LANES), F32),
            pltpu.VMEM((n, 8, length), F32),
            pltpu.SemaphoreType.DMA((n,)),
            pltpu.SemaphoreType.DMA((n,)),
            pltpu.SemaphoreType.DMA((2,)),
        ],
        "gate_stage",
        6 * 10**9,
        2,
    )


def mix_bwd_kernel(n, dy_r, u_i, u_s, pre_i, old_i, pre_s, old_s, raw, rows, h0, lam, hp,
                   taps_i, taps_s, po, go, gg,
                   d_i, d_s, d_raw, sm_i, sm_s, sm_h, o_po, o_go, o_gg,
                   pad, moved, run3, run_t, bias_m, scores, d_scores, heads_hl,
                   acc_r, acc_c, acc_d, acc_q, d_b, d_c, lo, ro, xo, bo, xg, bg,
                   head_i, tail_i, head_s, tail_s, next_i, next_s, zs, zr, ps, pr, hs):
    t = lax.axis_index("tensor")
    seqs, length, width = pre_i.shape
    pairs = width // LANES
    _plane_barrier(n)
    lines = _line_reduces(n, po, lo, ro, zs, zr)
    planes = (
        _PlaneReduce(go, xo, bo, ps.at[0], pr.at[0]), _PlaneReduce(gg, xg, bg, ps.at[1], pr.at[1])
    )
    for j in range(n - 1):
        for begin, _, _, _ in lines:
            begin(j)
    for plane in planes:
        plane.begin()
    sm_i[...] = jnp.zeros_like(sm_i)
    sm_s[...] = jnp.zeros_like(sm_s)
    sm_h[...] = jnp.zeros_like(sm_h)
    moved[0:8, :] = jnp.zeros((8, LANES), F32)
    moved[8 + length :, :] = jnp.zeros((8, LANES), F32)

    def conv_back(du, marks, taps, s, ch, d_o, head_o, tail_o, sm):
        total = None
        for k in range(KERNEL):
            m = du if k == 0 else du * marks[:, k : k + 1]
            moved[8 : 8 + length, :] = m
            sm[k : k + 1, ch] += jnp.sum(m * pad[8 - k : 8 - k + length, :], axis=0, keepdims=True)
            part = taps[k : k + 1, :] * moved[k : k + 8 + length, :]
            total = part if total is None else total + part
        sm[4:5, ch] += jnp.sum(du, axis=0, keepdims=True)
        head_o[s, :, ch] = total[0:8, :]
        d_o[s, :, ch] = total[8:, :].astype(BF)
        tail_o[s, :, ch] = total[length - 8 :, :]

    def one(s, _):
        rw = rows[s]
        marks = _marks(rw)
        v, delta, log_decay, running, entry, to_end = _head_scalars(raw[s], hp, marks, length)
        run3[...] = _split(running, 3)
        run_t[...] = running.T
        bias_m[...] = _bias_matrix(rw, marks, length)
        heads_hl[0] = _split(delta, 2)
        heads_hl[1] = _split(to_end, 2)
        heads_hl[2] = _split(entry, 2)
        ub, uc = u_s[s, :, :STATE], u_s[s, :, STATE:]
        sb, sc = _sig(ub), _sig(uc)
        b_map, c_map = (ub * sb).astype(BF), (uc * sc).astype(BF)
        scores[...] = _dot(c_map, b_map, 1, 1)
        d_scores[...] = jnp.zeros_like(d_scores)
        for acc in (acc_r, acc_c, acc_d, acc_q, d_b, d_c):
            acc[...] = jnp.zeros_like(acc)

        def pair(p, _):
            @pl.when(jnp.logical_and(s == 0, p == 3))
            def _():
                lines[0][1](1)

            @pl.when(jnp.logical_and(s == 0, p == 5))
            def _():
                for plane in planes:
                    plane.send_far()

            @pl.when(jnp.logical_and(s == 1, p == 0))
            def _():
                lines[1][1](1)

            @pl.when(jnp.logical_and(s == 1, p == 2))
            def _():
                lines[0][1](2)

            @pl.when(jnp.logical_and(s == 1, p == 3))
            def _():
                planes[0].send_near()

            @pl.when(jnp.logical_and(s == 1, p == 5))
            def _():
                lines[1][1](2)
                planes[1].send_near()

            ch = pl.ds(pl.multiple_of(p * LANES, LANES), LANES)
            at = pl.ds(pl.multiple_of(t * width + p * LANES, LANES), LANES)
            u = u_i[s, :, ch]
            sg = _sig(u)
            x = u * sg
            dy = dy_r[s, :, ch]
            spread, fold = _spreader(2 * LANES, p), _folder(2 * LANES, p)
            dl = _dot(heads_hl[0], spread)
            q = _dot(heads_hl[1], spread)
            e = _dot(heads_hl[2], spread)
            xd = x * dl
            xb, db = xd.astype(BF), dy.astype(BF)
            h_in, l_in = h0[s, :, ch], lam[s, :, ch]
            c_h = _dot(c_map, h_in)
            b_l = _dot(b_map, l_in)
            qx, ed = q * xd, e * dy
            d_b[...] += _dot(qx.astype(BF), l_in, 1, 1)
            d_c[...] += _dot(ed.astype(BF), h_in, 1, 1)
            late = qx * b_l
            dxd = q * b_l
            lane = lax.div(_iota(xb.shape, 1), HEAD_DIM)
            for a in range(2):
                h = 2 * p + a
                pick = (lax.rem(_iota((3 * LANES, length), 0), LANES) == h).astype(F32).astype(BF)
                decay = jnp.exp(_dot(run3[...], pick) - run_t[pl.ds(h, 1), :] + bias_m[...])
                da = jnp.where(lane == a, db, jnp.zeros_like(db))
                ld = decay * _dot(da, xb, 1, 1)
                d_scores[...] += ld
                both = (ld * scores[...]).astype(BF)
                mixing = (decay * scores[...]).astype(BF)
                dxd = dxd + _dot(mixing, da, 0, 0)
                col = (_iota((length, LANES), 1) == h).astype(F32).astype(BF)
                row = (_iota((LANES, length), 0) == h).astype(F32).astype(BF)
                acc_r[...] += _dot(both, col)
                acc_c[...] += _dot(row, both)
            acc_r[...] += _dot(_split(ed * c_h - late, 2), fold)
            acc_d[...] += _dot(_split(dxd * x, 2), fold)
            total = jnp.broadcast_to(jnp.sum(late, axis=0, keepdims=True), (8, LANES))
            acc_q[...] += _dot(_split(total, 2), fold)
            skip = _dot(_split(hp[...], 2), spread)[2:3, :]
            sm_i[5:6, ch] += jnp.sum(dy * x, axis=0, keepdims=True)
            du = (dxd * dl + skip * dy) * (sg * (1.0 + u * (1.0 - sg)))
            pad[0:8, :] = old_i[s, :, ch].astype(F32)[8:16, :]
            pad[8:, :] = pre_i[s, :, ch].astype(F32)
            conv_back(du, marks, taps_i[:, at], s, ch, d_i, head_i, tail_i, sm_i)
            return 0

        lax.fori_loop(0, pairs, pair, 0)
        ds = d_scores[...].astype(BF)
        grads = (d_b[...] + _dot(ds, c_map, 0, 0), d_c[...] + _dot(ds, b_map))
        for half, (g, u, sg) in enumerate(zip(grads, (ub, uc), (sb, sc))):
            ch = slice(half * STATE, (half + 1) * STATE)
            pad[0:8, :] = old_s[s, :, ch].astype(F32)[8:16, :]
            pad[8:, :] = pre_s[s, :, ch].astype(F32)
            du = g * (sg * (1.0 + u * (1.0 - sg)))
            conv_back(du, marks, taps_s[:, ch], s, ch, d_s, head_s, tail_s, sm_s)
        d_run = acc_r[...] - acc_c[...].T
        last = _iota(d_run.shape, 0) == length - 1
        d_run = d_run + jnp.where(last, acc_q[0:1, :], 0.0)
        upper = (_iota((length, length), 0) <= _iota((length, length), 1)).astype(F32).astype(BF)
        d_log = _three(_dot(upper, _split(d_run, 3)))
        d_delta = acc_d[...] - d_log * jnp.exp(hp[1:2, :])
        d_step = d_delta * _sig(v)
        d_raw[s] = d_step.astype(BF)
        sm_h[0:1, :] += jnp.sum(d_step, axis=0, keepdims=True)
        sm_h[1:2, :] += jnp.sum(d_log * log_decay, axis=0, keepdims=True)
        return 0

    lax.fori_loop(0, seqs, one, 0)
    dp, seq = lax.axis_index("dp"), lax.axis_index("seq")
    handed = [
        pltpu.make_async_remote_copy(
            src_ref=a, dst_ref=b, send_sem=hs.at[2 * i], recv_sem=hs.at[2 * i + 1],
            device_id=_dev(dp, 1 - seq, t), device_id_type=MESH,
        )
        for i, (a, b) in enumerate(((head_i, next_i), (head_s, next_s)))
    ]

    @pl.when(seq == 1)
    def _():
        for c in handed:
            c.start()

    planes[0].final(o_go)

    @pl.when(seq == 0)
    def _():
        for c, box, tail, out in zip(handed, (next_i, next_s), (tail_i, tail_s), (d_i, d_s)):
            c.wait_recv()
            for s in range(seqs):
                more = jnp.concatenate([jnp.zeros_like(box[s]), box[s]], axis=0)
                out[s, length - 16 :, :] = (tail[s] + more).astype(BF)

    @pl.when(seq == 1)
    def _():
        for c in handed:
            c.wait_send()

    planes[1].final(o_gg)
    for s, (_, _, final, _) in enumerate(lines):
        final(o_po.at[pl.ds(s, 1)])
    for plane in planes:
        plane.finish()
    for _, _, _, finish in lines:
        finish()


def mix_bwd(n, dy, u_i, u_s, pre_i, old_i, pre_s, old_s, raw, rows, h0, lam, hp, taps_i, taps_s,
            po, go, gg):
    seqs, length, width = pre_i.shape
    model = po.shape[2]
    box = pltpu.VMEM((n, seqs, length // n, model), BF)
    sd = jax.ShapeDtypeStruct
    square = pltpu.VMEM((length, length), F32)
    tall = pltpu.VMEM((length, LANES), F32)
    return _mixer_call(
        functools.partial(mix_bwd_kernel, n),
        (dy, u_i, u_s, pre_i, old_i, pre_s, old_s, raw, rows, h0, lam, hp, taps_i, taps_s, po, go,
         gg),
        (
            sd((seqs, length, width), BF),
            sd((seqs, length, 2 * STATE), BF),
            sd((seqs, length, LANES), BF),
            sd((8, width), F32),
            sd((8, 2 * STATE), F32),
            sd((8, LANES), F32),
            sd((seqs, length // n, model), F32),
            sd(go.shape[1:], F32),
            sd(gg.shape[1:], F32),
        ),
        [
            pltpu.VMEM((8 + length, LANES), F32),
            pltpu.VMEM((16 + length, LANES), F32),
            pltpu.VMEM((length, 3 * LANES), BF),
            pltpu.VMEM((LANES, length), F32),
            square, square, square,
            pltpu.VMEM((3, length, 2 * LANES), BF),
            tall, pltpu.VMEM((LANES, length), F32), tall, pltpu.VMEM((8, LANES), F32), tall, tall,
            box, box,
            pltpu.VMEM((4,) + go.shape[1:], BF),
            pltpu.VMEM((3,) + go.shape[1:], BF),
            pltpu.VMEM((4,) + gg.shape[1:], BF),
            pltpu.VMEM((3,) + gg.shape[1:], BF),
            pltpu.VMEM((seqs, 8, width), F32),
            pltpu.VMEM((seqs, 16, width), F32),
            pltpu.VMEM((seqs, 8, 2 * STATE), F32),
            pltpu.VMEM((seqs, 16, 2 * STATE), F32),
            pltpu.VMEM((seqs, 8, width), F32),
            pltpu.VMEM((seqs, 8, 2 * STATE), F32),
            pltpu.SemaphoreType.DMA((seqs, 2, n)),
            pltpu.SemaphoreType.DMA((seqs, 2, n)),
            pltpu.SemaphoreType.DMA((2, 7)),
            pltpu.SemaphoreType.DMA((2, 7)),
            pltpu.SemaphoreType.DMA((4,)),
        ],
        "mix_bwd",
        8 * 10**9,
        4,
    )


def reduce_kernel(n, normed, dg, di, ds, dr, wg, wi, ws, wt, gain, sm_i, sm_s, sm_h, g_gain,
                  o_pg, o_gi, o_gs, o_gt, o_sm,
                  pg, gi, gs, gt, lg, rg, xi, xs, xt, bi, bs, bt, mb,
                  xp, xb, xo2, zs, zr, ps, pr, ms, mr, es, er):
    _plane_barrier(n)
    seqs, length, width = di.shape
    model = normed.shape[2]
    blocks = 2
    rows = blocks * wi.shape[1]
    small = _Smalls(n, mb, o_sm, ms, mr)
    mb[0] = jnp.zeros(mb.shape[1:], F32)
    mb[0, 0:6, :] = sm_i[0:6, :]
    mb[0, 6:7, :] = g_gain[0:1, :]
    for k in range(5):
        at = 256 * (k % 3)
        mb[0, 9 + k // 3 : 10 + k // 3, at : at + 256] = sm_s[k : k + 1, :]
    mb[0, 10:11, 512:640] = sm_h[0:1, :]
    mb[0, 10:11, 640:768] = sm_h[1:2, :]

    lines = _line_reduces(n, pg, lg, rg, zs, zr)
    totals = [None] * (model // rows)
    for s in range(seqs):
        for b in range(model // rows):
            ch = slice(b * rows, (b + 1) * rows)
            near = slice(b * blocks, (b + 1) * blocks)
            part = None
            for d, w in zip((dg, di, ds, dr), (wg, wi, ws, wt)):
                more = _dot(d[s], w[near].reshape(rows, w.shape[2]), 1, 1)
                part = more if part is None else part + more
            pg[s, :, ch] = part.astype(BF)
            part = jnp.sum(part * normed[s, :, ch].astype(F32), axis=0, keepdims=True)
            totals[b] = part if totals[b] is None else totals[b] + part
        lines[s][0](0)
    for b, total in enumerate(totals):
        ch = slice(b * rows, (b + 1) * rows)
        mb[0, 7 + b // 2 : 8 + b // 2, (b % 2) * rows : (b % 2 + 1) * rows] = total / gain[:, ch]
    small.copy(0, small.near(0)).start()
    for j in range(1, n - 2):
        for line in lines:
            line[0](j)
    planes = [
        _PlaneReduce(part, pair, box, ps.at[i], pr.at[i])
        for i, (part, pair, box) in enumerate(((gs, xs, bs), (gt, xt, bt), (gi, xi, bi)))
    ]

    def weight(d, out):
        def one(b, _):
            ch = pl.ds(pl.multiple_of(b * rows, LANES), rows)
            total = None
            for s in range(seqs):
                part = _dot(normed[s, :, ch], d[s], 0, 0)
                total = part if total is None else total + part
            out[pl.ds(b * blocks, blocks)] = total.reshape(
                blocks, wi.shape[1], d.shape[2]
            ).astype(BF)
            return 0

        lax.fori_loop(0, model // rows, one, 0)

    weight(ds, gs)
    planes[0].begin()
    weight(dr, gt)
    planes[1].begin()
    small.step(0)
    weight(di, gi)
    planes[2].begin()
    lines[0][1](1)
    small.step(1)
    small.step(2)
    for line in lines:
        line[0](n - 2)
    lines[1][1](1)
    for p in planes:
        p.send_far()
    lines[0][1](2)
    for p in planes[:2]:
        p.send_near()
    planes[0].final(o_gs)
    planes[1].final(o_gt)
    quarter = xp.shape[1]
    for o in range(n):
        xp[o] = o_gs[o * quarter : (o + 1) * quarter, :].astype(BF)
    state = _LineSum(n, xp, xb, xo2, es, er)
    state.scatter()
    planes[2].send_near()
    lines[1][1](2)
    state.gather()
    planes[2].final(o_gi)
    small.final()
    for s, (_, _, final, _) in enumerate(lines):
        final(o_pg.at[pl.ds(s, 1)])
    state.arrive()
    for o in range(n):
        o_gs[o * quarter : (o + 1) * quarter, :] = xo2[o].astype(F32)
    for p in planes:
        p.finish()
    state.finish()
    small.finish()
    for _, _, _, finish in lines:
        finish()


def reduce_all(n, normed, dg, di, ds, dr, wg, wi, ws, wt, gain, sm_i, sm_s, sm_h, g_gain):
    seqs, length, model = normed.shape
    rows = length // n
    sd = jax.ShapeDtypeStruct
    box = pltpu.VMEM((n, seqs, rows, model), BF)
    quarter = pltpu.VMEM((n, ws.shape[1] // n, ws.shape[2]), BF)
    sums = (16, wi.shape[2])
    return _mixer_call(
        functools.partial(reduce_kernel, n),
        (normed, dg, di, ds, dr, wg, wi, ws, wt, gain, sm_i, sm_s, sm_h, g_gain),
        (sd((seqs, rows, model), F32),)
        + tuple(sd(w.shape[1:], F32) for w in (wi, ws, wt))
        + (sd((n,) + sums, F32),),
        [pltpu.VMEM((seqs, length, model), BF)]
        + [pltpu.VMEM(w.shape, BF) for w in (wi, ws, wt)]
        + [box, box]
        + [pltpu.VMEM((4,) + w.shape[1:], BF) for w in (wi, ws, wt)]
        + [pltpu.VMEM((3,) + w.shape[1:], BF) for w in (wi, ws, wt)]
        + [
            pltpu.VMEM((6,) + sums, F32),
            quarter, quarter, quarter,
            pltpu.SemaphoreType.DMA((seqs, 2, n)),
            pltpu.SemaphoreType.DMA((seqs, 2, n)),
            pltpu.SemaphoreType.DMA((3, 7)),
            pltpu.SemaphoreType.DMA((3, 7)),
            pltpu.SemaphoreType.DMA((3 + n,)),
            pltpu.SemaphoreType.DMA((3 + n,)),
            pltpu.SemaphoreType.DMA((2, n)),
            pltpu.SemaphoreType.DMA((2, n)),
        ],
        "reduce_all",
        6 * 10**9,
        1,
    )


def emit_kernel(n, heads, tok, cot, gain, branch, rows, gg, gi, gs, gt, go, sms,
                block_out, g_tok, g_in, o_gg, o_gi, o_gs, o_gt, o_ci, o_ib, o_cs, o_sb,
                o_shift, o_rate, o_skip, o_gain, o_go):
    for s in range(tok.shape[0]):
        v = tok[s].astype(F32)
        rms = lax.rsqrt(jnp.mean(v * v, axis=-1, keepdims=True) + EPS)
        block_out[s] = (v + branch[s]).astype(BF)
        scaled = rows[s] * gain[...]
        mean = jnp.mean(scaled * v, axis=-1, keepdims=True)
        g_tok[s] = cot[s].astype(F32) + rms * scaled - v * (rms * rms * rms * mean)
    o_gg[...] = gg[...]
    o_gi[...] = gi[...]
    o_gs[...] = gs[...]
    short = jnp.zeros((256 - gt.shape[0], LANES), F32)
    o_gt[...] = jnp.concatenate([gt[...], short], axis=0).T[:heads, : gt.shape[0]]
    o_go[...] = go[...]
    width = sms.shape[2]
    shared = None
    head_rows = None
    for t in range(n):
        ch = slice(t * width, (t + 1) * width)
        o_ci[:, ch] = sms[t, 0:4, :]
        o_ib[:, ch] = sms[t, 4:5, :]
        o_gain[:, ch] = sms[t, 6:7, :]
        block = sms[t, 8:16, :]
        shared = sms[t, 7:11, :] if shared is None else shared + sms[t, 7:11, :]
        lanes = _iota((3 * width, LANES), 0)
        chan = lax.rem(lanes, width)
        to = _iota((3 * width, LANES), 1) == heads * t + lax.div(chan, HEAD_DIM)
        skips = _dot(_split(sms[t, 0:8, :], 3), to.astype(F32).astype(BF))
        lanes = lax.rem(_iota((3 * LANES, LANES), 0), LANES)
        to = (_iota((3 * LANES, LANES), 1) == heads * t + lanes) & (lanes < heads)
        to = to.astype(F32).astype(BF)
        shift = _dot(_split(block[:, 512:640], 3), to)
        rate = _dot(_split(block[:, 640:768], 3), to)
        new = (skips[5:6, :], shift[2:3, :], rate[2:3, :])
        head_rows = new if head_rows is None else tuple(a + b for a, b in zip(head_rows, new))
    every = n * heads
    o_skip[...] = head_rows[0][:, :every]
    o_shift[...] = head_rows[1][:, :every]
    o_rate[...] = head_rows[2][:, :every]
    g_in[:, :width] = shared[0:1, :]
    g_in[:, width:] = shared[1:2, :]
    for k in range(4):
        at = 256 * (k % 3)
        o_cs[k : k + 1, :] = shared[2 + k // 3 : 3 + k // 3, at : at + 256]
    o_sb[...] = shared[3:4, 256:512]


def emit_all(n, heads, tok, cot, gain, branch, rows, gg, gi, gs, gt, go, sms):
    vm = pl.BlockSpec(memory_space=pltpu.VMEM)
    sd = lambda *shape: jax.ShapeDtypeStruct(shape, F32)
    width = sms.shape[2]
    outs = (
        jax.ShapeDtypeStruct(tok.shape, BF), sd(*tok.shape), sd(1, tok.shape[2]),
        sd(*gg.shape), sd(*gi.shape), sd(*gs.shape), sd(heads, gt.shape[0]),
        sd(4, n * width), sd(1, n * width), sd(4, 2 * STATE), sd(1, 2 * STATE),
        sd(1, n * heads), sd(1, n * heads), sd(1, n * heads), sd(1, n * width),
        sd(*go.shape),
    )
    return pl.pallas_call(
        functools.partial(emit_kernel, n, heads),
        out_shape=outs,
        in_specs=[vm] * 11,
        out_specs=(vm,) * len(outs),
        compiler_params=pltpu.CompilerParams(vmem_limit_bytes=28 << 20),
        name="emit_all",
    )(tok, cot, gain, branch, rows, gg, gi, gs, gt, go, sms)


def per_device(
    tokens,
    segments,
    input_gain,
    gate_proj,
    inner_proj,
    state_proj,
    step_proj,
    conv_inner,
    inner_bias,
    conv_state,
    state_bias,
    step_bias,
    log_rates,
    skip_gain,
    gated_gain,
    output_proj,
    cotangent,
):
    tensor_count = lax.axis_size("tensor")
    tensor_rank = lax.axis_index("tensor")
    residual = tokens.astype(jnp.float32)
    rms_in = lax.rsqrt(jnp.mean(residual * residual, axis=-1, keepdims=True) + EPS)
    normed_own = (residual * rms_in * input_gain).astype(jnp.bfloat16)
    normed, cot_rows = (
        lax.all_gather(normed_own, "tensor", axis=1, tiled=True),
        lax.all_gather(cotangent, "tensor", axis=1, tiled=True),
    )
    gate_full, inner_full, state_full, step_full, output_full = (
        lax.all_gather(gate_proj, ("dp", "seq"), axis=0, tiled=True),
        lax.all_gather(inner_proj, ("dp", "seq"), axis=0, tiled=True),
        lax.all_gather(state_proj, ("dp", "seq"), axis=0, tiled=True),
        lax.all_gather(step_proj, ("dp", "seq"), axis=0, tiled=True),
        lax.all_gather(output_proj, ("dp", "seq"), axis=1, tiled=True),
    )
    gate_in = jnp.dot(normed, gate_full, preferred_element_type=jnp.float32)
    inner_low = jnp.dot(normed, inner_full, preferred_element_type=jnp.float32).astype(jnp.bfloat16)
    state_low = jnp.dot(normed, state_full, preferred_element_type=jnp.float32).astype(jnp.bfloat16)
    step_raw = jnp.dot(normed, step_full, preferred_element_type=jnp.float32)
    margin = KERNEL - 1
    seg_float = segments.astype(jnp.float32)
    prior_inner, prior_state, prior_seg = passed_along(
        (
            inner_low[:, -margin:],
            state_low[:, -margin:],
            seg_float[:, -margin:].astype(jnp.bfloat16),
        ),
        "seq",
        1,
    )
    padded_inner = jnp.concatenate([prior_inner, inner_low], axis=1).astype(jnp.float32)
    padded_state = jnp.concatenate([prior_state, state_low], axis=1).astype(jnp.float32)
    seg_padded = jnp.concatenate([prior_seg.astype(jnp.float32), seg_float], axis=1)
    pieces = segments.shape[1] // BLOCK
    seg_blocks = blocked(seg_float, pieces)
    before = jnp.concatenate(
        [prior_seg[:, -1:].astype(jnp.float32), seg_blocks[:, :-1, -1]], axis=1
    )
    width_here = inner_full.shape[1]
    heads_here = step_full.shape[1]
    chan_start = tensor_rank * width_here
    head_start = tensor_rank * heads_here
    kernel_here = lax.dynamic_slice_in_dim(conv_inner, chan_start, width_here, 1)
    bias_here = lax.dynamic_slice_in_dim(inner_bias, chan_start, width_here, 0)
    gain_here = lax.dynamic_slice_in_dim(gated_gain, chan_start, width_here, 0)
    shift_here = lax.dynamic_slice_in_dim(step_bias, head_start, heads_here, 0)
    rates_here = lax.dynamic_slice_in_dim(log_rates, head_start, heads_here, 0)
    skip_here = lax.dynamic_slice_in_dim(skip_gain, head_start, heads_here, 0)

    def mixer_front(
        pad_inner, pad_state, raw_steps, kernel_w, kernel_b, state_w, state_b, step_shift, rate_logs
    ):
        inner = jax.nn.silu(causal_mix(pad_inner, seg_padded, kernel_w, kernel_b))
        inner = inner.reshape(inner.shape[0], inner.shape[1], -1, HEAD_DIM)
        both_maps = jax.nn.silu(causal_mix(pad_state, seg_padded, state_w, state_b))
        b_proj = both_maps[:, :, :STATE]
        c_proj = both_maps[:, :, STATE:]
        deltas = jax.nn.softplus(raw_steps + step_shift)
        log_decay = deltas * -jnp.exp(rate_logs)
        inflow, passing = block_sums(inner, deltas, log_decay, b_proj, seg_blocks, before)
        return (inner, deltas, log_decay, b_proj, c_proj, inflow, passing)

    def mixer_rear(inner, deltas, log_decay, b_proj, c_proj, inflow, passing, incoming, skips):
        running = jnp.cumsum(blocked(log_decay, pieces), axis=2)
        places = jnp.arange(running.shape[2])
        allowed = (seg_blocks[:, :, :, None] == seg_blocks[:, :, None, :]) & (
            places[:, None] >= places[None, :]
        )
        inside = allowed[..., None]
        decays = jnp.where(
            inside,
            jnp.exp(jnp.where(inside, running[:, :, :, None, :] - running[:, :, None, :, :], 0.0)),
            0.0,
        )
        scores = jnp.einsum(
            "scin,scjn->scij", blocked(c_proj, pieces), blocked(b_proj, pieces), precision=HIGH
        )
        mixing = decays * scores[..., None] * blocked(deltas, pieces)[:, :, None, :, :]
        direct = jnp.einsum("scijh,scjhp->scihp", mixing, blocked(inner, pieces), precision=HIGH)
        from_state, outgoing = state_reads(
            incoming, log_decay, c_proj, inflow, passing, seg_blocks, before
        )
        heads_out = (direct + from_state).reshape(inner.shape) + skips[:, None] * inner
        return (heads_out.reshape(inner.shape[0], inner.shape[1], -1), outgoing)

    front_args = (
        padded_inner,
        padded_state,
        step_raw,
        kernel_here,
        bias_here,
        conv_state,
        state_bias,
        shift_here,
        rates_here,
    )
    front_vals = mixer_front(*front_args)
    inner, deltas, log_decay, b_proj, c_proj, inflow, passing = front_vals
    span_decay = jnp.ones(passing[:, 0].shape, jnp.float32)
    span_state = jnp.zeros(inflow[:, 0].shape, jnp.float32)
    span_state = passing[:, 0, :, None, None] * span_state + inflow[:, 0]
    span_decay = span_decay * passing[:, 0]
    identity = (jnp.ones_like(span_decay), jnp.zeros_like(span_state))
    incoming = entering_2((span_decay, span_state), "seq", chain_link, identity)[1]
    mixed, outgoing = mixer_rear(*front_vals, incoming, skip_here)
    sigmoid_z = jax.nn.sigmoid(gate_in)
    silu_z = gate_in * sigmoid_z
    gated = mixed * silu_z
    full_width = tensor_count * gated.shape[-1]
    square_sum = lax.psum(jnp.sum(gated * gated, axis=-1), "tensor")
    rms_gate = lax.rsqrt(square_sum / full_width + EPS)[..., None]
    gate_normed = (gated * rms_gate * gain_here).astype(jnp.bfloat16)
    partial_out = jnp.dot(gate_normed, output_full, preferred_element_type=jnp.float32)
    branch_rows = lax.psum_scatter(partial_out, "tensor", scatter_dimension=1, tiled=True)
    block_out = (residual + branch_rows).astype(jnp.bfloat16)
    grad_output = jnp.einsum(
        "srk,srd->kd", gate_normed, cot_rows, preferred_element_type=jnp.float32
    )
    grad_gn = jnp.einsum("srd,kd->srk", cot_rows, output_full, preferred_element_type=jnp.float32)
    scaled = grad_gn * gain_here
    dot_sum = lax.psum(jnp.sum(scaled * gated, axis=-1), "tensor")
    grad_gain_here = jnp.sum(grad_gn * gated * rms_gate, axis=(0, 1))
    grad_gated = rms_gate * scaled - gated * rms_gate**3 * (dot_sum / full_width)[..., None]
    grad_mixed = grad_gated * silu_z
    grad_gate_in = (grad_gated * mixed * sigmoid_z * (1.0 + gate_in * (1.0 - sigmoid_z))).astype(
        jnp.bfloat16
    )
    front_vals, front_back = jax.vjp(mixer_front, *front_args)
    unused_rear, rear_back = jax.vjp(mixer_rear, *front_vals, incoming, skip_here)
    inner, deltas, log_decay, b_proj, c_proj, inflow, passing = front_vals
    grad_blocks = blocked(grad_mixed.reshape(inner.shape), pieces)
    unused_reads, read_back = jax.vjp(
        lambda memory_in: state_reads(
            memory_in, log_decay, c_proj, inflow, passing, seg_blocks, before
        )[0],
        incoming,
    )
    local_grad = read_back(grad_blocks)[0]
    outgoing_grad = carried_in((span_decay, local_grad), "seq", chain_link, identity)[1]
    rear_grads = rear_back((grad_mixed, outgoing_grad))
    grad_skip_here = rear_grads[8]
    (
        pad_grad_inner,
        pad_grad_state,
        grad_step_raw,
        grad_kernel_here,
        grad_bias_here,
        grad_conv_state,
        grad_state_bias,
        grad_shift_here,
        grad_rates_here,
    ) = front_back(tuple(rear_grads[:7]))
    from_next_inner, from_next_state = passed_along(
        (pad_grad_inner[:, :margin], pad_grad_state[:, :margin]), "seq", -1
    )
    grad_inner_pre = jnp.concatenate(
        [pad_grad_inner[:, margin:-margin], pad_grad_inner[:, -margin:] + from_next_inner], axis=1
    )
    grad_state_part = jnp.concatenate(
        [pad_grad_state[:, margin:-margin], pad_grad_state[:, -margin:] + from_next_state], axis=1
    )
    grad_state_pre = lax.psum(grad_state_part, "tensor").astype(jnp.bfloat16)
    grad_inner_low = grad_inner_pre.astype(jnp.bfloat16)
    grad_step_low = grad_step_raw.astype(jnp.bfloat16)
    grad_normed = jnp.einsum(
        "srk,dk->srd", grad_gate_in, gate_full, preferred_element_type=jnp.float32
    )
    grad_normed = grad_normed + jnp.einsum(
        "srk,dk->srd", grad_inner_low, inner_full, preferred_element_type=jnp.float32
    )
    grad_normed = grad_normed + jnp.einsum(
        "srk,dk->srd", grad_step_low, step_full, preferred_element_type=jnp.float32
    )
    grad_rows = lax.psum_scatter(grad_normed, "tensor", scatter_dimension=1, tiled=True)
    own_rows = tokens.shape[1]
    state_mine = lax.dynamic_slice_in_dim(grad_state_pre, tensor_rank * own_rows, own_rows, 1)
    grad_rows = grad_rows + jnp.einsum(
        "srk,dk->srd", state_mine, state_full, preferred_element_type=jnp.float32
    )
    grad_gate_w = jnp.einsum(
        "srd,srk->dk", normed, grad_gate_in, preferred_element_type=jnp.float32
    )
    grad_inner_w = jnp.einsum(
        "srd,srk->dk", normed, grad_inner_low, preferred_element_type=jnp.float32
    )
    grad_state_w = jnp.einsum(
        "srd,srk->dk", normed, grad_state_pre, preferred_element_type=jnp.float32
    )
    grad_step_w = jnp.einsum(
        "srd,srk->dk", normed, grad_step_low, preferred_element_type=jnp.float32
    )
    shard_gate, shard_inner, shard_state, shard_step, shard_output = (
        lax.psum_scatter(grad_gate_w, ("dp", "seq"), scatter_dimension=0, tiled=True),
        lax.psum_scatter(grad_inner_w, ("dp", "seq"), scatter_dimension=0, tiled=True),
        lax.psum_scatter(grad_state_w, ("dp", "seq"), scatter_dimension=0, tiled=True),
        lax.psum_scatter(grad_step_w, ("dp", "seq"), scatter_dimension=0, tiled=True),
        lax.psum_scatter(grad_output, ("dp", "seq"), scatter_dimension=1, tiled=True),
    )
    scaled_in = grad_rows * input_gain
    grad_input_gain = jnp.sum(grad_rows * residual * rms_in, axis=(0, 1))
    grad_tokens = (
        cotangent.astype(jnp.float32)
        + rms_in * scaled_in
        - residual * rms_in**3 * jnp.mean(scaled_in * residual, axis=-1, keepdims=True)
    )

    def placed(whole, piece_grad, start, axis_number):
        return lax.dynamic_update_slice_in_dim(
            jnp.zeros_like(whole), piece_grad, start, axis_number
        )

    smalls = lax.psum(
        (
            grad_input_gain,
            placed(conv_inner, grad_kernel_here, chan_start, 1),
            placed(inner_bias, grad_bias_here, chan_start, 0),
            grad_conv_state,
            grad_state_bias,
            placed(step_bias, grad_shift_here, head_start, 0),
            placed(log_rates, grad_rates_here, head_start, 0),
            placed(skip_gain, grad_skip_here, head_start, 0),
            placed(gated_gain, grad_gain_here, chan_start, 0),
        ),
        ("dp", "seq", "tensor"),
    )
    return (
        block_out,
        grad_tokens,
        smalls[0],
        shard_gate,
        shard_inner,
        shard_state,
        shard_step,
        smalls[1],
        smalls[2],
        smalls[3],
        smalls[4],
        smalls[5],
        smalls[6],
        smalls[7],
        smalls[8],
        shard_output,
    )


def per_device_fast(
    tokens,
    segments,
    input_gain,
    gate_proj,
    inner_proj,
    state_proj,
    step_proj,
    conv_inner,
    inner_bias,
    conv_state,
    state_bias,
    step_bias,
    log_rates,
    skip_gain,
    gated_gain,
    output_proj,
    cotangent,
):
    tensor_count = lax.axis_size("tensor")
    tensor_rank = lax.axis_index("tensor")
    heads = step_proj.shape[1]
    gain_row = input_gain[None]
    normed, seg_old, s8, t8, i8 = gather_all(
        tensor_count, tokens, gain_row, segments, (state_proj, step_proj.T, inner_proj)
    )
    heads_param = jnp.pad(
        lax.dynamic_slice_in_dim(
            jnp.stack([step_bias, log_rates, skip_gain]), tensor_rank * heads, heads, 1
        ),
        ((0, 5), (0, LANES - heads)),
    )
    (
        y_part, u_inner, u_state, entry, incoming, gate_in, cot_rows, o8, g8,
        inner_low, state_low, prior_inner, prior_state, step_raw, rows,
    ) = mix_fwd(
        tensor_count, segments, seg_old, heads_param,
        conv_inner, inner_bias[None], conv_state, state_bias[None],
        cotangent, output_proj.T, gate_proj, normed, i8, s8, t8,
    )
    grad_mixed, grad_gate_in, outgoing_grad, partial_out, grad_output, grad_gate, grad_gain = gate_stage(
        tensor_count, y_part, u_state, entry, incoming, gate_in, cot_rows, o8, gated_gain[None], normed
    )
    (
        d_inner, d_state, d_step, sm_i, sm_s, sm_h, branch_rows, shard_output, shard_gate
    ) = mix_bwd(
        tensor_count, grad_mixed, u_inner, u_state, inner_low, prior_inner, state_low, prior_state,
        step_raw, rows, incoming, outgoing_grad, heads_param, conv_inner, conv_state,
        partial_out, grad_output, grad_gate,
    )
    grad_rows, shard_inner, shard_state, shard_step, sms = reduce_all(
        tensor_count, normed, grad_gate_in, d_inner, d_state, d_step, g8, i8, s8, t8, gain_row,
        sm_i, sm_s, sm_h, grad_gain,
    )
    outs = emit_all(
        tensor_count, heads, tokens, cotangent, gain_row, branch_rows, grad_rows,
        shard_gate, shard_inner, shard_state, shard_step, shard_output, sms,
    )
    flat = (2, 8, 10, 11, 12, 13, 14)
    return tuple(
        o[0] if i in flat else o.T if i in (6, 15) else o for i, o in enumerate(outs)
    )


def solution(mesh):
    fast = mesh.shape["dp"] == 4 and mesh.shape["seq"] == 2
    placed = (
        P("dp", ("seq", "tensor"), None),
        P("dp", "seq"),
        P(),
        P(("dp", "seq"), "tensor"),
        P(("dp", "seq"), "tensor"),
        P(("dp", "seq"), None),
        P(("dp", "seq"), "tensor"),
        P(),
        P(),
        P(),
        P(),
        P(),
        P(),
        P(),
        P(),
        P("tensor", ("dp", "seq")),
        P("dp", ("seq", "tensor"), None),
    )
    return jax.shard_map(
        per_device_fast if fast else per_device,
        mesh=mesh,
        in_specs=placed,
        out_specs=(
            P("dp", ("seq", "tensor"), None),
            P("dp", ("seq", "tensor"), None),
            P(),
            P(("dp", "seq"), "tensor"),
            P(("dp", "seq"), "tensor"),
            P(("dp", "seq"), None),
            P(("dp", "seq"), "tensor"),
            P(),
            P(),
            P(),
            P(),
            P(),
            P(),
            P(),
            P(),
            P("tensor", ("dp", "seq")),
        ),
        check_vma=False,
    )
```

```python
import functools

import jax
import jax.numpy as jnp
from jax import lax
from jax.experimental import pallas as pl
from jax.experimental.pallas import tpu as pltpu
from jax.sharding import PartitionSpec as P

HEAD_DIM = 64
STATE = 128
KERNEL = 4
BLOCK = 256


EPS = 1e-05
HIGH = lax.Precision.HIGHEST


def passed_along(block, axis, distance):
    devices = range(lax.axis_size(axis))
    route = [(i - distance, i) for i in devices if i - distance in devices]
    return lax.ppermute(block, axis, route)


def entering_2(shard, axis, join, neutral):
    place = lax.axis_index(axis)
    gathered = jax.tree.map(
        lambda a, kind: lax.all_gather(a.astype(kind), axis), shard, (jnp.bfloat16, jnp.bfloat16)
    )
    state = jax.tree.map(lambda a, e: jnp.zeros_like(a) + jnp.asarray(e, a.dtype), shard, neutral)

    def one(hop, state):
        return join(
            state,
            jax.tree.map(
                lambda a, own: lax.dynamic_index_in_dim(a, hop, 0, False).astype(own.dtype),
                gathered,
                shard,
            ),
        )

    return lax.fori_loop(0, place, one, state)


def carried_in(shard, axis, combine, identity):
    length, here = (lax.axis_size(axis), lax.axis_index(axis))
    everything = jax.tree.map(
        lambda part, kind: lax.all_gather(part.astype(kind), axis),
        shard,
        jax.tree.map(lambda a: jnp.bfloat16 if a.dtype == jnp.float32 else a.dtype, shard),
    )
    start = jax.tree.map(
        lambda part, zero: jnp.broadcast_to(jnp.asarray(zero, part.dtype), part.shape),
        shard,
        identity,
    )

    def hop(k, before):
        at = length - 1 - k
        reached = at > here
        new = combine(
            before, jax.tree.map(lambda part, own: part[at].astype(own.dtype), everything, shard)
        )
        return jax.tree.map(lambda a, b: jnp.where(reached, a, b), new, before)

    return lax.fori_loop(0, length, hop, start)


def chain_link(earlier, later):
    return (earlier[0] * later[0], later[0][:, :, None, None] * earlier[1] + later[1])


def causal_mix(padded, seg_padded, kernel_w, kernel_b):
    margin = KERNEL - 1
    length = padded.shape[1] - margin
    seg_now = seg_padded[:, margin:]
    result = kernel_b + kernel_w[0] * padded[:, margin:]
    for offset in range(1, KERNEL):
        moved = padded[:, margin - offset : margin - offset + length]
        same_doc = (seg_padded[:, margin - offset : margin - offset + length] == seg_now).astype(
            jnp.float32
        )
        result = result + kernel_w[offset] * moved * same_doc[:, :, None]
    return result


def blocked(values, pieces):
    return values.reshape((values.shape[0], pieces, values.shape[1] // pieces) + values.shape[2:])


def block_sums(inner, deltas, log_decay, b_proj, seg_blocks, before):
    pieces = seg_blocks.shape[1]
    running = jnp.cumsum(blocked(log_decay, pieces), axis=2)
    same_end = (seg_blocks == seg_blocks[:, :, -1:]).astype(jnp.float32)
    to_end = (
        jnp.exp(running[:, :, -1:, :] - running) * same_end[:, :, :, None] * blocked(deltas, pieces)
    )
    inflow = jnp.einsum(
        "scjhp,scjn->schpn",
        to_end[..., None] * blocked(inner, pieces),
        blocked(b_proj, pieces),
        precision=HIGH,
    )
    passing = (
        jnp.exp(running[:, :, -1, :])
        * (seg_blocks[:, :, -1] == before).astype(jnp.float32)[:, :, None]
    )
    return (inflow, passing)


def state_reads(incoming, log_decay, c_proj, inflow, passing, seg_blocks, before):
    pieces = seg_blocks.shape[1]
    running = jnp.cumsum(blocked(log_decay, pieces), axis=2)
    memory = incoming
    entering = [memory]
    memory = passing[:, 0, :, None, None] * memory + inflow[:, 0]
    stacked = jnp.stack(entering, axis=1)
    entry = jnp.exp(running) * (seg_blocks == before[:, :, None]).astype(jnp.float32)[..., None]
    from_state = (
        jnp.einsum("scin,schpn->scihp", blocked(c_proj, pieces), stacked, precision=HIGH)
        * entry[..., None]
    )
    return (from_state, memory)


MESH = pl.DeviceIdType.MESH
BF = jnp.bfloat16
F32 = jnp.float32


def _peers():
    dp, seq, t = lax.axis_index("dp"), lax.axis_index("seq"), lax.axis_index("tensor")
    x, y = lax.rem(dp, 2), lax.div(dp, 2)
    x_dp = dp + 1 - 2 * x
    y_dp = dp + 2 - 4 * y
    d_dp = 3 - dp
    return dp, seq, t, x_dp, y_dp, d_dp


def _dev(dp, seq, t):
    return {"dp": dp, "seq": seq, "tensor": t}


def _plane_barrier(n):
    dp, seq, t, x_dp, y_dp, d_dp = _peers()
    bar = pltpu.get_barrier_semaphore()
    for who in (_dev(dp, 1 - seq, t), _dev(x_dp, seq, t), _dev(y_dp, seq, t)):
        pl.semaphore_signal(bar, inc=1, device_id=who, device_id_type=MESH)

    for step in range(1, n):
        pl.semaphore_signal(
            bar, inc=1, device_id=_dev(dp, seq, lax.rem(t + step, n)), device_id_type=MESH
        )
    pl.semaphore_wait(bar, 3 + n - 1)


class _Line:
    def __init__(self, n, ref, rows, ssem, rsem, own=None):
        self.n, self.ref, self.rows, self.ssem, self.rsem = n, ref, rows, ssem, rsem
        self.own = own

    def block(self, o):
        return self.ref.at[:, pl.ds(pl.multiple_of(o * self.rows, self.rows), self.rows), :]

    def copy(self, o, direction, own=False):
        dp, seq, t = lax.axis_index("dp"), lax.axis_index("seq"), lax.axis_index("tensor")
        return pltpu.make_async_remote_copy(
            src_ref=self.own if own else self.block(o),
            dst_ref=self.block(o),
            send_sem=self.ssem.at[0 if direction > 0 else 1, o],
            recv_sem=self.rsem.at[o],
            device_id=_dev(dp, seq, t + direction),
            device_id_type=MESH,
        )

    def step(self, d):
        n, t = self.n, lax.axis_index("tensor")
        for way in (1, -1):
            o = t - way * d
            here = jnp.logical_and(o >= 0, o < n)
            nxt = jnp.logical_and(t + way >= 0, t + way < n)

            @pl.when(here)
            def _(o=o, way=way, nxt=nxt):
                if d > 0:
                    self.copy(o, way).wait_recv()

                @pl.when(nxt)
                def _():
                    self.copy(o, way, d == 0 and self.own is not None).start()

    def finish(self):
        n, t = self.n, lax.axis_index("tensor")
        for d in range(n):
            for way in (1, -1):
                o = t - way * d
                ok = jnp.logical_and(
                    jnp.logical_and(o >= 0, o < n),
                    jnp.logical_and(t + way >= 0, t + way < n),
                )

                @pl.when(ok)
                def _(o=o, way=way):
                    self.copy(o, way).wait_send()


class _Plane:
    def __init__(self, own, full, ssem, rsem, lsem):
        self.own, self.full, self.ssem, self.rsem, self.lsem = own, full, ssem, rsem, lsem

    def copy(self, src, block, who, s):
        return pltpu.make_async_remote_copy(
            src_ref=src,
            dst_ref=self.full.at[block],
            send_sem=self.ssem.at[s],
            recv_sem=self.rsem.at[s],
            device_id=who,
            device_id_type=MESH,
        )

    def begin(self):
        dp, seq, t, x_dp, y_dp, d_dp = _peers()
        me = dp * 2 + seq
        pltpu.make_async_copy(self.own, self.full.at[me], self.lsem).start()
        self.copy(self.own, me, _dev(x_dp, seq, t), 0).start()
        self.copy(self.own, me, _dev(y_dp, seq, t), 1).start()
        self.copy(self.own, me, _dev(dp, 1 - seq, t), 3).start()

    def forward(self):
        dp, seq, t, x_dp, y_dp, d_dp = _peers()
        bx, by = x_dp * 2 + seq, y_dp * 2 + seq
        self.copy(self.own, bx, _dev(x_dp, seq, t), 0).wait_recv()
        self.copy(self.own, by, _dev(y_dp, seq, t), 1).wait_recv()

        @pl.when(seq == 0)
        def _():
            self.copy(self.full.at[by], by, _dev(x_dp, seq, t), 2).start()

        @pl.when(seq == 1)
        def _():
            self.copy(self.full.at[bx], bx, _dev(y_dp, seq, t), 2).start()

        self.copy(self.full.at[bx], bx, _dev(dp, 1 - seq, t), 4).start()
        self.copy(self.full.at[by], by, _dev(dp, 1 - seq, t), 5).start()

    def share(self):
        dp, seq, t, x_dp, y_dp, d_dp = _peers()
        bd = d_dp * 2 + seq
        self.copy(self.own, bd, _dev(x_dp, seq, t), 2).wait_recv()
        self.copy(self.full.at[bd], bd, _dev(dp, 1 - seq, t), 6).start()

    def arrive(self):
        dp, seq, t, x_dp, y_dp, d_dp = _peers()
        me = dp * 2 + seq
        pltpu.make_async_copy(self.own, self.full.at[me], self.lsem).wait()
        for s in (3, 4, 5, 6):
            self.copy(self.own, me, _dev(dp, 1 - seq, t), s).wait_recv()

    def finish(self):
        dp, seq, t, x_dp, y_dp, d_dp = _peers()
        me = dp * 2 + seq
        for s in range(7):
            self.copy(self.own, me, _dev(dp, 1 - seq, t), s).wait_send()


def gather_kernel(n, tok_far, gain, seg, ws, wt_t, wi, normed, seg_old, fs, ft, fi,
                  tok, wt, zs, zr, ps, pr, ls, hs):
    dp, seq, t = lax.axis_index("dp"), lax.axis_index("seq"), lax.axis_index("tensor")
    rows = tok.shape[1]
    near = pltpu.make_async_copy(tok_far, tok, ls.at[3])
    near.start()
    v = wt_t[...].astype(F32)
    v = jnp.concatenate([v, jnp.zeros((LANES - v.shape[0], v.shape[1]), F32)], axis=0)
    v = jnp.concatenate([v, jnp.zeros((LANES, 256 - v.shape[1]), F32)], axis=1)
    wt[...] = v.T[: wt.shape[0], :].astype(BF)
    _plane_barrier(n)
    planes = [
        _Plane(own, full, ps.at[i], pr.at[i], ls.at[i])
        for i, (own, full) in enumerate(((ws, fs), (wt, ft), (wi, fi)))
    ]
    handed = pltpu.make_async_remote_copy(
        src_ref=seg, dst_ref=seg_old, send_sem=hs.at[0], recv_sem=hs.at[1],
        device_id=_dev(dp, 1 - seq, t), device_id_type=MESH,
    )

    @pl.when(seq == 0)
    def _():
        handed.start()
        seg_old[...] = jnp.zeros_like(seg_old)

    for p in planes:
        p.begin()
    near.wait()
    mine = pl.ds(pl.multiple_of(t * rows, rows), rows)
    lines = []
    for s in range(tok.shape[0]):
        v = tok[s].astype(F32)
        rms = lax.rsqrt(jnp.mean(v * v, axis=-1, keepdims=True) + EPS)
        normed[s, mine, :] = (v * rms * gain[...]).astype(BF)
        lines.append(_Line(n, normed.at[pl.ds(s, 1)], rows, zs.at[s], zr.at[s]))
        lines[s].step(0)
    for line in lines:
        line.step(1)
    for p in planes:
        p.forward()
    lines[0].step(2)
    for p in planes:
        p.share()
    for line in lines[1:]:
        line.step(2)
    for d in range(3, n):
        for line in lines:
            line.step(d)
    for p in planes:
        p.arrive()

    @pl.when(seq == 0)
    def _():
        handed.wait_send()

    @pl.when(seq == 1)
    def _():
        handed.wait_recv()

    for line in lines:
        line.finish()
    for p in planes:
        p.finish()


def gather_all(n, tokens, gain, seg, weights):
    seqs, rows, width = tokens.shape
    vm = pl.BlockSpec(memory_space=pltpu.VMEM)
    far = pl.BlockSpec(memory_space=pltpu.HBM)
    wide = (weights[1].shape[1], LANES)
    full = lambda *shape: jax.ShapeDtypeStruct((8,) + shape, BF)
    act = jax.ShapeDtypeStruct((seqs, n * rows, width), BF)
    return pl.pallas_call(
        functools.partial(gather_kernel, n),
        out_shape=(
            act, jax.ShapeDtypeStruct(seg.shape, seg.dtype),
            full(*weights[0].shape), full(*wide), full(*weights[2].shape),
        ),
        in_specs=[far, vm, vm, far, vm, far],
        out_specs=(vm,) * 5,
        scratch_shapes=[
            pltpu.VMEM(tokens.shape, tokens.dtype),
            pltpu.VMEM(wide, BF),
            pltpu.SemaphoreType.DMA((seqs, 2, n)),
            pltpu.SemaphoreType.DMA((seqs, n)),
            pltpu.SemaphoreType.DMA((3, 7)),
            pltpu.SemaphoreType.DMA((3, 7)),
            pltpu.SemaphoreType.DMA((4,)),
            pltpu.SemaphoreType.DMA((2,)),
        ],
        compiler_params=pltpu.CompilerParams(
            collective_id=0, has_side_effects=True, vmem_limit_bytes=16 << 20
        ),
        cost_estimate=pl.CostEstimate(flops=30 * 10**9, bytes_accessed=1 << 20, transcendentals=0),
        name="gather_all",
    )(tokens, gain, seg, *weights)


def _line_reduce(n, part, left, right, ssem, rsem):
    dp, seq, t = lax.axis_index("dp"), lax.axis_index("seq"), lax.axis_index("tensor")
    rows = left.shape[2]

    def copy(src, box, o, way):
        return pltpu.make_async_remote_copy(
            src_ref=src, dst_ref=box.at[o],
            send_sem=ssem.at[0 if way > 0 else 1, o], recv_sem=rsem.at[0 if way > 0 else 1, o],
            device_id=_dev(dp, seq, t + way), device_id_type=MESH,
        )

    def block(o):
        return part.at[:, pl.ds(pl.multiple_of(o * rows, rows), rows), :]

    def begin(j):
        for way, box, place, o in ((1, left, t, n - 1 - j), (-1, right, n - 1 - t, j)):
            @pl.when(place == 0)
            def _():
                copy(block(o), box, o, way).start()

    def step(k):
        for way, box, place in ((1, left, t), (-1, right, n - 1 - t)):
            @pl.when(jnp.logical_and(place > 0, place <= k))
            def _():
                o = n - 1 - (k - place) if way > 0 else k - place
                copy(block(o), box, o, way).wait_recv()
                for s in range(part.shape[0]):
                    own = part[s, pl.ds(pl.multiple_of(o * rows, rows), rows), :].astype(F32)
                    box[o, s] = (box[o, s].astype(F32) + own).astype(BF)
                copy(box.at[o], box, o, way).start()

    def final(out):
        mine = pl.ds(pl.multiple_of(t * rows, rows), rows)
        for s in range(part.shape[0]):
            out[s] = part[s, mine, :].astype(F32)

        @pl.when(t > 0)
        def _():
            copy(left.at[0], left, t, 1).wait_recv()
            for s in range(part.shape[0]):
                out[s] = out[s] + left[t, s].astype(F32)

        @pl.when(t < n - 1)
        def _():
            copy(left.at[0], right, t, -1).wait_recv()
            for s in range(part.shape[0]):
                out[s] = out[s] + right[t, s].astype(F32)

    def finish():
        for j in range(n - 1):
            for way, box, o in ((1, left, n - 1 - j), (-1, right, j)):
                sends = (t < o) if way > 0 else (t > o)

                @pl.when(sends)
                def _():
                    copy(box.at[o], box, o, way).wait_send()

    return begin, step, final, finish


def _line_reduces(n, part, left, right, ssem, rsem):
    one = lambda s: pl.ds(s, 1)
    return [
        _line_reduce(
            n, part.at[one(s)], left.at[:, one(s)], right.at[:, one(s)], ssem.at[s], rsem.at[s]
        )
        for s in range(part.shape[0])
    ]


class _PlaneReduce:
    def __init__(self, part, pair, box, ssem, rsem):
        self.part, self.pair, self.box, self.ssem, self.rsem = part, pair, box, ssem, rsem

    def copy(self, src, dst, who, s):
        return pltpu.make_async_remote_copy(
            src_ref=src, dst_ref=dst, send_sem=self.ssem.at[s], recv_sem=self.rsem.at[s],
            device_id=who, device_id_type=MESH,
        )

    def begin(self):
        dp, seq, t, x_dp, y_dp, d_dp = _peers()
        for slot, chip in enumerate((d_dp, x_dp, y_dp, dp)):
            self.copy(self.part.at[chip * 2 + 1 - seq], self.pair.at[slot], _dev(dp, 1 - seq, t), slot).start()

    def _paired(self, slot, chip, also=None):
        dp, seq, t, x_dp, y_dp, d_dp = _peers()
        self.copy(self.pair.at[slot], self.pair.at[slot], _dev(dp, 1 - seq, t), slot).wait_recv()
        v = self.part[chip * 2 + seq].astype(F32) + self.pair[slot].astype(F32)
        self.pair[slot] = v.astype(BF)

    def send_far(self):
        dp, seq, t, x_dp, y_dp, d_dp = _peers()
        for slot, chip in enumerate((d_dp, x_dp, y_dp)):
            self._paired(slot, chip)
            if slot == 0:
                @pl.when(seq == 0)
                def _():
                    self.copy(self.pair.at[0], self.box.at[2], _dev(x_dp, seq, t), 4).start()

                @pl.when(seq == 1)
                def _():
                    self.copy(self.pair.at[0], self.box.at[2], _dev(y_dp, seq, t), 4).start()

        @pl.when(seq == 0)
        def _():
            self.copy(self.pair.at[1], self.box.at[0], _dev(x_dp, seq, t), 5).start()

        @pl.when(seq == 1)
        def _():
            self.copy(self.pair.at[2], self.box.at[1], _dev(y_dp, seq, t), 6).start()

    def send_near(self):
        dp, seq, t, x_dp, y_dp, d_dp = _peers()
        self.copy(self.pair.at[0], self.box.at[2], _dev(dp, seq, t), 4).wait_recv()

        @pl.when(seq == 0)
        def _():
            self.box[2] = (self.box[2].astype(F32) + self.pair[2].astype(F32)).astype(BF)
            self.copy(self.box.at[2], self.box.at[1], _dev(y_dp, seq, t), 6).start()

        @pl.when(seq == 1)
        def _():
            self.box[2] = (self.box[2].astype(F32) + self.pair[1].astype(F32)).astype(BF)
            self.copy(self.box.at[2], self.box.at[0], _dev(x_dp, seq, t), 5).start()

    def final(self, out):
        dp, seq, t, x_dp, y_dp, d_dp = _peers()
        self.copy(self.pair.at[3], self.pair.at[3], _dev(dp, seq, t), 3).wait_recv()
        self.copy(self.pair.at[0], self.box.at[0], _dev(dp, seq, t), 5).wait_recv()
        self.copy(self.pair.at[0], self.box.at[1], _dev(dp, seq, t), 6).wait_recv()
        out[...] = (
            self.part[dp * 2 + seq].astype(F32) + self.pair[3].astype(F32)
            + self.box[0].astype(F32) + self.box[1].astype(F32)
        )

    def finish(self):
        dp, seq, t, x_dp, y_dp, d_dp = _peers()
        for s in range(7):
            self.copy(self.pair.at[0], self.box.at[0], _dev(dp, 1 - seq, t), s).wait_send()


class _Smalls:
    def __init__(self, n, box, line, ssem, rsem):
        self.n, self.box, self.line, self.ssem, self.rsem = n, box, line, ssem, rsem

    def copy(self, j, who):
        return pltpu.make_async_remote_copy(
            src_ref=self.box.at[2 * j], dst_ref=self.box.at[2 * j + 1],
            send_sem=self.ssem.at[j], recv_sem=self.rsem.at[j],
            device_id=who, device_id_type=MESH,
        )

    def near(self, j):
        dp, seq, t, x_dp, y_dp, d_dp = _peers()
        return (_dev(dp, 1 - seq, t), _dev(x_dp, seq, t), _dev(y_dp, seq, t))[j]

    def begin(self, value):
        self.box[0] = value
        self.copy(0, self.near(0)).start()

    def step(self, j):
        self.copy(j, self.near(j)).wait_recv()
        total = self.box[2 * j] + self.box[2 * j + 1]
        if j < 2:
            self.box[2 * j + 2] = total
            self.copy(j + 1, self.near(j + 1)).start()
        else:
            t = lax.axis_index("tensor")
            self.line[t] = total.astype(self.line.dtype)
            for o in range(self.n):
                @pl.when(t != o)
                def _(o=o):
                    self.across(t, o).start()

    def across(self, src, who):
        dp, seq, t = lax.axis_index("dp"), lax.axis_index("seq"), lax.axis_index("tensor")
        return pltpu.make_async_remote_copy(
            src_ref=self.line.at[src], dst_ref=self.line.at[src],
            send_sem=self.ssem.at[3 + who], recv_sem=self.rsem.at[3 + src],
            device_id=_dev(dp, seq, who), device_id_type=MESH,
        )

    def final(self):
        t = lax.axis_index("tensor")
        for o in range(self.n):
            @pl.when(t != o)
            def _(o=o):
                self.across(o, o).wait_recv()

    def finish(self):
        t = lax.axis_index("tensor")
        for j in range(3):
            self.copy(j, self.near(j)).wait_send()
        for o in range(self.n):
            @pl.when(t != o)
            def _(o=o):
                self.across(t, o).wait_send()


class _LineSum:
    def __init__(self, n, part, box, out, ssem, rsem):
        self.n, self.part, self.box, self.out, self.ssem, self.rsem = n, part, box, out, ssem, rsem

    def copy(self, phase, src_block, dst_ref, who, origin):
        dp, seq = lax.axis_index("dp"), lax.axis_index("seq")
        return pltpu.make_async_remote_copy(
            src_ref=src_block, dst_ref=dst_ref,
            send_sem=self.ssem.at[phase, who], recv_sem=self.rsem.at[phase, origin],
            device_id=_dev(dp, seq, who), device_id_type=MESH,
        )

    def scatter(self):
        t = lax.axis_index("tensor")
        for o in range(self.n):
            @pl.when(t != o)
            def _(o=o):
                self.copy(0, self.part.at[o], self.box.at[t], o, t).start()

    def gather(self):
        t = lax.axis_index("tensor")
        total = self.part[t].astype(F32)
        for o in range(self.n):
            @pl.when(t != o)
            def _(o=o):
                self.copy(0, self.part.at[o], self.box.at[o], o, o).wait_recv()

            @pl.when(t == o)
            def _(o=o):
                self.box[o] = jnp.zeros(self.box.shape[1:], self.box.dtype)
        for o in range(self.n):
            total = total + self.box[o].astype(F32)
        self.out[t] = total.astype(self.out.dtype)
        for o in range(self.n):
            @pl.when(t != o)
            def _(o=o):
                self.copy(1, self.out.at[t], self.out.at[t], o, t).start()

    def arrive(self):
        t = lax.axis_index("tensor")
        for o in range(self.n):
            @pl.when(t != o)
            def _(o=o):
                self.copy(1, self.out.at[o], self.out.at[o], o, o).wait_recv()

    def finish(self):
        t = lax.axis_index("tensor")
        for o in range(self.n):
            @pl.when(t != o)
            def _(o=o):
                self.copy(0, self.part.at[o], self.box.at[o], o, o).wait_send()
                self.copy(1, self.part.at[o], self.box.at[o], o, o).wait_send()


LANES = 128


def _split(v, parts):
    out = []
    for _ in range(parts):
        b = v.astype(BF)
        out.append(b)
        v = v - b.astype(F32)
    return jnp.concatenate(out, axis=1)


def _dot(a, b, ca=1, cb=0):
    return lax.dot_general(a, b, (((ca,), (cb,)), ((), ())), preferred_element_type=F32)


def _iota(shape, axis):
    return lax.broadcasted_iota(jnp.int32, shape, axis)


def _spreader(rows, p):
    head = lax.rem(_iota((rows, LANES), 0), LANES)
    return (head == 2 * p + lax.div(_iota((rows, LANES), 1), HEAD_DIM)).astype(F32).astype(BF)


def _folder(rows, p):
    chan = lax.rem(_iota((rows, LANES), 0), LANES)
    return (_iota((rows, LANES), 1) == 2 * p + lax.div(chan, HEAD_DIM)).astype(F32).astype(BF)


def _sig(v):
    return 1.0 / (1.0 + jnp.exp(-v))


def _three(v):
    return v[:, :LANES] + v[:, LANES : 2 * LANES] + v[:, 2 * LANES :]


def _head_scalars(raw, hp, marks, length):
    v = raw + hp[0:1, :]
    delta = jnp.maximum(v, 0.0) + jnp.log1p(jnp.exp(-jnp.abs(v)))
    log_decay = -delta * jnp.exp(hp[1:2, :])
    lower = (_iota((length, length), 0) >= _iota((length, length), 1)).astype(F32).astype(BF)
    running = _three(_dot(lower, _split(log_decay, 3)))
    entry = jnp.exp(running) * marks[:, 4:5]
    to_end = jnp.exp(running[length - 1 :, :] - running) * marks[:, 5:6]
    return v, delta, log_decay, running, entry, to_end


def _marks(rows):
    full = jnp.concatenate([rows, jnp.zeros((LANES - rows.shape[0], rows.shape[1]), F32)], axis=0)
    return full.T


def _bias_matrix(rows, marks, length):
    ok = (_iota((length, length), 0) >= _iota((length, length), 1)) & (
        marks[:, 0:1] == rows[0:1, :]
    )
    return jnp.where(ok, 0.0, -1e30)


def _conv(pad, marks, taps, bias, length):
    total = bias + taps[0:1, :] * pad[8 : 8 + length, :]
    for k in range(1, KERNEL):
        total = total + taps[k : k + 1, :] * (pad[8 - k : 8 - k + length, :] * marks[:, k : k + 1])
    return total


def mix_fwd_kernel(n, seg, seg_old, hp, taps_i, bias_i, taps_s, bias_s, cot, wo, wg, normed, wi, ws, wt,
                   y, u_i, u_s, entry_o, incoming, gate, cot_full, fo, fg,
                   pre_i, pre_s, old_i, old_s, raw, rows,
                   pad, run3, run_t, bias_m, scores, heads_hl, inflow, zs, zr, ps, pr, ls, hs):
    dp, seq, t = lax.axis_index("dp"), lax.axis_index("seq"), lax.axis_index("tensor")
    seqs, length, width = pre_i.shape
    model = normed.shape[2]
    pairs = width // LANES
    wide = 2 * LANES
    _plane_barrier(n)
    lines = [
        _Line(n, cot_full.at[pl.ds(s, 1)], cot.shape[1], zs.at[s], zr.at[s], cot.at[pl.ds(s, 1)])
        for s in range(seqs)
    ]
    planes = (_Plane(wg, fg, ps.at[0], pr.at[0], ls.at[0]), _Plane(wo, fo, ps.at[1], pr.at[1], ls.at[1]))
    whole = _Line(n, cot_full, cot.shape[1], zs, zr)
    own = pltpu.make_async_copy(cot, whole.block(t), ls.at[2])
    own.start()
    for line in lines:
        line.step(0)
    for plane in planes:
        plane.begin()
    flat = normed[...].reshape(seqs * length, model)
    pre_s[...] = _dot(flat, ws[...].reshape(model, ws.shape[2])).astype(BF).reshape(pre_s.shape)

    def inner_part(c, _):
        ch = pl.ds(pl.multiple_of(c * wide, wide), wide)
        part = _dot(flat, wi[:, :, ch].reshape(model, wide))
        pre_i[:, :, ch] = part.astype(BF).reshape(seqs, length, wide)
        return 0

    lax.fori_loop(0, width // wide, inner_part, 0)
    ends = [
        pltpu.make_async_remote_copy(
            src_ref=a.at[:, pl.ds(length - 16, 16), :], dst_ref=b,
            send_sem=hs.at[2 + i], recv_sem=hs.at[4 + i],
            device_id=_dev(dp, 1 - seq, t), device_id_type=MESH,
        )
        for i, (a, b) in enumerate(((pre_i, old_i), (pre_s, old_s)))
    ]

    @pl.when(seq == 0)
    def _():
        for c in ends:
            c.start()
        old_i[...] = jnp.zeros_like(old_i)
        old_s[...] = jnp.zeros_like(old_s)

    raw[...] = _dot(flat, wt[...].reshape(model, LANES)).reshape(raw.shape)
    for s in range(seqs):
        now = seg[s : s + 1, :].astype(F32)
        old = seg_old[s : s + 1, :].astype(F32)
        both = jnp.broadcast_to(jnp.concatenate([old, now], axis=1), (8, 2 * length))
        here = jnp.broadcast_to(now, (8, length))
        place = _iota((8, length), 0)
        block = jnp.where(place == 0, here, 0.0)
        others = [pltpu.roll(both, k, 1)[:, length:] for k in range(1, KERNEL)]
        others += [both[:, length - 1 : length], both[:, 2 * length - 1 :]]
        for k, other in enumerate(others):
            block = jnp.where((place == k + 1) & (here == other), 1.0, block)
        rows[s] = block

    lines[0].step(1)

    @pl.when(seq == 1)
    def _():
        for c in ends:
            c.wait_recv()

    def one(s, _):
        rw = rows[s]
        marks = _marks(rw)
        v, delta, log_decay, running, entry, to_end = _head_scalars(raw[s], hp, marks, length)
        entry_o[s] = entry
        run3[...] = _split(running, 3)
        run_t[...] = running.T
        bias_m[...] = _bias_matrix(rw, marks, length)
        heads_hl[0] = _split(delta, 2)
        heads_hl[1] = _split(to_end, 2)
        maps = []
        for half in range(2):
            ch = slice(half * STATE, (half + 1) * STATE)
            pad[0:8, :] = old_s[s, :, ch].astype(F32)[8:16, :]
            pad[8:, :] = pre_s[s, :, ch].astype(F32)
            u = _conv(pad, marks, taps_s[:, ch], bias_s[:, ch], length)
            u_s[s, :, ch] = u
            maps.append((u * _sig(u)).astype(BF))
        b_map, c_map = maps
        scores[...] = _dot(c_map, b_map, 1, 1)

        def pair(p, _):
            @pl.when(jnp.logical_and(s == 0, p == 4))
            def _():
                lines[1].step(1)

            @pl.when(jnp.logical_and(s == 1, p == 0))
            def _():
                for plane in planes:
                    plane.forward()

            @pl.when(jnp.logical_and(s == 1, p == 1))
            def _():
                lines[0].step(2)

            @pl.when(jnp.logical_and(s == 1, p == 5))
            def _():
                lines[1].step(2)
                planes[0].share()

            ch = pl.ds(pl.multiple_of(p * LANES, LANES), LANES)
            at = pl.ds(pl.multiple_of(t * width + p * LANES, LANES), LANES)
            pad[0:8, :] = old_i[s, :, ch].astype(F32)[8:16, :]
            pad[8:, :] = pre_i[s, :, ch].astype(F32)
            u = _conv(pad, marks, taps_i[:, at], bias_i[:, at], length)
            u_i[s, :, ch] = u
            x = u * _sig(u)
            spread = _spreader(2 * LANES, p)
            xd = x * _dot(heads_hl[0], spread)
            inflow[s, :, ch] = _dot(b_map, (xd * _dot(heads_hl[1], spread)).astype(BF), 0, 0).astype(BF)
            skip = _dot(_split(hp[...], 2), spread)[2:3, :]
            total = skip * x
            xb = xd.astype(BF)
            lane = lax.div(_iota(xb.shape, 1), HEAD_DIM)
            for a in range(2):
                h = 2 * p + a
                pick = (lax.rem(_iota((3 * LANES, length), 0), LANES) == h).astype(F32).astype(BF)
                decay = jnp.exp(_dot(run3[...], pick) - run_t[pl.ds(h, 1), :] + bias_m[...])
                mixing = (decay * scores[...]).astype(BF)
                total = total + _dot(mixing, jnp.where(lane == a, xb, jnp.zeros_like(xb)))
            y[s, :, ch] = total
            return 0

        lax.fori_loop(0, pairs, pair, 0)
        return 0

    lax.fori_loop(0, seqs, one, 0)
    handed = pltpu.make_async_remote_copy(
        src_ref=inflow, dst_ref=incoming, send_sem=hs.at[0], recv_sem=hs.at[1],
        device_id=_dev(dp, 1 - seq, t), device_id_type=MESH,
    )

    @pl.when(seq == 0)
    def _():
        handed.start()
        incoming[...] = jnp.zeros_like(incoming)

    planes[1].share()
    for d in range(3, n):
        lines[0].step(d)
    planes[0].arrive()

    def gate_part(c, _):
        ch = pl.ds(pl.multiple_of(c * wide, wide), wide)
        part = _dot(flat, fg[:, :, ch].reshape(model, wide))
        gate[:, :, ch] = part.reshape(seqs, length, wide)
        return 0

    lax.fori_loop(0, width // wide, gate_part, 0)
    for d in range(3, n):
        lines[1].step(d)
    planes[1].arrive()
    own.wait()

    @pl.when(seq == 0)
    def _():
        handed.wait_send()
        for c in ends:
            c.wait_send()

    @pl.when(seq == 1)
    def _():
        handed.wait_recv()

    for line in lines:
        line.finish()
    for plane in planes:
        plane.finish()


def _mixer_call(kernel, ins, outs, scratch, name, cost, number, far=()):
    vm = pl.BlockSpec(memory_space=pltpu.VMEM)
    return pl.pallas_call(
        kernel,
        out_shape=outs,
        in_specs=[
            pl.BlockSpec(memory_space=pltpu.HBM if i in far else pltpu.VMEM) for i in range(len(ins))
        ],
        out_specs=(vm,) * len(outs),
        scratch_shapes=scratch,
        compiler_params=pltpu.CompilerParams(
            collective_id=number, has_side_effects=True, vmem_limit_bytes=28 << 20
        ),
        cost_estimate=pl.CostEstimate(flops=cost, bytes_accessed=1 << 20, transcendentals=0),
        name=name,
    )(*ins)


def mix_fwd(n, seg, seg_old, hp, taps_i, bias_i, taps_s, bias_s, cot, wo, wg, normed, wi, ws, wt):
    seqs, length, model = normed.shape
    width = wi.shape[2]
    sd = jax.ShapeDtypeStruct
    return _mixer_call(
        functools.partial(mix_fwd_kernel, n),
        (seg, seg_old, hp, taps_i, bias_i, taps_s, bias_s, cot, wo, wg, normed, wi, ws, wt),
        (
            sd((seqs, length, width), F32),
            sd((seqs, length, width), F32),
            sd((seqs, length, 2 * STATE), F32),
            sd((seqs, length, LANES), F32),
            sd((seqs, STATE, width), BF),
            sd((seqs, length, width), F32),
            sd((seqs, length, model), BF),
            sd((8,) + wo.shape, BF),
            sd((8,) + wg.shape, BF),
            sd((seqs, length, width), BF),
            sd((seqs, length, 2 * STATE), BF),
            sd((seqs, 16, width), BF),
            sd((seqs, 16, 2 * STATE), BF),
            sd((seqs, length, LANES), F32),
            sd((seqs, 8, length), F32),
        ),
        [
            pltpu.VMEM((8 + length, LANES), F32),
            pltpu.VMEM((length, 3 * LANES), BF),
            pltpu.VMEM((LANES, length), F32),
            pltpu.VMEM((length, length), F32),
            pltpu.VMEM((length, length), F32),
            pltpu.VMEM((2, length, 2 * LANES), BF),
            pltpu.VMEM((seqs, STATE, width), BF),
            pltpu.SemaphoreType.DMA((seqs, 2, n)),
            pltpu.SemaphoreType.DMA((seqs, n)),
            pltpu.SemaphoreType.DMA((2, 7)),
            pltpu.SemaphoreType.DMA((2, 7)),
            pltpu.SemaphoreType.DMA((3,)),
            pltpu.SemaphoreType.DMA((6,)),
        ],
        "mix_fwd",
        30 * 10**9,
        3,
        (7, 8, 9),
    )


def gate_kernel(n, y_part, u_s, entry, h0, gate, cot, wo, gain, tokens_in,
                d_mixed, d_gate, lam, po, go, gg, g_gain,
                mixed, gated, grad_gn, normed, local, acc, box, ss, rs, hs):
    dp, seq, t = lax.axis_index("dp"), lax.axis_index("seq"), lax.axis_index("tensor")
    seqs, length, width = y_part.shape
    model = cot.shape[2]
    wide = 2 * LANES
    bar = pltpu.get_barrier_semaphore()
    pl.semaphore_signal(bar, inc=1, device_id=_dev(dp, 1 - seq, t), device_id_type=MESH)
    for step in range(1, n):
        pl.semaphore_signal(
            bar, inc=1, device_id=_dev(dp, seq, lax.rem(t + step, n)), device_id_type=MESH
        )
    acc[...] = jnp.zeros_like(acc)
    g_gain[...] = jnp.zeros_like(g_gain)

    def spread_of(s, c):
        heads = _split(entry[s], 2)
        head = lax.rem(_iota((wide, wide), 0), LANES)
        one = head == 4 * c + lax.div(_iota((wide, wide), 1), HEAD_DIM)
        return _dot(heads, one.astype(F32).astype(BF))

    def maps(s):
        u = u_s[s, :, STATE:]
        return (u * _sig(u)).astype(BF)

    def first(c, _):
        ch = pl.ds(pl.multiple_of(c * wide, wide), wide)
        at = pl.ds(pl.multiple_of(t * width + c * wide, wide), wide)
        w = wo[:, :, ch].reshape(model, wide)
        for s in range(seqs):
            g = _dot(cot[s], w)
            grad_gn[s, :, ch] = g
            m = y_part[s, :, ch] + spread_of(s, c) * _dot(maps(s), h0[s, :, ch])
            z = gate[s, :, ch]
            gd = m * (z * _sig(z))
            mixed[s, :, ch] = m
            gated[s, :, ch] = gd
            sq, ds = gd * gd, g * gain[:, at] * gd
            acc[0, s] += sq[:, :LANES] + sq[:, LANES:]
            acc[1, s] += ds[:, :LANES] + ds[:, LANES:]
        return 0

    lax.fori_loop(0, width // wide, first, 0)
    ones = jnp.ones((8, wide), F32).astype(BF)
    row = _iota((8, length), 0)
    mine = jnp.zeros((8, length), F32)
    for kind in range(2):
        for s in range(seqs):
            sums = _dot(ones, _split(acc[kind, s], 2), 1, 1)
            mine = jnp.where(row == kind * seqs + s, sums, mine)
    box[t] = mine
    pl.semaphore_wait(bar, n)

    def copy(src, who):
        return pltpu.make_async_remote_copy(
            src_ref=box.at[src], dst_ref=box.at[src], send_sem=ss.at[who], recv_sem=rs.at[src],
            device_id=_dev(dp, seq, who), device_id_type=MESH,
        )

    for o in range(n):
        @pl.when(t != o)
        def _(o=o):
            copy(t, o).start()
    for o in range(n):
        @pl.when(t != o)
        def _(o=o):
            copy(o, o).wait_recv()
    full_width = n * width
    cols = _marks(jnp.sum(box[...], axis=0) / full_width)

    def second(c, _):
        ch = pl.ds(pl.multiple_of(c * wide, wide), wide)
        at = pl.ds(pl.multiple_of(t * width + c * wide, wide), wide)
        gn = gain[:, at]
        for s in range(seqs):
            rms = lax.rsqrt(cols[:, s : s + 1] + EPS)
            mean = cols[:, seqs + s : seqs + s + 1]
            g, gd, m, z = grad_gn[s, :, ch], gated[s, :, ch], mixed[s, :, ch], gate[s, :, ch]
            sg = _sig(z)
            scaled = gd * rms
            normed[s, :, ch] = (scaled * gn).astype(BF)
            g_gain[0:1, ch] += jnp.sum(g * scaled, axis=0, keepdims=True)
            d_gd = rms * (g * gn) - scaled * (rms * rms * mean)
            dm = d_gd * (z * sg)
            d_mixed[s, :, ch] = dm
            d_gate[s, :, ch] = (d_gd * m * sg * (1.0 + z * (1.0 - sg))).astype(BF)
            ed = (spread_of(s, c) * dm).astype(BF)
            local[s, :, ch] = _dot(maps(s), ed, 0, 0).astype(BF)
        return 0

    lax.fori_loop(0, width // wide, second, 0)
    handed = pltpu.make_async_remote_copy(
        src_ref=local, dst_ref=lam, send_sem=hs.at[0], recv_sem=hs.at[1],
        device_id=_dev(dp, 1 - seq, t), device_id_type=MESH,
    )

    @pl.when(seq == 1)
    def _():
        handed.start()
        lam[...] = jnp.zeros_like(lam)

    blocks = 2
    rows = blocks * wo.shape[1]

    def third(b, _):
        ch = pl.ds(pl.multiple_of(b * rows, LANES), rows)
        w = wo[pl.ds(b * blocks, blocks)].reshape(rows, width)
        total = None
        for s in range(seqs):
            po[s, :, ch] = _dot(normed[s], w, 1, 1).astype(BF)
            part = _dot(cot[s, :, ch], normed[s], 0, 0)
            total = part if total is None else total + part
        go[pl.ds(b * blocks, blocks)] = total.reshape(blocks, wo.shape[1], width).astype(BF)
        total = None
        for s in range(seqs):
            part = _dot(tokens_in[s, :, ch], d_gate[s], 0, 0)
            total = part if total is None else total + part
        gg[pl.ds(b * blocks, blocks)] = total.reshape(blocks, wo.shape[1], width).astype(BF)
        return 0

    lax.fori_loop(0, model // rows, third, 0)

    @pl.when(seq == 1)
    def _():
        handed.wait_send()

    @pl.when(seq == 0)
    def _():
        handed.wait_recv()

    for o in range(n):
        @pl.when(t != o)
        def _(o=o):
            copy(o, o).wait_send()


def gate_stage(n, y_part, u_s, entry, h0, gate, cot, wo, gain, tokens_in):
    seqs, length, width = y_part.shape
    sd = jax.ShapeDtypeStruct
    whole = pltpu.VMEM((seqs, length, width), F32)
    return _mixer_call(
        functools.partial(gate_kernel, n),
        (y_part, u_s, entry, h0, gate, cot, wo, gain, tokens_in),
        (
            sd((seqs, length, width), F32),
            sd((seqs, length, width), BF),
            sd((seqs, STATE, width), BF),
            sd((seqs, length, cot.shape[2]), BF),
            sd(wo.shape, BF),
            sd(wo.shape, BF),
            sd((8, width), F32),
        ),
        [
            whole, whole, whole,
            pltpu.VMEM((seqs, length, width), BF),
            pltpu.VMEM((seqs, STATE, width), BF),
            pltpu.VMEM((2, seqs, length, LANES), F32),
            pltpu.VMEM((n, 8, length), F32),
            pltpu.SemaphoreType.DMA((n,)),
            pltpu.SemaphoreType.DMA((n,)),
            pltpu.SemaphoreType.DMA((2,)),
        ],
        "gate_stage",
        6 * 10**9,
        2,
    )


def mix_bwd_kernel(n, dy_r, u_i, u_s, pre_i, old_i, pre_s, old_s, raw, rows, h0, lam, hp,
                   taps_i, taps_s, po, go, gg,
                   d_i, d_s, d_raw, sm_i, sm_s, sm_h, o_po, o_go, o_gg,
                   pad, moved, run3, run_t, bias_m, scores, d_scores, heads_hl,
                   acc_r, acc_c, acc_d, acc_q, d_b, d_c, lo, ro, xo, bo, xg, bg,
                   head_i, tail_i, head_s, tail_s, next_i, next_s, zs, zr, ps, pr, hs):
    t = lax.axis_index("tensor")
    seqs, length, width = pre_i.shape
    pairs = width // LANES
    _plane_barrier(n)
    lines = _line_reduces(n, po, lo, ro, zs, zr)
    planes = (
        _PlaneReduce(go, xo, bo, ps.at[0], pr.at[0]), _PlaneReduce(gg, xg, bg, ps.at[1], pr.at[1])
    )
    for j in range(n - 1):
        for begin, _, _, _ in lines:
            begin(j)
    for plane in planes:
        plane.begin()
    sm_i[...] = jnp.zeros_like(sm_i)
    sm_s[...] = jnp.zeros_like(sm_s)
    sm_h[...] = jnp.zeros_like(sm_h)
    moved[0:8, :] = jnp.zeros((8, LANES), F32)
    moved[8 + length :, :] = jnp.zeros((8, LANES), F32)

    def conv_back(du, marks, taps, s, ch, d_o, head_o, tail_o, sm):
        total = None
        for k in range(KERNEL):
            m = du if k == 0 else du * marks[:, k : k + 1]
            moved[8 : 8 + length, :] = m
            sm[k : k + 1, ch] += jnp.sum(m * pad[8 - k : 8 - k + length, :], axis=0, keepdims=True)
            part = taps[k : k + 1, :] * moved[k : k + 8 + length, :]
            total = part if total is None else total + part
        sm[4:5, ch] += jnp.sum(du, axis=0, keepdims=True)
        head_o[s, :, ch] = total[0:8, :]
        d_o[s, :, ch] = total[8:, :].astype(BF)
        tail_o[s, :, ch] = total[length - 8 :, :]

    def one(s, _):
        rw = rows[s]
        marks = _marks(rw)
        v, delta, log_decay, running, entry, to_end = _head_scalars(raw[s], hp, marks, length)
        run3[...] = _split(running, 3)
        run_t[...] = running.T
        bias_m[...] = _bias_matrix(rw, marks, length)
        heads_hl[0] = _split(delta, 2)
        heads_hl[1] = _split(to_end, 2)
        heads_hl[2] = _split(entry, 2)
        ub, uc = u_s[s, :, :STATE], u_s[s, :, STATE:]
        sb, sc = _sig(ub), _sig(uc)
        b_map, c_map = (ub * sb).astype(BF), (uc * sc).astype(BF)
        scores[...] = _dot(c_map, b_map, 1, 1)
        d_scores[...] = jnp.zeros_like(d_scores)
        for acc in (acc_r, acc_c, acc_d, acc_q, d_b, d_c):
            acc[...] = jnp.zeros_like(acc)

        def pair(p, _):
            @pl.when(jnp.logical_and(s == 0, p == 3))
            def _():
                lines[0][1](1)

            @pl.when(jnp.logical_and(s == 0, p == 5))
            def _():
                for plane in planes:
                    plane.send_far()

            @pl.when(jnp.logical_and(s == 1, p == 0))
            def _():
                lines[1][1](1)

            @pl.when(jnp.logical_and(s == 1, p == 2))
            def _():
                lines[0][1](2)

            @pl.when(jnp.logical_and(s == 1, p == 3))
            def _():
                planes[0].send_near()

            @pl.when(jnp.logical_and(s == 1, p == 5))
            def _():
                lines[1][1](2)
                planes[1].send_near()

            ch = pl.ds(pl.multiple_of(p * LANES, LANES), LANES)
            at = pl.ds(pl.multiple_of(t * width + p * LANES, LANES), LANES)
            u = u_i[s, :, ch]
            sg = _sig(u)
            x = u * sg
            dy = dy_r[s, :, ch]
            spread, fold = _spreader(2 * LANES, p), _folder(2 * LANES, p)
            dl = _dot(heads_hl[0], spread)
            q = _dot(heads_hl[1], spread)
            e = _dot(heads_hl[2], spread)
            xd = x * dl
            xb, db = xd.astype(BF), dy.astype(BF)
            h_in, l_in = h0[s, :, ch], lam[s, :, ch]
            c_h = _dot(c_map, h_in)
            b_l = _dot(b_map, l_in)
            qx, ed = q * xd, e * dy
            d_b[...] += _dot(qx.astype(BF), l_in, 1, 1)
            d_c[...] += _dot(ed.astype(BF), h_in, 1, 1)
            late = qx * b_l
            dxd = q * b_l
            sum_r = _dot(_split(ed * c_h - late, 2), fold)
            sum_s = sum_c = None
            lane = lax.div(_iota(xb.shape, 1), HEAD_DIM)
            for a in range(2):
                h = 2 * p + a
                pick = (lax.rem(_iota((3 * LANES, length), 0), LANES) == h).astype(F32).astype(BF)
                decay = jnp.exp(_dot(run3[...], pick) - run_t[pl.ds(h, 1), :] + bias_m[...])
                da = jnp.where(lane == a, db, jnp.zeros_like(db))
                ld = decay * _dot(da, xb, 1, 1)
                sum_s = ld if a == 0 else sum_s + ld
                both = (ld * scores[...]).astype(BF)
                mixing = (decay * scores[...]).astype(BF)
                dxd = dxd + _dot(mixing, da, 0, 0)
                col = (_iota((length, LANES), 1) == h).astype(F32).astype(BF)
                row = (_iota((LANES, length), 0) == h).astype(F32).astype(BF)
                sum_r = sum_r + _dot(both, col)
                part = _dot(row, both)
                sum_c = part if a == 0 else sum_c + part
            d_scores[...] += sum_s
            acc_r[...] += sum_r
            acc_c[...] += sum_c
            acc_d[...] += _dot(_split(dxd * x, 2), fold)
            total = jnp.broadcast_to(jnp.sum(late, axis=0, keepdims=True), (8, LANES))
            acc_q[...] += _dot(_split(total, 2), fold)
            skip = _dot(_split(hp[...], 2), spread)[2:3, :]
            sm_i[5:6, ch] += jnp.sum(dy * x, axis=0, keepdims=True)
            du = (dxd * dl + skip * dy) * (sg * (1.0 + u * (1.0 - sg)))
            pad[0:8, :] = old_i[s, :, ch].astype(F32)[8:16, :]
            pad[8:, :] = pre_i[s, :, ch].astype(F32)
            conv_back(du, marks, taps_i[:, at], s, ch, d_i, head_i, tail_i, sm_i)
            return 0

        lax.fori_loop(0, pairs, pair, 0)
        ds = d_scores[...].astype(BF)
        grads = (d_b[...] + _dot(ds, c_map, 0, 0), d_c[...] + _dot(ds, b_map))
        for half, (g, u, sg) in enumerate(zip(grads, (ub, uc), (sb, sc))):
            ch = slice(half * STATE, (half + 1) * STATE)
            pad[0:8, :] = old_s[s, :, ch].astype(F32)[8:16, :]
            pad[8:, :] = pre_s[s, :, ch].astype(F32)
            du = g * (sg * (1.0 + u * (1.0 - sg)))
            conv_back(du, marks, taps_s[:, ch], s, ch, d_s, head_s, tail_s, sm_s)
        d_run = acc_r[...] - acc_c[...].T
        last = _iota(d_run.shape, 0) == length - 1
        d_run = d_run + jnp.where(last, acc_q[0:1, :], 0.0)
        upper = (_iota((length, length), 0) <= _iota((length, length), 1)).astype(F32).astype(BF)
        d_log = _three(_dot(upper, _split(d_run, 3)))
        d_delta = acc_d[...] - d_log * jnp.exp(hp[1:2, :])
        d_step = d_delta * _sig(v)
        d_raw[s] = d_step.astype(BF)
        sm_h[0:1, :] += jnp.sum(d_step, axis=0, keepdims=True)
        sm_h[1:2, :] += jnp.sum(d_log * log_decay, axis=0, keepdims=True)
        return 0

    lax.fori_loop(0, seqs, one, 0)
    dp, seq = lax.axis_index("dp"), lax.axis_index("seq")
    handed = [
        pltpu.make_async_remote_copy(
            src_ref=a, dst_ref=b, send_sem=hs.at[2 * i], recv_sem=hs.at[2 * i + 1],
            device_id=_dev(dp, 1 - seq, t), device_id_type=MESH,
        )
        for i, (a, b) in enumerate(((head_i, next_i), (head_s, next_s)))
    ]

    @pl.when(seq == 1)
    def _():
        for c in handed:
            c.start()

    planes[0].final(o_go)

    @pl.when(seq == 0)
    def _():
        for c, box, tail, out in zip(handed, (next_i, next_s), (tail_i, tail_s), (d_i, d_s)):
            c.wait_recv()
            for s in range(seqs):
                more = jnp.concatenate([jnp.zeros_like(box[s]), box[s]], axis=0)
                out[s, length - 16 :, :] = (tail[s] + more).astype(BF)

    @pl.when(seq == 1)
    def _():
        for c in handed:
            c.wait_send()

    planes[1].final(o_gg)
    for s, (_, _, final, _) in enumerate(lines):
        final(o_po.at[pl.ds(s, 1)])
    for plane in planes:
        plane.finish()
    for _, _, _, finish in lines:
        finish()


def mix_bwd(n, dy, u_i, u_s, pre_i, old_i, pre_s, old_s, raw, rows, h0, lam, hp, taps_i, taps_s,
            po, go, gg):
    seqs, length, width = pre_i.shape
    model = po.shape[2]
    box = pltpu.VMEM((n, seqs, length // n, model), BF)
    sd = jax.ShapeDtypeStruct
    square = pltpu.VMEM((length, length), F32)
    tall = pltpu.VMEM((length, LANES), F32)
    return _mixer_call(
        functools.partial(mix_bwd_kernel, n),
        (dy, u_i, u_s, pre_i, old_i, pre_s, old_s, raw, rows, h0, lam, hp, taps_i, taps_s, po, go,
         gg),
        (
            sd((seqs, length, width), BF),
            sd((seqs, length, 2 * STATE), BF),
            sd((seqs, length, LANES), BF),
            sd((8, width), F32),
            sd((8, 2 * STATE), F32),
            sd((8, LANES), F32),
            sd((seqs, length // n, model), F32),
            sd(go.shape[1:], F32),
            sd(gg.shape[1:], F32),
        ),
        [
            pltpu.VMEM((8 + length, LANES), F32),
            pltpu.VMEM((16 + length, LANES), F32),
            pltpu.VMEM((length, 3 * LANES), BF),
            pltpu.VMEM((LANES, length), F32),
            square, square, square,
            pltpu.VMEM((3, length, 2 * LANES), BF),
            tall, pltpu.VMEM((LANES, length), F32), tall, pltpu.VMEM((8, LANES), F32), tall, tall,
            box, box,
            pltpu.VMEM((4,) + go.shape[1:], BF),
            pltpu.VMEM((3,) + go.shape[1:], BF),
            pltpu.VMEM((4,) + gg.shape[1:], BF),
            pltpu.VMEM((3,) + gg.shape[1:], BF),
            pltpu.VMEM((seqs, 8, width), F32),
            pltpu.VMEM((seqs, 16, width), F32),
            pltpu.VMEM((seqs, 8, 2 * STATE), F32),
            pltpu.VMEM((seqs, 16, 2 * STATE), F32),
            pltpu.VMEM((seqs, 8, width), F32),
            pltpu.VMEM((seqs, 8, 2 * STATE), F32),
            pltpu.SemaphoreType.DMA((seqs, 2, n)),
            pltpu.SemaphoreType.DMA((seqs, 2, n)),
            pltpu.SemaphoreType.DMA((2, 7)),
            pltpu.SemaphoreType.DMA((2, 7)),
            pltpu.SemaphoreType.DMA((4,)),
        ],
        "mix_bwd",
        8 * 10**9,
        4,
    )


def reduce_kernel(n, normed, dg, di, ds, dr, wg, wi, ws, wt, gain, sm_i, sm_s, sm_h, g_gain,
                  o_pg, o_gi, o_gs, o_gt, o_sm,
                  pg, gi, gs, gt, lg, rg, xi, xs, xt, bi, bs, bt, mb,
                  xp, xb, xo2, zs, zr, ps, pr, ms, mr, es, er):
    _plane_barrier(n)
    seqs, length, width = di.shape
    model = normed.shape[2]
    blocks = 2
    rows = blocks * wi.shape[1]
    small = _Smalls(n, mb, o_sm, ms, mr)
    mb[0] = jnp.zeros(mb.shape[1:], F32)
    mb[0, 0:6, :] = sm_i[0:6, :]
    mb[0, 6:7, :] = g_gain[0:1, :]
    for k in range(5):
        at = 256 * (k % 3)
        mb[0, 9 + k // 3 : 10 + k // 3, at : at + 256] = sm_s[k : k + 1, :]
    mb[0, 10:11, 512:640] = sm_h[0:1, :]
    mb[0, 10:11, 640:768] = sm_h[1:2, :]

    lines = _line_reduces(n, pg, lg, rg, zs, zr)
    totals = [None] * (model // rows)
    for s in range(seqs):
        for b in range(model // rows):
            ch = slice(b * rows, (b + 1) * rows)
            near = slice(b * blocks, (b + 1) * blocks)
            part = None
            for d, w in zip((dg, di, ds, dr), (wg, wi, ws, wt)):
                more = _dot(d[s], w[near].reshape(rows, w.shape[2]), 1, 1)
                part = more if part is None else part + more
            pg[s, :, ch] = part.astype(BF)
            part = jnp.sum(part * normed[s, :, ch].astype(F32), axis=0, keepdims=True)
            totals[b] = part if totals[b] is None else totals[b] + part
        lines[s][0](0)
    for b, total in enumerate(totals):
        ch = slice(b * rows, (b + 1) * rows)
        mb[0, 7 + b // 2 : 8 + b // 2, (b % 2) * rows : (b % 2 + 1) * rows] = total / gain[:, ch]
    small.copy(0, small.near(0)).start()
    for j in range(1, n - 2):
        for line in lines:
            line[0](j)
    planes = [
        _PlaneReduce(part, pair, box, ps.at[i], pr.at[i])
        for i, (part, pair, box) in enumerate(((gs, xs, bs), (gt, xt, bt), (gi, xi, bi)))
    ]

    def weight(d, out):
        def one(b, _):
            ch = pl.ds(pl.multiple_of(b * rows, LANES), rows)
            total = None
            for s in range(seqs):
                part = _dot(normed[s, :, ch], d[s], 0, 0)
                total = part if total is None else total + part
            out[pl.ds(b * blocks, blocks)] = total.reshape(
                blocks, wi.shape[1], d.shape[2]
            ).astype(BF)
            return 0

        lax.fori_loop(0, model // rows, one, 0)

    weight(ds, gs)
    planes[0].begin()
    weight(dr, gt)
    planes[1].begin()
    small.step(0)
    weight(di, gi)
    planes[2].begin()
    lines[0][1](1)
    small.step(1)
    lines[1][1](1)
    small.step(2)
    for line in lines:
        line[0](n - 2)
    for p in planes:
        p.send_far()
    lines[0][1](2)
    for p in planes[:2]:
        p.send_near()
    planes[0].final(o_gs)
    planes[1].final(o_gt)
    quarter = xp.shape[1]
    for o in range(n):
        xp[o] = o_gs[o * quarter : (o + 1) * quarter, :].astype(BF)
    state = _LineSum(n, xp, xb, xo2, es, er)
    state.scatter()
    planes[2].send_near()
    lines[1][1](2)
    state.gather()
    planes[2].final(o_gi)
    small.final()
    for s, (_, _, final, _) in enumerate(lines):
        final(o_pg.at[pl.ds(s, 1)])
    state.arrive()
    for o in range(n):
        o_gs[o * quarter : (o + 1) * quarter, :] = xo2[o].astype(F32)
    for p in planes:
        p.finish()
    state.finish()
    small.finish()
    for _, _, _, finish in lines:
        finish()


def reduce_all(n, normed, dg, di, ds, dr, wg, wi, ws, wt, gain, sm_i, sm_s, sm_h, g_gain):
    seqs, length, model = normed.shape
    rows = length // n
    sd = jax.ShapeDtypeStruct
    box = pltpu.VMEM((n, seqs, rows, model), BF)
    quarter = pltpu.VMEM((n, ws.shape[1] // n, ws.shape[2]), BF)
    sums = (16, wi.shape[2])
    return _mixer_call(
        functools.partial(reduce_kernel, n),
        (normed, dg, di, ds, dr, wg, wi, ws, wt, gain, sm_i, sm_s, sm_h, g_gain),
        (sd((seqs, rows, model), F32),)
        + tuple(sd(w.shape[1:], F32) for w in (wi, ws, wt))
        + (sd((n,) + sums, BF),),
        [pltpu.VMEM((seqs, length, model), BF)]
        + [pltpu.VMEM(w.shape, BF) for w in (wi, ws, wt)]
        + [box, box]
        + [pltpu.VMEM((4,) + w.shape[1:], BF) for w in (wi, ws, wt)]
        + [pltpu.VMEM((3,) + w.shape[1:], BF) for w in (wi, ws, wt)]
        + [
            pltpu.VMEM((6,) + sums, F32),
            quarter, quarter, quarter,
            pltpu.SemaphoreType.DMA((seqs, 2, n)),
            pltpu.SemaphoreType.DMA((seqs, 2, n)),
            pltpu.SemaphoreType.DMA((3, 7)),
            pltpu.SemaphoreType.DMA((3, 7)),
            pltpu.SemaphoreType.DMA((3 + n,)),
            pltpu.SemaphoreType.DMA((3 + n,)),
            pltpu.SemaphoreType.DMA((2, n)),
            pltpu.SemaphoreType.DMA((2, n)),
        ],
        "reduce_all",
        6 * 10**9,
        1,
    )


def emit_kernel(n, heads, tok, cot, gain, branch, rows, gg, gi, gs, gt, go, sms,
                block_out, g_tok, g_in, o_gg, o_gi, o_gs, o_gt, o_ci, o_ib, o_cs, o_sb,
                o_shift, o_rate, o_skip, o_gain, o_go):
    for s in range(tok.shape[0]):
        v = tok[s].astype(F32)
        rms = lax.rsqrt(jnp.mean(v * v, axis=-1, keepdims=True) + EPS)
        block_out[s] = (v + branch[s]).astype(BF)
        scaled = rows[s] * gain[...]
        mean = jnp.mean(scaled * v, axis=-1, keepdims=True)
        g_tok[s] = cot[s].astype(F32) + rms * scaled - v * (rms * rms * rms * mean)
    o_gg[...] = gg[...]
    o_gi[...] = gi[...]
    o_gs[...] = gs[...]
    short = jnp.zeros((256 - gt.shape[0], LANES), F32)
    o_gt[...] = jnp.concatenate([gt[...], short], axis=0).T[:heads, : gt.shape[0]]
    o_go[...] = go[...]
    width = sms.shape[2]
    shared = None
    head_rows = None
    for t in range(n):
        ch = slice(t * width, (t + 1) * width)
        every = sms[t].astype(F32)
        o_ci[:, ch] = every[0:4, :]
        o_ib[:, ch] = every[4:5, :]
        o_gain[:, ch] = every[6:7, :]
        block = every[8:16, :]
        shared = every[7:11, :] if shared is None else shared + every[7:11, :]
        lanes = _iota((3 * width, LANES), 0)
        chan = lax.rem(lanes, width)
        to = _iota((3 * width, LANES), 1) == heads * t + lax.div(chan, HEAD_DIM)
        skips = _dot(_split(every[0:8, :], 3), to.astype(F32).astype(BF))
        lanes = lax.rem(_iota((3 * LANES, LANES), 0), LANES)
        to = (_iota((3 * LANES, LANES), 1) == heads * t + lanes) & (lanes < heads)
        to = to.astype(F32).astype(BF)
        shift = _dot(_split(block[:, 512:640], 3), to)
        rate = _dot(_split(block[:, 640:768], 3), to)
        new = (skips[5:6, :], shift[2:3, :], rate[2:3, :])
        head_rows = new if head_rows is None else tuple(a + b for a, b in zip(head_rows, new))
    count = n * heads
    o_skip[...] = head_rows[0][:, :count]
    o_shift[...] = head_rows[1][:, :count]
    o_rate[...] = head_rows[2][:, :count]
    g_in[:, :width] = shared[0:1, :]
    g_in[:, width:] = shared[1:2, :]
    for k in range(4):
        at = 256 * (k % 3)
        o_cs[k : k + 1, :] = shared[2 + k // 3 : 3 + k // 3, at : at + 256]
    o_sb[...] = shared[3:4, 256:512]


def emit_all(n, heads, tok, cot, gain, branch, rows, gg, gi, gs, gt, go, sms):
    vm = pl.BlockSpec(memory_space=pltpu.VMEM)
    sd = lambda *shape: jax.ShapeDtypeStruct(shape, F32)
    width = sms.shape[2]
    outs = (
        jax.ShapeDtypeStruct(tok.shape, BF), sd(*tok.shape), sd(1, tok.shape[2]),
        sd(*gg.shape), sd(*gi.shape), sd(*gs.shape), sd(heads, gt.shape[0]),
        sd(4, n * width), sd(1, n * width), sd(4, 2 * STATE), sd(1, 2 * STATE),
        sd(1, n * heads), sd(1, n * heads), sd(1, n * heads), sd(1, n * width),
        sd(*go.shape),
    )
    return pl.pallas_call(
        functools.partial(emit_kernel, n, heads),
        out_shape=outs,
        in_specs=[vm] * 11,
        out_specs=(vm,) * len(outs),
        compiler_params=pltpu.CompilerParams(vmem_limit_bytes=28 << 20),
        name="emit_all",
    )(tok, cot, gain, branch, rows, gg, gi, gs, gt, go, sms)


def per_device(
    tokens,
    segments,
    input_gain,
    gate_proj,
    inner_proj,
    state_proj,
    step_proj,
    conv_inner,
    inner_bias,
    conv_state,
    state_bias,
    step_bias,
    log_rates,
    skip_gain,
    gated_gain,
    output_proj,
    cotangent,
):
    tensor_count = lax.axis_size("tensor")
    tensor_rank = lax.axis_index("tensor")
    residual = tokens.astype(jnp.float32)
    rms_in = lax.rsqrt(jnp.mean(residual * residual, axis=-1, keepdims=True) + EPS)
    normed_own = (residual * rms_in * input_gain).astype(jnp.bfloat16)
    normed, cot_rows = (
        lax.all_gather(normed_own, "tensor", axis=1, tiled=True),
        lax.all_gather(cotangent, "tensor", axis=1, tiled=True),
    )
    gate_full, inner_full, state_full, step_full, output_full = (
        lax.all_gather(gate_proj, ("dp", "seq"), axis=0, tiled=True),
        lax.all_gather(inner_proj, ("dp", "seq"), axis=0, tiled=True),
        lax.all_gather(state_proj, ("dp", "seq"), axis=0, tiled=True),
        lax.all_gather(step_proj, ("dp", "seq"), axis=0, tiled=True),
        lax.all_gather(output_proj, ("dp", "seq"), axis=1, tiled=True),
    )
    gate_in = jnp.dot(normed, gate_full, preferred_element_type=jnp.float32)
    inner_low = jnp.dot(normed, inner_full, preferred_element_type=jnp.float32).astype(jnp.bfloat16)
    state_low = jnp.dot(normed, state_full, preferred_element_type=jnp.float32).astype(jnp.bfloat16)
    step_raw = jnp.dot(normed, step_full, preferred_element_type=jnp.float32)
    margin = KERNEL - 1
    seg_float = segments.astype(jnp.float32)
    prior_inner, prior_state, prior_seg = passed_along(
        (
            inner_low[:, -margin:],
            state_low[:, -margin:],
            seg_float[:, -margin:].astype(jnp.bfloat16),
        ),
        "seq",
        1,
    )
    padded_inner = jnp.concatenate([prior_inner, inner_low], axis=1).astype(jnp.float32)
    padded_state = jnp.concatenate([prior_state, state_low], axis=1).astype(jnp.float32)
    seg_padded = jnp.concatenate([prior_seg.astype(jnp.float32), seg_float], axis=1)
    pieces = segments.shape[1] // BLOCK
    seg_blocks = blocked(seg_float, pieces)
    before = jnp.concatenate(
        [prior_seg[:, -1:].astype(jnp.float32), seg_blocks[:, :-1, -1]], axis=1
    )
    width_here = inner_full.shape[1]
    heads_here = step_full.shape[1]
    chan_start = tensor_rank * width_here
    head_start = tensor_rank * heads_here
    kernel_here = lax.dynamic_slice_in_dim(conv_inner, chan_start, width_here, 1)
    bias_here = lax.dynamic_slice_in_dim(inner_bias, chan_start, width_here, 0)
    gain_here = lax.dynamic_slice_in_dim(gated_gain, chan_start, width_here, 0)
    shift_here = lax.dynamic_slice_in_dim(step_bias, head_start, heads_here, 0)
    rates_here = lax.dynamic_slice_in_dim(log_rates, head_start, heads_here, 0)
    skip_here = lax.dynamic_slice_in_dim(skip_gain, head_start, heads_here, 0)

    def mixer_front(
        pad_inner, pad_state, raw_steps, kernel_w, kernel_b, state_w, state_b, step_shift, rate_logs
    ):
        inner = jax.nn.silu(causal_mix(pad_inner, seg_padded, kernel_w, kernel_b))
        inner = inner.reshape(inner.shape[0], inner.shape[1], -1, HEAD_DIM)
        both_maps = jax.nn.silu(causal_mix(pad_state, seg_padded, state_w, state_b))
        b_proj = both_maps[:, :, :STATE]
        c_proj = both_maps[:, :, STATE:]
        deltas = jax.nn.softplus(raw_steps + step_shift)
        log_decay = deltas * -jnp.exp(rate_logs)
        inflow, passing = block_sums(inner, deltas, log_decay, b_proj, seg_blocks, before)
        return (inner, deltas, log_decay, b_proj, c_proj, inflow, passing)

    def mixer_rear(inner, deltas, log_decay, b_proj, c_proj, inflow, passing, incoming, skips):
        running = jnp.cumsum(blocked(log_decay, pieces), axis=2)
        places = jnp.arange(running.shape[2])
        allowed = (seg_blocks[:, :, :, None] == seg_blocks[:, :, None, :]) & (
            places[:, None] >= places[None, :]
        )
        inside = allowed[..., None]
        decays = jnp.where(
            inside,
            jnp.exp(jnp.where(inside, running[:, :, :, None, :] - running[:, :, None, :, :], 0.0)),
            0.0,
        )
        scores = jnp.einsum(
            "scin,scjn->scij", blocked(c_proj, pieces), blocked(b_proj, pieces), precision=HIGH
        )
        mixing = decays * scores[..., None] * blocked(deltas, pieces)[:, :, None, :, :]
        direct = jnp.einsum("scijh,scjhp->scihp", mixing, blocked(inner, pieces), precision=HIGH)
        from_state, outgoing = state_reads(
            incoming, log_decay, c_proj, inflow, passing, seg_blocks, before
        )
        heads_out = (direct + from_state).reshape(inner.shape) + skips[:, None] * inner
        return (heads_out.reshape(inner.shape[0], inner.shape[1], -1), outgoing)

    front_args = (
        padded_inner,
        padded_state,
        step_raw,
        kernel_here,
        bias_here,
        conv_state,
        state_bias,
        shift_here,
        rates_here,
    )
    front_vals = mixer_front(*front_args)
    inner, deltas, log_decay, b_proj, c_proj, inflow, passing = front_vals
    span_decay = jnp.ones(passing[:, 0].shape, jnp.float32)
    span_state = jnp.zeros(inflow[:, 0].shape, jnp.float32)
    span_state = passing[:, 0, :, None, None] * span_state + inflow[:, 0]
    span_decay = span_decay * passing[:, 0]
    identity = (jnp.ones_like(span_decay), jnp.zeros_like(span_state))
    incoming = entering_2((span_decay, span_state), "seq", chain_link, identity)[1]
    mixed, outgoing = mixer_rear(*front_vals, incoming, skip_here)
    sigmoid_z = jax.nn.sigmoid(gate_in)
    silu_z = gate_in * sigmoid_z
    gated = mixed * silu_z
    full_width = tensor_count * gated.shape[-1]
    square_sum = lax.psum(jnp.sum(gated * gated, axis=-1), "tensor")
    rms_gate = lax.rsqrt(square_sum / full_width + EPS)[..., None]
    gate_normed = (gated * rms_gate * gain_here).astype(jnp.bfloat16)
    partial_out = jnp.dot(gate_normed, output_full, preferred_element_type=jnp.float32)
    branch_rows = lax.psum_scatter(partial_out, "tensor", scatter_dimension=1, tiled=True)
    block_out = (residual + branch_rows).astype(jnp.bfloat16)
    grad_output = jnp.einsum(
        "srk,srd->kd", gate_normed, cot_rows, preferred_element_type=jnp.float32
    )
    grad_gn = jnp.einsum("srd,kd->srk", cot_rows, output_full, preferred_element_type=jnp.float32)
    scaled = grad_gn * gain_here
    dot_sum = lax.psum(jnp.sum(scaled * gated, axis=-1), "tensor")
    grad_gain_here = jnp.sum(grad_gn * gated * rms_gate, axis=(0, 1))
    grad_gated = rms_gate * scaled - gated * rms_gate**3 * (dot_sum / full_width)[..., None]
    grad_mixed = grad_gated * silu_z
    grad_gate_in = (grad_gated * mixed * sigmoid_z * (1.0 + gate_in * (1.0 - sigmoid_z))).astype(
        jnp.bfloat16
    )
    front_vals, front_back = jax.vjp(mixer_front, *front_args)
    unused_rear, rear_back = jax.vjp(mixer_rear, *front_vals, incoming, skip_here)
    inner, deltas, log_decay, b_proj, c_proj, inflow, passing = front_vals
    grad_blocks = blocked(grad_mixed.reshape(inner.shape), pieces)
    unused_reads, read_back = jax.vjp(
        lambda memory_in: state_reads(
            memory_in, log_decay, c_proj, inflow, passing, seg_blocks, before
        )[0],
        incoming,
    )
    local_grad = read_back(grad_blocks)[0]
    outgoing_grad = carried_in((span_decay, local_grad), "seq", chain_link, identity)[1]
    rear_grads = rear_back((grad_mixed, outgoing_grad))
    grad_skip_here = rear_grads[8]
    (
        pad_grad_inner,
        pad_grad_state,
        grad_step_raw,
        grad_kernel_here,
        grad_bias_here,
        grad_conv_state,
        grad_state_bias,
        grad_shift_here,
        grad_rates_here,
    ) = front_back(tuple(rear_grads[:7]))
    from_next_inner, from_next_state = passed_along(
        (pad_grad_inner[:, :margin], pad_grad_state[:, :margin]), "seq", -1
    )
    grad_inner_pre = jnp.concatenate(
        [pad_grad_inner[:, margin:-margin], pad_grad_inner[:, -margin:] + from_next_inner], axis=1
    )
    grad_state_part = jnp.concatenate(
        [pad_grad_state[:, margin:-margin], pad_grad_state[:, -margin:] + from_next_state], axis=1
    )
    grad_state_pre = lax.psum(grad_state_part, "tensor").astype(jnp.bfloat16)
    grad_inner_low = grad_inner_pre.astype(jnp.bfloat16)
    grad_step_low = grad_step_raw.astype(jnp.bfloat16)
    grad_normed = jnp.einsum(
        "srk,dk->srd", grad_gate_in, gate_full, preferred_element_type=jnp.float32
    )
    grad_normed = grad_normed + jnp.einsum(
        "srk,dk->srd", grad_inner_low, inner_full, preferred_element_type=jnp.float32
    )
    grad_normed = grad_normed + jnp.einsum(
        "srk,dk->srd", grad_step_low, step_full, preferred_element_type=jnp.float32
    )
    grad_rows = lax.psum_scatter(grad_normed, "tensor", scatter_dimension=1, tiled=True)
    own_rows = tokens.shape[1]
    state_mine = lax.dynamic_slice_in_dim(grad_state_pre, tensor_rank * own_rows, own_rows, 1)
    grad_rows = grad_rows + jnp.einsum(
        "srk,dk->srd", state_mine, state_full, preferred_element_type=jnp.float32
    )
    grad_gate_w = jnp.einsum(
        "srd,srk->dk", normed, grad_gate_in, preferred_element_type=jnp.float32
    )
    grad_inner_w = jnp.einsum(
        "srd,srk->dk", normed, grad_inner_low, preferred_element_type=jnp.float32
    )
    grad_state_w = jnp.einsum(
        "srd,srk->dk", normed, grad_state_pre, preferred_element_type=jnp.float32
    )
    grad_step_w = jnp.einsum(
        "srd,srk->dk", normed, grad_step_low, preferred_element_type=jnp.float32
    )
    shard_gate, shard_inner, shard_state, shard_step, shard_output = (
        lax.psum_scatter(grad_gate_w, ("dp", "seq"), scatter_dimension=0, tiled=True),
        lax.psum_scatter(grad_inner_w, ("dp", "seq"), scatter_dimension=0, tiled=True),
        lax.psum_scatter(grad_state_w, ("dp", "seq"), scatter_dimension=0, tiled=True),
        lax.psum_scatter(grad_step_w, ("dp", "seq"), scatter_dimension=0, tiled=True),
        lax.psum_scatter(grad_output, ("dp", "seq"), scatter_dimension=1, tiled=True),
    )
    scaled_in = grad_rows * input_gain
    grad_input_gain = jnp.sum(grad_rows * residual * rms_in, axis=(0, 1))
    grad_tokens = (
        cotangent.astype(jnp.float32)
        + rms_in * scaled_in
        - residual * rms_in**3 * jnp.mean(scaled_in * residual, axis=-1, keepdims=True)
    )

    def placed(whole, piece_grad, start, axis_number):
        return lax.dynamic_update_slice_in_dim(
            jnp.zeros_like(whole), piece_grad, start, axis_number
        )

    smalls = lax.psum(
        (
            grad_input_gain,
            placed(conv_inner, grad_kernel_here, chan_start, 1),
            placed(inner_bias, grad_bias_here, chan_start, 0),
            grad_conv_state,
            grad_state_bias,
            placed(step_bias, grad_shift_here, head_start, 0),
            placed(log_rates, grad_rates_here, head_start, 0),
            placed(skip_gain, grad_skip_here, head_start, 0),
            placed(gated_gain, grad_gain_here, chan_start, 0),
        ),
        ("dp", "seq", "tensor"),
    )
    return (
        block_out,
        grad_tokens,
        smalls[0],
        shard_gate,
        shard_inner,
        shard_state,
        shard_step,
        smalls[1],
        smalls[2],
        smalls[3],
        smalls[4],
        smalls[5],
        smalls[6],
        smalls[7],
        smalls[8],
        shard_output,
    )


def per_device_fast(
    tokens,
    segments,
    input_gain,
    gate_proj,
    inner_proj,
    state_proj,
    step_proj,
    conv_inner,
    inner_bias,
    conv_state,
    state_bias,
    step_bias,
    log_rates,
    skip_gain,
    gated_gain,
    output_proj,
    cotangent,
):
    tensor_count = lax.axis_size("tensor")
    tensor_rank = lax.axis_index("tensor")
    heads = step_proj.shape[1]
    gain_row = input_gain[None]
    normed, seg_old, s8, t8, i8 = gather_all(
        tensor_count, tokens, gain_row, segments, (state_proj, step_proj.T, inner_proj)
    )
    heads_param = jnp.pad(
        lax.dynamic_slice_in_dim(
            jnp.stack([step_bias, log_rates, skip_gain]), tensor_rank * heads, heads, 1
        ),
        ((0, 5), (0, LANES - heads)),
    )
    (
        y_part, u_inner, u_state, entry, incoming, gate_in, cot_rows, o8, g8,
        inner_low, state_low, prior_inner, prior_state, step_raw, rows,
    ) = mix_fwd(
        tensor_count, segments, seg_old, heads_param,
        conv_inner, inner_bias[None], conv_state, state_bias[None],
        cotangent, output_proj.T, gate_proj, normed, i8, s8, t8,
    )
    grad_mixed, grad_gate_in, outgoing_grad, partial_out, grad_output, grad_gate, grad_gain = gate_stage(
        tensor_count, y_part, u_state, entry, incoming, gate_in, cot_rows, o8, gated_gain[None], normed
    )
    (
        d_inner, d_state, d_step, sm_i, sm_s, sm_h, branch_rows, shard_output, shard_gate
    ) = mix_bwd(
        tensor_count, grad_mixed, u_inner, u_state, inner_low, prior_inner, state_low, prior_state,
        step_raw, rows, incoming, outgoing_grad, heads_param, conv_inner, conv_state,
        partial_out, grad_output, grad_gate,
    )
    grad_rows, shard_inner, shard_state, shard_step, sms = reduce_all(
        tensor_count, normed, grad_gate_in, d_inner, d_state, d_step, g8, i8, s8, t8, gain_row,
        sm_i, sm_s, sm_h, grad_gain,
    )
    outs = emit_all(
        tensor_count, heads, tokens, cotangent, gain_row, branch_rows, grad_rows,
        shard_gate, shard_inner, shard_state, shard_step, shard_output, sms,
    )
    flat = (2, 8, 10, 11, 12, 13, 14)
    return tuple(
        o[0] if i in flat else o.T if i in (6, 15) else o for i, o in enumerate(outs)
    )


def solution(mesh):
    fast = mesh.shape["dp"] == 4 and mesh.shape["seq"] == 2
    placed = (
        P("dp", ("seq", "tensor"), None),
        P("dp", "seq"),
        P(),
        P(("dp", "seq"), "tensor"),
        P(("dp", "seq"), "tensor"),
        P(("dp", "seq"), None),
        P(("dp", "seq"), "tensor"),
        P(),
        P(),
        P(),
        P(),
        P(),
        P(),
        P(),
        P(),
        P("tensor", ("dp", "seq")),
        P("dp", ("seq", "tensor"), None),
    )
    return jax.shard_map(
        per_device_fast if fast else per_device,
        mesh=mesh,
        in_specs=placed,
        out_specs=(
            P("dp", ("seq", "tensor"), None),
            P("dp", ("seq", "tensor"), None),
            P(),
            P(("dp", "seq"), "tensor"),
            P(("dp", "seq"), "tensor"),
            P(("dp", "seq"), None),
            P(("dp", "seq"), "tensor"),
            P(),
            P(),
            P(),
            P(),
            P(),
            P(),
            P(),
            P(),
            P("tensor", ("dp", "seq")),
        ),
        check_vma=False,
    )
```

```python
import functools

import jax
import jax.numpy as jnp
from jax import lax
from jax.experimental import pallas as pl
from jax.experimental.pallas import tpu as pltpu
from jax.sharding import PartitionSpec as P

HEAD_DIM = 64
STATE = 128
KERNEL = 4
BLOCK = 256


EPS = 1e-05
HIGH = lax.Precision.HIGHEST


def passed_along(block, axis, distance):
    devices = range(lax.axis_size(axis))
    route = [(i - distance, i) for i in devices if i - distance in devices]
    return lax.ppermute(block, axis, route)


def entering_2(shard, axis, join, neutral):
    place = lax.axis_index(axis)
    gathered = jax.tree.map(
        lambda a, kind: lax.all_gather(a.astype(kind), axis), shard, (jnp.bfloat16, jnp.bfloat16)
    )
    state = jax.tree.map(lambda a, e: jnp.zeros_like(a) + jnp.asarray(e, a.dtype), shard, neutral)

    def one(hop, state):
        return join(
            state,
            jax.tree.map(
                lambda a, own: lax.dynamic_index_in_dim(a, hop, 0, False).astype(own.dtype),
                gathered,
                shard,
            ),
        )

    return lax.fori_loop(0, place, one, state)


def carried_in(shard, axis, combine, identity):
    length, here = (lax.axis_size(axis), lax.axis_index(axis))
    everything = jax.tree.map(
        lambda part, kind: lax.all_gather(part.astype(kind), axis),
        shard,
        jax.tree.map(lambda a: jnp.bfloat16 if a.dtype == jnp.float32 else a.dtype, shard),
    )
    start = jax.tree.map(
        lambda part, zero: jnp.broadcast_to(jnp.asarray(zero, part.dtype), part.shape),
        shard,
        identity,
    )

    def hop(k, before):
        at = length - 1 - k
        reached = at > here
        new = combine(
            before, jax.tree.map(lambda part, own: part[at].astype(own.dtype), everything, shard)
        )
        return jax.tree.map(lambda a, b: jnp.where(reached, a, b), new, before)

    return lax.fori_loop(0, length, hop, start)


def chain_link(earlier, later):
    return (earlier[0] * later[0], later[0][:, :, None, None] * earlier[1] + later[1])


def causal_mix(padded, seg_padded, kernel_w, kernel_b):
    margin = KERNEL - 1
    length = padded.shape[1] - margin
    seg_now = seg_padded[:, margin:]
    result = kernel_b + kernel_w[0] * padded[:, margin:]
    for offset in range(1, KERNEL):
        moved = padded[:, margin - offset : margin - offset + length]
        same_doc = (seg_padded[:, margin - offset : margin - offset + length] == seg_now).astype(
            jnp.float32
        )
        result = result + kernel_w[offset] * moved * same_doc[:, :, None]
    return result


def blocked(values, pieces):
    return values.reshape((values.shape[0], pieces, values.shape[1] // pieces) + values.shape[2:])


def block_sums(inner, deltas, log_decay, b_proj, seg_blocks, before):
    pieces = seg_blocks.shape[1]
    running = jnp.cumsum(blocked(log_decay, pieces), axis=2)
    same_end = (seg_blocks == seg_blocks[:, :, -1:]).astype(jnp.float32)
    to_end = (
        jnp.exp(running[:, :, -1:, :] - running) * same_end[:, :, :, None] * blocked(deltas, pieces)
    )
    inflow = jnp.einsum(
        "scjhp,scjn->schpn",
        to_end[..., None] * blocked(inner, pieces),
        blocked(b_proj, pieces),
        precision=HIGH,
    )
    passing = (
        jnp.exp(running[:, :, -1, :])
        * (seg_blocks[:, :, -1] == before).astype(jnp.float32)[:, :, None]
    )
    return (inflow, passing)


def state_reads(incoming, log_decay, c_proj, inflow, passing, seg_blocks, before):
    pieces = seg_blocks.shape[1]
    running = jnp.cumsum(blocked(log_decay, pieces), axis=2)
    memory = incoming
    entering = [memory]
    memory = passing[:, 0, :, None, None] * memory + inflow[:, 0]
    stacked = jnp.stack(entering, axis=1)
    entry = jnp.exp(running) * (seg_blocks == before[:, :, None]).astype(jnp.float32)[..., None]
    from_state = (
        jnp.einsum("scin,schpn->scihp", blocked(c_proj, pieces), stacked, precision=HIGH)
        * entry[..., None]
    )
    return (from_state, memory)


MESH = pl.DeviceIdType.MESH
BF = jnp.bfloat16
F32 = jnp.float32


def _peers():
    dp, seq, t = lax.axis_index("dp"), lax.axis_index("seq"), lax.axis_index("tensor")
    x, y = lax.rem(dp, 2), lax.div(dp, 2)
    x_dp = dp + 1 - 2 * x
    y_dp = dp + 2 - 4 * y
    d_dp = 3 - dp
    return dp, seq, t, x_dp, y_dp, d_dp


def _dev(dp, seq, t):
    return {"dp": dp, "seq": seq, "tensor": t}


def _plane_barrier(n):
    dp, seq, t, x_dp, y_dp, d_dp = _peers()
    bar = pltpu.get_barrier_semaphore()
    for who in (_dev(dp, 1 - seq, t), _dev(x_dp, seq, t), _dev(y_dp, seq, t)):
        pl.semaphore_signal(bar, inc=1, device_id=who, device_id_type=MESH)

    for step in range(1, n):
        pl.semaphore_signal(
            bar, inc=1, device_id=_dev(dp, seq, lax.rem(t + step, n)), device_id_type=MESH
        )
    pl.semaphore_wait(bar, 3 + n - 1)


class _Line:
    def __init__(self, n, ref, rows, ssem, rsem, own=None):
        self.n, self.ref, self.rows, self.ssem, self.rsem = n, ref, rows, ssem, rsem
        self.own = own

    def block(self, o):
        return self.ref.at[:, pl.ds(pl.multiple_of(o * self.rows, self.rows), self.rows), :]

    def copy(self, o, direction, own=False):
        dp, seq, t = lax.axis_index("dp"), lax.axis_index("seq"), lax.axis_index("tensor")
        return pltpu.make_async_remote_copy(
            src_ref=self.own if own else self.block(o),
            dst_ref=self.block(o),
            send_sem=self.ssem.at[0 if direction > 0 else 1, o],
            recv_sem=self.rsem.at[o],
            device_id=_dev(dp, seq, t + direction),
            device_id_type=MESH,
        )

    def step(self, d):
        n, t = self.n, lax.axis_index("tensor")
        for way in (1, -1):
            o = t - way * d
            here = jnp.logical_and(o >= 0, o < n)
            nxt = jnp.logical_and(t + way >= 0, t + way < n)

            @pl.when(here)
            def _(o=o, way=way, nxt=nxt):
                if d > 0:
                    self.copy(o, way).wait_recv()

                @pl.when(nxt)
                def _():
                    self.copy(o, way, d == 0 and self.own is not None).start()

    def finish(self):
        n, t = self.n, lax.axis_index("tensor")
        for d in range(n):
            for way in (1, -1):
                o = t - way * d
                ok = jnp.logical_and(
                    jnp.logical_and(o >= 0, o < n),
                    jnp.logical_and(t + way >= 0, t + way < n),
                )

                @pl.when(ok)
                def _(o=o, way=way):
                    self.copy(o, way).wait_send()


class _Plane:
    def __init__(self, own, full, ssem, rsem, lsem):
        self.own, self.full, self.ssem, self.rsem, self.lsem = own, full, ssem, rsem, lsem

    def copy(self, src, block, who, s):
        return pltpu.make_async_remote_copy(
            src_ref=src,
            dst_ref=self.full.at[block],
            send_sem=self.ssem.at[s],
            recv_sem=self.rsem.at[s],
            device_id=who,
            device_id_type=MESH,
        )

    def begin(self):
        dp, seq, t, x_dp, y_dp, d_dp = _peers()
        me = dp * 2 + seq
        pltpu.make_async_copy(self.own, self.full.at[me], self.lsem).start()
        self.copy(self.own, me, _dev(x_dp, seq, t), 0).start()
        self.copy(self.own, me, _dev(y_dp, seq, t), 1).start()
        self.copy(self.own, me, _dev(dp, 1 - seq, t), 3).start()

    def forward(self):
        dp, seq, t, x_dp, y_dp, d_dp = _peers()
        bx, by = x_dp * 2 + seq, y_dp * 2 + seq
        self.copy(self.own, bx, _dev(x_dp, seq, t), 0).wait_recv()
        self.copy(self.own, by, _dev(y_dp, seq, t), 1).wait_recv()

        @pl.when(seq == 0)
        def _():
            self.copy(self.full.at[by], by, _dev(x_dp, seq, t), 2).start()

        @pl.when(seq == 1)
        def _():
            self.copy(self.full.at[bx], bx, _dev(y_dp, seq, t), 2).start()

        self.copy(self.full.at[bx], bx, _dev(dp, 1 - seq, t), 4).start()
        self.copy(self.full.at[by], by, _dev(dp, 1 - seq, t), 5).start()

    def share(self):
        dp, seq, t, x_dp, y_dp, d_dp = _peers()
        bd = d_dp * 2 + seq
        self.copy(self.own, bd, _dev(x_dp, seq, t), 2).wait_recv()
        self.copy(self.full.at[bd], bd, _dev(dp, 1 - seq, t), 6).start()

    def arrive(self):
        dp, seq, t, x_dp, y_dp, d_dp = _peers()
        me = dp * 2 + seq
        pltpu.make_async_copy(self.own, self.full.at[me], self.lsem).wait()
        for s in (3, 4, 5, 6):
            self.copy(self.own, me, _dev(dp, 1 - seq, t), s).wait_recv()

    def finish(self):
        dp, seq, t, x_dp, y_dp, d_dp = _peers()
        me = dp * 2 + seq
        for s in range(7):
            self.copy(self.own, me, _dev(dp, 1 - seq, t), s).wait_send()


def gather_kernel(n, tok_far, gain, seg, ws, wt_t, wi, normed, seg_old, fs, ft, fi,
                  tok, wt, zs, zr, ps, pr, ls, hs):
    dp, seq, t = lax.axis_index("dp"), lax.axis_index("seq"), lax.axis_index("tensor")
    rows = tok.shape[1]
    near = pltpu.make_async_copy(tok_far, tok, ls.at[3])
    near.start()
    v = wt_t[...].astype(F32)
    v = jnp.concatenate([v, jnp.zeros((LANES - v.shape[0], v.shape[1]), F32)], axis=0)
    v = jnp.concatenate([v, jnp.zeros((LANES, 256 - v.shape[1]), F32)], axis=1)
    wt[...] = v.T[: wt.shape[0], :].astype(BF)
    _plane_barrier(n)
    planes = [
        _Plane(own, full, ps.at[i], pr.at[i], ls.at[i])
        for i, (own, full) in enumerate(((ws, fs), (wt, ft), (wi, fi)))
    ]
    handed = pltpu.make_async_remote_copy(
        src_ref=seg, dst_ref=seg_old, send_sem=hs.at[0], recv_sem=hs.at[1],
        device_id=_dev(dp, 1 - seq, t), device_id_type=MESH,
    )

    @pl.when(seq == 0)
    def _():
        handed.start()
        seg_old[...] = jnp.zeros_like(seg_old)

    for p in planes:
        p.begin()
    near.wait()
    mine = pl.ds(pl.multiple_of(t * rows, rows), rows)
    lines = []
    for s in range(tok.shape[0]):
        v = tok[s].astype(F32)
        rms = lax.rsqrt(jnp.mean(v * v, axis=-1, keepdims=True) + EPS)
        normed[s, mine, :] = (v * rms * gain[...]).astype(BF)
        lines.append(_Line(n, normed.at[pl.ds(s, 1)], rows, zs.at[s], zr.at[s]))
        lines[s].step(0)
    for line in lines:
        line.step(1)
    for p in planes:
        p.forward()
    lines[0].step(2)
    for p in planes:
        p.share()
    for line in lines[1:]:
        line.step(2)
    for d in range(3, n):
        for line in lines:
            line.step(d)
    for p in planes:
        p.arrive()

    @pl.when(seq == 0)
    def _():
        handed.wait_send()

    @pl.when(seq == 1)
    def _():
        handed.wait_recv()

    for line in lines:
        line.finish()
    for p in planes:
        p.finish()


def gather_all(n, tokens, gain, seg, weights):
    seqs, rows, width = tokens.shape
    vm = pl.BlockSpec(memory_space=pltpu.VMEM)
    far = pl.BlockSpec(memory_space=pltpu.HBM)
    wide = (weights[1].shape[1], LANES)
    full = lambda *shape: jax.ShapeDtypeStruct((8,) + shape, BF)
    act = jax.ShapeDtypeStruct((seqs, n * rows, width), BF)
    return pl.pallas_call(
        functools.partial(gather_kernel, n),
        out_shape=(
            act, jax.ShapeDtypeStruct(seg.shape, seg.dtype),
            full(*weights[0].shape), full(*wide), full(*weights[2].shape),
        ),
        in_specs=[far, vm, vm, far, vm, far],
        out_specs=(vm,) * 5,
        scratch_shapes=[
            pltpu.VMEM(tokens.shape, tokens.dtype),
            pltpu.VMEM(wide, BF),
            pltpu.SemaphoreType.DMA((seqs, 2, n)),
            pltpu.SemaphoreType.DMA((seqs, n)),
            pltpu.SemaphoreType.DMA((3, 7)),
            pltpu.SemaphoreType.DMA((3, 7)),
            pltpu.SemaphoreType.DMA((4,)),
            pltpu.SemaphoreType.DMA((2,)),
        ],
        compiler_params=pltpu.CompilerParams(
            collective_id=0, has_side_effects=True, vmem_limit_bytes=16 << 20
        ),
        cost_estimate=pl.CostEstimate(flops=30 * 10**9, bytes_accessed=1 << 20, transcendentals=0),
        name="gather_all",
    )(tokens, gain, seg, *weights)


def _line_reduce(n, part, left, right, ssem, rsem):
    dp, seq, t = lax.axis_index("dp"), lax.axis_index("seq"), lax.axis_index("tensor")
    rows = left.shape[2]

    def copy(src, box, o, way):
        return pltpu.make_async_remote_copy(
            src_ref=src, dst_ref=box.at[o],
            send_sem=ssem.at[0 if way > 0 else 1, o], recv_sem=rsem.at[0 if way > 0 else 1, o],
            device_id=_dev(dp, seq, t + way), device_id_type=MESH,
        )

    def block(o):
        return part.at[:, pl.ds(pl.multiple_of(o * rows, rows), rows), :]

    def begin(j):
        for way, box, place, o in ((1, left, t, n - 1 - j), (-1, right, n - 1 - t, j)):
            @pl.when(place == 0)
            def _():
                copy(block(o), box, o, way).start()

    def step(k):
        for way, box, place in ((1, left, t), (-1, right, n - 1 - t)):
            @pl.when(jnp.logical_and(place > 0, place <= k))
            def _():
                o = n - 1 - (k - place) if way > 0 else k - place
                copy(block(o), box, o, way).wait_recv()
                for s in range(part.shape[0]):
                    own = part[s, pl.ds(pl.multiple_of(o * rows, rows), rows), :].astype(F32)
                    box[o, s] = (box[o, s].astype(F32) + own).astype(BF)
                copy(box.at[o], box, o, way).start()

    def final(out):
        mine = pl.ds(pl.multiple_of(t * rows, rows), rows)
        for s in range(part.shape[0]):
            out[s] = part[s, mine, :].astype(F32)

        @pl.when(t > 0)
        def _():
            copy(left.at[0], left, t, 1).wait_recv()
            for s in range(part.shape[0]):
                out[s] = out[s] + left[t, s].astype(F32)

        @pl.when(t < n - 1)
        def _():
            copy(left.at[0], right, t, -1).wait_recv()
            for s in range(part.shape[0]):
                out[s] = out[s] + right[t, s].astype(F32)

    def finish():
        for j in range(n - 1):
            for way, box, o in ((1, left, n - 1 - j), (-1, right, j)):
                sends = (t < o) if way > 0 else (t > o)

                @pl.when(sends)
                def _():
                    copy(box.at[o], box, o, way).wait_send()

    return begin, step, final, finish


def _line_reduces(n, part, left, right, ssem, rsem):
    one = lambda s: pl.ds(s, 1)
    return [
        _line_reduce(
            n, part.at[one(s)], left.at[:, one(s)], right.at[:, one(s)], ssem.at[s], rsem.at[s]
        )
        for s in range(part.shape[0])
    ]


class _PlaneReduce:
    def __init__(self, part, pair, box, ssem, rsem):
        self.part, self.pair, self.box, self.ssem, self.rsem = part, pair, box, ssem, rsem

    def copy(self, src, dst, who, s):
        return pltpu.make_async_remote_copy(
            src_ref=src, dst_ref=dst, send_sem=self.ssem.at[s], recv_sem=self.rsem.at[s],
            device_id=who, device_id_type=MESH,
        )

    def begin(self):
        dp, seq, t, x_dp, y_dp, d_dp = _peers()
        for slot, chip in enumerate((d_dp, x_dp, y_dp, dp)):
            self.copy(self.part.at[chip * 2 + 1 - seq], self.pair.at[slot], _dev(dp, 1 - seq, t), slot).start()

    def _paired(self, slot, chip, also=None):
        dp, seq, t, x_dp, y_dp, d_dp = _peers()
        self.copy(self.pair.at[slot], self.pair.at[slot], _dev(dp, 1 - seq, t), slot).wait_recv()
        v = self.part[chip * 2 + seq].astype(F32) + self.pair[slot].astype(F32)
        self.pair[slot] = v.astype(BF)

    def send_far(self):
        dp, seq, t, x_dp, y_dp, d_dp = _peers()
        for slot, chip in enumerate((d_dp, x_dp, y_dp)):
            self._paired(slot, chip)
            if slot == 0:
                @pl.when(seq == 0)
                def _():
                    self.copy(self.pair.at[0], self.box.at[2], _dev(x_dp, seq, t), 4).start()

                @pl.when(seq == 1)
                def _():
                    self.copy(self.pair.at[0], self.box.at[2], _dev(y_dp, seq, t), 4).start()

        @pl.when(seq == 0)
        def _():
            self.copy(self.pair.at[1], self.box.at[0], _dev(x_dp, seq, t), 5).start()

        @pl.when(seq == 1)
        def _():
            self.copy(self.pair.at[2], self.box.at[1], _dev(y_dp, seq, t), 6).start()

    def send_near(self):
        dp, seq, t, x_dp, y_dp, d_dp = _peers()
        self.copy(self.pair.at[0], self.box.at[2], _dev(dp, seq, t), 4).wait_recv()

        @pl.when(seq == 0)
        def _():
            self.box[2] = (self.box[2].astype(F32) + self.pair[2].astype(F32)).astype(BF)
            self.copy(self.box.at[2], self.box.at[1], _dev(y_dp, seq, t), 6).start()

        @pl.when(seq == 1)
        def _():
            self.box[2] = (self.box[2].astype(F32) + self.pair[1].astype(F32)).astype(BF)
            self.copy(self.box.at[2], self.box.at[0], _dev(x_dp, seq, t), 5).start()

    def final(self, out):
        dp, seq, t, x_dp, y_dp, d_dp = _peers()
        self.copy(self.pair.at[3], self.pair.at[3], _dev(dp, seq, t), 3).wait_recv()
        self.copy(self.pair.at[0], self.box.at[0], _dev(dp, seq, t), 5).wait_recv()
        self.copy(self.pair.at[0], self.box.at[1], _dev(dp, seq, t), 6).wait_recv()
        out[...] = (
            self.part[dp * 2 + seq].astype(F32) + self.pair[3].astype(F32)
            + self.box[0].astype(F32) + self.box[1].astype(F32)
        )

    def finish(self):
        dp, seq, t, x_dp, y_dp, d_dp = _peers()
        for s in range(7):
            self.copy(self.pair.at[0], self.box.at[0], _dev(dp, 1 - seq, t), s).wait_send()


class _Smalls:
    def __init__(self, n, box, line, ssem, rsem):
        self.n, self.box, self.line, self.ssem, self.rsem = n, box, line, ssem, rsem

    def copy(self, j, who):
        return pltpu.make_async_remote_copy(
            src_ref=self.box.at[2 * j], dst_ref=self.box.at[2 * j + 1],
            send_sem=self.ssem.at[j], recv_sem=self.rsem.at[j],
            device_id=who, device_id_type=MESH,
        )

    def near(self, j):
        dp, seq, t, x_dp, y_dp, d_dp = _peers()
        return (_dev(dp, 1 - seq, t), _dev(x_dp, seq, t), _dev(y_dp, seq, t))[j]

    def begin(self, value):
        self.box[0] = value
        self.copy(0, self.near(0)).start()

    def step(self, j):
        self.copy(j, self.near(j)).wait_recv()
        total = self.box[2 * j] + self.box[2 * j + 1]
        if j < 2:
            self.box[2 * j + 2] = total
            self.copy(j + 1, self.near(j + 1)).start()
        else:
            t = lax.axis_index("tensor")
            high = total.astype(BF).astype(F32)
            row = _iota(total.shape, 0)
            rest = pltpu.roll(total - high, 4, 0)
            self.line[t] = jnp.where((row > 10) & (row < 15), rest, high).astype(BF)
            for o in range(self.n):
                @pl.when(t != o)
                def _(o=o):
                    self.across(t, o).start()

    def across(self, src, who):
        dp, seq, t = lax.axis_index("dp"), lax.axis_index("seq"), lax.axis_index("tensor")
        return pltpu.make_async_remote_copy(
            src_ref=self.line.at[src], dst_ref=self.line.at[src],
            send_sem=self.ssem.at[3 + who], recv_sem=self.rsem.at[3 + src],
            device_id=_dev(dp, seq, who), device_id_type=MESH,
        )

    def final(self):
        t = lax.axis_index("tensor")
        for o in range(self.n):
            @pl.when(t != o)
            def _(o=o):
                self.across(o, o).wait_recv()

    def finish(self):
        t = lax.axis_index("tensor")
        for j in range(3):
            self.copy(j, self.near(j)).wait_send()
        for o in range(self.n):
            @pl.when(t != o)
            def _(o=o):
                self.across(t, o).wait_send()


class _LineSum:
    def __init__(self, n, part, box, out, ssem, rsem):
        self.n, self.part, self.box, self.out, self.ssem, self.rsem = n, part, box, out, ssem, rsem

    def copy(self, phase, src_block, dst_ref, who, origin):
        dp, seq = lax.axis_index("dp"), lax.axis_index("seq")
        return pltpu.make_async_remote_copy(
            src_ref=src_block, dst_ref=dst_ref,
            send_sem=self.ssem.at[phase, who], recv_sem=self.rsem.at[phase, origin],
            device_id=_dev(dp, seq, who), device_id_type=MESH,
        )

    def scatter(self):
        t = lax.axis_index("tensor")
        for o in range(self.n):
            @pl.when(t != o)
            def _(o=o):
                self.copy(0, self.part.at[o], self.box.at[t], o, t).start()

    def gather(self):
        t = lax.axis_index("tensor")
        total = self.part[t].astype(F32)
        for o in range(self.n):
            @pl.when(t != o)
            def _(o=o):
                self.copy(0, self.part.at[o], self.box.at[o], o, o).wait_recv()

            @pl.when(t == o)
            def _(o=o):
                self.box[o] = jnp.zeros(self.box.shape[1:], self.box.dtype)
        for o in range(self.n):
            total = total + self.box[o].astype(F32)
        self.out[t] = total.astype(self.out.dtype)
        for o in range(self.n):
            @pl.when(t != o)
            def _(o=o):
                self.copy(1, self.out.at[t], self.out.at[t], o, t).start()

    def arrive(self):
        t = lax.axis_index("tensor")
        for o in range(self.n):
            @pl.when(t != o)
            def _(o=o):
                self.copy(1, self.out.at[o], self.out.at[o], o, o).wait_recv()

    def finish(self):
        t = lax.axis_index("tensor")
        for o in range(self.n):
            @pl.when(t != o)
            def _(o=o):
                self.copy(0, self.part.at[o], self.box.at[o], o, o).wait_send()
                self.copy(1, self.part.at[o], self.box.at[o], o, o).wait_send()


LANES = 128


def _split(v, parts):
    out = []
    for _ in range(parts):
        b = v.astype(BF)
        out.append(b)
        v = v - b.astype(F32)
    return jnp.concatenate(out, axis=1)


def _dot(a, b, ca=1, cb=0):
    return lax.dot_general(a, b, (((ca,), (cb,)), ((), ())), preferred_element_type=F32)


def _iota(shape, axis):
    return lax.broadcasted_iota(jnp.int32, shape, axis)


def _spreader(rows, p):
    head = lax.rem(_iota((rows, LANES), 0), LANES)
    return (head == 2 * p + lax.div(_iota((rows, LANES), 1), HEAD_DIM)).astype(F32).astype(BF)


def _folder(rows, p):
    chan = lax.rem(_iota((rows, LANES), 0), LANES)
    return (_iota((rows, LANES), 1) == 2 * p + lax.div(chan, HEAD_DIM)).astype(F32).astype(BF)


def _sig(v):
    return 1.0 / (1.0 + jnp.exp(-v))


def _three(v):
    return v[:, :LANES] + v[:, LANES : 2 * LANES] + v[:, 2 * LANES :]


def _head_scalars(raw, hp, marks, length):
    v = raw + hp[0:1, :]
    delta = jnp.maximum(v, 0.0) + jnp.log1p(jnp.exp(-jnp.abs(v)))
    log_decay = -delta * jnp.exp(hp[1:2, :])
    lower = (_iota((length, length), 0) >= _iota((length, length), 1)).astype(F32).astype(BF)
    running = _three(_dot(lower, _split(log_decay, 3)))
    entry = jnp.exp(running) * marks[:, 4:5]
    to_end = jnp.exp(running[length - 1 :, :] - running) * marks[:, 5:6]
    return v, delta, log_decay, running, entry, to_end


def _marks(rows):
    full = jnp.concatenate([rows, jnp.zeros((LANES - rows.shape[0], rows.shape[1]), F32)], axis=0)
    return full.T


def _bias_matrix(rows, marks, length):
    ok = (_iota((length, length), 0) >= _iota((length, length), 1)) & (
        marks[:, 0:1] == rows[0:1, :]
    )
    return jnp.where(ok, 0.0, -1e30)


def _conv(pad, marks, taps, bias, length):
    total = bias + taps[0:1, :] * pad[8 : 8 + length, :]
    for k in range(1, KERNEL):
        total = total + taps[k : k + 1, :] * (pad[8 - k : 8 - k + length, :] * marks[:, k : k + 1])
    return total


def mix_fwd_kernel(n, seg, seg_old, hp, taps_i, bias_i, taps_s, bias_s, cot, wo, wg, normed, wi, ws, wt,
                   y, u_i, u_s, entry_o, incoming, gate, cot_full, fo, fg,
                   pre_i, pre_s, old_i, old_s, raw, rows,
                   pad, run3, run_t, bias_m, scores, heads_hl, inflow, zs, zr, ps, pr, ls, hs):
    dp, seq, t = lax.axis_index("dp"), lax.axis_index("seq"), lax.axis_index("tensor")
    seqs, length, width = pre_i.shape
    model = normed.shape[2]
    pairs = width // LANES
    wide = 2 * LANES
    _plane_barrier(n)
    lines = [
        _Line(n, cot_full.at[pl.ds(s, 1)], cot.shape[1], zs.at[s], zr.at[s], cot.at[pl.ds(s, 1)])
        for s in range(seqs)
    ]
    planes = (_Plane(wg, fg, ps.at[0], pr.at[0], ls.at[0]), _Plane(wo, fo, ps.at[1], pr.at[1], ls.at[1]))
    whole = _Line(n, cot_full, cot.shape[1], zs, zr)
    own = pltpu.make_async_copy(cot, whole.block(t), ls.at[2])
    own.start()
    for line in lines:
        line.step(0)
    for plane in planes:
        plane.begin()
    flat = normed[...].reshape(seqs * length, model)
    pre_s[...] = _dot(flat, ws[...].reshape(model, ws.shape[2])).astype(BF).reshape(pre_s.shape)

    def inner_part(c, _):
        ch = pl.ds(pl.multiple_of(c * wide, wide), wide)
        part = _dot(flat, wi[:, :, ch].reshape(model, wide))
        pre_i[:, :, ch] = part.astype(BF).reshape(seqs, length, wide)
        return 0

    lax.fori_loop(0, width // wide, inner_part, 0)
    ends = [
        pltpu.make_async_remote_copy(
            src_ref=a.at[:, pl.ds(length - 16, 16), :], dst_ref=b,
            send_sem=hs.at[2 + i], recv_sem=hs.at[4 + i],
            device_id=_dev(dp, 1 - seq, t), device_id_type=MESH,
        )
        for i, (a, b) in enumerate(((pre_i, old_i), (pre_s, old_s)))
    ]

    @pl.when(seq == 0)
    def _():
        for c in ends:
            c.start()
        old_i[...] = jnp.zeros_like(old_i)
        old_s[...] = jnp.zeros_like(old_s)

    raw[...] = _dot(flat, wt[...].reshape(model, LANES)).reshape(raw.shape)
    for s in range(seqs):
        now = seg[s : s + 1, :].astype(F32)
        old = seg_old[s : s + 1, :].astype(F32)
        both = jnp.broadcast_to(jnp.concatenate([old, now], axis=1), (8, 2 * length))
        here = jnp.broadcast_to(now, (8, length))
        place = _iota((8, length), 0)
        block = jnp.where(place == 0, here, 0.0)
        others = [pltpu.roll(both, k, 1)[:, length:] for k in range(1, KERNEL)]
        others += [both[:, length - 1 : length], both[:, 2 * length - 1 :]]
        for k, other in enumerate(others):
            block = jnp.where((place == k + 1) & (here == other), 1.0, block)
        rows[s] = block

    lines[0].step(1)

    @pl.when(seq == 1)
    def _():
        for c in ends:
            c.wait_recv()

    def one(s, _):
        rw = rows[s]
        marks = _marks(rw)
        v, delta, log_decay, running, entry, to_end = _head_scalars(raw[s], hp, marks, length)
        entry_o[s] = entry
        run3[...] = _split(running, 3)
        run_t[...] = running.T
        bias_m[...] = _bias_matrix(rw, marks, length)
        heads_hl[0] = _split(delta, 2)
        heads_hl[1] = _split(to_end, 2)
        maps = []
        for half in range(2):
            ch = slice(half * STATE, (half + 1) * STATE)
            pad[0:8, :] = old_s[s, :, ch].astype(F32)[8:16, :]
            pad[8:, :] = pre_s[s, :, ch].astype(F32)
            u = _conv(pad, marks, taps_s[:, ch], bias_s[:, ch], length)
            u_s[s, :, ch] = u
            maps.append((u * _sig(u)).astype(BF))
        b_map, c_map = maps
        scores[...] = _dot(c_map, b_map, 1, 1)

        def pair(p, _):
            @pl.when(jnp.logical_and(s == 0, p == 4))
            def _():
                lines[1].step(1)

            @pl.when(jnp.logical_and(s == 1, p == 0))
            def _():
                for plane in planes:
                    plane.forward()

            @pl.when(jnp.logical_and(s == 1, p == 1))
            def _():
                lines[0].step(2)

            @pl.when(jnp.logical_and(s == 1, p == 5))
            def _():
                lines[1].step(2)
                planes[0].share()

            ch = pl.ds(pl.multiple_of(p * LANES, LANES), LANES)
            at = pl.ds(pl.multiple_of(t * width + p * LANES, LANES), LANES)
            pad[0:8, :] = old_i[s, :, ch].astype(F32)[8:16, :]
            pad[8:, :] = pre_i[s, :, ch].astype(F32)
            u = _conv(pad, marks, taps_i[:, at], bias_i[:, at], length)
            u_i[s, :, ch] = u
            x = u * _sig(u)
            spread = _spreader(2 * LANES, p)
            xd = x * _dot(heads_hl[0], spread)
            inflow[s, :, ch] = _dot(b_map, (xd * _dot(heads_hl[1], spread)).astype(BF), 0, 0).astype(BF)
            skip = _dot(_split(hp[...], 2), spread)[2:3, :]
            total = skip * x
            xb = xd.astype(BF)
            lane = lax.div(_iota(xb.shape, 1), HEAD_DIM)
            for a in range(2):
                h = 2 * p + a
                pick = (lax.rem(_iota((3 * LANES, length), 0), LANES) == h).astype(F32).astype(BF)
                decay = jnp.exp(_dot(run3[...], pick) - run_t[pl.ds(h, 1), :] + bias_m[...])
                mixing = (decay * scores[...]).astype(BF)
                total = total + _dot(mixing, jnp.where(lane == a, xb, jnp.zeros_like(xb)))
            y[s, :, ch] = total
            return 0

        lax.fori_loop(0, pairs, pair, 0)
        return 0

    lax.fori_loop(0, seqs, one, 0)
    handed = pltpu.make_async_remote_copy(
        src_ref=inflow, dst_ref=incoming, send_sem=hs.at[0], recv_sem=hs.at[1],
        device_id=_dev(dp, 1 - seq, t), device_id_type=MESH,
    )

    @pl.when(seq == 0)
    def _():
        handed.start()
        incoming[...] = jnp.zeros_like(incoming)

    planes[1].share()
    for d in range(3, n):
        lines[0].step(d)
    planes[0].arrive()

    def gate_part(c, _):
        ch = pl.ds(pl.multiple_of(c * wide, wide), wide)
        part = _dot(flat, fg[:, :, ch].reshape(model, wide))
        gate[:, :, ch] = part.reshape(seqs, length, wide)
        return 0

    lax.fori_loop(0, width // wide, gate_part, 0)
    for d in range(3, n):
        lines[1].step(d)
    planes[1].arrive()
    own.wait()

    @pl.when(seq == 0)
    def _():
        handed.wait_send()
        for c in ends:
            c.wait_send()

    @pl.when(seq == 1)
    def _():
        handed.wait_recv()

    for line in lines:
        line.finish()
    for plane in planes:
        plane.finish()


def _mixer_call(kernel, ins, outs, scratch, name, cost, number, far=()):
    vm = pl.BlockSpec(memory_space=pltpu.VMEM)
    return pl.pallas_call(
        kernel,
        out_shape=outs,
        in_specs=[
            pl.BlockSpec(memory_space=pltpu.HBM if i in far else pltpu.VMEM) for i in range(len(ins))
        ],
        out_specs=(vm,) * len(outs),
        scratch_shapes=scratch,
        compiler_params=pltpu.CompilerParams(
            collective_id=number, has_side_effects=True, vmem_limit_bytes=28 << 20
        ),
        cost_estimate=pl.CostEstimate(flops=cost, bytes_accessed=1 << 20, transcendentals=0),
        name=name,
    )(*ins)


def mix_fwd(n, seg, seg_old, hp, taps_i, bias_i, taps_s, bias_s, cot, wo, wg, normed, wi, ws, wt):
    seqs, length, model = normed.shape
    width = wi.shape[2]
    sd = jax.ShapeDtypeStruct
    return _mixer_call(
        functools.partial(mix_fwd_kernel, n),
        (seg, seg_old, hp, taps_i, bias_i, taps_s, bias_s, cot, wo, wg, normed, wi, ws, wt),
        (
            sd((seqs, length, width), F32),
            sd((seqs, length, width), F32),
            sd((seqs, length, 2 * STATE), F32),
            sd((seqs, length, LANES), F32),
            sd((seqs, STATE, width), BF),
            sd((seqs, length, width), F32),
            sd((seqs, length, model), BF),
            sd((8,) + wo.shape, BF),
            sd((8,) + wg.shape, BF),
            sd((seqs, length, width), BF),
            sd((seqs, length, 2 * STATE), BF),
            sd((seqs, 16, width), BF),
            sd((seqs, 16, 2 * STATE), BF),
            sd((seqs, length, LANES), F32),
            sd((seqs, 8, length), F32),
        ),
        [
            pltpu.VMEM((8 + length, LANES), F32),
            pltpu.VMEM((length, 3 * LANES), BF),
            pltpu.VMEM((LANES, length), F32),
            pltpu.VMEM((length, length), F32),
            pltpu.VMEM((length, length), F32),
            pltpu.VMEM((2, length, 2 * LANES), BF),
            pltpu.VMEM((seqs, STATE, width), BF),
            pltpu.SemaphoreType.DMA((seqs, 2, n)),
            pltpu.SemaphoreType.DMA((seqs, n)),
            pltpu.SemaphoreType.DMA((2, 7)),
            pltpu.SemaphoreType.DMA((2, 7)),
            pltpu.SemaphoreType.DMA((3,)),
            pltpu.SemaphoreType.DMA((6,)),
        ],
        "mix_fwd",
        30 * 10**9,
        3,
        (7, 8, 9),
    )


def gate_kernel(n, y_part, u_s, entry, h0, gate, cot, wo, gain, tokens_in,
                d_mixed, d_gate, lam, po, go, gg, g_gain,
                mixed, gated, grad_gn, normed, local, acc, box, ss, rs, hs):
    dp, seq, t = lax.axis_index("dp"), lax.axis_index("seq"), lax.axis_index("tensor")
    seqs, length, width = y_part.shape
    model = cot.shape[2]
    wide = 2 * LANES
    bar = pltpu.get_barrier_semaphore()
    pl.semaphore_signal(bar, inc=1, device_id=_dev(dp, 1 - seq, t), device_id_type=MESH)
    for step in range(1, n):
        pl.semaphore_signal(
            bar, inc=1, device_id=_dev(dp, seq, lax.rem(t + step, n)), device_id_type=MESH
        )
    acc[...] = jnp.zeros_like(acc)
    g_gain[...] = jnp.zeros_like(g_gain)

    def spread_of(s, c):
        heads = _split(entry[s], 2)
        head = lax.rem(_iota((wide, wide), 0), LANES)
        one = head == 4 * c + lax.div(_iota((wide, wide), 1), HEAD_DIM)
        return _dot(heads, one.astype(F32).astype(BF))

    def maps(s):
        u = u_s[s, :, STATE:]
        return (u * _sig(u)).astype(BF)

    def first(c, _):
        ch = pl.ds(pl.multiple_of(c * wide, wide), wide)
        at = pl.ds(pl.multiple_of(t * width + c * wide, wide), wide)
        w = wo[:, :, ch].reshape(model, wide)
        for s in range(seqs):
            g = _dot(cot[s], w)
            grad_gn[s, :, ch] = g
            m = y_part[s, :, ch] + spread_of(s, c) * _dot(maps(s), h0[s, :, ch])
            z = gate[s, :, ch]
            gd = m * (z * _sig(z))
            mixed[s, :, ch] = m
            gated[s, :, ch] = gd
            sq, ds = gd * gd, g * gain[:, at] * gd
            acc[0, s] += sq[:, :LANES] + sq[:, LANES:]
            acc[1, s] += ds[:, :LANES] + ds[:, LANES:]
        return 0

    lax.fori_loop(0, width // wide, first, 0)
    ones = jnp.ones((8, wide), F32).astype(BF)
    row = _iota((8, length), 0)
    mine = jnp.zeros((8, length), F32)
    for kind in range(2):
        for s in range(seqs):
            sums = _dot(ones, _split(acc[kind, s], 2), 1, 1)
            mine = jnp.where(row == kind * seqs + s, sums, mine)
    box[t] = mine
    pl.semaphore_wait(bar, n)

    def copy(src, who):
        return pltpu.make_async_remote_copy(
            src_ref=box.at[src], dst_ref=box.at[src], send_sem=ss.at[who], recv_sem=rs.at[src],
            device_id=_dev(dp, seq, who), device_id_type=MESH,
        )

    for o in range(n):
        @pl.when(t != o)
        def _(o=o):
            copy(t, o).start()
    for o in range(n):
        @pl.when(t != o)
        def _(o=o):
            copy(o, o).wait_recv()
    full_width = n * width
    cols = _marks(jnp.sum(box[...], axis=0) / full_width)

    def second(c, _):
        ch = pl.ds(pl.multiple_of(c * wide, wide), wide)
        at = pl.ds(pl.multiple_of(t * width + c * wide, wide), wide)
        gn = gain[:, at]
        for s in range(seqs):
            rms = lax.rsqrt(cols[:, s : s + 1] + EPS)
            mean = cols[:, seqs + s : seqs + s + 1]
            g, gd, m, z = grad_gn[s, :, ch], gated[s, :, ch], mixed[s, :, ch], gate[s, :, ch]
            sg = _sig(z)
            scaled = gd * rms
            normed[s, :, ch] = (scaled * gn).astype(BF)
            g_gain[0:1, ch] += jnp.sum(g * scaled, axis=0, keepdims=True)
            d_gd = rms * (g * gn) - scaled * (rms * rms * mean)
            dm = d_gd * (z * sg)
            d_mixed[s, :, ch] = dm
            d_gate[s, :, ch] = (d_gd * m * sg * (1.0 + z * (1.0 - sg))).astype(BF)
            ed = (spread_of(s, c) * dm).astype(BF)
            local[s, :, ch] = _dot(maps(s), ed, 0, 0).astype(BF)
        return 0

    lax.fori_loop(0, width // wide, second, 0)
    handed = pltpu.make_async_remote_copy(
        src_ref=local, dst_ref=lam, send_sem=hs.at[0], recv_sem=hs.at[1],
        device_id=_dev(dp, 1 - seq, t), device_id_type=MESH,
    )

    @pl.when(seq == 1)
    def _():
        handed.start()
        lam[...] = jnp.zeros_like(lam)

    blocks = 2
    rows = blocks * wo.shape[1]

    def third(b, _):
        ch = pl.ds(pl.multiple_of(b * rows, LANES), rows)
        w = wo[pl.ds(b * blocks, blocks)].reshape(rows, width)
        total = None
        for s in range(seqs):
            po[s, :, ch] = _dot(normed[s], w, 1, 1).astype(BF)
            part = _dot(cot[s, :, ch], normed[s], 0, 0)
            total = part if total is None else total + part
        go[pl.ds(b * blocks, blocks)] = total.reshape(blocks, wo.shape[1], width).astype(BF)
        total = None
        for s in range(seqs):
            part = _dot(tokens_in[s, :, ch], d_gate[s], 0, 0)
            total = part if total is None else total + part
        gg[pl.ds(b * blocks, blocks)] = total.reshape(blocks, wo.shape[1], width).astype(BF)
        return 0

    lax.fori_loop(0, model // rows, third, 0)

    @pl.when(seq == 1)
    def _():
        handed.wait_send()

    @pl.when(seq == 0)
    def _():
        handed.wait_recv()

    for o in range(n):
        @pl.when(t != o)
        def _(o=o):
            copy(o, o).wait_send()


def gate_stage(n, y_part, u_s, entry, h0, gate, cot, wo, gain, tokens_in):
    seqs, length, width = y_part.shape
    sd = jax.ShapeDtypeStruct
    whole = pltpu.VMEM((seqs, length, width), F32)
    return _mixer_call(
        functools.partial(gate_kernel, n),
        (y_part, u_s, entry, h0, gate, cot, wo, gain, tokens_in),
        (
            sd((seqs, length, width), F32),
            sd((seqs, length, width), BF),
            sd((seqs, STATE, width), BF),
            sd((seqs, length, cot.shape[2]), BF),
            sd(wo.shape, BF),
            sd(wo.shape, BF),
            sd((8, width), F32),
        ),
        [
            whole, whole, whole,
            pltpu.VMEM((seqs, length, width), BF),
            pltpu.VMEM((seqs, STATE, width), BF),
            pltpu.VMEM((2, seqs, length, LANES), F32),
            pltpu.VMEM((n, 8, length), F32),
            pltpu.SemaphoreType.DMA((n,)),
            pltpu.SemaphoreType.DMA((n,)),
            pltpu.SemaphoreType.DMA((2,)),
        ],
        "gate_stage",
        6 * 10**9,
        2,
    )


def mix_bwd_kernel(n, dy_r, u_i, u_s, pre_i, old_i, pre_s, old_s, raw, rows, h0, lam, hp,
                   taps_i, taps_s, po, go, gg,
                   d_i, d_s, d_raw, sm_i, sm_s, sm_h, o_po, o_go, o_gg,
                   pad, moved, run3, run_t, bias_m, scores, d_scores, heads_hl,
                   acc_r, acc_c, acc_d, acc_q, d_b, d_c, lo, ro, xo, bo, xg, bg,
                   head_i, tail_i, head_s, tail_s, next_i, next_s, zs, zr, ps, pr, hs):
    t = lax.axis_index("tensor")
    seqs, length, width = pre_i.shape
    pairs = width // LANES
    _plane_barrier(n)
    lines = _line_reduces(n, po, lo, ro, zs, zr)
    planes = (
        _PlaneReduce(go, xo, bo, ps.at[0], pr.at[0]), _PlaneReduce(gg, xg, bg, ps.at[1], pr.at[1])
    )
    for j in range(n - 1):
        for begin, _, _, _ in lines:
            begin(j)
    for plane in planes:
        plane.begin()
    sm_i[...] = jnp.zeros_like(sm_i)
    sm_s[...] = jnp.zeros_like(sm_s)
    sm_h[...] = jnp.zeros_like(sm_h)
    moved[0:8, :] = jnp.zeros((8, LANES), F32)
    moved[8 + length :, :] = jnp.zeros((8, LANES), F32)

    def conv_back(du, marks, taps, s, ch, d_o, head_o, tail_o, sm):
        total = None
        for k in range(KERNEL):
            m = du if k == 0 else du * marks[:, k : k + 1]
            moved[8 : 8 + length, :] = m
            sm[k : k + 1, ch] += jnp.sum(m * pad[8 - k : 8 - k + length, :], axis=0, keepdims=True)
            part = taps[k : k + 1, :] * moved[k : k + 8 + length, :]
            total = part if total is None else total + part
        sm[4:5, ch] += jnp.sum(du, axis=0, keepdims=True)
        head_o[s, :, ch] = total[0:8, :]
        d_o[s, :, ch] = total[8:, :].astype(BF)
        tail_o[s, :, ch] = total[length - 8 :, :]

    def one(s, _):
        rw = rows[s]
        marks = _marks(rw)
        v, delta, log_decay, running, entry, to_end = _head_scalars(raw[s], hp, marks, length)
        run3[...] = _split(running, 3)
        run_t[...] = running.T
        bias_m[...] = _bias_matrix(rw, marks, length)
        heads_hl[0] = _split(delta, 2)
        heads_hl[1] = _split(to_end, 2)
        heads_hl[2] = _split(entry, 2)
        ub, uc = u_s[s, :, :STATE], u_s[s, :, STATE:]
        sb, sc = _sig(ub), _sig(uc)
        b_map, c_map = (ub * sb).astype(BF), (uc * sc).astype(BF)
        scores[...] = _dot(c_map, b_map, 1, 1)
        d_scores[...] = jnp.zeros_like(d_scores)
        for acc in (acc_r, acc_c, acc_d, acc_q, d_b, d_c):
            acc[...] = jnp.zeros_like(acc)

        def pair(p, _):
            @pl.when(jnp.logical_and(s == 0, p == 3))
            def _():
                lines[0][1](1)

            @pl.when(jnp.logical_and(s == 0, p == 5))
            def _():
                for plane in planes:
                    plane.send_far()

            @pl.when(jnp.logical_and(s == 1, p == 0))
            def _():
                lines[1][1](1)

            @pl.when(jnp.logical_and(s == 1, p == 2))
            def _():
                lines[0][1](2)

            @pl.when(jnp.logical_and(s == 1, p == 3))
            def _():
                planes[0].send_near()

            @pl.when(jnp.logical_and(s == 1, p == 5))
            def _():
                lines[1][1](2)
                planes[1].send_near()

            ch = pl.ds(pl.multiple_of(p * LANES, LANES), LANES)
            at = pl.ds(pl.multiple_of(t * width + p * LANES, LANES), LANES)
            u = u_i[s, :, ch]
            sg = _sig(u)
            x = u * sg
            dy = dy_r[s, :, ch]
            spread, fold = _spreader(2 * LANES, p), _folder(2 * LANES, p)
            dl = _dot(heads_hl[0], spread)
            q = _dot(heads_hl[1], spread)
            e = _dot(heads_hl[2], spread)
            xd = x * dl
            xb, db = xd.astype(BF), dy.astype(BF)
            h_in, l_in = h0[s, :, ch], lam[s, :, ch]
            c_h = _dot(c_map, h_in)
            b_l = _dot(b_map, l_in)
            qx, ed = q * xd, e * dy
            d_b[...] += _dot(qx.astype(BF), l_in, 1, 1)
            d_c[...] += _dot(ed.astype(BF), h_in, 1, 1)
            late = qx * b_l
            dxd = q * b_l
            sum_r = _dot(_split(ed * c_h - late, 2), fold)
            sum_s = sum_c = None
            lane = lax.div(_iota(xb.shape, 1), HEAD_DIM)
            for a in range(2):
                h = 2 * p + a
                pick = (lax.rem(_iota((3 * LANES, length), 0), LANES) == h).astype(F32).astype(BF)
                decay = jnp.exp(_dot(run3[...], pick) - run_t[pl.ds(h, 1), :] + bias_m[...])
                da = jnp.where(lane == a, db, jnp.zeros_like(db))
                ld = decay * _dot(da, xb, 1, 1)
                sum_s = ld if a == 0 else sum_s + ld
                both = (ld * scores[...]).astype(BF)
                mixing = (decay * scores[...]).astype(BF)
                dxd = dxd + _dot(mixing, da, 0, 0)
                col = (_iota((length, LANES), 1) == h).astype(F32).astype(BF)
                row = (_iota((LANES, length), 0) == h).astype(F32).astype(BF)
                sum_r = sum_r + _dot(both, col)
                part = _dot(row, both)
                sum_c = part if a == 0 else sum_c + part
            d_scores[...] += sum_s
            acc_r[...] += sum_r
            acc_c[...] += sum_c
            acc_d[...] += _dot(_split(dxd * x, 2), fold)
            total = jnp.broadcast_to(jnp.sum(late, axis=0, keepdims=True), (8, LANES))
            acc_q[...] += _dot(_split(total, 2), fold)
            skip = _dot(_split(hp[...], 2), spread)[2:3, :]
            sm_i[5:6, ch] += jnp.sum(dy * x, axis=0, keepdims=True)
            du = (dxd * dl + skip * dy) * (sg * (1.0 + u * (1.0 - sg)))
            pad[0:8, :] = old_i[s, :, ch].astype(F32)[8:16, :]
            pad[8:, :] = pre_i[s, :, ch].astype(F32)
            conv_back(du, marks, taps_i[:, at], s, ch, d_i, head_i, tail_i, sm_i)
            return 0

        lax.fori_loop(0, pairs, pair, 0)
        ds = d_scores[...].astype(BF)
        grads = (d_b[...] + _dot(ds, c_map, 0, 0), d_c[...] + _dot(ds, b_map))
        for half, (g, u, sg) in enumerate(zip(grads, (ub, uc), (sb, sc))):
            ch = slice(half * STATE, (half + 1) * STATE)
            pad[0:8, :] = old_s[s, :, ch].astype(F32)[8:16, :]
            pad[8:, :] = pre_s[s, :, ch].astype(F32)
            du = g * (sg * (1.0 + u * (1.0 - sg)))
            conv_back(du, marks, taps_s[:, ch], s, ch, d_s, head_s, tail_s, sm_s)
        d_run = acc_r[...] - acc_c[...].T
        last = _iota(d_run.shape, 0) == length - 1
        d_run = d_run + jnp.where(last, acc_q[0:1, :], 0.0)
        upper = (_iota((length, length), 0) <= _iota((length, length), 1)).astype(F32).astype(BF)
        d_log = _three(_dot(upper, _split(d_run, 3)))
        d_delta = acc_d[...] - d_log * jnp.exp(hp[1:2, :])
        d_step = d_delta * _sig(v)
        d_raw[s] = d_step.astype(BF)
        sm_h[0:1, :] += jnp.sum(d_step, axis=0, keepdims=True)
        sm_h[1:2, :] += jnp.sum(d_log * log_decay, axis=0, keepdims=True)
        return 0

    lax.fori_loop(0, seqs, one, 0)
    dp, seq = lax.axis_index("dp"), lax.axis_index("seq")
    handed = [
        pltpu.make_async_remote_copy(
            src_ref=a, dst_ref=b, send_sem=hs.at[2 * i], recv_sem=hs.at[2 * i + 1],
            device_id=_dev(dp, 1 - seq, t), device_id_type=MESH,
        )
        for i, (a, b) in enumerate(((head_i, next_i), (head_s, next_s)))
    ]

    @pl.when(seq == 1)
    def _():
        for c in handed:
            c.start()

    planes[0].final(o_go)

    @pl.when(seq == 0)
    def _():
        for c, box, tail, out in zip(handed, (next_i, next_s), (tail_i, tail_s), (d_i, d_s)):
            c.wait_recv()
            for s in range(seqs):
                more = jnp.concatenate([jnp.zeros_like(box[s]), box[s]], axis=0)
                out[s, length - 16 :, :] = (tail[s] + more).astype(BF)

    @pl.when(seq == 1)
    def _():
        for c in handed:
            c.wait_send()

    planes[1].final(o_gg)
    for s, (_, _, final, _) in enumerate(lines):
        final(o_po.at[pl.ds(s, 1)])
    for plane in planes:
        plane.finish()
    for _, _, _, finish in lines:
        finish()


def mix_bwd(n, dy, u_i, u_s, pre_i, old_i, pre_s, old_s, raw, rows, h0, lam, hp, taps_i, taps_s,
            po, go, gg):
    seqs, length, width = pre_i.shape
    model = po.shape[2]
    box = pltpu.VMEM((n, seqs, length // n, model), BF)
    sd = jax.ShapeDtypeStruct
    square = pltpu.VMEM((length, length), F32)
    tall = pltpu.VMEM((length, LANES), F32)
    return _mixer_call(
        functools.partial(mix_bwd_kernel, n),
        (dy, u_i, u_s, pre_i, old_i, pre_s, old_s, raw, rows, h0, lam, hp, taps_i, taps_s, po, go,
         gg),
        (
            sd((seqs, length, width), BF),
            sd((seqs, length, 2 * STATE), BF),
            sd((seqs, length, LANES), BF),
            sd((8, width), F32),
            sd((8, 2 * STATE), F32),
            sd((8, LANES), F32),
            sd((seqs, length // n, model), F32),
            sd(go.shape[1:], F32),
            sd(gg.shape[1:], F32),
        ),
        [
            pltpu.VMEM((8 + length, LANES), F32),
            pltpu.VMEM((16 + length, LANES), F32),
            pltpu.VMEM((length, 3 * LANES), BF),
            pltpu.VMEM((LANES, length), F32),
            square, square, square,
            pltpu.VMEM((3, length, 2 * LANES), BF),
            tall, pltpu.VMEM((LANES, length), F32), tall, pltpu.VMEM((8, LANES), F32), tall, tall,
            box, box,
            pltpu.VMEM((4,) + go.shape[1:], BF),
            pltpu.VMEM((3,) + go.shape[1:], BF),
            pltpu.VMEM((4,) + gg.shape[1:], BF),
            pltpu.VMEM((3,) + gg.shape[1:], BF),
            pltpu.VMEM((seqs, 8, width), F32),
            pltpu.VMEM((seqs, 16, width), F32),
            pltpu.VMEM((seqs, 8, 2 * STATE), F32),
            pltpu.VMEM((seqs, 16, 2 * STATE), F32),
            pltpu.VMEM((seqs, 8, width), F32),
            pltpu.VMEM((seqs, 8, 2 * STATE), F32),
            pltpu.SemaphoreType.DMA((seqs, 2, n)),
            pltpu.SemaphoreType.DMA((seqs, 2, n)),
            pltpu.SemaphoreType.DMA((2, 7)),
            pltpu.SemaphoreType.DMA((2, 7)),
            pltpu.SemaphoreType.DMA((4,)),
        ],
        "mix_bwd",
        8 * 10**9,
        4,
    )


def reduce_kernel(n, normed, dg, di, ds, dr, wg, wi, ws, wt, gain, sm_i, sm_s, sm_h, g_gain,
                  o_pg, o_gi, o_gs, o_gt, o_sm,
                  pg, gi, gs, gt, lg, rg, xi, xs, xt, bi, bs, bt, mb,
                  xp, xb, xo2, zs, zr, ps, pr, ms, mr, es, er):
    _plane_barrier(n)
    seqs, length, width = di.shape
    model = normed.shape[2]
    blocks = 2
    rows = blocks * wi.shape[1]
    small = _Smalls(n, mb, o_sm, ms, mr)
    mb[0] = jnp.zeros(mb.shape[1:], F32)
    mb[0, 0:6, :] = sm_i[0:6, :]
    mb[0, 6:7, :] = g_gain[0:1, :]
    for k in range(5):
        at = 256 * (k % 3)
        mb[0, 9 + k // 3 : 10 + k // 3, at : at + 256] = sm_s[k : k + 1, :]
    mb[0, 10:11, 512:640] = sm_h[0:1, :]
    mb[0, 10:11, 640:768] = sm_h[1:2, :]

    lines = _line_reduces(n, pg, lg, rg, zs, zr)
    totals = [None] * (model // rows)
    for s in range(seqs):
        for b in range(model // rows):
            ch = slice(b * rows, (b + 1) * rows)
            near = slice(b * blocks, (b + 1) * blocks)
            part = None
            for d, w in zip((dg, di, ds, dr), (wg, wi, ws, wt)):
                more = _dot(d[s], w[near].reshape(rows, w.shape[2]), 1, 1)
                part = more if part is None else part + more
            pg[s, :, ch] = part.astype(BF)
            part = jnp.sum(part * normed[s, :, ch].astype(F32), axis=0, keepdims=True)
            totals[b] = part if totals[b] is None else totals[b] + part
        lines[s][0](0)
    for b, total in enumerate(totals):
        ch = slice(b * rows, (b + 1) * rows)
        mb[0, 7 + b // 2 : 8 + b // 2, (b % 2) * rows : (b % 2 + 1) * rows] = total / gain[:, ch]
    small.copy(0, small.near(0)).start()
    for j in range(1, n - 2):
        for line in lines:
            line[0](j)
    planes = [
        _PlaneReduce(part, pair, box, ps.at[i], pr.at[i])
        for i, (part, pair, box) in enumerate(((gs, xs, bs), (gt, xt, bt), (gi, xi, bi)))
    ]

    def weight(d, out):
        def one(b, _):
            ch = pl.ds(pl.multiple_of(b * rows, LANES), rows)
            total = None
            for s in range(seqs):
                part = _dot(normed[s, :, ch], d[s], 0, 0)
                total = part if total is None else total + part
            out[pl.ds(b * blocks, blocks)] = total.reshape(
                blocks, wi.shape[1], d.shape[2]
            ).astype(BF)
            return 0

        lax.fori_loop(0, model // rows, one, 0)

    weight(ds, gs)
    planes[0].begin()
    weight(dr, gt)
    planes[1].begin()
    small.step(0)
    weight(di, gi)
    planes[2].begin()
    lines[0][1](1)
    small.step(1)
    lines[1][1](1)
    small.step(2)
    for line in lines:
        line[0](n - 2)
    for p in planes:
        p.send_far()
    lines[0][1](2)
    for p in planes[:2]:
        p.send_near()
    planes[0].final(o_gs)
    planes[1].final(o_gt)
    quarter = xp.shape[1]
    for o in range(n):
        xp[o] = o_gs[o * quarter : (o + 1) * quarter, :].astype(BF)
    state = _LineSum(n, xp, xb, xo2, es, er)
    state.scatter()
    planes[2].send_near()
    lines[1][1](2)
    state.gather()
    planes[2].final(o_gi)
    small.final()
    for s, (_, _, final, _) in enumerate(lines):
        final(o_pg.at[pl.ds(s, 1)])
    state.arrive()
    for o in range(n):
        o_gs[o * quarter : (o + 1) * quarter, :] = xo2[o].astype(F32)
    for p in planes:
        p.finish()
    state.finish()
    small.finish()
    for _, _, _, finish in lines:
        finish()


def reduce_all(n, normed, dg, di, ds, dr, wg, wi, ws, wt, gain, sm_i, sm_s, sm_h, g_gain):
    seqs, length, model = normed.shape
    rows = length // n
    sd = jax.ShapeDtypeStruct
    box = pltpu.VMEM((n, seqs, rows, model), BF)
    quarter = pltpu.VMEM((n, ws.shape[1] // n, ws.shape[2]), BF)
    sums = (16, wi.shape[2])
    return _mixer_call(
        functools.partial(reduce_kernel, n),
        (normed, dg, di, ds, dr, wg, wi, ws, wt, gain, sm_i, sm_s, sm_h, g_gain),
        (sd((seqs, rows, model), F32),)
        + tuple(sd(w.shape[1:], F32) for w in (wi, ws, wt))
        + (sd((n,) + sums, BF),),
        [pltpu.VMEM((seqs, length, model), BF)]
        + [pltpu.VMEM(w.shape, BF) for w in (wi, ws, wt)]
        + [box, box]
        + [pltpu.VMEM((4,) + w.shape[1:], BF) for w in (wi, ws, wt)]
        + [pltpu.VMEM((3,) + w.shape[1:], BF) for w in (wi, ws, wt)]
        + [
            pltpu.VMEM((6,) + sums, F32),
            quarter, quarter, quarter,
            pltpu.SemaphoreType.DMA((seqs, 2, n)),
            pltpu.SemaphoreType.DMA((seqs, 2, n)),
            pltpu.SemaphoreType.DMA((3, 7)),
            pltpu.SemaphoreType.DMA((3, 7)),
            pltpu.SemaphoreType.DMA((3 + n,)),
            pltpu.SemaphoreType.DMA((3 + n,)),
            pltpu.SemaphoreType.DMA((2, n)),
            pltpu.SemaphoreType.DMA((2, n)),
        ],
        "reduce_all",
        6 * 10**9,
        1,
    )


def emit_kernel(n, heads, tok, cot, gain, branch, rows, gg, gi, gs, gt, go, sms,
                block_out, g_tok, g_in, o_gg, o_gi, o_gs, o_gt, o_ci, o_ib, o_cs, o_sb,
                o_shift, o_rate, o_skip, o_gain, o_go):
    for s in range(tok.shape[0]):
        v = tok[s].astype(F32)
        rms = lax.rsqrt(jnp.mean(v * v, axis=-1, keepdims=True) + EPS)
        block_out[s] = (v + branch[s]).astype(BF)
        scaled = rows[s] * gain[...]
        mean = jnp.mean(scaled * v, axis=-1, keepdims=True)
        g_tok[s] = cot[s].astype(F32) + rms * scaled - v * (rms * rms * rms * mean)
    o_gg[...] = gg[...]
    o_gi[...] = gi[...]
    o_gs[...] = gs[...]
    short = jnp.zeros((256 - gt.shape[0], LANES), F32)
    o_gt[...] = jnp.concatenate([gt[...], short], axis=0).T[:heads, : gt.shape[0]]
    o_go[...] = go[...]
    width = sms.shape[2]
    shared = None
    head_rows = None
    for t in range(n):
        ch = slice(t * width, (t + 1) * width)
        every = sms[t].astype(F32)
        o_ci[:, ch] = every[0:4, :]
        o_ib[:, ch] = every[4:5, :]
        o_gain[:, ch] = every[6:7, :]
        whole = every[7:11, :] + every[11:15, :]
        block = jnp.concatenate([whole, whole], axis=0)
        shared = whole if shared is None else shared + whole
        lanes = _iota((3 * width, LANES), 0)
        chan = lax.rem(lanes, width)
        to = _iota((3 * width, LANES), 1) == heads * t + lax.div(chan, HEAD_DIM)
        skips = _dot(_split(every[0:8, :], 3), to.astype(F32).astype(BF))
        lanes = lax.rem(_iota((3 * LANES, LANES), 0), LANES)
        to = (_iota((3 * LANES, LANES), 1) == heads * t + lanes) & (lanes < heads)
        to = to.astype(F32).astype(BF)
        shift = _dot(_split(block[:, 512:640], 3), to)
        rate = _dot(_split(block[:, 640:768], 3), to)
        new = (skips[5:6, :], shift[3:4, :], rate[3:4, :])
        head_rows = new if head_rows is None else tuple(a + b for a, b in zip(head_rows, new))
    count = n * heads
    o_skip[...] = head_rows[0][:, :count]
    o_shift[...] = head_rows[1][:, :count]
    o_rate[...] = head_rows[2][:, :count]
    g_in[:, :width] = shared[0:1, :]
    g_in[:, width:] = shared[1:2, :]
    for k in range(4):
        at = 256 * (k % 3)
        o_cs[k : k + 1, :] = shared[2 + k // 3 : 3 + k // 3, at : at + 256]
    o_sb[...] = shared[3:4, 256:512]


def emit_all(n, heads, tok, cot, gain, branch, rows, gg, gi, gs, gt, go, sms):
    vm = pl.BlockSpec(memory_space=pltpu.VMEM)
    sd = lambda *shape: jax.ShapeDtypeStruct(shape, F32)
    width = sms.shape[2]
    outs = (
        jax.ShapeDtypeStruct(tok.shape, BF), sd(*tok.shape), sd(1, tok.shape[2]),
        sd(*gg.shape), sd(*gi.shape), sd(*gs.shape), sd(heads, gt.shape[0]),
        sd(4, n * width), sd(1, n * width), sd(4, 2 * STATE), sd(1, 2 * STATE),
        sd(1, n * heads), sd(1, n * heads), sd(1, n * heads), sd(1, n * width),
        sd(*go.shape),
    )
    return pl.pallas_call(
        functools.partial(emit_kernel, n, heads),
        out_shape=outs,
        in_specs=[vm] * 11,
        out_specs=(vm,) * len(outs),
        compiler_params=pltpu.CompilerParams(vmem_limit_bytes=28 << 20),
        name="emit_all",
    )(tok, cot, gain, branch, rows, gg, gi, gs, gt, go, sms)


def per_device(
    tokens,
    segments,
    input_gain,
    gate_proj,
    inner_proj,
    state_proj,
    step_proj,
    conv_inner,
    inner_bias,
    conv_state,
    state_bias,
    step_bias,
    log_rates,
    skip_gain,
    gated_gain,
    output_proj,
    cotangent,
):
    tensor_count = lax.axis_size("tensor")
    tensor_rank = lax.axis_index("tensor")
    residual = tokens.astype(jnp.float32)
    rms_in = lax.rsqrt(jnp.mean(residual * residual, axis=-1, keepdims=True) + EPS)
    normed_own = (residual * rms_in * input_gain).astype(jnp.bfloat16)
    normed, cot_rows = (
        lax.all_gather(normed_own, "tensor", axis=1, tiled=True),
        lax.all_gather(cotangent, "tensor", axis=1, tiled=True),
    )
    gate_full, inner_full, state_full, step_full, output_full = (
        lax.all_gather(gate_proj, ("dp", "seq"), axis=0, tiled=True),
        lax.all_gather(inner_proj, ("dp", "seq"), axis=0, tiled=True),
        lax.all_gather(state_proj, ("dp", "seq"), axis=0, tiled=True),
        lax.all_gather(step_proj, ("dp", "seq"), axis=0, tiled=True),
        lax.all_gather(output_proj, ("dp", "seq"), axis=1, tiled=True),
    )
    gate_in = jnp.dot(normed, gate_full, preferred_element_type=jnp.float32)
    inner_low = jnp.dot(normed, inner_full, preferred_element_type=jnp.float32).astype(jnp.bfloat16)
    state_low = jnp.dot(normed, state_full, preferred_element_type=jnp.float32).astype(jnp.bfloat16)
    step_raw = jnp.dot(normed, step_full, preferred_element_type=jnp.float32)
    margin = KERNEL - 1
    seg_float = segments.astype(jnp.float32)
    prior_inner, prior_state, prior_seg = passed_along(
        (
            inner_low[:, -margin:],
            state_low[:, -margin:],
            seg_float[:, -margin:].astype(jnp.bfloat16),
        ),
        "seq",
        1,
    )
    padded_inner = jnp.concatenate([prior_inner, inner_low], axis=1).astype(jnp.float32)
    padded_state = jnp.concatenate([prior_state, state_low], axis=1).astype(jnp.float32)
    seg_padded = jnp.concatenate([prior_seg.astype(jnp.float32), seg_float], axis=1)
    pieces = segments.shape[1] // BLOCK
    seg_blocks = blocked(seg_float, pieces)
    before = jnp.concatenate(
        [prior_seg[:, -1:].astype(jnp.float32), seg_blocks[:, :-1, -1]], axis=1
    )
    width_here = inner_full.shape[1]
    heads_here = step_full.shape[1]
    chan_start = tensor_rank * width_here
    head_start = tensor_rank * heads_here
    kernel_here = lax.dynamic_slice_in_dim(conv_inner, chan_start, width_here, 1)
    bias_here = lax.dynamic_slice_in_dim(inner_bias, chan_start, width_here, 0)
    gain_here = lax.dynamic_slice_in_dim(gated_gain, chan_start, width_here, 0)
    shift_here = lax.dynamic_slice_in_dim(step_bias, head_start, heads_here, 0)
    rates_here = lax.dynamic_slice_in_dim(log_rates, head_start, heads_here, 0)
    skip_here = lax.dynamic_slice_in_dim(skip_gain, head_start, heads_here, 0)

    def mixer_front(
        pad_inner, pad_state, raw_steps, kernel_w, kernel_b, state_w, state_b, step_shift, rate_logs
    ):
        inner = jax.nn.silu(causal_mix(pad_inner, seg_padded, kernel_w, kernel_b))
        inner = inner.reshape(inner.shape[0], inner.shape[1], -1, HEAD_DIM)
        both_maps = jax.nn.silu(causal_mix(pad_state, seg_padded, state_w, state_b))
        b_proj = both_maps[:, :, :STATE]
        c_proj = both_maps[:, :, STATE:]
        deltas = jax.nn.softplus(raw_steps + step_shift)
        log_decay = deltas * -jnp.exp(rate_logs)
        inflow, passing = block_sums(inner, deltas, log_decay, b_proj, seg_blocks, before)
        return (inner, deltas, log_decay, b_proj, c_proj, inflow, passing)

    def mixer_rear(inner, deltas, log_decay, b_proj, c_proj, inflow, passing, incoming, skips):
        running = jnp.cumsum(blocked(log_decay, pieces), axis=2)
        places = jnp.arange(running.shape[2])
        allowed = (seg_blocks[:, :, :, None] == seg_blocks[:, :, None, :]) & (
            places[:, None] >= places[None, :]
        )
        inside = allowed[..., None]
        decays = jnp.where(
            inside,
            jnp.exp(jnp.where(inside, running[:, :, :, None, :] - running[:, :, None, :, :], 0.0)),
            0.0,
        )
        scores = jnp.einsum(
            "scin,scjn->scij", blocked(c_proj, pieces), blocked(b_proj, pieces), precision=HIGH
        )
        mixing = decays * scores[..., None] * blocked(deltas, pieces)[:, :, None, :, :]
        direct = jnp.einsum("scijh,scjhp->scihp", mixing, blocked(inner, pieces), precision=HIGH)
        from_state, outgoing = state_reads(
            incoming, log_decay, c_proj, inflow, passing, seg_blocks, before
        )
        heads_out = (direct + from_state).reshape(inner.shape) + skips[:, None] * inner
        return (heads_out.reshape(inner.shape[0], inner.shape[1], -1), outgoing)

    front_args = (
        padded_inner,
        padded_state,
        step_raw,
        kernel_here,
        bias_here,
        conv_state,
        state_bias,
        shift_here,
        rates_here,
    )
    front_vals = mixer_front(*front_args)
    inner, deltas, log_decay, b_proj, c_proj, inflow, passing = front_vals
    span_decay = jnp.ones(passing[:, 0].shape, jnp.float32)
    span_state = jnp.zeros(inflow[:, 0].shape, jnp.float32)
    span_state = passing[:, 0, :, None, None] * span_state + inflow[:, 0]
    span_decay = span_decay * passing[:, 0]
    identity = (jnp.ones_like(span_decay), jnp.zeros_like(span_state))
    incoming = entering_2((span_decay, span_state), "seq", chain_link, identity)[1]
    mixed, outgoing = mixer_rear(*front_vals, incoming, skip_here)
    sigmoid_z = jax.nn.sigmoid(gate_in)
    silu_z = gate_in * sigmoid_z
    gated = mixed * silu_z
    full_width = tensor_count * gated.shape[-1]
    square_sum = lax.psum(jnp.sum(gated * gated, axis=-1), "tensor")
    rms_gate = lax.rsqrt(square_sum / full_width + EPS)[..., None]
    gate_normed = (gated * rms_gate * gain_here).astype(jnp.bfloat16)
    partial_out = jnp.dot(gate_normed, output_full, preferred_element_type=jnp.float32)
    branch_rows = lax.psum_scatter(partial_out, "tensor", scatter_dimension=1, tiled=True)
    block_out = (residual + branch_rows).astype(jnp.bfloat16)
    grad_output = jnp.einsum(
        "srk,srd->kd", gate_normed, cot_rows, preferred_element_type=jnp.float32
    )
    grad_gn = jnp.einsum("srd,kd->srk", cot_rows, output_full, preferred_element_type=jnp.float32)
    scaled = grad_gn * gain_here
    dot_sum = lax.psum(jnp.sum(scaled * gated, axis=-1), "tensor")
    grad_gain_here = jnp.sum(grad_gn * gated * rms_gate, axis=(0, 1))
    grad_gated = rms_gate * scaled - gated * rms_gate**3 * (dot_sum / full_width)[..., None]
    grad_mixed = grad_gated * silu_z
    grad_gate_in = (grad_gated * mixed * sigmoid_z * (1.0 + gate_in * (1.0 - sigmoid_z))).astype(
        jnp.bfloat16
    )
    front_vals, front_back = jax.vjp(mixer_front, *front_args)
    unused_rear, rear_back = jax.vjp(mixer_rear, *front_vals, incoming, skip_here)
    inner, deltas, log_decay, b_proj, c_proj, inflow, passing = front_vals
    grad_blocks = blocked(grad_mixed.reshape(inner.shape), pieces)
    unused_reads, read_back = jax.vjp(
        lambda memory_in: state_reads(
            memory_in, log_decay, c_proj, inflow, passing, seg_blocks, before
        )[0],
        incoming,
    )
    local_grad = read_back(grad_blocks)[0]
    outgoing_grad = carried_in((span_decay, local_grad), "seq", chain_link, identity)[1]
    rear_grads = rear_back((grad_mixed, outgoing_grad))
    grad_skip_here = rear_grads[8]
    (
        pad_grad_inner,
        pad_grad_state,
        grad_step_raw,
        grad_kernel_here,
        grad_bias_here,
        grad_conv_state,
        grad_state_bias,
        grad_shift_here,
        grad_rates_here,
    ) = front_back(tuple(rear_grads[:7]))
    from_next_inner, from_next_state = passed_along(
        (pad_grad_inner[:, :margin], pad_grad_state[:, :margin]), "seq", -1
    )
    grad_inner_pre = jnp.concatenate(
        [pad_grad_inner[:, margin:-margin], pad_grad_inner[:, -margin:] + from_next_inner], axis=1
    )
    grad_state_part = jnp.concatenate(
        [pad_grad_state[:, margin:-margin], pad_grad_state[:, -margin:] + from_next_state], axis=1
    )
    grad_state_pre = lax.psum(grad_state_part, "tensor").astype(jnp.bfloat16)
    grad_inner_low = grad_inner_pre.astype(jnp.bfloat16)
    grad_step_low = grad_step_raw.astype(jnp.bfloat16)
    grad_normed = jnp.einsum(
        "srk,dk->srd", grad_gate_in, gate_full, preferred_element_type=jnp.float32
    )
    grad_normed = grad_normed + jnp.einsum(
        "srk,dk->srd", grad_inner_low, inner_full, preferred_element_type=jnp.float32
    )
    grad_normed = grad_normed + jnp.einsum(
        "srk,dk->srd", grad_step_low, step_full, preferred_element_type=jnp.float32
    )
    grad_rows = lax.psum_scatter(grad_normed, "tensor", scatter_dimension=1, tiled=True)
    own_rows = tokens.shape[1]
    state_mine = lax.dynamic_slice_in_dim(grad_state_pre, tensor_rank * own_rows, own_rows, 1)
    grad_rows = grad_rows + jnp.einsum(
        "srk,dk->srd", state_mine, state_full, preferred_element_type=jnp.float32
    )
    grad_gate_w = jnp.einsum(
        "srd,srk->dk", normed, grad_gate_in, preferred_element_type=jnp.float32
    )
    grad_inner_w = jnp.einsum(
        "srd,srk->dk", normed, grad_inner_low, preferred_element_type=jnp.float32
    )
    grad_state_w = jnp.einsum(
        "srd,srk->dk", normed, grad_state_pre, preferred_element_type=jnp.float32
    )
    grad_step_w = jnp.einsum(
        "srd,srk->dk", normed, grad_step_low, preferred_element_type=jnp.float32
    )
    shard_gate, shard_inner, shard_state, shard_step, shard_output = (
        lax.psum_scatter(grad_gate_w, ("dp", "seq"), scatter_dimension=0, tiled=True),
        lax.psum_scatter(grad_inner_w, ("dp", "seq"), scatter_dimension=0, tiled=True),
        lax.psum_scatter(grad_state_w, ("dp", "seq"), scatter_dimension=0, tiled=True),
        lax.psum_scatter(grad_step_w, ("dp", "seq"), scatter_dimension=0, tiled=True),
        lax.psum_scatter(grad_output, ("dp", "seq"), scatter_dimension=1, tiled=True),
    )
    scaled_in = grad_rows * input_gain
    grad_input_gain = jnp.sum(grad_rows * residual * rms_in, axis=(0, 1))
    grad_tokens = (
        cotangent.astype(jnp.float32)
        + rms_in * scaled_in
        - residual * rms_in**3 * jnp.mean(scaled_in * residual, axis=-1, keepdims=True)
    )

    def placed(whole, piece_grad, start, axis_number):
        return lax.dynamic_update_slice_in_dim(
            jnp.zeros_like(whole), piece_grad, start, axis_number
        )

    smalls = lax.psum(
        (
            grad_input_gain,
            placed(conv_inner, grad_kernel_here, chan_start, 1),
            placed(inner_bias, grad_bias_here, chan_start, 0),
            grad_conv_state,
            grad_state_bias,
            placed(step_bias, grad_shift_here, head_start, 0),
            placed(log_rates, grad_rates_here, head_start, 0),
            placed(skip_gain, grad_skip_here, head_start, 0),
            placed(gated_gain, grad_gain_here, chan_start, 0),
        ),
        ("dp", "seq", "tensor"),
    )
    return (
        block_out,
        grad_tokens,
        smalls[0],
        shard_gate,
        shard_inner,
        shard_state,
        shard_step,
        smalls[1],
        smalls[2],
        smalls[3],
        smalls[4],
        smalls[5],
        smalls[6],
        smalls[7],
        smalls[8],
        shard_output,
    )


def per_device_fast(
    tokens,
    segments,
    input_gain,
    gate_proj,
    inner_proj,
    state_proj,
    step_proj,
    conv_inner,
    inner_bias,
    conv_state,
    state_bias,
    step_bias,
    log_rates,
    skip_gain,
    gated_gain,
    output_proj,
    cotangent,
):
    tensor_count = lax.axis_size("tensor")
    tensor_rank = lax.axis_index("tensor")
    heads = step_proj.shape[1]
    gain_row = input_gain[None]
    normed, seg_old, s8, t8, i8 = gather_all(
        tensor_count, tokens, gain_row, segments, (state_proj, step_proj.T, inner_proj)
    )
    heads_param = jnp.pad(
        lax.dynamic_slice_in_dim(
            jnp.stack([step_bias, log_rates, skip_gain]), tensor_rank * heads, heads, 1
        ),
        ((0, 5), (0, LANES - heads)),
    )
    (
        y_part, u_inner, u_state, entry, incoming, gate_in, cot_rows, o8, g8,
        inner_low, state_low, prior_inner, prior_state, step_raw, rows,
    ) = mix_fwd(
        tensor_count, segments, seg_old, heads_param,
        conv_inner, inner_bias[None], conv_state, state_bias[None],
        cotangent, output_proj.T, gate_proj, normed, i8, s8, t8,
    )
    grad_mixed, grad_gate_in, outgoing_grad, partial_out, grad_output, grad_gate, grad_gain = gate_stage(
        tensor_count, y_part, u_state, entry, incoming, gate_in, cot_rows, o8, gated_gain[None], normed
    )
    (
        d_inner, d_state, d_step, sm_i, sm_s, sm_h, branch_rows, shard_output, shard_gate
    ) = mix_bwd(
        tensor_count, grad_mixed, u_inner, u_state, inner_low, prior_inner, state_low, prior_state,
        step_raw, rows, incoming, outgoing_grad, heads_param, conv_inner, conv_state,
        partial_out, grad_output, grad_gate,
    )
    grad_rows, shard_inner, shard_state, shard_step, sms = reduce_all(
        tensor_count, normed, grad_gate_in, d_inner, d_state, d_step, g8, i8, s8, t8, gain_row,
        sm_i, sm_s, sm_h, grad_gain,
    )
    outs = emit_all(
        tensor_count, heads, tokens, cotangent, gain_row, branch_rows, grad_rows,
        shard_gate, shard_inner, shard_state, shard_step, shard_output, sms,
    )
    flat = (2, 8, 10, 11, 12, 13, 14)
    return tuple(
        o[0] if i in flat else o.T if i in (6, 15) else o for i, o in enumerate(outs)
    )


def solution(mesh):
    fast = mesh.shape["dp"] == 4 and mesh.shape["seq"] == 2
    placed = (
        P("dp", ("seq", "tensor"), None),
        P("dp", "seq"),
        P(),
        P(("dp", "seq"), "tensor"),
        P(("dp", "seq"), "tensor"),
        P(("dp", "seq"), None),
        P(("dp", "seq"), "tensor"),
        P(),
        P(),
        P(),
        P(),
        P(),
        P(),
        P(),
        P(),
        P("tensor", ("dp", "seq")),
        P("dp", ("seq", "tensor"), None),
    )
    return jax.shard_map(
        per_device_fast if fast else per_device,
        mesh=mesh,
        in_specs=placed,
        out_specs=(
            P("dp", ("seq", "tensor"), None),
            P("dp", ("seq", "tensor"), None),
            P(),
            P(("dp", "seq"), "tensor"),
            P(("dp", "seq"), "tensor"),
            P(("dp", "seq"), None),
            P(("dp", "seq"), "tensor"),
            P(),
            P(),
            P(),
            P(),
            P(),
            P(),
            P(),
            P(),
            P("tensor", ("dp", "seq")),
        ),
        check_vma=False,
    )
```
